32 devices in a mesh: dp: 8 (over z, y), mp: 4 (over x, core).
Axes of the slice: x: 2, y: 2, z: 4, core: 2. Of those that a mesh axis runs over, the one named last changes fastest.
Arguments:
- tokens: bfloat16 [16384, 1024], P('dp'), may hold values from -6 to 6
- cotangent: bfloat16 [16384, 1024], P('dp'), may hold values from -6 to 6
- group_ids: int32 [16384], P('dp'), may hold values from 0 to 15
- pre_gain: bfloat16 [1024], replicated, may hold values from 0.5 to 1.5
- pre_shift: bfloat16 [1024], replicated, may hold values from -1.25 to 1.25
- frozen_triple_weight: bfloat16 [1024, 3, 1024], P('dp', None, 'mp'), may hold values from -0.1875 to 0.1875
- frozen_triple_bias: bfloat16 [3, 1024], P(None, 'mp'), may hold values from -1.25 to 1.25
- out_weight: bfloat16 [1024, 1024], P('mp', 'dp'), may hold values from -0.75 to 0.75
- out_bias: bfloat16 [1024], replicated, may hold values from -1.25 to 1.25
- mid_gain: bfloat16 [1024], replicated, may hold values from 0.099609375 to 1.8984375
- mid_shift: bfloat16 [1024], replicated, may hold values from -1.25 to 1.25
- fc_weight: bfloat16 [1024, 4096], P('dp', 'mp'), may hold values from -0.1875 to 0.1875
- fc_bias: bfloat16 [4096], P('mp'), may hold values from -1.25 to 1.25
- proj_weight: bfloat16 [4096, 1024], P('mp', 'dp'), may hold values from -0.09375 to 0.09375
- proj_bias: bfloat16 [1024], P('mp'), may hold values from -1.25 to 1.25
- down_master: float32 [2, 4, 1024], replicated, may hold values from -0.1875 to 0.1875
- up_master: float32 [2, 4, 1024], P(None, None, 'mp'), may hold values from -0.1875 to 0.1875
- down_first: float32 [2, 4, 1024], replicated, as said below
- down_second: float32 [2, 4, 1024], replicated, as said below
- up_first: float32 [2, 4, 1024], P(None, None, 'mp'), as said below
- up_second: float32 [2, 4, 1024], P(None, None, 'mp'), as said below
- learn_rate: float32 [], replicated, may hold values from 0.02 to 0.04
Outputs:
- output: bfloat16 [16384, 1024], P('dp', 'mp')
- input_grad: bfloat16 [16384, 1024], P('dp', 'mp')
- down_new: float32 [2, 4, 1024], replicated
- down_moment: float32 [2, 4, 1024], replicated
- down_square: float32 [2, 4, 1024], replicated
- down_copy: bfloat16 [2, 4, 1024], replicated
- up_new: float32 [2, 4, 1024], P(None, None, 'mp')
- up_moment: float32 [2, 4, 1024], P(None, None, 'mp')
- up_square: float32 [2, 4, 1024], P(None, None, 'mp')
- up_copy: bfloat16 [2, 4, 1024], P(None, None, 'mp')
The draws below stay inside these ranges and needn't reach their ends.
Inputs may be any that keep to these rules, and one draw needn't show every extreme that they name: `down_first`: first moments of the down maps, of both signs. `down_second`: second moments of the down maps, positive. `up_first`: first moments of the up maps, of both signs. `up_second`: second moments of the up maps, positive.
All inputs are finite; a program needn't handle non-finite values.
Results may differ from the reference program's by a relative error of at most 0.02.
Values may be sent and summed in bfloat16 or wider, within the bound.
No kernel may reach another device: no remote copies, remote signals or barrier semaphores. Data moves between devices by JAX's collectives and lax.ppermute only.
A program may use at most 192 MiB of HBM per device.

```python
import math
import jax
import jax.numpy as jnp
from jax import lax

MODEL_DIMENSION = 1024
HEADS = 16
HEAD_DIM = 64
FF = 4096
ADAPTER_RANK = 4
GROUPS = 16
STEP = 3
LEN = 1024
TOK_DEV = 2048
TOKENS = 16384
N_MP = 4


def draw_group_ids(key, part):
    key_wide, key_narrow, key_level = jax.random.split(key, 3)
    positions = jnp.arange(TOKENS, dtype=jnp.int32)
    owner = positions // TOK_DEV
    owners = TOKENS // TOK_DEV
    wide_ids = jax.random.randint(key_wide, (TOKENS,), 0, GROUPS, dtype=jnp.int32)
    narrow_ids = jax.random.randint(key_narrow, (TOKENS,), 0, GROUPS // 4, dtype=jnp.int32)
    level = jax.random.randint(key_level, (TOKENS,), 0, 1000, dtype=jnp.int32)
    limit = owner * 800 // max(owners - 1, 1)
    return jnp.where(level < limit, narrow_ids, wide_ids).astype(jnp.int32)


def moment_scale(query_size, value_size):
    root_tokens = jnp.sqrt(jnp.float32(TOKENS))
    query_part = jnp.full((1, ADAPTER_RANK, MODEL_DIMENSION), query_size, jnp.float32)
    value_part = jnp.full((1, ADAPTER_RANK, MODEL_DIMENSION), value_size, jnp.float32)
    return jnp.concatenate([query_part, value_part], axis=0) * root_tokens


def draw_first(key, query_size, value_size):
    return jax.random.normal(key, (2, ADAPTER_RANK, MODEL_DIMENSION), jnp.float32) * moment_scale(query_size, value_size)


def draw_second(key, query_size, value_size):
    scale = moment_scale(query_size, value_size)
    factor = jnp.exp(jax.random.uniform(key, (2, ADAPTER_RANK, MODEL_DIMENSION), jnp.float32, math.log(0.5), math.log(8.0)))
    return factor * scale * scale


def draw_down_first(key, part):
    return draw_first(jax.random.fold_in(key, 11), 3.0, 12.0)


def draw_down_second(key, part):
    return draw_second(jax.random.fold_in(key, 12), 3.0, 12.0)


def draw_up_first(key, part):
    return draw_first(jax.random.fold_in(key, 13), 5.0, 20.0)


def draw_up_second(key, part):
    return draw_second(jax.random.fold_in(key, 14), 5.0, 20.0)


def block_scale(rng, shape, pieces, least, top_value):
    def one(position, shards_of):
        draws = jax.random.uniform(jax.random.fold_in(jax.random.fold_in(rng, 6), position), (shards_of,), jnp.float32, least / len(pieces), top_value / len(pieces))
        return jnp.repeat(jnp.exp(draws), shape[position] // shards_of).reshape((-1,) + (1,) * (len(shape) - position - 1))

    level = one(*pieces[0])
    for cut in pieces[1:]:
        level = level * one(*cut)
    return level


def centred(rng, shape, deviation, most, cuts=(), held_as=jnp.bfloat16):
    array = jax.random.normal(rng, shape, jnp.float32) * deviation
    if len(cuts) > 0:
        array = block_scale(rng, shape, cuts, -0.22, 0.18) * array
    return jnp.clip(array, min=-most, max=most).astype(held_as)


def setup_inputs(seed: int = 0) -> dict:
    keys = jax.random.split(jax.random.key(seed), 23)
    return {
        "tokens": centred(keys[0], (TOKENS, MODEL_DIMENSION), 1.0, 6.0, ((0, 8),)),
        "cotangent": centred(keys[1], (TOKENS, MODEL_DIMENSION), 1.0, 6.0, ((0, 8),)),
        "group_ids": draw_group_ids(jax.random.fold_in(keys[22], 71), 0),
        "pre_gain": jnp.clip(1.0 + 0.1 * jax.random.normal(keys[3], (MODEL_DIMENSION,), jnp.float32), 0.5, 1.5).astype(jnp.bfloat16),
        "pre_shift": centred(keys[4], (MODEL_DIMENSION,), 0.2, 1.25),
        "frozen_triple_weight": centred(keys[5], (MODEL_DIMENSION, 3, MODEL_DIMENSION), MODEL_DIMENSION ** -0.5, 0.1875, ((0, 8), (2, 4))),
        "frozen_triple_bias": centred(keys[6], (3, MODEL_DIMENSION), 0.2, 1.25, ((1, 4),)),
        "out_weight": centred(keys[7], (MODEL_DIMENSION, MODEL_DIMENSION), (MODEL_DIMENSION // 16) ** -0.5, 0.75, ((0, 4), (1, 8))),
        "out_bias": centred(keys[8], (MODEL_DIMENSION,), 0.2, 1.25),
        "mid_gain": jnp.clip(1.0 + 0.18 * jax.random.normal(keys[9], (MODEL_DIMENSION,), jnp.float32), 0.099609375, 1.8984375).astype(jnp.bfloat16),
        "mid_shift": centred(keys[10], (MODEL_DIMENSION,), 0.2, 1.25),
        "fc_weight": centred(keys[11], (MODEL_DIMENSION, FF), MODEL_DIMENSION ** -0.5, 0.1875, ((0, 8), (1, 4))),
        "fc_bias": centred(keys[12], (FF,), 0.2, 1.25, ((0, 4),)),
        "proj_weight": centred(keys[13], (FF, MODEL_DIMENSION), FF ** -0.5, 0.09375, ((0, 4), (1, 8))),
        "proj_bias": centred(keys[14], (MODEL_DIMENSION,), 0.2, 1.25, ((0, 4),)),
        "down_master": centred(keys[15], (2, ADAPTER_RANK, MODEL_DIMENSION), MODEL_DIMENSION ** -0.5, 0.1875, (), jnp.float32),
        "up_master": centred(keys[16], (2, ADAPTER_RANK, MODEL_DIMENSION), 0.03, 0.1875, ((2, 4),), jnp.float32),
        "down_first": draw_down_first(jax.random.fold_in(keys[22], 71), 0),
        "down_second": draw_down_second(jax.random.fold_in(keys[22], 71), 0),
        "up_first": draw_up_first(jax.random.fold_in(keys[22], 71), 0),
        "up_second": draw_up_second(jax.random.fold_in(keys[22], 71), 0),
        "learn_rate": jnp.clip(jax.random.uniform(keys[21], (), jnp.float32, 0.02, 0.04), 0.02, 0.04),
    }


@jax.custom_vjp
def reduced_rank(v):
    return lax.optimization_barrier(v.astype(jnp.bfloat16)).astype(jnp.float32)

@jax.custom_vjp
def reduced_backward(v):
    return v

def low_keep(v):
    return (reduced_rank(v), None)

def low_pass(kept, grad):
    return (grad,)

def back_keep(v):
    return (v, None)

def back_low(kept, grad):
    return (reduced_rank(grad),)
reduced_rank.defvjp(low_keep, low_pass)
reduced_backward.defvjp(back_keep, back_low)
ADAPTER_SCALE = 8.0
NORM_EPS = 1e-05
MASKED = -1e+30
BETA_ONE = 0.5
BETA_TWO = 0.5
ADAM_EPS = 1e-08
DECAY = 0.01

def matrix_product(left, right):
    return jnp.dot(left, right, precision=lax.Precision.HIGHEST, preferred_element_type=jnp.float32)

def layer_norm(values, gain, shift):
    center = values - lax.optimization_barrier(jnp.mean(values, axis=-1, keepdims=True))
    spread = lax.optimization_barrier(jnp.mean(center * center, axis=-1, keepdims=True))
    return center * lax.rsqrt(spread + NORM_EPS) * gain + shift

def block_rows(rows, frozen, reduced_lower, reduced_raise):
    pre_gain, pre_shift, frozen_triple_weight, frozen_triple_bias, out_weight, out_bias, mid_gain, mid_shift, fc_weight, fc_bias, proj_weight, proj_bias = frozen
    row_count = rows.shape[0]
    packed = row_count // LEN
    head_cols = MODEL_DIMENSION // N_MP
    head_local = HEADS // N_MP
    unit_cols = FF // N_MP
    score_scale = HEAD_DIM ** (-0.5)
    allowed = jnp.arange(LEN, dtype=jnp.int32)[:, None] >= jnp.arange(LEN, dtype=jnp.int32)[None, :]
    adapter_input = reduced_lower.reshape(2 * ADAPTER_RANK, MODEL_DIMENSION)
    normed = reduced_rank(layer_norm(rows, pre_gain, pre_shift))
    attended_sum = jnp.zeros_like(rows)
    for section in range(N_MP):
        common_factor = reduced_backward(normed)
        column_begin = section * head_cols
        column_stop = column_begin + head_cols
        bottleneck = reduced_backward(reduced_rank(matrix_product(common_factor, adapter_input.T)))
        query_wide_float = matrix_product(common_factor, frozen_triple_weight[:, 0, column_begin:column_stop]) + frozen_triple_bias[0, column_begin:column_stop] + ADAPTER_SCALE * matrix_product(bottleneck[:, :ADAPTER_RANK], reduced_raise[0][:, column_begin:column_stop])
        key_f = matrix_product(common_factor, frozen_triple_weight[:, 1, column_begin:column_stop]) + frozen_triple_bias[1, column_begin:column_stop]
        value_wide_float = matrix_product(common_factor, frozen_triple_weight[:, 2, column_begin:column_stop]) + frozen_triple_bias[2, column_begin:column_stop] + ADAPTER_SCALE * matrix_product(bottleneck[:, ADAPTER_RANK:], reduced_raise[1][:, column_begin:column_stop])
        queries = reduced_backward(reduced_rank(query_wide_float)).reshape(packed, LEN, head_local, HEAD_DIM)
        key_rows = reduced_backward(reduced_rank(key_f)).reshape(packed, LEN, head_local, HEAD_DIM)
        value_rows = reduced_backward(reduced_rank(value_wide_float)).reshape(packed, LEN, head_local, HEAD_DIM)
        scores = jnp.einsum('sqhd,skhd->shqk', queries, key_rows, precision=lax.Precision.HIGHEST) * score_scale
        scores = reduced_backward(jnp.where(allowed[None, None], scores, MASKED))
        row_top = lax.optimization_barrier(jnp.max(scores, axis=-1, keepdims=True))
        exp_terms = jnp.exp(scores - row_top)
        probs = reduced_rank(exp_terms / lax.optimization_barrier(jnp.sum(exp_terms, axis=-1, keepdims=True)))
        mixed = jnp.einsum('shqk,skhd->sqhd', probs, value_rows, precision=lax.Precision.HIGHEST)
        mixed = reduced_backward(reduced_rank(mixed.reshape(row_count, head_cols)))
        attended_sum = attended_sum + reduced_backward(reduced_rank(matrix_product(mixed, out_weight[column_begin:column_stop, :])))
    hidden = rows + attended_sum + out_bias
    normed_mid = reduced_rank(layer_norm(hidden, mid_gain, mid_shift))
    unit_sum = jnp.zeros_like(rows)
    for section in range(N_MP):
        common_factor = reduced_backward(normed_mid)
        unit_start = section * unit_cols
        unit_end = unit_start + unit_cols
        pre_act = reduced_backward(matrix_product(common_factor, fc_weight[:, unit_start:unit_end]) + fc_bias[unit_start:unit_end])
        active = reduced_rank(jax.nn.gelu(pre_act, approximate=True))
        unit_sum = unit_sum + reduced_backward(reduced_rank(matrix_product(active, proj_weight[unit_start:unit_end, :])))
    return hidden + unit_sum + proj_bias

def adam_update(master, first, second, grad, step_value, learn_rate):
    new_first = BETA_ONE * first + (1.0 - BETA_ONE) * grad
    new_second = BETA_TWO * second + (1.0 - BETA_TWO) * grad * grad
    fix_one = 1.0 - jnp.power(jnp.float32(BETA_ONE), step_value)
    fix_two = 1.0 - jnp.power(jnp.float32(BETA_TWO), step_value)
    update = new_first / fix_one / (jnp.sqrt(new_second / fix_two) + ADAM_EPS)
    new_master = master - learn_rate * (update + DECAY * master)
    return (new_master, new_first, new_second)

def reference(tokens, cotangent, group_ids, pre_gain, pre_shift, frozen_triple_weight, frozen_triple_bias, out_weight, out_bias, mid_gain, mid_shift, fc_weight, fc_bias, proj_weight, proj_bias, down_master, up_master, down_first, down_second, up_first, up_second, learn_rate):
    frozen = tuple((array_item.astype(jnp.float32) for array_item in (pre_gain, pre_shift, frozen_triple_weight, frozen_triple_bias, out_weight, out_bias, mid_gain, mid_shift, fc_weight, fc_bias, proj_weight, proj_bias)))
    total_seqs = TOKENS // LEN
    packed = max((cand for cand in range(1, total_seqs + 1) if total_seqs % cand == 0 and cand * LEN <= 4096))

    def forward(inputs, down_matrix, up_matrix):
        reduced_lower = reduced_rank(down_matrix)
        reduced_raise = reduced_rank(up_matrix)
        blocks = inputs.reshape(total_seqs // packed, packed * LEN, MODEL_DIMENSION)

        def one_block(rows):
            return block_rows(rows, frozen, reduced_lower, reduced_raise)
        saved = jax.checkpoint(one_block)

        def scan_step(carry, rows):
            return (carry, saved(rows))
        _, results = lax.scan(scan_step, jnp.float32(0.0), blocks)
        return results.reshape(TOKENS, MODEL_DIMENSION)
    onehot = group_ids[:, None] == jnp.arange(GROUPS, dtype=jnp.int32)[None, :]
    totals = lax.optimization_barrier(jnp.sum(onehot.astype(jnp.int32), axis=0)).astype(jnp.float32)
    own_count = lax.optimization_barrier(jnp.sum(jnp.where(onehot, totals[None, :], jnp.float32(0.0)), axis=1))
    token_weight = jnp.float32(TOKENS) / (GROUPS * own_count)
    out_grad = cotangent.astype(jnp.float32) * token_weight[:, None]
    result, pullback = jax.vjp(forward, tokens.astype(jnp.float32), down_master, up_master)
    input_grad, down_grad, up_grad = pullback(out_grad)
    step_value = jnp.float32(STEP)
    down_new, down_moment, down_square = adam_update(down_master, down_first, down_second, down_grad, step_value, learn_rate)
    up_new, up_moment, up_square = adam_update(up_master, up_first, up_second, up_grad, step_value, learn_rate)
    return (result.astype(jnp.bfloat16), input_grad.astype(jnp.bfloat16), down_new, down_moment, down_square, down_new.astype(jnp.bfloat16), up_new, up_moment, up_square, up_new.astype(jnp.bfloat16))
```

```python
import jax
import jax.numpy as jnp
from jax import lax
from jax.experimental import pallas as pl
from jax.experimental.pallas import tpu as pltpu
from jax.sharding import PartitionSpec as P

HEAD_DIM = 64
ADAPTER_RANK = 4
GROUPS = 16
STEP = 3
MICRO = 2


ADAPTER_SCALE = 8.0
NORM_EPS = 1e-05
MASKED = -1e30
BETA_ONE = 0.5
BETA_TWO = 0.5
ADAM_EPS = 1e-08
DECAY = 0.01


def layer_stats(values):
    center = values - jnp.mean(values, axis=-1, keepdims=True)
    spread = jnp.mean(center * center, axis=-1, keepdims=True)
    scaler = lax.rsqrt(spread + NORM_EPS)
    return (center * scaler, scaler)


def norm_back(normal_hat, scaler, scaled_grad):
    first_mean = jnp.mean(scaled_grad, axis=-1, keepdims=True)
    second_mean = jnp.mean(scaled_grad * normal_hat, axis=-1, keepdims=True)
    return scaler * (scaled_grad - first_mean - normal_hat * second_mean)


def gelu_tanh(values):
    return jax.nn.gelu(values, approximate=True)


def fetch_frozen(frozen_triple_weight, fc_weight, out_weight, proj_weight):
    return (
        lax.all_gather(frozen_triple_weight, "dp", axis=0, tiled=True),
        lax.all_gather(fc_weight, "dp", axis=0, tiled=True),
        lax.all_gather(out_weight, "dp", axis=1, tiled=True),
        lax.all_gather(proj_weight, "dp", axis=1, tiled=True),
    )


def score_block(query_part, key_heads, start, block_rows, key_count):
    score_scale = HEAD_DIM ** (-0.5)
    scores = (
        jnp.einsum("qhd,khd->hqk", query_part, key_heads, preferred_element_type=jnp.float32)
        * score_scale
    )
    allowed = (start + jnp.arange(block_rows, dtype=jnp.int32))[:, None] >= jnp.arange(
        key_count, dtype=jnp.int32
    )[None, :]
    return jnp.where(allowed[None], scores, MASKED)


def attend(queries, key_rows, value_rows):
    length, col_width = queries.shape
    head_count = col_width // HEAD_DIM
    block_rows = min(512, length)
    query_heads = queries.reshape(length, head_count, HEAD_DIM)
    key_heads = key_rows.reshape(length, head_count, HEAD_DIM)
    value_heads = value_rows.reshape(length, head_count, HEAD_DIM)
    mixed_parts = []
    logsum_parts = []
    for index in range(length // block_rows):
        start = index * block_rows
        stop = start + block_rows
        query_part = query_heads[start:stop]
        scores = score_block(query_part, key_heads[:stop], start, block_rows, stop)
        row_top = jnp.max(scores, axis=-1, keepdims=True)
        exp_terms = jnp.exp(scores - row_top)
        row_total = jnp.sum(exp_terms, axis=-1, keepdims=True)
        probs = (exp_terms / row_total).astype(jnp.bfloat16)
        mixed = jnp.einsum(
            "hqk,khd->qhd", probs, value_heads[:stop], preferred_element_type=jnp.float32
        )
        mixed_parts.append(mixed.reshape(block_rows, col_width))
        logsum_parts.append((row_top + jnp.log(row_total))[..., 0])
    return (jnp.concatenate(mixed_parts, axis=0), logsum_parts)


def attend_back(queries, key_rows, value_rows, logsum, mixed_grad):
    length, col_width = queries.shape
    head_count = col_width // HEAD_DIM
    block_rows = min(512, length)
    score_scale = HEAD_DIM ** (-0.5)
    query_heads = queries.reshape(length, head_count, HEAD_DIM)
    key_heads = key_rows.reshape(length, head_count, HEAD_DIM)
    value_heads = value_rows.reshape(length, head_count, HEAD_DIM)
    grad_heads = mixed_grad.reshape(length, head_count, HEAD_DIM)
    key_acc = jnp.zeros((length, head_count, HEAD_DIM), jnp.float32)
    value_acc = jnp.zeros((length, head_count, HEAD_DIM), jnp.float32)
    query_parts = []
    for index in range(length // block_rows):
        start = index * block_rows
        stop = start + block_rows
        query_part = query_heads[start:stop]
        grad_part = grad_heads[start:stop]
        key_part = key_heads[:stop]
        scores = score_block(query_part, key_part, start, block_rows, stop)
        probs = jnp.exp(scores - logsum[index][:, :, None])
        prob_grad = jnp.einsum(
            "qhd,khd->hqk", grad_part, value_heads[:stop], preferred_element_type=jnp.float32
        )
        inner = jnp.sum(prob_grad * probs, axis=-1, keepdims=True)
        score_grad = (probs * (prob_grad - inner)).astype(jnp.bfloat16)
        query_grad = (
            jnp.einsum("hqk,khd->qhd", score_grad, key_part, preferred_element_type=jnp.float32)
            * score_scale
        )
        key_acc = key_acc.at[:stop].add(
            jnp.einsum("hqk,qhd->khd", score_grad, query_part, preferred_element_type=jnp.float32)
            * score_scale
        )
        value_acc = value_acc.at[:stop].add(
            jnp.einsum(
                "hqk,qhd->khd",
                probs.astype(jnp.bfloat16),
                grad_part,
                preferred_element_type=jnp.float32,
            )
        )
        query_parts.append(query_grad.reshape(block_rows, col_width))
    return (
        jnp.concatenate(query_parts, axis=0),
        key_acc.reshape(length, col_width),
        value_acc.reshape(length, col_width),
    )


def adam_update(master, first, second, grad, step_value, learn_rate):
    new_first = BETA_ONE * first + (1.0 - BETA_ONE) * grad
    new_second = BETA_TWO * second + (1.0 - BETA_TWO) * grad * grad
    fix_one = 1.0 - jnp.power(jnp.float32(BETA_ONE), step_value)
    fix_two = 1.0 - jnp.power(jnp.float32(BETA_TWO), step_value)
    update = new_first / fix_one / (jnp.sqrt(new_second / fix_two) + ADAM_EPS)
    new_master = master - learn_rate * (update + DECAY * master)
    return (new_master, new_first, new_second)


def on_device_general(
    tokens,
    cotangent,
    group_ids,
    pre_gain,
    pre_shift,
    frozen_triple_weight,
    frozen_triple_bias,
    out_weight,
    out_bias,
    mid_gain,
    mid_shift,
    fc_weight,
    fc_bias,
    proj_weight,
    proj_bias,
    down_master,
    up_master,
    down_first,
    down_second,
    up_first,
    up_second,
    learn_rate,
):
    tok_dev = tokens.shape[0]
    model_width = tokens.shape[1]
    length = tok_dev // MICRO
    shard_width = model_width // lax.axis_size("mp")
    shard_start = lax.axis_index("mp") * shard_width
    pre_gain_f = pre_gain.astype(jnp.float32)
    pre_shift_f = pre_shift.astype(jnp.float32)
    mid_gain_f = mid_gain.astype(jnp.float32)
    mid_shift_f = mid_shift.astype(jnp.float32)
    out_bias_f = out_bias.astype(jnp.float32)
    fc_bias_f = fc_bias.astype(jnp.float32)
    proj_bias_f = proj_bias.astype(jnp.float32)
    bias_flat = frozen_triple_bias.astype(jnp.float32).reshape(-1)
    onehot = group_ids[:, None] == jnp.arange(GROUPS, dtype=jnp.int32)[None, :]
    local_counts = jnp.sum(onehot.astype(jnp.int32), axis=0)
    totals = lax.psum(local_counts, "dp").astype(jnp.float32)
    own_count = jnp.sum(jnp.where(onehot, totals[None, :], jnp.float32(0.0)), axis=1)
    token_weight = jnp.float32(tok_dev * lax.axis_size("dp")) / (GROUPS * own_count)
    down_low = down_master.astype(jnp.bfloat16).reshape(2 * ADAPTER_RANK, model_width)
    raise_reduced = up_master.astype(jnp.bfloat16)
    grad_down = jnp.zeros((2 * ADAPTER_RANK, model_width), jnp.float32)
    raise_gradient = jnp.zeros(up_master.shape, jnp.float32)
    output_parts = []
    input_parts = []
    for micro_index in range(MICRO):
        current = fetch_frozen(frozen_triple_weight, fc_weight, out_weight, proj_weight)
        qkv_full, fc_full, out_full, proj_full = current
        qkv_flat = qkv_full.reshape(model_width, -1)
        head_width = qkv_flat.shape[1] // 3
        row_start = micro_index * length
        rows_f = lax.dynamic_slice_in_dim(tokens, row_start, length, 0).astype(jnp.float32)
        pre_hat, pre_scale = layer_stats(rows_f)
        normed = (pre_hat * pre_gain_f + pre_shift_f).astype(jnp.bfloat16)
        mixed_proj = jnp.dot(normed, qkv_flat, preferred_element_type=jnp.float32) + bias_flat
        bottleneck = jnp.einsum(
            "td,rd->tr", normed, down_low, preferred_element_type=jnp.float32
        ).astype(jnp.bfloat16)
        queries = (
            mixed_proj[:, :head_width]
            + ADAPTER_SCALE
            * jnp.dot(
                bottleneck[:, :ADAPTER_RANK], raise_reduced[0], preferred_element_type=jnp.float32
            )
        ).astype(jnp.bfloat16)
        key_rows = mixed_proj[:, head_width : 2 * head_width].astype(jnp.bfloat16)
        value_rows = (
            mixed_proj[:, 2 * head_width :]
            + ADAPTER_SCALE
            * jnp.dot(
                bottleneck[:, ADAPTER_RANK:], raise_reduced[1], preferred_element_type=jnp.float32
            )
        ).astype(jnp.bfloat16)
        attended, logsum = attend(queries, key_rows, value_rows)
        attended_low = attended.astype(jnp.bfloat16)
        head_term = jnp.dot(attended_low, out_full, preferred_element_type=jnp.float32).astype(
            jnp.bfloat16
        )
        attn_sum = lax.psum(head_term, "mp").astype(jnp.float32)
        hidden = rows_f + attn_sum + out_bias_f
        mid_hat, mid_scale = layer_stats(hidden)
        normed_mid = (mid_hat * mid_gain_f + mid_shift_f).astype(jnp.bfloat16)
        pre_act = jnp.dot(normed_mid, fc_full, preferred_element_type=jnp.float32) + fc_bias_f
        active, gelu_pullback = jax.vjp(gelu_tanh, pre_act)
        unit_part = jnp.dot(
            active.astype(jnp.bfloat16), proj_full, preferred_element_type=jnp.float32
        ).astype(jnp.bfloat16)
        unit_share = lax.psum_scatter(unit_part, "mp", scatter_dimension=1, tiled=True).astype(
            jnp.float32
        )
        hidden_share = lax.dynamic_slice_in_dim(hidden, shard_start, shard_width, 1)
        output_parts.append((hidden_share + unit_share + proj_bias_f).astype(jnp.bfloat16))
        weight_rows = lax.dynamic_slice_in_dim(token_weight, row_start, length, 0)
        out_grad = (
            lax.dynamic_slice_in_dim(cotangent, row_start, length, 0).astype(jnp.float32)
            * weight_rows[:, None]
        )
        out_low = out_grad.astype(jnp.bfloat16)
        active_grad = jnp.einsum(
            "td,fd->tf", out_low, proj_full, preferred_element_type=jnp.float32
        )
        pre_grad = gelu_pullback(active_grad)[0].astype(jnp.bfloat16)
        mid_part = jnp.einsum(
            "tf,df->td", pre_grad, fc_full, preferred_element_type=jnp.float32
        ).astype(jnp.bfloat16)
        mid_grad = lax.psum(mid_part, "mp").astype(jnp.float32)
        hidden_grad = out_grad + norm_back(mid_hat, mid_scale, mid_gain_f * mid_grad)
        hidden_low = hidden_grad.astype(jnp.bfloat16)
        attended_grad = jnp.einsum(
            "td,hd->th", hidden_low, out_full, preferred_element_type=jnp.float32
        ).astype(jnp.bfloat16)
        query_grad, key_grad, value_grad = attend_back(
            queries, key_rows, value_rows, logsum, attended_grad
        )
        query_low = query_grad.astype(jnp.bfloat16)
        key_low = key_grad.astype(jnp.bfloat16)
        value_low = value_grad.astype(jnp.bfloat16)
        proj_grad = jnp.concatenate([query_low, key_low, value_low], axis=1)
        in_part = jnp.einsum("tc,dc->td", proj_grad, qkv_flat, preferred_element_type=jnp.float32)
        bottleneck_gradient = ADAPTER_SCALE * jnp.concatenate(
            [
                jnp.einsum(
                    "tc,rc->tr", query_low, raise_reduced[0], preferred_element_type=jnp.float32
                ),
                jnp.einsum(
                    "tc,rc->tr", value_low, raise_reduced[1], preferred_element_type=jnp.float32
                ),
            ],
            axis=1,
        )
        latent_low = bottleneck_gradient.astype(jnp.bfloat16)
        in_part = (
            in_part + jnp.dot(latent_low, down_low, preferred_element_type=jnp.float32)
        ).astype(jnp.bfloat16)
        grad_down = grad_down + jnp.einsum(
            "tr,td->rd", latent_low, normed, preferred_element_type=jnp.float32
        )
        raise_gradient = raise_gradient + ADAPTER_SCALE * jnp.stack(
            [
                jnp.einsum(
                    "tr,tc->rc",
                    bottleneck[:, :ADAPTER_RANK],
                    query_low,
                    preferred_element_type=jnp.float32,
                ),
                jnp.einsum(
                    "tr,tc->rc",
                    bottleneck[:, ADAPTER_RANK:],
                    value_low,
                    preferred_element_type=jnp.float32,
                ),
            ],
            axis=0,
        )
        hidden_grad_share = lax.dynamic_slice_in_dim(hidden_grad, shard_start, shard_width, 1)
        in_grad = lax.psum(in_part, "mp").astype(jnp.float32)
        full_grad = norm_back(pre_hat, pre_scale, pre_gain_f * in_grad)
        input_parts.append(
            (
                hidden_grad_share + lax.dynamic_slice_in_dim(full_grad, shard_start, shard_width, 1)
            ).astype(jnp.bfloat16)
        )
    output = jnp.concatenate(output_parts, axis=0)
    input_grad = jnp.concatenate(input_parts, axis=0)
    down_grad = lax.psum(grad_down, ("dp", "mp")).reshape(down_master.shape)
    up_grad = lax.psum(raise_gradient, "dp")
    step_value = jnp.float32(STEP)
    down_new, down_moment, down_square = adam_update(
        down_master, down_first, down_second, down_grad, step_value, learn_rate
    )
    up_new, up_moment, up_square = adam_update(
        up_master, up_first, up_second, up_grad, step_value, learn_rate
    )
    return (
        output,
        input_grad,
        down_new,
        down_moment,
        down_square,
        down_new.astype(jnp.bfloat16),
        up_new,
        up_moment,
        up_square,
        up_new.astype(jnp.bfloat16),
    )


LEN = 1024
BLK = 256
LANES = 128
LOG2E = 1.4426950408889634
NT = (((1,), (1,)), ((), ()))
TN = (((0,), (0,)), ((), ()))
VMEM_LIMIT = 60 << 20
F32 = jnp.float32
BF16 = jnp.bfloat16
AXES = ("dp", "mp")
ANY = pl.BlockSpec(memory_space=pl.ANY)


def cost(flops, nbytes, trans=0):
    return pl.CostEstimate(flops=int(flops), bytes_accessed=int(nbytes), transcendentals=int(trans))


def shape(rows, cols, dtype=BF16):
    return jax.ShapeDtypeStruct((rows, cols), dtype)


def full(rows, cols):
    return pl.BlockSpec((rows, cols), lambda i, ix: (0, 0))


def call(body, name, grid, in_specs, out_specs, out_shape, scratch, est):
    return pl.pallas_call(
        body,
        grid_spec=pltpu.PrefetchScalarGridSpec(
            num_scalar_prefetch=1,
            grid=(grid,),
            in_specs=in_specs,
            out_specs=out_specs,
            scratch_shapes=scratch,
        ),
        out_shape=out_shape,
        compiler_params=pltpu.CompilerParams(vmem_limit_bytes=VMEM_LIMIT),
        cost_estimate=est,
        name=name,
    )


def hop(value, half_bit, dp_bits):
    ranks = lax.axis_size("mp") // 2
    width = lax.axis_size("mp")
    total = lax.axis_size("dp") * width
    flip = dp_bits * width + half_bit * ranks
    return lax.ppermute(value, AXES, [(i, i ^ flip) for i in range(total)])


def core_swap(value):
    total = lax.axis_size("dp") * lax.axis_size("mp")
    return lax.ppermute(value, AXES, [(i, i ^ 1) for i in range(total)])


def after(value, *others):
    return lax.optimization_barrier((value, *others))[0]


def gather_blocks(own, heavy):
    zs = [hop(own, 0, 2 * c) for c in (1, 2, 3)]
    far = jnp.stack(zs)
    x0, y0 = hop(own, 1, 0), hop(own, 0, 1)
    x3, y3 = hop(far, 1, 0), hop(far, 0, 1)
    if heavy == "x":
        d0 = hop(x0, 0, 1)
        d3 = hop(y3, 1, 0)
    else:
        d0 = hop(y0, 1, 0)
        d3 = hop(x3, 0, 1)
    found = [(own, None, 0, 0), (x0, None, 1, 0), (y0, None, 0, 1), (d0, None, 1, 1)]
    for c in (1, 2, 3):
        found += [(far, c - 1, 0, 2 * c), (x3, c - 1, 1, 2 * c), (y3, c - 1, 0, 2 * c + 1), (d3, c - 1, 1, 2 * c + 1)]
    return found


def operands(found):
    arrays = []
    table = []
    for array, slot, half_bit, dp_bits in found:
        for k, held in enumerate(arrays):
            if held is array:
                break
        else:
            k = len(arrays)
            arrays.append(array)
        table.append((k, slot, half_bit, dp_bits))
    return arrays, table


def block_of(refs, entry):
    k, slot, _, _ = entry
    return refs[k] if slot is None else refs[k].at[slot]


def load_all(pairs, sems):
    copies = [pltpu.make_async_copy(src, dst, sems.at[n]) for n, (src, dst) in enumerate(pairs)]
    for copy in copies:
        copy.start()
    for copy in copies:
        copy.wait()


def at_rows(index, size):
    return pl.ds(pl.multiple_of(index * size, size), size)


def pick(low, value, which):
    zero = jnp.zeros((), value.dtype)
    return jnp.where(low, value, zero) if which == 0 else jnp.where(low, zero, value)


def row_stats(values):
    center = values - jnp.mean(values, axis=-1, keepdims=True)
    scaler = lax.rsqrt(jnp.mean(center * center, axis=-1, keepdims=True) + NORM_EPS)
    return center * scaler, scaler


def token_weights(ids, table):
    lanes = lax.broadcasted_iota(jnp.int32, (ids.shape[0], LANES), 1)
    return jnp.sum(jnp.where(ids == lanes, table, 0.0), axis=-1, keepdims=True)


def project_heads(idx, tokens, gain, shift, bias, down, up, found):
    model = tokens.shape[1]
    arrays, table = operands(found)
    step_rows, cols = found[0][0].shape
    part = cols // 3
    n = len(arrays)

    def body(ix, tok, gain_ref, shift_ref, bias_ref, down_ref, up_ref, *rest):
        msgs = rest[:n]
        q_ref, k_ref, v_ref, normed_ref, latent_ref, w, sems = rest[n:]

        @pl.when(pl.program_id(0) == 0)
        def _():
            load_all(
                [(block_of(msgs, e), w.at[e[2], at_rows(ix[0] ^ e[3], step_rows), :]) for e in table],
                sems,
            )

        hat, _ = row_stats(tok[...].astype(F32))
        normed = (hat * gain_ref[...] + shift_ref[...]).astype(BF16)
        normed_ref[...] = normed
        latent = lax.dot_general(normed, down_ref[...], NT, preferred_element_type=F32).astype(BF16)
        latent_ref[...] = latent
        for a in range(2):
            r = jnp.dot(normed, w[a], preferred_element_type=F32) + bias_ref[a : a + 1, :]
            r = r + jnp.dot(latent, up_ref[a], preferred_element_type=F32)
            for out, s in ((q_ref, 0), (k_ref, 1), (v_ref, 2)):
                out[:, a * part : (a + 1) * part] = r[:, s * part : (s + 1) * part].astype(BF16)

    row = pl.BlockSpec((BLK, 2 * part), lambda i, ix: (i, 0))
    blocks = LEN // BLK
    return call(
        body,
        "project_heads",
        blocks,
        [
            pl.BlockSpec((BLK, model), lambda i, ix: (ix[1] * blocks + i, 0)),
            full(1, model),
            full(1, model),
            full(2, cols),
            full(LANES, model),
            pl.BlockSpec((2, LANES, cols), lambda i, ix: (0, 0, 0)),
        ]
        + [ANY] * n,
        [row, row, row, pl.BlockSpec((BLK, model), lambda i, ix: (i, 0)), pl.BlockSpec((BLK, LANES), lambda i, ix: (i, 0))],
        [shape(LEN, 2 * part)] * 3 + [shape(LEN, model), shape(LEN, LANES)],
        [pltpu.VMEM((2, model, cols), BF16), pltpu.SemaphoreType.DMA((len(table),))],
        cost(4 * LEN * model * cols, 16 * LEN * model),
    )(idx, tokens, gain, shift, bias, down, up, *arrays)


def attend_fast(queries, key_rows, value_rows):
    length, width = queries.shape
    pairs = width // LANES

    def body(q_ref, k_ref, v_ref, o_ref, lse_ref):
        scale = HEAD_DIM**-0.5 * LOG2E
        low = lax.broadcasted_iota(jnp.int32, (1, LANES), 1) < HEAD_DIM
        k = k_ref[...]
        v = v_ref[...]
        value_of = [pick(low, v, h) for h in range(2)]
        for i in range(length // BLK):
            stop = (i + 1) * BLK
            qb = q_ref[i * BLK : stop, :]
            causal = (lax.broadcasted_iota(jnp.int32, (BLK, stop), 0) + i * BLK) >= lax.broadcasted_iota(
                jnp.int32, (BLK, stop), 1
            )
            out = jnp.zeros((BLK, LANES), F32)
            logs = []
            for h in range(2):
                s = lax.dot_general(pick(low, qb, h), k[:stop], NT, preferred_element_type=F32) * scale
                s = jnp.where(causal, s, MASKED)
                top = jnp.max(s, axis=-1, keepdims=True)
                p = jnp.exp2(s - top)
                total = jnp.sum(p, axis=-1, keepdims=True)
                probs = (p * (1.0 / total)).astype(BF16)
                out = out + jnp.dot(probs, value_of[h][:stop], preferred_element_type=F32)
                logs.append(top + jnp.log2(total))
            o_ref[i * BLK : stop, :] = out.astype(BF16)
            both = jnp.where(
                low, jnp.broadcast_to(logs[0], (BLK, LANES)), jnp.broadcast_to(logs[1], (BLK, LANES))
            ).T
            lse_ref[0, 0:1, i * BLK : stop] = both[0:1]
            lse_ref[0, 1:2, i * BLK : stop] = both[HEAD_DIM : HEAD_DIM + 1]

    spec = pl.BlockSpec((length, LANES), lambda i: (0, i))
    return pl.pallas_call(
        body,
        grid=(pairs,),
        out_shape=(shape(length, width), jax.ShapeDtypeStruct((pairs, 8, length), F32)),
        in_specs=[spec] * 3,
        out_specs=(spec, pl.BlockSpec((1, 8, length), lambda i: (i, 0, 0))),
        compiler_params=pltpu.CompilerParams(vmem_limit_bytes=VMEM_LIMIT),
        cost_estimate=cost(8 * length * length * width, 8 * length * width, 2 * pairs * length * length),
        name="attend",
    )(queries, key_rows, value_rows)


def out_weight_pairs(msgs, table, w, ix, first_row):
    pairs = []
    rows, cols = w.shape[0] // 2, LANES
    for e in table:
        src = block_of(msgs, e).at[pl.ds(first_row, rows), :]
        pairs.append((src, w.at[pl.ds(e[2] * rows, rows), at_rows(ix[0] ^ e[3], cols)]))
    return pairs


def attention_out_send(idx, attended, found, first_row):
    width = attended.shape[1]
    arrays, table = operands(found)
    n = len(arrays)
    model = LANES * len(table) // 2
    half_blocks = LEN // BLK // 2

    def body(ix, att, *rest):
        msgs = rest[:n]
        out, w, sems = rest[n:]

        @pl.when(pl.program_id(0) == 0)
        def _():
            load_all(out_weight_pairs(msgs, table, w, ix, first_row), sems)

        out[...] = jnp.dot(att[...], w[...], preferred_element_type=F32).astype(BF16)

    return call(
        body,
        "attention_out_send",
        half_blocks,
        [pl.BlockSpec((BLK, width), lambda i, ix: ((1 - ix[2]) * half_blocks + i, 0))] + [ANY] * n,
        pl.BlockSpec((BLK, model), lambda i, ix: (i, 0)),
        shape(LEN // 2, model),
        [pltpu.VMEM((width, model), BF16), pltpu.SemaphoreType.DMA((len(table),))],
        cost(LEN * width * model, 2 * LEN * model),
    )(idx, attended, *arrays)


def attention_out_own(idx, attended, received, tokens, out_bias, gain, shift, found, first_row):
    width = attended.shape[1]
    arrays, table = operands(found)
    n = len(arrays)
    model = LANES * len(table) // 2
    half_blocks = LEN // BLK // 2

    def body(ix, att, recv, tok, bias_ref, gain_ref, shift_ref, *rest):
        msgs = rest[:n]
        hidden_ref, normed_ref, w, sems = rest[n:]

        @pl.when(pl.program_id(0) == 0)
        def _():
            load_all(out_weight_pairs(msgs, table, w, ix, first_row), sems)

        term = jnp.dot(att[...], w[...], preferred_element_type=F32)
        hidden = tok[...].astype(F32) + term + recv[...].astype(F32) + bias_ref[...]
        hidden_ref[...] = hidden
        hat, _ = row_stats(hidden)
        normed_ref[...] = (hat * gain_ref[...] + shift_ref[...]).astype(BF16)

    row = pl.BlockSpec((BLK, model), lambda i, ix: (i, 0))
    return call(
        body,
        "attention_out_own",
        half_blocks,
        [
            pl.BlockSpec((BLK, width), lambda i, ix: (ix[2] * half_blocks + i, 0)),
            row,
            pl.BlockSpec((BLK, model), lambda i, ix: ((2 * ix[1] + ix[2]) * half_blocks + i, 0)),
            full(1, model),
            full(1, model),
            full(1, model),
        ]
        + [ANY] * n,
        [row, row],
        [shape(LEN // 2, model, F32), shape(LEN // 2, model)],
        [pltpu.VMEM((width, model), BF16), pltpu.SemaphoreType.DMA((len(table),))],
        cost(LEN * width * model, 5 * LEN * model),
    )(idx, attended, received, tokens, out_bias, gain, shift, *arrays)


def expand_units(idx, own, other, bias, found):
    model = own.shape[1]
    arrays, table = operands(found)
    n = len(arrays)
    step_rows, part = found[0][0].shape
    units = 2 * part
    half_blocks = LEN // BLK // 2
    chunk = 512
    c0 = 0.7978845608028654
    c1 = 0.044715

    def body(ix, own_ref, other_ref, bias_ref, *rest):
        msgs = rest[:n]
        active_ref, slope_ref, w, sems = rest[n:]
        step = pl.program_id(0)

        @pl.when(step == 0)
        def _():
            load_all(
                [
                    (block_of(msgs, e), w.at[at_rows(ix[0] ^ e[3], step_rows), pl.ds(e[2] * part, part)])
                    for e in table
                ],
                sems,
            )

        rows = jnp.where(step < half_blocks, own_ref[...], other_ref[...])
        for c in range(units // chunk):
            cols = slice(c * chunk, (c + 1) * chunk)
            x = jnp.dot(rows, w[:, cols], preferred_element_type=F32) + bias_ref[:, cols]
            sq = x * x
            th = jnp.tanh(c0 * x * (1.0 + c1 * sq))
            left = 0.5 * (1.0 + th)
            active_ref[:, cols] = (x * left).astype(BF16)
            slope_ref[:, cols] = (left + 0.5 * x * (1.0 - th * th) * (c0 + (3.0 * c0 * c1) * sq)).astype(BF16)

    row = pl.BlockSpec((BLK, units), lambda i, ix: (i, 0))
    return call(
        body,
        "expand_units",
        2 * half_blocks,
        [
            pl.BlockSpec((BLK, model), lambda i, ix: (jnp.minimum(i, half_blocks - 1), 0)),
            pl.BlockSpec((BLK, model), lambda i, ix: (jnp.maximum(i - half_blocks, 0), 0)),
            full(1, units),
        ]
        + [ANY] * n,
        [row, row],
        [shape(LEN, units)] * 2,
        [pltpu.VMEM((model, units), BF16), pltpu.SemaphoreType.DMA((len(table),))],
        cost(2 * LEN * units * model, 6 * LEN * units, LEN * units),
    )(idx, own, other, bias, *arrays)


def proj_pairs(msgs, table, w, ix):
    rows = w.shape[0] // 2
    return [
        (
            block_of(msgs, e).at[pl.ds(0, rows), :],
            w.at[pl.ds(e[2] * rows, rows), at_rows(ix[0] ^ e[3], LANES)],
        )
        for e in table
    ]


def units_back(idx, mine, cotangent, ids, weight_table, slope, fc_found, proj_found):
    model = cotangent.shape[1]
    units = slope.shape[1]
    fc_arrays, fc_table = operands(fc_found)
    pj_arrays, pj_table = operands(proj_found)
    nf, np_ = len(fc_arrays), len(pj_arrays)
    step_rows, part = fc_found[0][0].shape
    half_blocks = LEN // BLK // 2
    chunk = 512
    first = 0 if mine else half_blocks

    def body(ix, cot, ids_ref, table_ref, slope_ref, *rest):
        fmsgs, pmsgs = rest[:nf], rest[nf : nf + np_]
        out, fc_w, pj_w, sems = rest[nf + np_ :]

        @pl.when(pl.program_id(0) == 0)
        def _():
            load_all(
                proj_pairs(pmsgs, pj_table, pj_w, ix)
                + [
                    (block_of(fmsgs, e), fc_w.at[at_rows(ix[0] ^ e[3], step_rows), pl.ds(e[2] * part, part)])
                    for e in fc_table
                ],
                sems,
            )

        weight = token_weights(ids_ref[...], table_ref[...])
        grad = (cot[...].astype(F32) * weight).astype(BF16)
        total = jnp.zeros((BLK, model), F32)
        for c in range(units // chunk):
            cols = slice(c * chunk, (c + 1) * chunk)
            up = lax.dot_general(grad, pj_w[cols, :], NT, preferred_element_type=F32)
            pre = (up * slope_ref[:, cols].astype(F32)).astype(BF16)
            total = total + lax.dot_general(pre, fc_w[:, cols], NT, preferred_element_type=F32)
        out[...] = total.astype(out.dtype)

    def token_rows(i, ix):
        rank = ix[2] if mine else 1 - ix[2]
        return ((2 * ix[1] + rank) * half_blocks + i, 0)

    return call(
        body,
        "units_back_own" if mine else "units_back_send",
        half_blocks,
        [
            pl.BlockSpec((BLK, model), token_rows),
            pl.BlockSpec((BLK, 1), token_rows),
            full(1, LANES),
            pl.BlockSpec((BLK, units), lambda i, ix: (first + i, 0)),
        ]
        + [ANY] * (nf + np_),
        pl.BlockSpec((BLK, model), lambda i, ix: (i, 0)),
        shape(LEN // 2, model, F32 if mine else BF16),
        [
            pltpu.VMEM((model, units), BF16),
            pltpu.VMEM((units, model), BF16),
            pltpu.SemaphoreType.DMA((len(fc_table) + len(pj_table),)),
        ],
        cost(2 * LEN * units * model, 4 * units * model),
    )(idx, cotangent, ids, weight_table, slope, *fc_arrays, *pj_arrays)


def units_out(idx, mine, active, hidden, proj_found):
    units = active.shape[1]
    arrays, table = operands(proj_found)
    n = len(arrays)
    model = LANES * len(table) // 2
    half_blocks = LEN // BLK // 2
    first = 0 if mine else half_blocks

    def body(ix, act, *rest):
        extra = rest[:1] if mine else ()
        rest = rest[len(extra) :]
        msgs = rest[:n]
        out, w, sems = rest[n:]

        @pl.when(pl.program_id(0) == 0)
        def _():
            load_all(proj_pairs(msgs, table, w, ix), sems)

        term = jnp.dot(act[...], w[...], preferred_element_type=F32)
        if mine:
            term = term + extra[0][...]
        out[...] = term.astype(out.dtype)

    row = pl.BlockSpec((BLK, model), lambda i, ix: (i, 0))
    return call(
        body,
        "units_out_own" if mine else "units_out_send",
        half_blocks,
        [pl.BlockSpec((BLK, units), lambda i, ix: (first + i, 0))] + ([row] if mine else []) + [ANY] * n,
        row,
        shape(LEN // 2, model, F32 if mine else BF16),
        [pltpu.VMEM((units, model), BF16), pltpu.SemaphoreType.DMA((len(table),))],
        cost(LEN * units * model, 4 * units * model),
    )(idx, active, *((hidden,) if mine else ()), *arrays)


def hidden_back(idx, mid_own, mid_recv, cotangent, ids, weight_table, hidden, gain):
    model = cotangent.shape[1]
    half_blocks = LEN // BLK // 2

    def body(ix, own, recv, cot, ids_ref, table_ref, hid, gain_ref, grad_ref, low_ref):
        e = gain_ref[...] * (own[...] + recv[...].astype(F32))
        hat, scaler = row_stats(hid[...])
        grad = cot[...].astype(F32) * token_weights(ids_ref[...], table_ref[...])
        grad = grad + norm_back(hat, scaler, e)
        grad_ref[...] = grad
        low_ref[...] = grad.astype(BF16)

    def token_rows(i, ix):
        return ((2 * ix[1] + ix[2]) * half_blocks + i, 0)

    row = pl.BlockSpec((BLK, model), lambda i, ix: (i, 0))
    return call(
        body,
        "hidden_back",
        half_blocks,
        [
            row,
            row,
            pl.BlockSpec((BLK, model), token_rows),
            pl.BlockSpec((BLK, 1), token_rows),
            full(1, LANES),
            row,
            full(1, model),
        ],
        [row, row],
        [shape(LEN // 2, model, F32), shape(LEN // 2, model)],
        [],
        cost(20 * LEN * model, 8 * LEN * model),
    )(idx, mid_own, mid_recv, cotangent, ids, weight_table, hidden, gain)


def attended_back(idx, own, other, found, first_row, width):
    model = own.shape[1]
    arrays, table = operands(found)
    n = len(arrays)
    half_blocks = LEN // BLK // 2

    def body(ix, own_ref, other_ref, *rest):
        msgs = rest[:n]
        out, w, sems = rest[n:]
        step = pl.program_id(0)

        @pl.when(step == 0)
        def _():
            load_all(out_weight_pairs(msgs, table, w, ix, first_row), sems)

        rows = jnp.where(step < half_blocks, own_ref[...], other_ref[...])
        out[...] = lax.dot_general(rows, w[...], NT, preferred_element_type=F32).astype(BF16)

    def out_rows(i, ix):
        mine = ix[2] * half_blocks + i
        return (jnp.where(i < half_blocks, mine, (1 - ix[2]) * half_blocks + i - half_blocks), 0)

    return call(
        body,
        "attended_back",
        2 * half_blocks,
        [
            pl.BlockSpec((BLK, model), lambda i, ix: (jnp.minimum(i, half_blocks - 1), 0)),
            pl.BlockSpec((BLK, model), lambda i, ix: (jnp.maximum(i - half_blocks, 0), 0)),
        ]
        + [ANY] * n,
        pl.BlockSpec((BLK, width), out_rows),
        shape(LEN, width),
        [pltpu.VMEM((width, model), BF16), pltpu.SemaphoreType.DMA((len(table),))],
        cost(2 * LEN * width * model, 4 * LEN * model),
    )(idx, own, other, *arrays)


def attend_back_fast(queries, key_rows, value_rows, mixed, mixed_grad, logsum):
    length, width = queries.shape
    pairs = width // LANES

    def body(q_ref, k_ref, v_ref, o_ref, g_ref, lse_ref, dq_ref, dk_ref, dv_ref, dq_acc):
        scale = HEAD_DIM**-0.5 * LOG2E
        low = lax.broadcasted_iota(jnp.int32, (1, LANES), 1) < HEAD_DIM
        q = q_ref[...]
        g = g_ref[...]
        qm = [pick(low, q, h) for h in range(2)]
        gm = [pick(low, g, h) for h in range(2)]
        prod = (g.astype(F32) * o_ref[...].astype(F32)).T
        delta = [
            jnp.sum(prod[:HEAD_DIM], axis=0, keepdims=True),
            jnp.sum(prod[HEAD_DIM:], axis=0, keepdims=True),
        ]
        dq_acc[...] = jnp.zeros_like(dq_acc)
        for j in range(length // BLK):
            start = j * BLK
            stop = start + BLK
            span = length - start
            kb = k_ref[start:stop, :]
            vb = v_ref[start:stop, :]
            causal = lax.broadcasted_iota(jnp.int32, (BLK, span), 1) >= lax.broadcasted_iota(
                jnp.int32, (BLK, span), 0
            )
            dk = jnp.zeros((BLK, LANES), F32)
            dv = jnp.zeros((BLK, LANES), F32)
            for h in range(2):
                km = pick(low, kb, h)
                s = lax.dot_general(km, q[start:], NT, preferred_element_type=F32) * scale
                s = jnp.where(causal, s - lse_ref[0, h : h + 1, start:], MASKED)
                p = jnp.exp2(s)
                dp = lax.dot_general(pick(low, vb, h), g[start:], NT, preferred_element_type=F32)
                ds = (p * (dp - delta[h][:, start:])).astype(BF16)
                dk = dk + jnp.dot(ds, qm[h][start:], preferred_element_type=F32)
                dv = dv + jnp.dot(p.astype(BF16), gm[h][start:], preferred_element_type=F32)
                dq_acc[start:, :] += lax.dot_general(ds, km, TN, preferred_element_type=F32)
            dk_ref[start:stop, :] = (dk * HEAD_DIM**-0.5).astype(BF16)
            dv_ref[start:stop, :] = dv.astype(BF16)
        dq_ref[...] = (dq_acc[...] * HEAD_DIM**-0.5).astype(BF16)

    spec = pl.BlockSpec((length, LANES), lambda i: (0, i))
    return pl.pallas_call(
        body,
        grid=(pairs,),
        out_shape=(shape(length, width),) * 3,
        in_specs=[spec] * 5 + [pl.BlockSpec((1, 8, length), lambda i: (i, 0, 0))],
        out_specs=(spec,) * 3,
        scratch_shapes=[pltpu.VMEM((length, LANES), F32)],
        compiler_params=pltpu.CompilerParams(vmem_limit_bytes=VMEM_LIMIT),
        cost_estimate=cost(20 * length * length * width, 16 * length * width, 2 * pairs * length * length),
        name="attend_back",
    )(queries, key_rows, value_rows, mixed, mixed_grad, logsum)


def adapter_back(idx, dq, dv, normed, latent, up):
    model = normed.shape[1]
    width = dq.shape[1]
    part = width // 2
    cols = up.shape[2]

    def body(ix, dq_ref, dv_ref, normed_ref, latent_ref, up_ref, low_ref, down_ref, raise_ref):
        @pl.when(pl.program_id(0) == 0)
        def _():
            down_ref[...] = jnp.zeros_like(down_ref)
            raise_ref[...] = jnp.zeros_like(raise_ref)

        grad = jnp.zeros((BLK, LANES), F32)
        latent = latent_ref[...]
        for a in range(2):
            for n, ref in ((0, dq_ref), (1, dv_ref)):
                piece = ref[:, a * part : (a + 1) * part]
                weight = up_ref[a, :, 2 * n * part : (2 * n + 1) * part]
                grad = grad + lax.dot_general(piece, weight, NT, preferred_element_type=F32)
                term = lax.dot_general(latent, piece, TN, preferred_element_type=F32)
                raise_ref[:, (2 * a + n) * part : (2 * a + n + 1) * part] += term[:8]
        low = grad.astype(BF16)
        low_ref[...] = low
        down_ref[...] += lax.dot_general(low, normed_ref[...], TN, preferred_element_type=F32)[:8]

    row = lambda c: pl.BlockSpec((BLK, c), lambda i, ix: (i, 0))
    return call(
        body,
        "adapter_back",
        LEN // BLK,
        [row(width), row(width), row(model), row(LANES), pl.BlockSpec((2, LANES, cols), lambda i, ix: (0, 0, 0))],
        [row(LANES), full(8, model), full(8, 4 * part)],
        [shape(LEN, LANES), shape(8, model, F32), shape(8, 4 * part, F32)],
        [],
        cost(6 * LEN * model * LANES, 8 * LEN * model),
    )(idx, dq, dv, normed, latent, up)


def heads_back(idx, mine, dq, dk, dv, latent_low, down, found):
    width = dq.shape[1]
    part = width // 2
    model = down.shape[1]
    arrays, table = operands(found)
    step_rows, cols = found[0][0].shape
    n = len(arrays)
    half_blocks = LEN // BLK // 2

    def body(ix, dq_ref, dk_ref, dv_ref, low_ref, down_ref, *rest):
        msgs = rest[:n]
        out, w, sems = rest[n:]

        @pl.when(pl.program_id(0) == 0)
        def _():
            load_all(
                [(block_of(msgs, e), w.at[e[2], at_rows(ix[0] ^ e[3], step_rows), :]) for e in table],
                sems,
            )

        total = jnp.dot(low_ref[...], down_ref[...], preferred_element_type=F32)
        for a in range(2):
            piece = jnp.concatenate([r[:, a * part : (a + 1) * part] for r in (dq_ref, dk_ref, dv_ref)], axis=1)
            total = total + lax.dot_general(piece, w[a], NT, preferred_element_type=F32)
        out[...] = total.astype(out.dtype)

    def rows(i, ix):
        return ((ix[2] if mine else 1 - ix[2]) * half_blocks + i, 0)

    row = pl.BlockSpec((BLK, width), rows)
    return call(
        body,
        "heads_back_own" if mine else "heads_back_send",
        half_blocks,
        [row, row, row, pl.BlockSpec((BLK, LANES), rows), full(LANES, model)] + [ANY] * n,
        pl.BlockSpec((BLK, model), lambda i, ix: (i, 0)),
        shape(LEN // 2, model, F32 if mine else BF16),
        [pltpu.VMEM((2, model, cols), BF16), pltpu.SemaphoreType.DMA((len(table),))],
        cost(2 * LEN * model * cols, 4 * model * cols),
    )(idx, dq, dk, dv, latent_low, down, *arrays)


def tokens_back(idx, in_own, in_recv, tokens, hidden_grad, gain):
    model = tokens.shape[1]
    half_blocks = LEN // BLK // 2
    parts = 4
    part = model // parts

    def body(ix, own, recv, tok, hg, gain_ref, *rest):
        outs, held = rest[:parts], rest[parts]
        e = gain_ref[...] * (own[...] + recv[...].astype(F32))
        hat, scaler = row_stats(tok[...].astype(F32))
        held[...] = (hg[...] + norm_back(hat, scaler, e)).astype(BF16)
        for k, out in enumerate(outs):
            out[...] = held[:, at_rows((2 * ix[1] + ix[2]) ^ k, part)]

    row = pl.BlockSpec((BLK, model), lambda i, ix: (i, 0))
    return call(
        body,
        "tokens_back",
        half_blocks,
        [row, row, pl.BlockSpec((BLK, model), lambda i, ix: ((2 * ix[1] + ix[2]) * half_blocks + i, 0)), row, full(1, model)],
        [pl.BlockSpec((BLK, part), lambda i, ix: (i, 0))] * parts,
        [shape(LEN // 2, part)] * parts,
        [pltpu.VMEM((BLK, model), BF16)],
        cost(20 * LEN * model, 8 * LEN * model),
    )(idx, in_own, in_recv, tokens, hidden_grad, gain)


def output_rows(idx, own, recv):
    model = own.shape[1]
    half_blocks = LEN // BLK // 2
    parts = 4
    part = model // parts

    def body(ix, own_ref, recv_ref, *rest):
        outs, held = rest[:parts], rest[parts]
        held[...] = (own_ref[...] + recv_ref[...].astype(F32)).astype(BF16)
        for k, out in enumerate(outs):
            out[...] = held[:, at_rows((2 * ix[1] + ix[2]) ^ k, part)]

    row = pl.BlockSpec((BLK, model), lambda i, ix: (i, 0))
    return call(
        body,
        "output_rows",
        half_blocks,
        [row, row],
        [pl.BlockSpec((BLK, part), lambda i, ix: (i, 0))] * parts,
        [shape(LEN // 2, part)] * parts,
        [pltpu.VMEM((BLK, model), BF16)],
        cost(2 * LEN * model, 6 * LEN * model),
    )(idx, own, recv)


def to_features(idx, pieces, bias):
    pieces = [pieces[0], core_swap(pieces[1]), hop(pieces[2], 1, 0), both_swap(pieces[3])]
    rows, part = pieces[0].shape
    parts = len(pieces)

    def body(ix, bias_ref, *rest):
        outs = rest[parts]
        for k in range(parts):
            value = rest[k][...]
            if bias is not None:
                value = (value.astype(F32) + bias_ref[...]).astype(BF16)
            outs[at_rows((2 * ix[1] + ix[2]) ^ k, rows), :] = value

    extra = jnp.zeros((1, part), F32) if bias is None else bias
    return call(
        body,
        "to_features",
        1,
        [full(1, part)] + [full(rows, part)] * parts,
        full(parts * rows, part),
        shape(parts * rows, part),
        [],
        cost(parts * rows * part, 4 * parts * rows * part),
    )(idx, extra, *pieces)


def both_swap(value):
    total = lax.axis_size("dp") * lax.axis_size("mp")
    return lax.ppermute(value, AXES, [(i, i ^ 3) for i in range(total)])


def on_device_fast(
    tokens,
    cotangent,
    group_ids,
    pre_gain,
    pre_shift,
    frozen_triple_weight,
    frozen_triple_bias,
    out_weight,
    out_bias,
    mid_gain,
    mid_shift,
    fc_weight,
    fc_bias,
    proj_weight,
    proj_bias,
    down_master,
    up_master,
    down_first,
    down_second,
    up_first,
    up_second,
    learn_rate,
):
    tok_dev, model = tokens.shape
    ranks = lax.axis_size("mp") // 2
    place = lax.axis_index("mp")
    idx = jnp.stack([lax.axis_index("dp"), place // ranks, place % ranks]).astype(jnp.int32)
    line = lambda v: v.astype(F32).reshape(1, -1)
    step_rows, _, head_part = frozen_triple_weight.shape
    qkv_own = frozen_triple_weight.reshape(step_rows, 3 * head_part)
    proj_rows = proj_weight.shape[0]
    rest_own = jnp.concatenate([proj_weight, out_weight], axis=0)
    qkv = gather_blocks(qkv_own, "x")
    rest_own = after(rest_own, qkv[4][0])
    rest = gather_blocks(rest_own, "y")
    fc_own = after(fc_weight, rest[4][0])
    fc = gather_blocks(fc_own, "x")
    up_low = up_master.astype(BF16).reshape(2 * ADAPTER_RANK, head_part)
    fc_rows = fc_bias.reshape(-1, head_part)
    small = jnp.concatenate([frozen_triple_bias, fc_rows, up_low], axis=0)
    small = jnp.stack([small, hop(small, 1, 0)])
    bias = small[:, :3].reshape(2, 3 * head_part).astype(F32)
    fc_line = small[:, 3 : 3 + fc_rows.shape[0]].reshape(1, -1).astype(F32)
    up_both = small[:, 3 + fc_rows.shape[0] :] * jnp.bfloat16(ADAPTER_SCALE)
    r = ADAPTER_RANK
    up = jnp.zeros((2, LANES, 3 * head_part), BF16)
    up = up.at[:, :r, :head_part].set(up_both[:, :r]).at[:, r : 2 * r, 2 * head_part :].set(up_both[:, r:])
    down = jnp.zeros((LANES, model), BF16).at[: 2 * r].set(down_master.reshape(2 * r, model).astype(BF16))
    groups = jnp.arange(LANES, dtype=jnp.int32)[None, :]
    ids = group_ids[:, None]
    counts = jnp.sum((ids == groups).astype(jnp.int32), axis=0, keepdims=True)
    bits = 1
    while bits < lax.axis_size("dp"):
        counts = counts + hop(counts, 0, bits)
        bits *= 2
    weight_table = F32(tok_dev * lax.axis_size("dp")) / (GROUPS * counts.astype(F32))

    queries, keys, values, normed, latent = project_heads(idx, tokens, line(pre_gain), line(pre_shift), bias, down, up, qkv)
    mixed, logsum = attend_fast(queries, keys, values)
    sent = core_swap(attention_out_send(idx, mixed, rest, proj_rows))
    hidden, normed_mid = attention_out_own(
        idx, mixed, sent, tokens, line(out_bias), line(mid_gain), line(mid_shift), rest, proj_rows
    )
    normed_other = core_swap(normed_mid)
    active, slope = expand_units(idx, normed_mid, normed_other, fc_line, fc)
    proj = rest
    mid_recv = core_swap(units_back(idx, False, cotangent, ids, weight_table, slope, fc, proj))
    mid_own = units_back(idx, True, cotangent, ids, weight_table, slope, fc, proj)
    hidden_grad, hidden_low = hidden_back(idx, mid_own, mid_recv, cotangent, ids, weight_table, hidden, line(mid_gain))
    hidden_other = core_swap(hidden_low)
    out_recv = core_swap(units_out(idx, False, active, hidden, proj))
    out_own = units_out(idx, True, active, hidden, proj)
    mixed_grad = attended_back(idx, hidden_low, hidden_other, rest, proj_rows, mixed.shape[1])
    dq, dk, dv = attend_back_fast(queries, keys, values, mixed, mixed_grad, logsum)
    latent_low, down_term, up_term = adapter_back(idx, dq, dv, normed, latent, up)
    in_recv = core_swap(heads_back(idx, False, dq, dk, dv, latent_low, down, qkv))
    in_own = heads_back(idx, True, dq, dk, dv, latent_low, down, qkv)
    output = to_features(idx, output_rows(idx, out_own, out_recv), line(proj_bias))
    input_grad = to_features(idx, tokens_back(idx, in_own, in_recv, tokens, hidden_grad, line(pre_gain)), None)
    up_term = up_term.reshape(2 * r, 2, 2, head_part)
    mine = jnp.concatenate([up_term[:r, 0, 0], up_term[r:, 0, 1]], axis=0)
    theirs = jnp.concatenate([up_term[:r, 1, 0], up_term[r:, 1, 1]], axis=0)
    down_sum = down_term + core_swap(down_term)
    got = hop(jnp.concatenate([down_sum, theirs], axis=1), 1, 0)
    both = jnp.concatenate([down_sum, mine], axis=1) + got
    bits = 1
    while bits < lax.axis_size("dp"):
        both = both + hop(both, 0, bits)
        bits *= 2
    down_grad = both[:, :model].reshape(down_master.shape)
    up_grad = ADAPTER_SCALE * both[:, model:].reshape(up_master.shape)
    step_value = jnp.float32(STEP)
    down_new, down_moment, down_square = adam_update(
        down_master, down_first, down_second, down_grad, step_value, learn_rate
    )
    up_new, up_moment, up_square = adam_update(up_master, up_first, up_second, up_grad, step_value, learn_rate)
    return (
        output,
        input_grad,
        down_new,
        down_moment,
        down_square,
        down_new.astype(BF16),
        up_new,
        up_moment,
        up_square,
        up_new.astype(BF16),
    )


def pick_body(mesh):
    return on_device_fast if mesh.shape["dp"] == 8 and mesh.shape["mp"] == 4 else on_device_general


def solution(mesh):
    body = pick_body(mesh)
    return jax.shard_map(
        body,
        mesh=mesh,
        in_specs=(
            P("dp", None),
            P("dp", None),
            P("dp"),
            P(),
            P(),
            P("dp", None, "mp"),
            P(None, "mp"),
            P("mp", "dp"),
            P(),
            P(),
            P(),
            P("dp", "mp"),
            P("mp"),
            P("mp", "dp"),
            P("mp"),
            P(),
            P(None, None, "mp"),
            P(),
            P(),
            P(None, None, "mp"),
            P(None, None, "mp"),
            P(),
        ),
        out_specs=(
            P("dp", "mp"),
            P("dp", "mp"),
            P(),
            P(),
            P(),
            P(),
            P(None, None, "mp"),
            P(None, None, "mp"),
            P(None, None, "mp"),
            P(None, None, "mp"),
        ),
        check_vma=False,
    )
```

```python
import jax
import jax.numpy as jnp
from jax import lax
from jax.experimental import pallas as pl
from jax.experimental.pallas import tpu as pltpu
from jax.sharding import PartitionSpec as P

HEAD_DIM = 64
ADAPTER_RANK = 4
GROUPS = 16
STEP = 3
MICRO = 2


ADAPTER_SCALE = 8.0
NORM_EPS = 1e-05
MASKED = -1e30
BETA_ONE = 0.5
BETA_TWO = 0.5
ADAM_EPS = 1e-08
DECAY = 0.01


def layer_stats(values):
    center = values - jnp.mean(values, axis=-1, keepdims=True)
    spread = jnp.mean(center * center, axis=-1, keepdims=True)
    scaler = lax.rsqrt(spread + NORM_EPS)
    return (center * scaler, scaler)


def norm_back(normal_hat, scaler, scaled_grad):
    first_mean = jnp.mean(scaled_grad, axis=-1, keepdims=True)
    second_mean = jnp.mean(scaled_grad * normal_hat, axis=-1, keepdims=True)
    return scaler * (scaled_grad - first_mean - normal_hat * second_mean)


def gelu_tanh(values):
    return jax.nn.gelu(values, approximate=True)


def fetch_frozen(frozen_triple_weight, fc_weight, out_weight, proj_weight):
    return (
        lax.all_gather(frozen_triple_weight, "dp", axis=0, tiled=True),
        lax.all_gather(fc_weight, "dp", axis=0, tiled=True),
        lax.all_gather(out_weight, "dp", axis=1, tiled=True),
        lax.all_gather(proj_weight, "dp", axis=1, tiled=True),
    )


def score_block(query_part, key_heads, start, block_rows, key_count):
    score_scale = HEAD_DIM ** (-0.5)
    scores = (
        jnp.einsum("qhd,khd->hqk", query_part, key_heads, preferred_element_type=jnp.float32)
        * score_scale
    )
    allowed = (start + jnp.arange(block_rows, dtype=jnp.int32))[:, None] >= jnp.arange(
        key_count, dtype=jnp.int32
    )[None, :]
    return jnp.where(allowed[None], scores, MASKED)


def attend(queries, key_rows, value_rows):
    length, col_width = queries.shape
    head_count = col_width // HEAD_DIM
    block_rows = min(512, length)
    query_heads = queries.reshape(length, head_count, HEAD_DIM)
    key_heads = key_rows.reshape(length, head_count, HEAD_DIM)
    value_heads = value_rows.reshape(length, head_count, HEAD_DIM)
    mixed_parts = []
    logsum_parts = []
    for index in range(length // block_rows):
        start = index * block_rows
        stop = start + block_rows
        query_part = query_heads[start:stop]
        scores = score_block(query_part, key_heads[:stop], start, block_rows, stop)
        row_top = jnp.max(scores, axis=-1, keepdims=True)
        exp_terms = jnp.exp(scores - row_top)
        row_total = jnp.sum(exp_terms, axis=-1, keepdims=True)
        probs = (exp_terms / row_total).astype(jnp.bfloat16)
        mixed = jnp.einsum(
            "hqk,khd->qhd", probs, value_heads[:stop], preferred_element_type=jnp.float32
        )
        mixed_parts.append(mixed.reshape(block_rows, col_width))
        logsum_parts.append((row_top + jnp.log(row_total))[..., 0])
    return (jnp.concatenate(mixed_parts, axis=0), logsum_parts)


def attend_back(queries, key_rows, value_rows, logsum, mixed_grad):
    length, col_width = queries.shape
    head_count = col_width // HEAD_DIM
    block_rows = min(512, length)
    score_scale = HEAD_DIM ** (-0.5)
    query_heads = queries.reshape(length, head_count, HEAD_DIM)
    key_heads = key_rows.reshape(length, head_count, HEAD_DIM)
    value_heads = value_rows.reshape(length, head_count, HEAD_DIM)
    grad_heads = mixed_grad.reshape(length, head_count, HEAD_DIM)
    key_acc = jnp.zeros((length, head_count, HEAD_DIM), jnp.float32)
    value_acc = jnp.zeros((length, head_count, HEAD_DIM), jnp.float32)
    query_parts = []
    for index in range(length // block_rows):
        start = index * block_rows
        stop = start + block_rows
        query_part = query_heads[start:stop]
        grad_part = grad_heads[start:stop]
        key_part = key_heads[:stop]
        scores = score_block(query_part, key_part, start, block_rows, stop)
        probs = jnp.exp(scores - logsum[index][:, :, None])
        prob_grad = jnp.einsum(
            "qhd,khd->hqk", grad_part, value_heads[:stop], preferred_element_type=jnp.float32
        )
        inner = jnp.sum(prob_grad * probs, axis=-1, keepdims=True)
        score_grad = (probs * (prob_grad - inner)).astype(jnp.bfloat16)
        query_grad = (
            jnp.einsum("hqk,khd->qhd", score_grad, key_part, preferred_element_type=jnp.float32)
            * score_scale
        )
        key_acc = key_acc.at[:stop].add(
            jnp.einsum("hqk,qhd->khd", score_grad, query_part, preferred_element_type=jnp.float32)
            * score_scale
        )
        value_acc = value_acc.at[:stop].add(
            jnp.einsum(
                "hqk,qhd->khd",
                probs.astype(jnp.bfloat16),
                grad_part,
                preferred_element_type=jnp.float32,
            )
        )
        query_parts.append(query_grad.reshape(block_rows, col_width))
    return (
        jnp.concatenate(query_parts, axis=0),
        key_acc.reshape(length, col_width),
        value_acc.reshape(length, col_width),
    )


def adam_update(master, first, second, grad, step_value, learn_rate):
    new_first = BETA_ONE * first + (1.0 - BETA_ONE) * grad
    new_second = BETA_TWO * second + (1.0 - BETA_TWO) * grad * grad
    fix_one = 1.0 - jnp.power(jnp.float32(BETA_ONE), step_value)
    fix_two = 1.0 - jnp.power(jnp.float32(BETA_TWO), step_value)
    update = new_first / fix_one / (jnp.sqrt(new_second / fix_two) + ADAM_EPS)
    new_master = master - learn_rate * (update + DECAY * master)
    return (new_master, new_first, new_second)


def on_device_general(
    tokens,
    cotangent,
    group_ids,
    pre_gain,
    pre_shift,
    frozen_triple_weight,
    frozen_triple_bias,
    out_weight,
    out_bias,
    mid_gain,
    mid_shift,
    fc_weight,
    fc_bias,
    proj_weight,
    proj_bias,
    down_master,
    up_master,
    down_first,
    down_second,
    up_first,
    up_second,
    learn_rate,
):
    tok_dev = tokens.shape[0]
    model_width = tokens.shape[1]
    length = tok_dev // MICRO
    shard_width = model_width // lax.axis_size("mp")
    shard_start = lax.axis_index("mp") * shard_width
    pre_gain_f = pre_gain.astype(jnp.float32)
    pre_shift_f = pre_shift.astype(jnp.float32)
    mid_gain_f = mid_gain.astype(jnp.float32)
    mid_shift_f = mid_shift.astype(jnp.float32)
    out_bias_f = out_bias.astype(jnp.float32)
    fc_bias_f = fc_bias.astype(jnp.float32)
    proj_bias_f = proj_bias.astype(jnp.float32)
    bias_flat = frozen_triple_bias.astype(jnp.float32).reshape(-1)
    onehot = group_ids[:, None] == jnp.arange(GROUPS, dtype=jnp.int32)[None, :]
    local_counts = jnp.sum(onehot.astype(jnp.int32), axis=0)
    totals = lax.psum(local_counts, "dp").astype(jnp.float32)
    own_count = jnp.sum(jnp.where(onehot, totals[None, :], jnp.float32(0.0)), axis=1)
    token_weight = jnp.float32(tok_dev * lax.axis_size("dp")) / (GROUPS * own_count)
    down_low = down_master.astype(jnp.bfloat16).reshape(2 * ADAPTER_RANK, model_width)
    raise_reduced = up_master.astype(jnp.bfloat16)
    grad_down = jnp.zeros((2 * ADAPTER_RANK, model_width), jnp.float32)
    raise_gradient = jnp.zeros(up_master.shape, jnp.float32)
    output_parts = []
    input_parts = []
    for micro_index in range(MICRO):
        current = fetch_frozen(frozen_triple_weight, fc_weight, out_weight, proj_weight)
        qkv_full, fc_full, out_full, proj_full = current
        qkv_flat = qkv_full.reshape(model_width, -1)
        head_width = qkv_flat.shape[1] // 3
        row_start = micro_index * length
        rows_f = lax.dynamic_slice_in_dim(tokens, row_start, length, 0).astype(jnp.float32)
        pre_hat, pre_scale = layer_stats(rows_f)
        normed = (pre_hat * pre_gain_f + pre_shift_f).astype(jnp.bfloat16)
        mixed_proj = jnp.dot(normed, qkv_flat, preferred_element_type=jnp.float32) + bias_flat
        bottleneck = jnp.einsum(
            "td,rd->tr", normed, down_low, preferred_element_type=jnp.float32
        ).astype(jnp.bfloat16)
        queries = (
            mixed_proj[:, :head_width]
            + ADAPTER_SCALE
            * jnp.dot(
                bottleneck[:, :ADAPTER_RANK], raise_reduced[0], preferred_element_type=jnp.float32
            )
        ).astype(jnp.bfloat16)
        key_rows = mixed_proj[:, head_width : 2 * head_width].astype(jnp.bfloat16)
        value_rows = (
            mixed_proj[:, 2 * head_width :]
            + ADAPTER_SCALE
            * jnp.dot(
                bottleneck[:, ADAPTER_RANK:], raise_reduced[1], preferred_element_type=jnp.float32
            )
        ).astype(jnp.bfloat16)
        attended, logsum = attend(queries, key_rows, value_rows)
        attended_low = attended.astype(jnp.bfloat16)
        head_term = jnp.dot(attended_low, out_full, preferred_element_type=jnp.float32).astype(
            jnp.bfloat16
        )
        attn_sum = lax.psum(head_term, "mp").astype(jnp.float32)
        hidden = rows_f + attn_sum + out_bias_f
        mid_hat, mid_scale = layer_stats(hidden)
        normed_mid = (mid_hat * mid_gain_f + mid_shift_f).astype(jnp.bfloat16)
        pre_act = jnp.dot(normed_mid, fc_full, preferred_element_type=jnp.float32) + fc_bias_f
        active, gelu_pullback = jax.vjp(gelu_tanh, pre_act)
        unit_part = jnp.dot(
            active.astype(jnp.bfloat16), proj_full, preferred_element_type=jnp.float32
        ).astype(jnp.bfloat16)
        unit_share = lax.psum_scatter(unit_part, "mp", scatter_dimension=1, tiled=True).astype(
            jnp.float32
        )
        hidden_share = lax.dynamic_slice_in_dim(hidden, shard_start, shard_width, 1)
        output_parts.append((hidden_share + unit_share + proj_bias_f).astype(jnp.bfloat16))
        weight_rows = lax.dynamic_slice_in_dim(token_weight, row_start, length, 0)
        out_grad = (
            lax.dynamic_slice_in_dim(cotangent, row_start, length, 0).astype(jnp.float32)
            * weight_rows[:, None]
        )
        out_low = out_grad.astype(jnp.bfloat16)
        active_grad = jnp.einsum(
            "td,fd->tf", out_low, proj_full, preferred_element_type=jnp.float32
        )
        pre_grad = gelu_pullback(active_grad)[0].astype(jnp.bfloat16)
        mid_part = jnp.einsum(
            "tf,df->td", pre_grad, fc_full, preferred_element_type=jnp.float32
        ).astype(jnp.bfloat16)
        mid_grad = lax.psum(mid_part, "mp").astype(jnp.float32)
        hidden_grad = out_grad + norm_back(mid_hat, mid_scale, mid_gain_f * mid_grad)
        hidden_low = hidden_grad.astype(jnp.bfloat16)
        attended_grad = jnp.einsum(
            "td,hd->th", hidden_low, out_full, preferred_element_type=jnp.float32
        ).astype(jnp.bfloat16)
        query_grad, key_grad, value_grad = attend_back(
            queries, key_rows, value_rows, logsum, attended_grad
        )
        query_low = query_grad.astype(jnp.bfloat16)
        key_low = key_grad.astype(jnp.bfloat16)
        value_low = value_grad.astype(jnp.bfloat16)
        proj_grad = jnp.concatenate([query_low, key_low, value_low], axis=1)
        in_part = jnp.einsum("tc,dc->td", proj_grad, qkv_flat, preferred_element_type=jnp.float32)
        bottleneck_gradient = ADAPTER_SCALE * jnp.concatenate(
            [
                jnp.einsum(
                    "tc,rc->tr", query_low, raise_reduced[0], preferred_element_type=jnp.float32
                ),
                jnp.einsum(
                    "tc,rc->tr", value_low, raise_reduced[1], preferred_element_type=jnp.float32
                ),
            ],
            axis=1,
        )
        latent_low = bottleneck_gradient.astype(jnp.bfloat16)
        in_part = (
            in_part + jnp.dot(latent_low, down_low, preferred_element_type=jnp.float32)
        ).astype(jnp.bfloat16)
        grad_down = grad_down + jnp.einsum(
            "tr,td->rd", latent_low, normed, preferred_element_type=jnp.float32
        )
        raise_gradient = raise_gradient + ADAPTER_SCALE * jnp.stack(
            [
                jnp.einsum(
                    "tr,tc->rc",
                    bottleneck[:, :ADAPTER_RANK],
                    query_low,
                    preferred_element_type=jnp.float32,
                ),
                jnp.einsum(
                    "tr,tc->rc",
                    bottleneck[:, ADAPTER_RANK:],
                    value_low,
                    preferred_element_type=jnp.float32,
                ),
            ],
            axis=0,
        )
        hidden_grad_share = lax.dynamic_slice_in_dim(hidden_grad, shard_start, shard_width, 1)
        in_grad = lax.psum(in_part, "mp").astype(jnp.float32)
        full_grad = norm_back(pre_hat, pre_scale, pre_gain_f * in_grad)
        input_parts.append(
            (
                hidden_grad_share + lax.dynamic_slice_in_dim(full_grad, shard_start, shard_width, 1)
            ).astype(jnp.bfloat16)
        )
    output = jnp.concatenate(output_parts, axis=0)
    input_grad = jnp.concatenate(input_parts, axis=0)
    down_grad = lax.psum(grad_down, ("dp", "mp")).reshape(down_master.shape)
    up_grad = lax.psum(raise_gradient, "dp")
    step_value = jnp.float32(STEP)
    down_new, down_moment, down_square = adam_update(
        down_master, down_first, down_second, down_grad, step_value, learn_rate
    )
    up_new, up_moment, up_square = adam_update(
        up_master, up_first, up_second, up_grad, step_value, learn_rate
    )
    return (
        output,
        input_grad,
        down_new,
        down_moment,
        down_square,
        down_new.astype(jnp.bfloat16),
        up_new,
        up_moment,
        up_square,
        up_new.astype(jnp.bfloat16),
    )


LEN = 1024
BLK = 256
LANES = 128
LOG2E = 1.4426950408889634
NT = (((1,), (1,)), ((), ()))
TN = (((0,), (0,)), ((), ()))
VMEM_LIMIT = 60 << 20
F32 = jnp.float32
BF16 = jnp.bfloat16
AXES = ("dp", "mp")
ANY = pl.BlockSpec(memory_space=pl.ANY)


def cost(flops, nbytes, trans=0):
    return pl.CostEstimate(flops=int(flops), bytes_accessed=int(nbytes), transcendentals=int(trans))


def shape(rows, cols, dtype=BF16):
    return jax.ShapeDtypeStruct((rows, cols), dtype)


def full(rows, cols):
    return pl.BlockSpec((rows, cols), lambda i, ix: (0, 0))


def call(body, name, grid, in_specs, out_specs, out_shape, scratch, est):
    return pl.pallas_call(
        body,
        grid_spec=pltpu.PrefetchScalarGridSpec(
            num_scalar_prefetch=1,
            grid=(grid,),
            in_specs=in_specs,
            out_specs=out_specs,
            scratch_shapes=scratch,
        ),
        out_shape=out_shape,
        compiler_params=pltpu.CompilerParams(vmem_limit_bytes=VMEM_LIMIT),
        cost_estimate=est,
        name=name,
    )


def hop(value, half_bit, dp_bits):
    ranks = lax.axis_size("mp") // 2
    width = lax.axis_size("mp")
    total = lax.axis_size("dp") * width
    flip = dp_bits * width + half_bit * ranks
    return lax.ppermute(value, AXES, [(i, i ^ flip) for i in range(total)])


def core_swap(value):
    total = lax.axis_size("dp") * lax.axis_size("mp")
    return lax.ppermute(value, AXES, [(i, i ^ 1) for i in range(total)])


def after(value, *others):
    return lax.optimization_barrier((value, *others))[0]


def inner_z():
    z = lax.axis_index("dp") // 2
    return jnp.logical_or(z == 1, z == 2)


def z_hop(value, pairs):
    width = lax.axis_size("mp")
    perm = []
    for source, target in pairs:
        for rest in range(2 * width):
            perm.append((source * 2 * width + rest, target * 2 * width + rest))
    return lax.ppermute(value, AXES, perm)


MIDDLE = ((1, 2), (2, 1))
OUTWARD = ((1, 0), (2, 3))


def gather_z(own, first):
    begin = after(own, *first)
    z1 = hop(begin, 0, 2)
    m1 = z_hop(begin, MIDDLE)
    m2 = z_hop(z1, MIDDLE)
    f1 = z_hop(m1, OUTWARD)
    f2 = z_hop(m2, OUTWARD)
    inner = inner_z()
    near = jnp.stack([own, z1])
    far = jnp.stack([jnp.where(inner, m2, f1), jnp.where(inner, m1, f2)])
    return near, far, (z1, m1, m2, f1, f2)


def gather_xy(near, far, first_near, first_far):
    near_b = after(near, *first_near)
    far_b = after(far, *first_far)
    x_near, y_near = hop(near_b, 1, 0), hop(near_b, 0, 1)
    x_far, y_far = hop(far_b, 1, 0), hop(far_b, 0, 1)
    d_near, d_far = hop(x_near, 0, 1), hop(y_far, 1, 0)
    found = []
    for c in (0, 1):
        for array, half_bit, bit in ((near, 0, 0), (x_near, 1, 0), (y_near, 0, 1), (d_near, 1, 1)):
            found.append((array, c, half_bit, 2 * c + bit))
        for array, half_bit, bit in ((far, 0, 0), (x_far, 1, 0), (y_far, 0, 1), (d_far, 1, 1)):
            found.append((array, c, half_bit, 4 + 2 * c + bit))
    return found, (x_near, y_near, x_far, y_far, d_near, d_far)


def swapped_blocks(found):
    arrays, table = operands(found)
    arrays = [core_swap(array) for array in arrays]
    return [(arrays[e[0]], *e[1:]) for e in table]


def operands(found):
    arrays = []
    table = []
    for array, *entry in found:
        for k, held in enumerate(arrays):
            if held is array:
                break
        else:
            k = len(arrays)
            arrays.append(array)
        table.append((k, *entry))
    return arrays, table


def copies_of(pairs, sems, start=0):
    return [pltpu.make_async_copy(src, dst, sems.at[start + n]) for n, (src, dst) in enumerate(pairs)]


def load_all(pairs, sems):
    copies = copies_of(pairs, sems)
    for copy in copies:
        copy.start()
    for copy in copies:
        copy.wait()


def at_rows(index, size):
    return pl.ds(pl.multiple_of(index * size, size), size)


def at_lanes(index, size):
    return pl.ds(pl.multiple_of(index * size, LANES), size)


def column_pairs(refs, table, w, ix, first, count, spread):
    pairs = []
    for k, slot, half_bit, dp_bits in table:
        src = refs[k].at[slot, :, pl.ds(first, count)]
        rows = at_rows(ix[0] ^ dp_bits, src.shape[0])
        dst = w.at[half_bit, rows, :] if spread else w.at[rows, pl.ds(half_bit * count, count)]
        pairs.append((src, dst))
    return pairs


def block_pairs(refs, table, w, ix, half_bit, slot_out):
    return [
        (refs[k].at[slot], w.at[slot_out, at_rows(ix[0] ^ dp_bits, refs[k].shape[1]), :])
        for k, slot, a, dp_bits in table
        if a == half_bit
    ]


def pick(low, value, which):
    zero = jnp.zeros((), value.dtype)
    return jnp.where(low, value, zero) if which == 0 else jnp.where(low, zero, value)


def row_stats(values):
    center = values - jnp.mean(values, axis=-1, keepdims=True)
    scaler = lax.rsqrt(jnp.mean(center * center, axis=-1, keepdims=True) + NORM_EPS)
    return center * scaler, scaler


def token_weights(ids, table):
    lanes = lax.broadcasted_iota(jnp.int32, (ids.shape[0], LANES), 1)
    return jnp.sum(jnp.where(ids == lanes, table, 0.0), axis=-1, keepdims=True)


def norm_rows(idx, tokens, vec, down):
    model = tokens.shape[1]
    blocks = LEN // BLK

    def body(ix, tok, vec_ref, down_ref, normed_ref, latent_ref):
        hat, _ = row_stats(tok[...].astype(F32))
        normed = (hat * vec_ref[0:1, :] + vec_ref[1:2, :]).astype(BF16)
        normed_ref[...] = normed
        latent_ref[...] = lax.dot_general(normed, down_ref[...], NT, preferred_element_type=F32).astype(BF16)

    row = lambda c: pl.BlockSpec((BLK, c), lambda i, ix: (i, 0))
    return call(
        body,
        "norm_rows",
        blocks,
        [pl.BlockSpec((BLK, model), lambda i, ix: (ix[1] * blocks + i, 0)), full(8, model), full(LANES, model)],
        [row(model), row(LANES)],
        [shape(LEN, model), shape(LEN, LANES)],
        [],
        cost(2 * LEN * model * LANES, 4 * LEN * model),
    )(idx, tokens, vec, down)


def project_heads(idx, normed, latent, bias, up, found):
    model = normed.shape[1]
    arrays, table = operands(found)
    cols = bias.shape[1]
    part = cols // 3
    n = len(arrays)

    def body(ix, normed_ref, latent_ref, bias_ref, up_ref, *rest):
        msgs = rest[:n]
        q_ref, k_ref, v_ref, w, sems = rest[n:]

        @pl.when(pl.program_id(0) == 0)
        def _():
            load_all(column_pairs(msgs, table, w, ix, 0, cols, True), sems)

        for a in range(2):
            r = jnp.dot(normed_ref[...], w[a], preferred_element_type=F32) + bias_ref[a : a + 1, :]
            r = r + jnp.dot(latent_ref[...], up_ref[a], preferred_element_type=F32)
            for out, s in ((q_ref, 0), (k_ref, 1), (v_ref, 2)):
                out[:, a * part : (a + 1) * part] = r[:, s * part : (s + 1) * part].astype(BF16)

    row = lambda c: pl.BlockSpec((BLK, c), lambda i, ix: (i, 0))
    return call(
        body,
        "project_heads",
        LEN // BLK,
        [row(model), row(LANES), full(2, cols), pl.BlockSpec((2, LANES, cols), lambda i, ix: (0, 0, 0))] + [ANY] * n,
        [row(2 * part)] * 3,
        [shape(LEN, 2 * part)] * 3,
        [pltpu.VMEM((2, model, cols), BF16), pltpu.SemaphoreType.DMA((len(table),))],
        cost(4 * LEN * model * cols, 16 * LEN * model),
    )(idx, normed, latent, bias, up, *arrays)


def attend_fast(queries, key_rows, value_rows):
    length, width = queries.shape
    pairs = width // LANES

    def body(q_ref, k_ref, v_ref, o_ref, lse_ref):
        scale = HEAD_DIM**-0.5 * LOG2E
        low = lax.broadcasted_iota(jnp.int32, (1, LANES), 1) < HEAD_DIM
        k = k_ref[...]
        v = v_ref[...]
        value_of = [pick(low, v, h) for h in range(2)]
        for i in range(length // BLK):
            stop = (i + 1) * BLK
            qb = q_ref[i * BLK : stop, :]
            causal = (lax.broadcasted_iota(jnp.int32, (BLK, stop), 0) + i * BLK) >= lax.broadcasted_iota(
                jnp.int32, (BLK, stop), 1
            )
            out = jnp.zeros((BLK, LANES), F32)
            logs = []
            for h in range(2):
                s = lax.dot_general(pick(low, qb, h), k[:stop], NT, preferred_element_type=F32) * scale
                s = jnp.where(causal, s, MASKED)
                top = jnp.max(s, axis=-1, keepdims=True)
                p = jnp.exp2(s - top)
                total = jnp.sum(p, axis=-1, keepdims=True)
                probs = (p * (1.0 / total)).astype(BF16)
                out = out + jnp.dot(probs, value_of[h][:stop], preferred_element_type=F32)
                logs.append(top + jnp.log2(total))
            o_ref[i * BLK : stop, :] = out.astype(BF16)
            both = jnp.where(
                low, jnp.broadcast_to(logs[0], (BLK, LANES)), jnp.broadcast_to(logs[1], (BLK, LANES))
            ).T
            lse_ref[0, 0:1, i * BLK : stop] = both[0:1]
            lse_ref[0, 1:2, i * BLK : stop] = both[HEAD_DIM : HEAD_DIM + 1]

    spec = pl.BlockSpec((length, LANES), lambda i: (0, i))
    return pl.pallas_call(
        body,
        grid=(pairs,),
        out_shape=(shape(length, width), jax.ShapeDtypeStruct((pairs, 8, length), F32)),
        in_specs=[spec] * 3,
        out_specs=(spec, pl.BlockSpec((1, 8, length), lambda i: (i, 0, 0))),
        compiler_params=pltpu.CompilerParams(vmem_limit_bytes=VMEM_LIMIT),
        cost_estimate=cost(8 * length * length * width, 8 * length * width, 2 * pairs * length * length),
        name="attend",
    )(queries, key_rows, value_rows)


def attention_out_send(idx, attended, found, first):
    width = attended.shape[1]
    arrays, table = operands(found)
    n = len(arrays)
    model = LANES * lax.axis_size("dp")
    half_blocks = LEN // BLK // 2

    def body(ix, att, *rest):
        msgs = rest[:n]
        out, w, sems = rest[n:]

        @pl.when(pl.program_id(0) == 0)
        def _():
            load_all(column_pairs(msgs, table, w, ix, first, width // 2, False), sems)

        out[...] = lax.dot_general(att[...], w[...], NT, preferred_element_type=F32).astype(BF16)

    return call(
        body,
        "attention_out_send",
        half_blocks,
        [pl.BlockSpec((BLK, width), lambda i, ix: ((1 - ix[2]) * half_blocks + i, 0))] + [ANY] * n,
        pl.BlockSpec((BLK, model), lambda i, ix: (i, 0)),
        shape(LEN // 2, model),
        [pltpu.VMEM((model, width), BF16), pltpu.SemaphoreType.DMA((len(table),))],
        cost(LEN * width * model, 2 * LEN * model),
    )(idx, attended, *arrays)


def attention_out_own(idx, attended, received, tokens, vec, found, first):
    width = attended.shape[1]
    arrays, table = operands(found)
    n = len(arrays)
    model = tokens.shape[1]
    half_blocks = LEN // BLK // 2

    def body(ix, att, recv, tok, vec_ref, *rest):
        msgs = rest[:n]
        hidden_ref, normed_ref, w, sems = rest[n:]

        @pl.when(pl.program_id(0) == 0)
        def _():
            load_all(column_pairs(msgs, table, w, ix, first, width // 2, False), sems)

        term = lax.dot_general(att[...], w[...], NT, preferred_element_type=F32)
        hidden = tok[...].astype(F32) + term + recv[...].astype(F32) + vec_ref[2:3, :]
        hidden_ref[...] = hidden
        hat, _ = row_stats(hidden)
        normed_ref[...] = (hat * vec_ref[3:4, :] + vec_ref[4:5, :]).astype(BF16)

    row = pl.BlockSpec((BLK, model), lambda i, ix: (i, 0))
    return call(
        body,
        "attention_out_own",
        half_blocks,
        [
            pl.BlockSpec((BLK, width), lambda i, ix: (ix[2] * half_blocks + i, 0)),
            row,
            pl.BlockSpec((BLK, model), lambda i, ix: ((2 * ix[1] + ix[2]) * half_blocks + i, 0)),
            full(8, model),
        ]
        + [ANY] * n,
        [row, row],
        [shape(LEN // 2, model, F32), shape(LEN // 2, model)],
        [pltpu.VMEM((model, width), BF16), pltpu.SemaphoreType.DMA((len(table),))],
        cost(LEN * width * model, 5 * LEN * model),
    )(idx, attended, received, tokens, vec, *arrays)


def units_main(idx, half_bit, normed, cotangent, ids, weight_table, bias, vec, mine, other, carried, hidden):
    rows, model = normed.shape
    sources = [operands(f) for f in (mine, other)]
    part = sources[0][0][0].shape[2] // 2
    counts = [len(arrays) for arrays, _ in sources]
    last = hidden is not None
    parts = 4
    piece = model // parts
    chunk = 256
    per = part // chunk
    c0 = 0.7978845608028654
    c1 = 0.044715

    def body(ix, normed_ref, cot, ids_ref, table_ref, bias_ref, vec_ref, *rest):
        carry = rest[: len(carried)]
        rest = rest[len(carried) :]
        hid_ref, rest = (rest[0], rest[1:]) if last else (None, rest)
        msgs = (rest[: counts[0]], rest[counts[0] : sum(counts)])
        rest = rest[sum(counts) :]
        n_out = 2 + parts if last else 2
        outs, (w, grad_ref, x_ref, g_ref, pre_ref, act_ref, sems, *held) = rest[:n_out], rest[n_out:]
        groups = []
        used = 0
        for o in range(2):
            pairs = block_pairs(msgs[o], sources[o][1], w, ix, half_bit, o)
            groups.append(copies_of(pairs, sems, used))
            used += len(pairs)
        for group in groups:
            for copy in group:
                copy.start()
        weight = token_weights(ids_ref[...], table_ref[...])
        grad_ref[...] = (cot[...].astype(F32) * weight).astype(BF16)

        def multiply(o, c, slot):
            x_ref[slot] = jnp.dot(normed_ref[...], w[o, :, at_lanes(c, chunk)], preferred_element_type=F32)
            g_ref[slot] = jnp.dot(grad_ref[...], w[o, :, at_lanes(c + per, chunk)], preferred_element_type=F32)

        def bend(o, c, slot):
            at = at_lanes(o * per + c, chunk)
            x = x_ref[slot] + bias_ref[:, at]
            sq = x * x
            th = jnp.tanh(c0 * x * (1.0 + c1 * sq))
            left = 0.5 * (1.0 + th)
            slope = left + 0.5 * x * (1.0 - th * th) * (c0 + (3.0 * c0 * c1) * sq)
            pre_ref[:, at] = (slope * g_ref[slot]).astype(BF16)
            act_ref[:, at] = (x * left).astype(BF16)

        for o in range(2):
            for copy in groups[o]:
                copy.wait()
            if o == 0:
                multiply(0, 0, 0)

                def step(c, _):
                    multiply(0, c, lax.rem(c, 2))
                    bend(0, c - 1, lax.rem(c + 1, 2))
                    return 0

                lax.fori_loop(1, per, step, 0)
            else:
                multiply(1, 0, 0)
                bend(0, per - 1, (per - 1) % 2)

                def step(c, _):
                    multiply(1, c, lax.rem(c, 2))
                    bend(1, c - 1, lax.rem(c + 1, 2))
                    return 0

                lax.fori_loop(1, per, step, 0)
                bend(1, per - 1, (per - 1) % 2)

        def mid_of(n):
            at = at_rows(n, chunk)
            lanes = at_lanes(n, chunk)
            mid = lax.dot_general(pre_ref[:, :part], w[0, at, :part], NT, preferred_element_type=F32)
            mid = mid + lax.dot_general(pre_ref[:, part:], w[1, at, :part], NT, preferred_element_type=F32)
            unit = lax.dot_general(act_ref[:, :part], w[0, at, part:], NT, preferred_element_type=F32)
            unit = unit + lax.dot_general(act_ref[:, part:], w[1, at, part:], NT, preferred_element_type=F32)
            if carry:
                mid = mid + carry[0][:, lanes]
                unit = unit + carry[1][:, lanes]
            return mid, unit, lanes

        if not last:

            def finish(n, _):
                mid, unit, lanes = mid_of(n)
                outs[0][:, lanes] = mid
                outs[1][:, lanes] = unit
                return 0

            lax.fori_loop(0, model // chunk, finish, 0)
            return
        out_low, = held

        def finish(n, _):
            mid, unit, lanes = mid_of(n)
            outs[0][:, lanes] = mid * vec_ref[3:4, lanes]
            out_low[:, lanes] = (unit + hid_ref[:, lanes]).astype(BF16)
            return 0

        lax.fori_loop(0, model // chunk, finish, 0)
        for k in range(parts):
            outs[2 + k][...] = out_low[:, at_lanes((2 * ix[1] + ix[2]) ^ k, piece)]
        step_rows = 128

        def end(r, _):
            at = at_rows(r, step_rows)
            hat, scaler = row_stats(hid_ref[at, :])
            grad = cot[at, :].astype(F32) * token_weights(ids_ref[at, :], table_ref[...])
            grad = grad + norm_back(hat, scaler, outs[0][at, :])
            outs[0][at, :] = grad
            outs[1][at, :] = grad.astype(BF16)
            return 0

        lax.fori_loop(0, rows // step_rows, end, 0)

    def token_rows(i, ix):
        return (2 * ix[1] + ix[2], 0)

    block = full(rows, model)
    specs = [
        block,
        pl.BlockSpec((rows, model), token_rows),
        pl.BlockSpec((rows, 1), token_rows),
        full(1, LANES),
        pl.BlockSpec((1, 2 * part), lambda i, ix: (0, half_bit)),
        full(8, model),
    ]
    specs += [block] * (len(carried) + (1 if last else 0))
    if last:
        out_specs = [block, block] + [full(rows, piece)] * parts
        out_shape = [shape(rows, model, F32), shape(rows, model)] + [shape(rows, piece)] * parts
    else:
        out_specs = [block, block]
        out_shape = [shape(rows, model, F32)] * 2
    arrays = [array for found, _ in sources for array in found]
    return call(
        body,
        "units_main_last" if last else "units_main_first",
        1,
        specs + [ANY] * len(arrays),
        out_specs,
        out_shape,
        [
            pltpu.VMEM((2, model, 2 * part), BF16),
            pltpu.VMEM((rows, model), BF16),
            pltpu.VMEM((2, rows, chunk), F32),
            pltpu.VMEM((2, rows, chunk), F32),
            pltpu.VMEM((rows, 2 * part), BF16),
            pltpu.VMEM((rows, 2 * part), BF16),
            pltpu.SemaphoreType.DMA((sum(len(table) for _, table in sources) // 2,)),
        ]
        + ([pltpu.VMEM((rows, model), BF16)] if last else []),
        cost(16 * rows * part * model, 12 * part * model, 2 * rows * part),
    )(idx, normed, cotangent, ids, weight_table, bias, vec, *carried, *((hidden,) if last else ()), *arrays)


def attend_back_fast(idx, queries, key_rows, value_rows, mixed, grad_own, grad_other, logsum, found, first):
    length, width = queries.shape
    pairs = width // LANES
    half, model = grad_own.shape
    arrays, table = operands(found)
    n = len(arrays)

    def body(ix, q_ref, k_ref, v_ref, o_ref, own_ref, other_ref, lse_ref, *rest):
        msgs = rest[:n]
        dq_ref, dk_ref, dv_ref, dq_acc, g_ref, w, sems = rest[n:]
        pair = pl.program_id(0)

        @pl.when(pair == 0)
        def _():
            load_all(column_pairs(msgs, table, w, ix, first, width // 2, False), sems)

        weight = w[:, at_lanes(pair, LANES)]
        for ref, rank in ((own_ref, ix[2]), (other_ref, 1 - ix[2])):
            g_ref[at_rows(rank, half), :] = jnp.dot(ref[...], weight, preferred_element_type=F32).astype(BF16)
        scale = HEAD_DIM**-0.5 * LOG2E
        low = lax.broadcasted_iota(jnp.int32, (1, LANES), 1) < HEAD_DIM
        q = q_ref[...]
        g = g_ref[...]
        qm = [pick(low, q, h) for h in range(2)]
        gm = [pick(low, g, h) for h in range(2)]
        prod = (g.astype(F32) * o_ref[...].astype(F32)).T
        delta = [
            jnp.sum(prod[:HEAD_DIM], axis=0, keepdims=True),
            jnp.sum(prod[HEAD_DIM:], axis=0, keepdims=True),
        ]
        dq_acc[...] = jnp.zeros_like(dq_acc)
        for j in range(length // BLK):
            start = j * BLK
            stop = start + BLK
            span = length - start
            kb = k_ref[start:stop, :]
            vb = v_ref[start:stop, :]
            causal = lax.broadcasted_iota(jnp.int32, (BLK, span), 1) >= lax.broadcasted_iota(
                jnp.int32, (BLK, span), 0
            )
            dk = jnp.zeros((BLK, LANES), F32)
            dv = jnp.zeros((BLK, LANES), F32)
            for h in range(2):
                km = pick(low, kb, h)
                s = lax.dot_general(km, q[start:], NT, preferred_element_type=F32) * scale
                s = jnp.where(causal, s - lse_ref[0, h : h + 1, start:], MASKED)
                p = jnp.exp2(s)
                dp = lax.dot_general(pick(low, vb, h), g[start:], NT, preferred_element_type=F32)
                ds = (p * (dp - delta[h][:, start:])).astype(BF16)
                dk = dk + jnp.dot(ds, qm[h][start:], preferred_element_type=F32)
                dv = dv + jnp.dot(p.astype(BF16), gm[h][start:], preferred_element_type=F32)
                dq_acc[start:, :] += lax.dot_general(ds, km, TN, preferred_element_type=F32)
            dk_ref[start:stop, :] = (dk * HEAD_DIM**-0.5).astype(BF16)
            dv_ref[start:stop, :] = dv.astype(BF16)
        dq_ref[...] = (dq_acc[...] * HEAD_DIM**-0.5).astype(BF16)

    spec = pl.BlockSpec((length, LANES), lambda i, ix: (0, i))
    return call(
        body,
        "attend_back",
        pairs,
        [spec] * 4 + [full(half, model)] * 2 + [pl.BlockSpec((1, 8, length), lambda i, ix: (i, 0, 0))] + [ANY] * n,
        [spec] * 3,
        [shape(length, width)] * 3,
        [
            pltpu.VMEM((length, LANES), F32),
            pltpu.VMEM((length, LANES), BF16),
            pltpu.VMEM((model, width), BF16),
            pltpu.SemaphoreType.DMA((len(table),)),
        ],
        cost(20 * length * length * width, 16 * length * width, 2 * pairs * length * length),
    )(idx, queries, key_rows, value_rows, mixed, grad_own, grad_other, logsum, *arrays)


def heads_back(idx, dq, dk, dv, normed, latent, up, down, found):
    width = dq.shape[1]
    part = width // 2
    model = down.shape[1]
    arrays, table = operands(found)
    cols = 3 * part
    n = len(arrays)
    half_blocks = LEN // BLK // 2

    def body(ix, dq_ref, dk_ref, dv_ref, normed_ref, latent_ref, up_ref, down_ref, *rest):
        msgs = rest[:n]
        send_ref, own_ref, low_ref, raise_ref, w, sems = rest[n:]
        step = pl.program_id(0)

        @pl.when(step == 0)
        def _():
            copies = copies_of(column_pairs(msgs, table, w, ix, 0, cols, True), sems)
            for copy in copies:
                copy.start()
            low_ref[...] = jnp.zeros_like(low_ref)
            raise_ref[...] = jnp.zeros_like(raise_ref)
            for copy in copies:
                copy.wait()

        latent = latent_ref[...]
        low = jnp.zeros((BLK, LANES), F32)
        total = jnp.zeros((BLK, model), F32)
        for a in range(2):
            cut = slice(a * part, (a + 1) * part)
            piece = jnp.concatenate([dq_ref[:, cut], dk_ref[:, cut], dv_ref[:, cut]], axis=1)
            total = total + lax.dot_general(piece, w[a], NT, preferred_element_type=F32)
            low = low + lax.dot_general(piece, up_ref[a], NT, preferred_element_type=F32)
            term = lax.dot_general(latent, piece, TN, preferred_element_type=F32)
            raise_ref[:, a * cols : (a + 1) * cols] += term[:8]
        low = low.astype(BF16)
        total = total + jnp.dot(low, down_ref[...], preferred_element_type=F32)
        low_ref[...] += lax.dot_general(low, normed_ref[...], TN, preferred_element_type=F32)[:8]

        @pl.when(step < half_blocks)
        def _():
            send_ref[...] = total.astype(BF16)

        @pl.when(step >= half_blocks)
        def _():
            own_ref[...] = total

    def rows(i, ix):
        rank = jnp.where(i < half_blocks, 1 - ix[2], ix[2])
        return (rank * half_blocks + lax.rem(i, half_blocks), 0)

    row = lambda c: pl.BlockSpec((BLK, c), rows)
    return call(
        body,
        "heads_back",
        2 * half_blocks,
        [row(width)] * 3
        + [row(model), row(LANES), pl.BlockSpec((2, LANES, cols), lambda i, ix: (0, 0, 0)), full(LANES, model)]
        + [ANY] * n,
        [
            pl.BlockSpec((BLK, model), lambda i, ix: (jnp.minimum(i, half_blocks - 1), 0)),
            pl.BlockSpec((BLK, model), lambda i, ix: (jnp.maximum(i - half_blocks, 0), 0)),
            full(8, model),
            full(8, 2 * cols),
        ],
        [shape(LEN // 2, model), shape(LEN // 2, model, F32), shape(8, model, F32), shape(8, 2 * cols, F32)],
        [pltpu.VMEM((2, model, cols), BF16), pltpu.SemaphoreType.DMA((len(table),))],
        cost(4 * LEN * model * cols, 8 * model * cols),
    )(idx, dq, dk, dv, normed, latent, up, down, *arrays)


def tokens_back(idx, in_own, in_recv, tokens, hidden_grad, vec):
    model = tokens.shape[1]
    half_blocks = LEN // BLK // 2
    parts = 4
    part = model // parts

    def body(ix, own, recv, tok, hg, vec_ref, *rest):
        outs, held = rest[:parts], rest[parts]
        e = vec_ref[0:1, :] * (own[...] + recv[...].astype(F32))
        hat, scaler = row_stats(tok[...].astype(F32))
        held[...] = (hg[...] + norm_back(hat, scaler, e)).astype(BF16)
        for k, out in enumerate(outs):
            out[...] = held[:, at_lanes((2 * ix[1] + ix[2]) ^ k, part)]

    row = pl.BlockSpec((BLK, model), lambda i, ix: (i, 0))
    return call(
        body,
        "tokens_back",
        half_blocks,
        [row, row, pl.BlockSpec((BLK, model), lambda i, ix: ((2 * ix[1] + ix[2]) * half_blocks + i, 0)), row, full(8, model)],
        [pl.BlockSpec((BLK, part), lambda i, ix: (i, 0))] * parts,
        [shape(LEN // 2, part)] * parts,
        [pltpu.VMEM((BLK, model), BF16)],
        cost(20 * LEN * model, 8 * LEN * model),
    )(idx, in_own, in_recv, tokens, hidden_grad, vec)


def to_features(idx, pieces, bias):
    pieces = [pieces[0], core_swap(pieces[1]), hop(pieces[2], 1, 0), both_swap(pieces[3])]
    rows, part = pieces[0].shape
    parts = len(pieces)

    def body(ix, bias_ref, *rest):
        outs = rest[parts]
        for k in range(parts):
            value = rest[k][...]
            if bias is not None:
                value = (value.astype(F32) + bias_ref[...]).astype(BF16)
            outs[at_rows((2 * ix[1] + ix[2]) ^ k, rows), :] = value

    extra = jnp.zeros((1, part), F32) if bias is None else bias
    return call(
        body,
        "to_features",
        1,
        [full(1, part)] + [full(rows, part)] * parts,
        full(parts * rows, part),
        shape(parts * rows, part),
        [],
        cost(parts * rows * part, 4 * parts * rows * part),
    )(idx, extra, *pieces)


def both_swap(value):
    total = lax.axis_size("dp") * lax.axis_size("mp")
    return lax.ppermute(value, AXES, [(i, i ^ 3) for i in range(total)])


def on_device_fast(
    tokens,
    cotangent,
    group_ids,
    pre_gain,
    pre_shift,
    frozen_triple_weight,
    frozen_triple_bias,
    out_weight,
    out_bias,
    mid_gain,
    mid_shift,
    fc_weight,
    fc_bias,
    proj_weight,
    proj_bias,
    down_master,
    up_master,
    down_first,
    down_second,
    up_first,
    up_second,
    learn_rate,
):
    tok_dev, model = tokens.shape
    ranks = lax.axis_size("mp") // 2
    place = lax.axis_index("mp")
    idx = jnp.stack([lax.axis_index("dp"), place // ranks, place % ranks]).astype(jnp.int32)
    r = ADAPTER_RANK
    step_rows, _, head_part = frozen_triple_weight.shape
    heads_cols = 3 * head_part
    heads_own = jnp.concatenate([frozen_triple_weight.reshape(step_rows, heads_cols), out_weight.T], axis=1)
    units_own = jnp.concatenate([fc_weight, proj_weight.T], axis=1)
    down = jnp.zeros((LANES, model), BF16).at[: 2 * r].set(down_master.reshape(2 * r, model).astype(BF16))
    zero_line = jnp.zeros_like(pre_gain)
    vec = jnp.stack([pre_gain, pre_shift, out_bias, mid_gain, mid_shift, zero_line, zero_line, zero_line]).astype(F32)
    h_near, h_far, h_z = gather_z(heads_own, ())
    u_near, u_far, u_z = gather_z(units_own, (h_z[3],))
    heads, h_xy = gather_xy(h_near, h_far, (), ())
    units, u_xy = gather_xy(u_near, u_far, (h_xy[2], h_xy[3]), ())
    units_other = swapped_blocks(units)
    up_low = up_master.astype(BF16).reshape(2 * ADAPTER_RANK, head_part)
    fc_rows = fc_bias.reshape(-1, head_part)
    small = jnp.concatenate([frozen_triple_bias, fc_rows, up_low], axis=0)
    small = jnp.stack([small, hop(after(small, h_z[0]), 1, 0)])
    bias = small[:, :3].reshape(2, 3 * head_part).astype(F32)
    fc_mine = small[:, 3 : 3 + fc_rows.shape[0]].reshape(2, 1, -1)
    fc_line = jnp.concatenate([fc_mine, core_swap(fc_mine)], axis=1).reshape(1, -1).astype(F32)
    up_both = small[:, 3 + fc_rows.shape[0] :] * jnp.bfloat16(ADAPTER_SCALE)
    up = jnp.zeros((2, LANES, 3 * head_part), BF16)
    up = up.at[:, :r, :head_part].set(up_both[:, :r]).at[:, r : 2 * r, 2 * head_part :].set(up_both[:, r:])
    groups = jnp.arange(LANES, dtype=jnp.int32)[None, :]
    ids = group_ids[:, None]
    normed, latent = norm_rows(idx, tokens, vec, down)
    queries, keys, values = project_heads(idx, normed, latent, bias, up, heads)
    mixed, logsum = attend_fast(queries, keys, values)
    counts = jnp.sum((ids == groups).astype(jnp.int32), axis=0, keepdims=True)
    counts = after(counts, queries)
    bits = 1
    while bits < lax.axis_size("dp"):
        counts = counts + hop(counts, 0, bits)
        bits *= 2
    weight_table = F32(tok_dev * lax.axis_size("dp")) / (GROUPS * counts.astype(F32))

    sent = core_swap(attention_out_send(idx, mixed, heads, heads_cols))
    hidden, normed_mid = attention_out_own(idx, mixed, sent, tokens, vec, heads, heads_cols)
    rows = (normed_mid, cotangent, ids, weight_table, fc_line, vec)
    carried = units_main(idx, 0, *rows, units, units_other, (), None)
    hidden_grad, hidden_low, *out_pieces = units_main(idx, 1, *rows, units, units_other, carried, hidden)
    hidden_other = core_swap(hidden_low)
    dq, dk, dv = attend_back_fast(
        idx, queries, keys, values, mixed, hidden_low, hidden_other, logsum, heads, heads_cols
    )
    in_send, in_own, down_term, up_term = heads_back(idx, dq, dk, dv, normed, latent, up, down, heads)
    in_recv = core_swap(in_send)
    output = to_features(idx, out_pieces, proj_bias.astype(F32).reshape(1, -1))
    input_grad = to_features(idx, tokens_back(idx, in_own, in_recv, tokens, hidden_grad, vec), None)
    up_term = up_term.reshape(2 * r, 2, 3, head_part)
    mine = jnp.concatenate([up_term[:r, 0, 0], up_term[r:, 0, 2]], axis=0)
    theirs = jnp.concatenate([up_term[:r, 1, 0], up_term[r:, 1, 2]], axis=0)
    down_sum = down_term + core_swap(down_term)
    got = hop(jnp.concatenate([down_sum, theirs], axis=1), 1, 0)
    both = jnp.concatenate([down_sum, mine], axis=1) + got
    bits = 1
    while bits < lax.axis_size("dp"):
        both = both + hop(both, 0, bits)
        bits *= 2
    down_grad = both[:, :model].reshape(down_master.shape)
    up_grad = ADAPTER_SCALE * both[:, model:].reshape(up_master.shape)
    step_value = jnp.float32(STEP)
    down_new, down_moment, down_square = adam_update(
        down_master, down_first, down_second, down_grad, step_value, learn_rate
    )
    up_new, up_moment, up_square = adam_update(up_master, up_first, up_second, up_grad, step_value, learn_rate)
    return (
        output,
        input_grad,
        down_new,
        down_moment,
        down_square,
        down_new.astype(BF16),
        up_new,
        up_moment,
        up_square,
        up_new.astype(BF16),
    )


def pick_body(mesh):
    return on_device_fast if mesh.shape["dp"] == 8 and mesh.shape["mp"] == 4 else on_device_general


def solution(mesh):
    body = pick_body(mesh)
    return jax.shard_map(
        body,
        mesh=mesh,
        in_specs=(
            P("dp", None),
            P("dp", None),
            P("dp"),
            P(),
            P(),
            P("dp", None, "mp"),
            P(None, "mp"),
            P("mp", "dp"),
            P(),
            P(),
            P(),
            P("dp", "mp"),
            P("mp"),
            P("mp", "dp"),
            P("mp"),
            P(),
            P(None, None, "mp"),
            P(),
            P(),
            P(None, None, "mp"),
            P(None, None, "mp"),
            P(),
        ),
        out_specs=(
            P("dp", "mp"),
            P("dp", "mp"),
            P(),
            P(),
            P(),
            P(),
            P(None, None, "mp"),
            P(None, None, "mp"),
            P(None, None, "mp"),
            P(None, None, "mp"),
        ),
        check_vma=False,
    )
```

```python
import jax
import jax.numpy as jnp
from jax import lax
from jax.experimental import pallas as pl
from jax.experimental.pallas import tpu as pltpu
from jax.sharding import PartitionSpec as P

HEAD_DIM = 64
ADAPTER_RANK = 4
GROUPS = 16
STEP = 3
MICRO = 2


ADAPTER_SCALE = 8.0
NORM_EPS = 1e-05
MASKED = -1e30
BETA_ONE = 0.5
BETA_TWO = 0.5
ADAM_EPS = 1e-08
DECAY = 0.01


def layer_stats(values):
    center = values - jnp.mean(values, axis=-1, keepdims=True)
    spread = jnp.mean(center * center, axis=-1, keepdims=True)
    scaler = lax.rsqrt(spread + NORM_EPS)
    return (center * scaler, scaler)


def norm_back(normal_hat, scaler, scaled_grad):
    first_mean = jnp.mean(scaled_grad, axis=-1, keepdims=True)
    second_mean = jnp.mean(scaled_grad * normal_hat, axis=-1, keepdims=True)
    return scaler * (scaled_grad - first_mean - normal_hat * second_mean)


def gelu_tanh(values):
    return jax.nn.gelu(values, approximate=True)


def fetch_frozen(frozen_triple_weight, fc_weight, out_weight, proj_weight):
    return (
        lax.all_gather(frozen_triple_weight, "dp", axis=0, tiled=True),
        lax.all_gather(fc_weight, "dp", axis=0, tiled=True),
        lax.all_gather(out_weight, "dp", axis=1, tiled=True),
        lax.all_gather(proj_weight, "dp", axis=1, tiled=True),
    )


def score_block(query_part, key_heads, start, block_rows, key_count):
    score_scale = HEAD_DIM ** (-0.5)
    scores = (
        jnp.einsum("qhd,khd->hqk", query_part, key_heads, preferred_element_type=jnp.float32)
        * score_scale
    )
    allowed = (start + jnp.arange(block_rows, dtype=jnp.int32))[:, None] >= jnp.arange(
        key_count, dtype=jnp.int32
    )[None, :]
    return jnp.where(allowed[None], scores, MASKED)


def attend(queries, key_rows, value_rows):
    length, col_width = queries.shape
    head_count = col_width // HEAD_DIM
    block_rows = min(512, length)
    query_heads = queries.reshape(length, head_count, HEAD_DIM)
    key_heads = key_rows.reshape(length, head_count, HEAD_DIM)
    value_heads = value_rows.reshape(length, head_count, HEAD_DIM)
    mixed_parts = []
    logsum_parts = []
    for index in range(length // block_rows):
        start = index * block_rows
        stop = start + block_rows
        query_part = query_heads[start:stop]
        scores = score_block(query_part, key_heads[:stop], start, block_rows, stop)
        row_top = jnp.max(scores, axis=-1, keepdims=True)
        exp_terms = jnp.exp(scores - row_top)
        row_total = jnp.sum(exp_terms, axis=-1, keepdims=True)
        probs = (exp_terms / row_total).astype(jnp.bfloat16)
        mixed = jnp.einsum(
            "hqk,khd->qhd", probs, value_heads[:stop], preferred_element_type=jnp.float32
        )
        mixed_parts.append(mixed.reshape(block_rows, col_width))
        logsum_parts.append((row_top + jnp.log(row_total))[..., 0])
    return (jnp.concatenate(mixed_parts, axis=0), logsum_parts)


def attend_back(queries, key_rows, value_rows, logsum, mixed_grad):
    length, col_width = queries.shape
    head_count = col_width // HEAD_DIM
    block_rows = min(512, length)
    score_scale = HEAD_DIM ** (-0.5)
    query_heads = queries.reshape(length, head_count, HEAD_DIM)
    key_heads = key_rows.reshape(length, head_count, HEAD_DIM)
    value_heads = value_rows.reshape(length, head_count, HEAD_DIM)
    grad_heads = mixed_grad.reshape(length, head_count, HEAD_DIM)
    key_acc = jnp.zeros((length, head_count, HEAD_DIM), jnp.float32)
    value_acc = jnp.zeros((length, head_count, HEAD_DIM), jnp.float32)
    query_parts = []
    for index in range(length // block_rows):
        start = index * block_rows
        stop = start + block_rows
        query_part = query_heads[start:stop]
        grad_part = grad_heads[start:stop]
        key_part = key_heads[:stop]
        scores = score_block(query_part, key_part, start, block_rows, stop)
        probs = jnp.exp(scores - logsum[index][:, :, None])
        prob_grad = jnp.einsum(
            "qhd,khd->hqk", grad_part, value_heads[:stop], preferred_element_type=jnp.float32
        )
        inner = jnp.sum(prob_grad * probs, axis=-1, keepdims=True)
        score_grad = (probs * (prob_grad - inner)).astype(jnp.bfloat16)
        query_grad = (
            jnp.einsum("hqk,khd->qhd", score_grad, key_part, preferred_element_type=jnp.float32)
            * score_scale
        )
        key_acc = key_acc.at[:stop].add(
            jnp.einsum("hqk,qhd->khd", score_grad, query_part, preferred_element_type=jnp.float32)
            * score_scale
        )
        value_acc = value_acc.at[:stop].add(
            jnp.einsum(
                "hqk,qhd->khd",
                probs.astype(jnp.bfloat16),
                grad_part,
                preferred_element_type=jnp.float32,
            )
        )
        query_parts.append(query_grad.reshape(block_rows, col_width))
    return (
        jnp.concatenate(query_parts, axis=0),
        key_acc.reshape(length, col_width),
        value_acc.reshape(length, col_width),
    )


def adam_update(master, first, second, grad, step_value, learn_rate):
    new_first = BETA_ONE * first + (1.0 - BETA_ONE) * grad
    new_second = BETA_TWO * second + (1.0 - BETA_TWO) * grad * grad
    fix_one = 1.0 - jnp.power(jnp.float32(BETA_ONE), step_value)
    fix_two = 1.0 - jnp.power(jnp.float32(BETA_TWO), step_value)
    update = new_first / fix_one / (jnp.sqrt(new_second / fix_two) + ADAM_EPS)
    new_master = master - learn_rate * (update + DECAY * master)
    return (new_master, new_first, new_second)


def on_device_general(
    tokens,
    cotangent,
    group_ids,
    pre_gain,
    pre_shift,
    frozen_triple_weight,
    frozen_triple_bias,
    out_weight,
    out_bias,
    mid_gain,
    mid_shift,
    fc_weight,
    fc_bias,
    proj_weight,
    proj_bias,
    down_master,
    up_master,
    down_first,
    down_second,
    up_first,
    up_second,
    learn_rate,
):
    tok_dev = tokens.shape[0]
    model_width = tokens.shape[1]
    length = tok_dev // MICRO
    shard_width = model_width // lax.axis_size("mp")
    shard_start = lax.axis_index("mp") * shard_width
    pre_gain_f = pre_gain.astype(jnp.float32)
    pre_shift_f = pre_shift.astype(jnp.float32)
    mid_gain_f = mid_gain.astype(jnp.float32)
    mid_shift_f = mid_shift.astype(jnp.float32)
    out_bias_f = out_bias.astype(jnp.float32)
    fc_bias_f = fc_bias.astype(jnp.float32)
    proj_bias_f = proj_bias.astype(jnp.float32)
    bias_flat = frozen_triple_bias.astype(jnp.float32).reshape(-1)
    onehot = group_ids[:, None] == jnp.arange(GROUPS, dtype=jnp.int32)[None, :]
    local_counts = jnp.sum(onehot.astype(jnp.int32), axis=0)
    totals = lax.psum(local_counts, "dp").astype(jnp.float32)
    own_count = jnp.sum(jnp.where(onehot, totals[None, :], jnp.float32(0.0)), axis=1)
    token_weight = jnp.float32(tok_dev * lax.axis_size("dp")) / (GROUPS * own_count)
    down_low = down_master.astype(jnp.bfloat16).reshape(2 * ADAPTER_RANK, model_width)
    raise_reduced = up_master.astype(jnp.bfloat16)
    grad_down = jnp.zeros((2 * ADAPTER_RANK, model_width), jnp.float32)
    raise_gradient = jnp.zeros(up_master.shape, jnp.float32)
    output_parts = []
    input_parts = []
    for micro_index in range(MICRO):
        current = fetch_frozen(frozen_triple_weight, fc_weight, out_weight, proj_weight)
        qkv_full, fc_full, out_full, proj_full = current
        qkv_flat = qkv_full.reshape(model_width, -1)
        head_width = qkv_flat.shape[1] // 3
        row_start = micro_index * length
        rows_f = lax.dynamic_slice_in_dim(tokens, row_start, length, 0).astype(jnp.float32)
        pre_hat, pre_scale = layer_stats(rows_f)
        normed = (pre_hat * pre_gain_f + pre_shift_f).astype(jnp.bfloat16)
        mixed_proj = jnp.dot(normed, qkv_flat, preferred_element_type=jnp.float32) + bias_flat
        bottleneck = jnp.einsum(
            "td,rd->tr", normed, down_low, preferred_element_type=jnp.float32
        ).astype(jnp.bfloat16)
        queries = (
            mixed_proj[:, :head_width]
            + ADAPTER_SCALE
            * jnp.dot(
                bottleneck[:, :ADAPTER_RANK], raise_reduced[0], preferred_element_type=jnp.float32
            )
        ).astype(jnp.bfloat16)
        key_rows = mixed_proj[:, head_width : 2 * head_width].astype(jnp.bfloat16)
        value_rows = (
            mixed_proj[:, 2 * head_width :]
            + ADAPTER_SCALE
            * jnp.dot(
                bottleneck[:, ADAPTER_RANK:], raise_reduced[1], preferred_element_type=jnp.float32
            )
        ).astype(jnp.bfloat16)
        attended, logsum = attend(queries, key_rows, value_rows)
        attended_low = attended.astype(jnp.bfloat16)
        head_term = jnp.dot(attended_low, out_full, preferred_element_type=jnp.float32).astype(
            jnp.bfloat16
        )
        attn_sum = lax.psum(head_term, "mp").astype(jnp.float32)
        hidden = rows_f + attn_sum + out_bias_f
        mid_hat, mid_scale = layer_stats(hidden)
        normed_mid = (mid_hat * mid_gain_f + mid_shift_f).astype(jnp.bfloat16)
        pre_act = jnp.dot(normed_mid, fc_full, preferred_element_type=jnp.float32) + fc_bias_f
        active, gelu_pullback = jax.vjp(gelu_tanh, pre_act)
        unit_part = jnp.dot(
            active.astype(jnp.bfloat16), proj_full, preferred_element_type=jnp.float32
        ).astype(jnp.bfloat16)
        unit_share = lax.psum_scatter(unit_part, "mp", scatter_dimension=1, tiled=True).astype(
            jnp.float32
        )
        hidden_share = lax.dynamic_slice_in_dim(hidden, shard_start, shard_width, 1)
        output_parts.append((hidden_share + unit_share + proj_bias_f).astype(jnp.bfloat16))
        weight_rows = lax.dynamic_slice_in_dim(token_weight, row_start, length, 0)
        out_grad = (
            lax.dynamic_slice_in_dim(cotangent, row_start, length, 0).astype(jnp.float32)
            * weight_rows[:, None]
        )
        out_low = out_grad.astype(jnp.bfloat16)
        active_grad = jnp.einsum(
            "td,fd->tf", out_low, proj_full, preferred_element_type=jnp.float32
        )
        pre_grad = gelu_pullback(active_grad)[0].astype(jnp.bfloat16)
        mid_part = jnp.einsum(
            "tf,df->td", pre_grad, fc_full, preferred_element_type=jnp.float32
        ).astype(jnp.bfloat16)
        mid_grad = lax.psum(mid_part, "mp").astype(jnp.float32)
        hidden_grad = out_grad + norm_back(mid_hat, mid_scale, mid_gain_f * mid_grad)
        hidden_low = hidden_grad.astype(jnp.bfloat16)
        attended_grad = jnp.einsum(
            "td,hd->th", hidden_low, out_full, preferred_element_type=jnp.float32
        ).astype(jnp.bfloat16)
        query_grad, key_grad, value_grad = attend_back(
            queries, key_rows, value_rows, logsum, attended_grad
        )
        query_low = query_grad.astype(jnp.bfloat16)
        key_low = key_grad.astype(jnp.bfloat16)
        value_low = value_grad.astype(jnp.bfloat16)
        proj_grad = jnp.concatenate([query_low, key_low, value_low], axis=1)
        in_part = jnp.einsum("tc,dc->td", proj_grad, qkv_flat, preferred_element_type=jnp.float32)
        bottleneck_gradient = ADAPTER_SCALE * jnp.concatenate(
            [
                jnp.einsum(
                    "tc,rc->tr", query_low, raise_reduced[0], preferred_element_type=jnp.float32
                ),
                jnp.einsum(
                    "tc,rc->tr", value_low, raise_reduced[1], preferred_element_type=jnp.float32
                ),
            ],
            axis=1,
        )
        latent_low = bottleneck_gradient.astype(jnp.bfloat16)
        in_part = (
            in_part + jnp.dot(latent_low, down_low, preferred_element_type=jnp.float32)
        ).astype(jnp.bfloat16)
        grad_down = grad_down + jnp.einsum(
            "tr,td->rd", latent_low, normed, preferred_element_type=jnp.float32
        )
        raise_gradient = raise_gradient + ADAPTER_SCALE * jnp.stack(
            [
                jnp.einsum(
                    "tr,tc->rc",
                    bottleneck[:, :ADAPTER_RANK],
                    query_low,
                    preferred_element_type=jnp.float32,
                ),
                jnp.einsum(
                    "tr,tc->rc",
                    bottleneck[:, ADAPTER_RANK:],
                    value_low,
                    preferred_element_type=jnp.float32,
                ),
            ],
            axis=0,
        )
        hidden_grad_share = lax.dynamic_slice_in_dim(hidden_grad, shard_start, shard_width, 1)
        in_grad = lax.psum(in_part, "mp").astype(jnp.float32)
        full_grad = norm_back(pre_hat, pre_scale, pre_gain_f * in_grad)
        input_parts.append(
            (
                hidden_grad_share + lax.dynamic_slice_in_dim(full_grad, shard_start, shard_width, 1)
            ).astype(jnp.bfloat16)
        )
    output = jnp.concatenate(output_parts, axis=0)
    input_grad = jnp.concatenate(input_parts, axis=0)
    down_grad = lax.psum(grad_down, ("dp", "mp")).reshape(down_master.shape)
    up_grad = lax.psum(raise_gradient, "dp")
    step_value = jnp.float32(STEP)
    down_new, down_moment, down_square = adam_update(
        down_master, down_first, down_second, down_grad, step_value, learn_rate
    )
    up_new, up_moment, up_square = adam_update(
        up_master, up_first, up_second, up_grad, step_value, learn_rate
    )
    return (
        output,
        input_grad,
        down_new,
        down_moment,
        down_square,
        down_new.astype(jnp.bfloat16),
        up_new,
        up_moment,
        up_square,
        up_new.astype(jnp.bfloat16),
    )


LEN = 1024
BLK = 256
LANES = 128
LOG2E = 1.4426950408889634
NT = (((1,), (1,)), ((), ()))
TN = (((0,), (0,)), ((), ()))
VMEM_LIMIT = 24 << 20
F32 = jnp.float32
BF16 = jnp.bfloat16
AXES = ("dp", "mp")
ANY = pl.BlockSpec(memory_space=pl.ANY)


def cost(flops, nbytes, trans=0):
    return pl.CostEstimate(flops=int(flops), bytes_accessed=int(nbytes), transcendentals=int(trans))


def shape(rows, cols, dtype=BF16):
    return jax.ShapeDtypeStruct((rows, cols), dtype)


def full(rows, cols):
    return pl.BlockSpec((rows, cols), lambda i, ix: (0, 0))


def call(body, name, grid, in_specs, out_specs, out_shape, scratch, est):
    return pl.pallas_call(
        body,
        grid_spec=pltpu.PrefetchScalarGridSpec(
            num_scalar_prefetch=1,
            grid=(grid,),
            in_specs=in_specs,
            out_specs=out_specs,
            scratch_shapes=scratch,
        ),
        out_shape=out_shape,
        compiler_params=pltpu.CompilerParams(vmem_limit_bytes=VMEM_LIMIT),
        cost_estimate=est,
        name=name,
    )


def hop(value, half_bit, dp_bits):
    ranks = lax.axis_size("mp") // 2
    width = lax.axis_size("mp")
    total = lax.axis_size("dp") * width
    flip = dp_bits * width + half_bit * ranks
    return lax.ppermute(value, AXES, [(i, i ^ flip) for i in range(total)])


def core_swap(value):
    total = lax.axis_size("dp") * lax.axis_size("mp")
    return lax.ppermute(value, AXES, [(i, i ^ 1) for i in range(total)])


def after(value, *others):
    return lax.optimization_barrier((value, *others))[0]


def inner_z():
    z = lax.axis_index("dp") // 2
    return jnp.logical_or(z == 1, z == 2)


def z_hop(value, pairs):
    width = lax.axis_size("mp")
    perm = []
    for source, target in pairs:
        for rest in range(2 * width):
            perm.append((source * 2 * width + rest, target * 2 * width + rest))
    return lax.ppermute(value, AXES, perm)


DIGIT = 64
EXTRA = 8
MIDDLE = ((1, 2), (2, 1))
OUTWARD = ((1, 0), (2, 3))


def gather_z(own, first):
    begin = after(own, *first)
    z1 = hop(begin, 0, 2)
    m1 = z_hop(begin, MIDDLE)
    m2 = z_hop(z1, MIDDLE)
    f1 = z_hop(m1, OUTWARD)
    f2 = z_hop(m2, OUTWARD)
    inner = inner_z()
    near = jnp.stack([own, z1])
    far = jnp.stack([jnp.where(inner, m2, f1), jnp.where(inner, m1, f2)])
    return near, far, (z1, m1, m2, f1, f2)


def pair_xy(value):
    return hop(value, 1, 0), hop(value, 0, 1)


def corners(x_near, y_far):
    return hop(x_near, 0, 1), hop(y_far, 1, 0)


def all_blocks(near, x_near, y_near, d_near, far, x_far, y_far, d_far):
    found = []
    for c in (0, 1):
        for array, half_bit, bit in ((near, 0, 0), (x_near, 1, 0), (y_near, 0, 1), (d_near, 1, 1)):
            found.append((array, c, half_bit, 2 * c + bit))
        for array, half_bit, bit in ((far, 0, 0), (x_far, 1, 0), (y_far, 0, 1), (d_far, 1, 1)):
            found.append((array, c, half_bit, 4 + 2 * c + bit))
    return found


def swapped_blocks(found):
    arrays, table = operands(found)
    arrays = [core_swap(array) for array in arrays]
    return [(arrays[e[0]], *e[1:]) for e in table]


def operands(found):
    arrays = []
    table = []
    for array, *entry in found:
        for k, held in enumerate(arrays):
            if held is array:
                break
        else:
            k = len(arrays)
            arrays.append(array)
        table.append((k, *entry))
    return arrays, table


def copies_of(pairs, sems, start=0):
    return [pltpu.make_async_copy(src, dst, sems.at[start + n]) for n, (src, dst) in enumerate(pairs)]


def load_all(pairs, sems):
    copies = copies_of(pairs, sems)
    for copy in copies:
        copy.start()
    for copy in copies:
        copy.wait()


def at_rows(index, size):
    return pl.ds(pl.multiple_of(index * size, size), size)


def at_lanes(index, size):
    return pl.ds(pl.multiple_of(index * size, LANES), size)


def column_pairs(refs, table, w, ix, first, count, spread):
    pairs = []
    for k, slot, half_bit, dp_bits in table:
        src = refs[k].at[slot, pl.ds(0, LANES), pl.ds(first, count)]
        rows = at_rows(ix[0] ^ dp_bits, LANES)
        dst = w.at[half_bit, rows, :] if spread else w.at[rows, pl.ds(half_bit * count, count)]
        pairs.append((src, dst))
    return pairs


def block_pairs(refs, table, w, ix, half_bit, slot_out):
    return [
        (refs[k].at[slot], w.at[slot_out, at_rows(ix[0] ^ dp_bits, refs[k].shape[1]), :])
        for k, slot, a, dp_bits in table
        if a == half_bit
    ]


def pick(low, value, which):
    zero = jnp.zeros((), value.dtype)
    return jnp.where(low, value, zero) if which == 0 else jnp.where(low, zero, value)


def row_stats(values):
    center = values - jnp.mean(values, axis=-1, keepdims=True)
    scaler = lax.rsqrt(jnp.mean(center * center, axis=-1, keepdims=True) + NORM_EPS)
    return center * scaler, scaler


def token_weights(ids, table):
    lanes = lax.broadcasted_iota(jnp.int32, (ids.shape[0], LANES), 1)
    return jnp.sum(jnp.where(ids == lanes, table, 0.0), axis=-1, keepdims=True)


def norm_rows(idx, tokens, vec, down):
    model = tokens.shape[1]
    blocks = LEN // BLK

    def body(ix, tok, vec_ref, down_ref, normed_ref, latent_ref):
        hat, _ = row_stats(tok[...].astype(F32))
        normed = (hat * vec_ref[0:1, :] + vec_ref[1:2, :]).astype(BF16)
        normed_ref[...] = normed
        latent_ref[...] = lax.dot_general(normed, down_ref[...], NT, preferred_element_type=F32).astype(BF16)

    row = lambda c: pl.BlockSpec((BLK, c), lambda i, ix: (i, 0))
    return call(
        body,
        "norm_rows",
        blocks,
        [pl.BlockSpec((BLK, model), lambda i, ix: (ix[1] * blocks + i, 0)), full(8, model), full(LANES, model)],
        [row(model), row(LANES)],
        [shape(LEN, model), shape(LEN, LANES)],
        [],
        cost(2 * LEN * model * LANES, 4 * LEN * model),
    )(idx, tokens, vec, down)


def project_heads(idx, normed, latent, bias, up, found):
    model = normed.shape[1]
    arrays, table = operands(found)
    cols = bias.shape[1]
    part = cols // 3
    n = len(arrays)

    def body(ix, normed_ref, latent_ref, bias_ref, up_ref, *rest):
        msgs = rest[:n]
        q_ref, k_ref, v_ref, w, sems = rest[n:]

        @pl.when(pl.program_id(0) == 0)
        def _():
            load_all(column_pairs(msgs, table, w, ix, 0, cols, True), sems)

        for a in range(2):
            r = jnp.dot(normed_ref[...], w[a], preferred_element_type=F32) + bias_ref[a : a + 1, :]
            r = r + jnp.dot(latent_ref[...], up_ref[a], preferred_element_type=F32)
            for out, s in ((q_ref, 0), (k_ref, 1), (v_ref, 2)):
                out[:, a * part : (a + 1) * part] = r[:, s * part : (s + 1) * part].astype(BF16)

    row = lambda c: pl.BlockSpec((BLK, c), lambda i, ix: (i, 0))
    return call(
        body,
        "project_heads",
        LEN // BLK,
        [row(model), row(LANES), full(2, cols), pl.BlockSpec((2, LANES, cols), lambda i, ix: (0, 0, 0))] + [ANY] * n,
        [row(2 * part)] * 3,
        [shape(LEN, 2 * part)] * 3,
        [pltpu.VMEM((2, model, cols), BF16), pltpu.SemaphoreType.DMA((len(table),))],
        cost(4 * LEN * model * cols, 16 * LEN * model),
    )(idx, normed, latent, bias, up, *arrays)


def attend_fast(queries, key_rows, value_rows):
    length, width = queries.shape
    pairs = width // LANES

    def body(q_ref, k_ref, v_ref, o_ref, lse_ref):
        scale = HEAD_DIM**-0.5 * LOG2E
        low = lax.broadcasted_iota(jnp.int32, (1, LANES), 1) < HEAD_DIM
        k = k_ref[...]
        v = v_ref[...]
        value_of = [pick(low, v, h) for h in range(2)]
        for i in range(length // BLK):
            stop = (i + 1) * BLK
            qb = q_ref[i * BLK : stop, :]
            causal = (lax.broadcasted_iota(jnp.int32, (BLK, stop), 0) + i * BLK) >= lax.broadcasted_iota(
                jnp.int32, (BLK, stop), 1
            )
            out = jnp.zeros((BLK, LANES), F32)
            logs = []
            for h in range(2):
                s = lax.dot_general(pick(low, qb, h), k[:stop], NT, preferred_element_type=F32) * scale
                s = jnp.where(causal, s, MASKED)
                top = jnp.max(s, axis=-1, keepdims=True)
                p = jnp.exp2(s - top)
                total = jnp.sum(p, axis=-1, keepdims=True)
                probs = (p * (1.0 / total)).astype(BF16)
                out = out + jnp.dot(probs, value_of[h][:stop], preferred_element_type=F32)
                logs.append(top + jnp.log2(total))
            o_ref[i * BLK : stop, :] = out.astype(BF16)
            both = jnp.where(
                low, jnp.broadcast_to(logs[0], (BLK, LANES)), jnp.broadcast_to(logs[1], (BLK, LANES))
            ).T
            lse_ref[0, 0:1, i * BLK : stop] = both[0:1]
            lse_ref[0, 1:2, i * BLK : stop] = both[HEAD_DIM : HEAD_DIM + 1]

    spec = pl.BlockSpec((length, LANES), lambda i: (0, i))
    return pl.pallas_call(
        body,
        grid=(pairs,),
        out_shape=(shape(length, width), jax.ShapeDtypeStruct((pairs, 8, length), F32)),
        in_specs=[spec] * 3,
        out_specs=(spec, pl.BlockSpec((1, 8, length), lambda i: (i, 0, 0))),
        compiler_params=pltpu.CompilerParams(vmem_limit_bytes=VMEM_LIMIT),
        cost_estimate=cost(8 * length * length * width, 8 * length * width, 2 * pairs * length * length),
        name="attend",
    )(queries, key_rows, value_rows)


def attention_out_send(idx, attended, found, first):
    width = attended.shape[1]
    arrays, table = operands(found)
    n = len(arrays)
    model = LANES * lax.axis_size("dp")
    half_blocks = LEN // BLK // 2

    def body(ix, att, *rest):
        msgs = rest[:n]
        out, w, sems = rest[n:]

        @pl.when(pl.program_id(0) == 0)
        def _():
            load_all(column_pairs(msgs, table, w, ix, first, width // 2, False), sems)

        out[...] = lax.dot_general(att[...], w[...], NT, preferred_element_type=F32).astype(BF16)

    return call(
        body,
        "attention_out_send",
        half_blocks,
        [pl.BlockSpec((BLK, width), lambda i, ix: ((1 - ix[2]) * half_blocks + i, 0))] + [ANY] * n,
        pl.BlockSpec((BLK, model), lambda i, ix: (i, 0)),
        shape(LEN // 2, model),
        [pltpu.VMEM((model, width), BF16), pltpu.SemaphoreType.DMA((len(table),))],
        cost(LEN * width * model, 2 * LEN * model),
    )(idx, attended, *arrays)


def attention_out_own(idx, attended, received, tokens, vec, found, first):
    width = attended.shape[1]
    arrays, table = operands(found)
    n = len(arrays)
    model = tokens.shape[1]
    half_blocks = LEN // BLK // 2

    def body(ix, att, recv, tok, vec_ref, *rest):
        msgs = rest[:n]
        hidden_ref, normed_ref, w, sems = rest[n:]

        @pl.when(pl.program_id(0) == 0)
        def _():
            load_all(column_pairs(msgs, table, w, ix, first, width // 2, False), sems)

        term = lax.dot_general(att[...], w[...], NT, preferred_element_type=F32)
        hidden = tok[...].astype(F32) + term + recv[...].astype(F32) + vec_ref[2:3, :]
        hidden_ref[...] = hidden
        hat, _ = row_stats(hidden)
        normed_ref[...] = (hat * vec_ref[3:4, :] + vec_ref[4:5, :]).astype(BF16)

    row = pl.BlockSpec((BLK, model), lambda i, ix: (i, 0))
    return call(
        body,
        "attention_out_own",
        half_blocks,
        [
            pl.BlockSpec((BLK, width), lambda i, ix: (ix[2] * half_blocks + i, 0)),
            row,
            pl.BlockSpec((BLK, model), lambda i, ix: ((2 * ix[1] + ix[2]) * half_blocks + i, 0)),
            full(8, model),
        ]
        + [ANY] * n,
        [row, row],
        [shape(LEN // 2, model, F32), shape(LEN // 2, model)],
        [pltpu.VMEM((model, width), BF16), pltpu.SemaphoreType.DMA((len(table),))],
        cost(LEN * width * model, 5 * LEN * model),
    )(idx, attended, received, tokens, vec, *arrays)


def units_main(idx, half_bit, normed, cotangent, ids, weight_table, bias, vec, mine, other, carried, hidden):
    rows, model = normed.shape
    sources = [operands(f) for f in (mine, other)]
    part = sources[0][0][0].shape[2] // 2
    counts = [len(arrays) for arrays, _ in sources]
    last = hidden is not None
    parts = 4
    piece = model // parts
    chunk = 256
    per = part // chunk
    c0 = 0.7978845608028654
    c1 = 0.044715

    def body(ix, normed_ref, cot, ids_ref, table_ref, bias_ref, vec_ref, *rest):
        carry = rest[: len(carried)]
        rest = rest[len(carried) :]
        hid_ref, rest = (rest[0], rest[1:]) if last else (None, rest)
        msgs = (rest[: counts[0]], rest[counts[0] : sum(counts)])
        rest = rest[sum(counts) :]
        n_out = 2 + parts if last else 2
        outs, (w, grad_ref, x_ref, g_ref, pre_ref, act_ref, sems, *held) = rest[:n_out], rest[n_out:]
        groups = []
        used = 0
        for o in range(2):
            pairs = block_pairs(msgs[o], sources[o][1], w, ix, half_bit, o)
            groups.append(copies_of(pairs, sems, used))
            used += len(pairs)
        for group in groups:
            for copy in group:
                copy.start()
        weight = token_weights(ids_ref[...], table_ref[...])
        grad_ref[...] = (cot[...].astype(F32) * weight).astype(BF16)

        def multiply(o, c, slot):
            x_ref[slot] = jnp.dot(normed_ref[...], w[o, :, at_lanes(c, chunk)], preferred_element_type=F32)
            g_ref[slot] = jnp.dot(grad_ref[...], w[o, :, at_lanes(c + per, chunk)], preferred_element_type=F32)

        def bend(o, c, slot):
            at = at_lanes(o * per + c, chunk)
            x = x_ref[slot] + bias_ref[:, at]
            sq = x * x
            th = jnp.tanh(c0 * x * (1.0 + c1 * sq))
            left = 0.5 * (1.0 + th)
            slope = left + 0.5 * x * (1.0 - th * th) * (c0 + (3.0 * c0 * c1) * sq)
            pre_ref[:, at] = (slope * g_ref[slot]).astype(BF16)
            act_ref[:, at] = (x * left).astype(BF16)

        for o in range(2):
            for copy in groups[o]:
                copy.wait()
            if o == 0:
                multiply(0, 0, 0)

                def step(c, _):
                    multiply(0, c, lax.rem(c, 2))
                    bend(0, c - 1, lax.rem(c + 1, 2))
                    return 0

                lax.fori_loop(1, per, step, 0)
            else:
                multiply(1, 0, 0)
                bend(0, per - 1, (per - 1) % 2)

                def step(c, _):
                    multiply(1, c, lax.rem(c, 2))
                    bend(1, c - 1, lax.rem(c + 1, 2))
                    return 0

                lax.fori_loop(1, per, step, 0)
                bend(1, per - 1, (per - 1) % 2)

        def mid_of(n):
            at = at_rows(n, chunk)
            lanes = at_lanes(n, chunk)
            mid = lax.dot_general(pre_ref[:, :part], w[0, at, :part], NT, preferred_element_type=F32)
            mid = mid + lax.dot_general(pre_ref[:, part:], w[1, at, :part], NT, preferred_element_type=F32)
            unit = lax.dot_general(act_ref[:, :part], w[0, at, part:], NT, preferred_element_type=F32)
            unit = unit + lax.dot_general(act_ref[:, part:], w[1, at, part:], NT, preferred_element_type=F32)
            if carry:
                mid = mid + carry[0][:, lanes]
                unit = unit + carry[1][:, lanes]
            return mid, unit, lanes

        if not last:

            def finish(n, _):
                mid, unit, lanes = mid_of(n)
                outs[0][:, lanes] = mid
                outs[1][:, lanes] = unit
                return 0

            lax.fori_loop(0, model // chunk, finish, 0)
            return
        out_low, = held

        def finish(n, _):
            mid, unit, lanes = mid_of(n)
            outs[0][:, lanes] = mid * vec_ref[3:4, lanes]
            out_low[:, lanes] = (unit + hid_ref[:, lanes]).astype(BF16)
            return 0

        lax.fori_loop(0, model // chunk, finish, 0)
        for k in range(parts):
            outs[2 + k][...] = out_low[:, at_lanes((2 * ix[1] + ix[2]) ^ k, piece)]
        step_rows = 128

        def end(r, _):
            at = at_rows(r, step_rows)
            hat, scaler = row_stats(hid_ref[at, :])
            grad = cot[at, :].astype(F32) * token_weights(ids_ref[at, :], table_ref[...])
            grad = grad + norm_back(hat, scaler, outs[0][at, :])
            outs[0][at, :] = grad
            outs[1][at, :] = grad.astype(BF16)
            return 0

        lax.fori_loop(0, rows // step_rows, end, 0)

    def token_rows(i, ix):
        return (2 * ix[1] + ix[2], 0)

    block = full(rows, model)
    specs = [
        block,
        pl.BlockSpec((rows, model), token_rows),
        pl.BlockSpec((rows, 1), token_rows),
        full(1, LANES),
        pl.BlockSpec((1, 2 * part), lambda i, ix: (0, half_bit)),
        full(8, model),
    ]
    specs += [block] * (len(carried) + (1 if last else 0))
    if last:
        out_specs = [block, block] + [full(rows, piece)] * parts
        out_shape = [shape(rows, model, F32), shape(rows, model)] + [shape(rows, piece)] * parts
    else:
        out_specs = [block, block]
        out_shape = [shape(rows, model, F32)] * 2
    arrays = [array for found, _ in sources for array in found]
    return call(
        body,
        "units_main_last" if last else "units_main_first",
        1,
        specs + [ANY] * len(arrays),
        out_specs,
        out_shape,
        [
            pltpu.VMEM((2, model, 2 * part), BF16),
            pltpu.VMEM((rows, model), BF16),
            pltpu.VMEM((2, rows, chunk), F32),
            pltpu.VMEM((2, rows, chunk), F32),
            pltpu.VMEM((rows, 2 * part), BF16),
            pltpu.VMEM((rows, 2 * part), BF16),
            pltpu.SemaphoreType.DMA((sum(len(table) for _, table in sources),)),
        ]
        + ([pltpu.VMEM((rows, model), BF16)] if last else []),
        cost(16 * rows * part * model, 12 * part * model, 2 * rows * part),
    )(idx, normed, cotangent, ids, weight_table, bias, vec, *carried, *((hidden,) if last else ()), *arrays)


def attend_back_fast(idx, queries, key_rows, value_rows, mixed, grad_own, grad_other, logsum, found, first):
    length, width = queries.shape
    pairs = width // LANES
    half, model = grad_own.shape
    arrays, table = operands(found)
    n = len(arrays)

    def body(ix, q_ref, k_ref, v_ref, o_ref, own_ref, other_ref, lse_ref, *rest):
        msgs = rest[:n]
        dq_ref, dk_ref, dv_ref, dq_acc, g_ref, w, sems = rest[n:]
        pair = pl.program_id(0)

        @pl.when(pair == 0)
        def _():
            load_all(column_pairs(msgs, table, w, ix, first, width // 2, False), sems)

        weight = w[:, at_lanes(pair, LANES)]
        for ref, rank in ((own_ref, ix[2]), (other_ref, 1 - ix[2])):
            g_ref[at_rows(rank, half), :] = jnp.dot(ref[...], weight, preferred_element_type=F32).astype(BF16)
        scale = HEAD_DIM**-0.5 * LOG2E
        low = lax.broadcasted_iota(jnp.int32, (1, LANES), 1) < HEAD_DIM
        q = q_ref[...]
        g = g_ref[...]
        qm = [pick(low, q, h) for h in range(2)]
        gm = [pick(low, g, h) for h in range(2)]
        prod = (g.astype(F32) * o_ref[...].astype(F32)).T
        delta = [
            jnp.sum(prod[:HEAD_DIM], axis=0, keepdims=True),
            jnp.sum(prod[HEAD_DIM:], axis=0, keepdims=True),
        ]
        dq_acc[...] = jnp.zeros_like(dq_acc)
        for j in range(length // BLK):
            start = j * BLK
            stop = start + BLK
            span = length - start
            kb = k_ref[start:stop, :]
            vb = v_ref[start:stop, :]
            causal = lax.broadcasted_iota(jnp.int32, (BLK, span), 1) >= lax.broadcasted_iota(
                jnp.int32, (BLK, span), 0
            )
            dk = jnp.zeros((BLK, LANES), F32)
            dv = jnp.zeros((BLK, LANES), F32)
            for h in range(2):
                km = pick(low, kb, h)
                s = lax.dot_general(km, q[start:], NT, preferred_element_type=F32) * scale
                s = jnp.where(causal, s - lse_ref[0, h : h + 1, start:], MASKED)
                p = jnp.exp2(s)
                dp = lax.dot_general(pick(low, vb, h), g[start:], NT, preferred_element_type=F32)
                ds = (p * (dp - delta[h][:, start:])).astype(BF16)
                dk = dk + jnp.dot(ds, qm[h][start:], preferred_element_type=F32)
                dv = dv + jnp.dot(p.astype(BF16), gm[h][start:], preferred_element_type=F32)
                dq_acc[start:, :] += lax.dot_general(ds, km, TN, preferred_element_type=F32)
            dk_ref[start:stop, :] = (dk * HEAD_DIM**-0.5).astype(BF16)
            dv_ref[start:stop, :] = dv.astype(BF16)
        dq_ref[...] = (dq_acc[...] * HEAD_DIM**-0.5).astype(BF16)

    spec = pl.BlockSpec((length, LANES), lambda i, ix: (0, i))
    return call(
        body,
        "attend_back",
        pairs,
        [spec] * 4 + [full(half, model)] * 2 + [pl.BlockSpec((1, 8, length), lambda i, ix: (i, 0, 0))] + [ANY] * n,
        [spec] * 3,
        [shape(length, width)] * 3,
        [
            pltpu.VMEM((length, LANES), F32),
            pltpu.VMEM((length, LANES), BF16),
            pltpu.VMEM((model, width), BF16),
            pltpu.SemaphoreType.DMA((len(table),)),
        ],
        cost(20 * length * length * width, 16 * length * width, 2 * pairs * length * length),
    )(idx, queries, key_rows, value_rows, mixed, grad_own, grad_other, logsum, *arrays)


def heads_back(idx, dq, dk, dv, normed, latent, up, down, found):
    width = dq.shape[1]
    part = width // 2
    model = down.shape[1]
    arrays, table = operands(found)
    cols = 3 * part
    n = len(arrays)
    half_blocks = LEN // BLK // 2

    def body(ix, dq_ref, dk_ref, dv_ref, normed_ref, latent_ref, up_ref, down_ref, *rest):
        msgs = rest[:n]
        send_ref, own_ref, low_ref, raise_ref, w, sems = rest[n:]
        step = pl.program_id(0)

        @pl.when(step == 0)
        def _():
            copies = copies_of(column_pairs(msgs, table, w, ix, 0, cols, True), sems)
            for copy in copies:
                copy.start()
            low_ref[...] = jnp.zeros_like(low_ref)
            raise_ref[...] = jnp.zeros_like(raise_ref)
            for copy in copies:
                copy.wait()

        latent = latent_ref[...]
        low = jnp.zeros((BLK, LANES), F32)
        total = jnp.zeros((BLK, model), F32)
        for a in range(2):
            cut = slice(a * part, (a + 1) * part)
            piece = jnp.concatenate([dq_ref[:, cut], dk_ref[:, cut], dv_ref[:, cut]], axis=1)
            total = total + lax.dot_general(piece, w[a], NT, preferred_element_type=F32)
            low = low + lax.dot_general(piece, up_ref[a], NT, preferred_element_type=F32)
            term = lax.dot_general(latent, piece, TN, preferred_element_type=F32)
            raise_ref[:, a * cols : (a + 1) * cols] += term[:8]
        low = low.astype(BF16)
        total = total + jnp.dot(low, down_ref[...], preferred_element_type=F32)
        low_ref[...] += lax.dot_general(low, normed_ref[...], TN, preferred_element_type=F32)[:8]

        @pl.when(step < half_blocks)
        def _():
            send_ref[...] = total.astype(BF16)

        @pl.when(step >= half_blocks)
        def _():
            own_ref[...] = total

    def rows(i, ix):
        rank = jnp.where(i < half_blocks, 1 - ix[2], ix[2])
        return (rank * half_blocks + lax.rem(i, half_blocks), 0)

    row = lambda c: pl.BlockSpec((BLK, c), rows)
    return call(
        body,
        "heads_back",
        2 * half_blocks,
        [row(width)] * 3
        + [row(model), row(LANES), pl.BlockSpec((2, LANES, cols), lambda i, ix: (0, 0, 0)), full(LANES, model)]
        + [ANY] * n,
        [
            pl.BlockSpec((BLK, model), lambda i, ix: (jnp.minimum(i, half_blocks - 1), 0)),
            pl.BlockSpec((BLK, model), lambda i, ix: (jnp.maximum(i - half_blocks, 0), 0)),
            full(8, model),
            full(8, 2 * cols),
        ],
        [shape(LEN // 2, model), shape(LEN // 2, model, F32), shape(8, model, F32), shape(8, 2 * cols, F32)],
        [pltpu.VMEM((2, model, cols), BF16), pltpu.SemaphoreType.DMA((len(table),))],
        cost(4 * LEN * model * cols, 8 * model * cols),
    )(idx, dq, dk, dv, normed, latent, up, down, *arrays)


def tokens_back(idx, in_own, in_recv, tokens, hidden_grad, vec):
    model = tokens.shape[1]
    half_blocks = LEN // BLK // 2
    parts = 4
    part = model // parts

    def body(ix, own, recv, tok, hg, vec_ref, *rest):
        outs, held = rest[:parts], rest[parts]
        e = vec_ref[0:1, :] * (own[...] + recv[...].astype(F32))
        hat, scaler = row_stats(tok[...].astype(F32))
        held[...] = (hg[...] + norm_back(hat, scaler, e)).astype(BF16)
        for k, out in enumerate(outs):
            out[...] = held[:, at_lanes((2 * ix[1] + ix[2]) ^ k, part)]

    row = pl.BlockSpec((BLK, model), lambda i, ix: (i, 0))
    return call(
        body,
        "tokens_back",
        half_blocks,
        [row, row, pl.BlockSpec((BLK, model), lambda i, ix: ((2 * ix[1] + ix[2]) * half_blocks + i, 0)), row, full(8, model)],
        [pl.BlockSpec((BLK, part), lambda i, ix: (i, 0))] * parts,
        [shape(LEN // 2, part)] * parts,
        [pltpu.VMEM((BLK, model), BF16)],
        cost(20 * LEN * model, 8 * LEN * model),
    )(idx, in_own, in_recv, tokens, hidden_grad, vec)


def to_features(idx, pieces, bias):
    pieces = [pieces[0], core_swap(pieces[1]), hop(pieces[2], 1, 0), both_swap(pieces[3])]
    rows, part = pieces[0].shape
    parts = len(pieces)

    def body(ix, bias_ref, *rest):
        outs = rest[parts]
        for k in range(parts):
            value = rest[k][...]
            if bias is not None:
                value = (value.astype(F32) + bias_ref[...]).astype(BF16)
            outs[at_rows((2 * ix[1] + ix[2]) ^ k, rows), :] = value

    extra = jnp.zeros((1, part), F32) if bias is None else bias
    return call(
        body,
        "to_features",
        1,
        [full(1, part)] + [full(rows, part)] * parts,
        full(parts * rows, part),
        shape(parts * rows, part),
        [],
        cost(parts * rows * part, 4 * parts * rows * part),
    )(idx, extra, *pieces)


def both_swap(value):
    total = lax.axis_size("dp") * lax.axis_size("mp")
    return lax.ppermute(value, AXES, [(i, i ^ 3) for i in range(total)])


def on_device_fast(
    tokens,
    cotangent,
    group_ids,
    pre_gain,
    pre_shift,
    frozen_triple_weight,
    frozen_triple_bias,
    out_weight,
    out_bias,
    mid_gain,
    mid_shift,
    fc_weight,
    fc_bias,
    proj_weight,
    proj_bias,
    down_master,
    up_master,
    down_first,
    down_second,
    up_first,
    up_second,
    learn_rate,
):
    tok_dev, model = tokens.shape
    ranks = lax.axis_size("mp") // 2
    place = lax.axis_index("mp")
    idx = jnp.stack([lax.axis_index("dp"), place // ranks, place % ranks]).astype(jnp.int32)
    r = ADAPTER_RANK
    step_rows, _, head_part = frozen_triple_weight.shape
    heads_cols = 3 * head_part
    ids = group_ids[:, None]
    groups = jnp.arange(LANES, dtype=jnp.int32)[None, :]
    counts = jnp.sum((ids == groups).astype(jnp.int32), axis=0)
    up_low = up_master.astype(BF16).reshape(2 * r, head_part)
    fc_rows = fc_bias.reshape(-1, head_part)
    small = jnp.concatenate([frozen_triple_bias, fc_rows, up_low], axis=0)
    n_fc, n_small = fc_rows.shape[0], small.shape[0]
    digits = jnp.concatenate([counts // DIGIT, counts % DIGIT]).astype(BF16).reshape(1, head_part)
    spare = 4 * EXTRA - 1 - n_small
    extra = jnp.concatenate([digits, small, jnp.zeros((spare, head_part), BF16)], axis=0).reshape(EXTRA, model)
    heads_own = jnp.concatenate([frozen_triple_weight.reshape(step_rows, heads_cols), out_weight.T], axis=1)
    heads_own = jnp.concatenate([heads_own, extra], axis=0)
    units_own = jnp.concatenate([fc_weight, proj_weight.T], axis=1)
    down = jnp.zeros((LANES, model), BF16).at[: 2 * r].set(down_master.reshape(2 * r, model).astype(BF16))
    zero_line = jnp.zeros_like(pre_gain)
    vec = jnp.stack([pre_gain, pre_shift, out_bias, mid_gain, mid_shift, zero_line, zero_line, zero_line]).astype(F32)
    h_near, h_far, h_z = gather_z(heads_own, ())
    hx_near, hy_near = pair_xy(h_near)
    hx_far, hy_far = pair_xy(after(h_far, hx_near, hy_near))
    hd_near, hd_far = corners(after(hx_near, h_far), hy_far)
    heads = all_blocks(h_near, hx_near, hy_near, hd_near, h_far, hx_far, hy_far, hd_far)
    u_near, u_far, u_z = gather_z(units_own, (hx_near, hy_near))
    theirs_small = hx_near[0, step_rows:].reshape(-1, head_part)[1 : 1 + n_small]
    small = jnp.stack([small, theirs_small])
    bias = small[:, :3].reshape(2, 3 * head_part).astype(F32)
    fc_mine = small[:, 3 : 3 + n_fc].reshape(2, 1, -1)
    fc_line = jnp.concatenate([fc_mine, core_swap(fc_mine)], axis=1).reshape(1, -1).astype(F32)
    up_both = small[:, 3 + n_fc :] * jnp.bfloat16(ADAPTER_SCALE)
    up = jnp.zeros((2, LANES, 3 * head_part), BF16)
    up = up.at[:, :r, :head_part].set(up_both[:, :r]).at[:, r : 2 * r, 2 * head_part :].set(up_both[:, r:])
    tallies = jnp.stack([v[c, step_rows] for v in (h_near, h_far, hy_near, hy_far) for c in (0, 1)]).astype(F32)
    tallies = jnp.sum(tallies[:, :head_part].reshape(-1, 2, LANES), axis=0)
    weight_table = F32(tok_dev * lax.axis_size("dp")) / (GROUPS * (DIGIT * tallies[:1] + tallies[1:]))
    normed, latent = norm_rows(idx, tokens, vec, down)
    near_go = after(u_near, hd_near, hd_far)
    ux_near, uy_near = pair_xy(near_go)
    queries, keys, values = project_heads(idx, normed, latent, bias, up, heads)
    mixed, logsum = attend_fast(queries, keys, values)
    far_go = after(u_far, queries)
    ux_far, uy_far = pair_xy(far_go)
    sent = core_swap(attention_out_send(idx, mixed, heads, heads_cols))
    hidden, normed_mid = attention_out_own(idx, mixed, sent, tokens, vec, heads, heads_cols)
    straight = all_blocks(u_near, ux_near, uy_near, None, u_far, ux_far, uy_far, None)
    first_mine = [e for e in straight if e[2] == 0]
    first_other = swapped_blocks(first_mine)
    rows = (normed_mid, cotangent, ids, weight_table, fc_line, vec)
    ux_near, uy_near, uy_far, _, _ = lax.optimization_barrier((ux_near, uy_near, uy_far, ux_far, normed_mid))
    ud_near, ud_far = corners(ux_near, uy_far)
    carried = units_main(idx, 0, *rows, first_mine, first_other, (), None)
    ud_near, ud_far, _ = lax.optimization_barrier((ud_near, ud_far, carried[0]))
    units = all_blocks(u_near, ux_near, uy_near, ud_near, u_far, ux_far, uy_far, ud_far)
    last_mine = [e for e in units if e[2] == 1]
    last_other = swapped_blocks(last_mine)
    hidden_grad, hidden_low, *out_pieces = units_main(idx, 1, *rows, last_mine, last_other, carried, hidden)
    hidden_other = core_swap(hidden_low)
    dq, dk, dv = attend_back_fast(
        idx, queries, keys, values, mixed, hidden_low, hidden_other, logsum, heads, heads_cols
    )
    in_send, in_own, down_term, up_term = heads_back(idx, dq, dk, dv, normed, latent, up, down, heads)
    in_recv = core_swap(in_send)
    output = to_features(idx, out_pieces, proj_bias.astype(F32).reshape(1, -1))
    input_grad = to_features(idx, tokens_back(idx, in_own, in_recv, tokens, hidden_grad, vec), None)
    up_term = up_term.reshape(2 * r, 2, 3, head_part)
    mine = jnp.concatenate([up_term[:r, 0, 0], up_term[r:, 0, 2]], axis=0)
    theirs = jnp.concatenate([up_term[:r, 1, 0], up_term[r:, 1, 2]], axis=0)
    down_sum = down_term + core_swap(down_term)
    got = hop(jnp.concatenate([down_sum, theirs], axis=1), 1, 0)
    both = jnp.concatenate([down_sum, mine], axis=1) + got
    bits = 1
    while bits < lax.axis_size("dp"):
        both = both + hop(both, 0, bits)
        bits *= 2
    down_grad = both[:, :model].reshape(down_master.shape)
    up_grad = ADAPTER_SCALE * both[:, model:].reshape(up_master.shape)
    step_value = jnp.float32(STEP)
    down_new, down_moment, down_square = adam_update(
        down_master, down_first, down_second, down_grad, step_value, learn_rate
    )
    up_new, up_moment, up_square = adam_update(up_master, up_first, up_second, up_grad, step_value, learn_rate)
    return (
        output,
        input_grad,
        down_new,
        down_moment,
        down_square,
        down_new.astype(BF16),
        up_new,
        up_moment,
        up_square,
        up_new.astype(BF16),
    )


def pick_body(mesh):
    return on_device_fast if mesh.shape["dp"] == 8 and mesh.shape["mp"] == 4 else on_device_general


def solution(mesh):
    body = pick_body(mesh)
    return jax.shard_map(
        body,
        mesh=mesh,
        in_specs=(
            P("dp", None),
            P("dp", None),
            P("dp"),
            P(),
            P(),
            P("dp", None, "mp"),
            P(None, "mp"),
            P("mp", "dp"),
            P(),
            P(),
            P(),
            P("dp", "mp"),
            P("mp"),
            P("mp", "dp"),
            P("mp"),
            P(),
            P(None, None, "mp"),
            P(),
            P(),
            P(None, None, "mp"),
            P(None, None, "mp"),
            P(),
        ),
        out_specs=(
            P("dp", "mp"),
            P("dp", "mp"),
            P(),
            P(),
            P(),
            P(),
            P(None, None, "mp"),
            P(None, None, "mp"),
            P(None, None, "mp"),
            P(None, None, "mp"),
        ),
        check_vma=False,
    )
```

```python
import jax
import jax.numpy as jnp
from jax import lax
from jax.experimental import pallas as pl
from jax.experimental.pallas import tpu as pltpu
from jax.sharding import PartitionSpec as P

HEAD_DIM = 64
ADAPTER_RANK = 4
GROUPS = 16
STEP = 3
MICRO = 2


ADAPTER_SCALE = 8.0
NORM_EPS = 1e-05
MASKED = -1e30
BETA_ONE = 0.5
BETA_TWO = 0.5
ADAM_EPS = 1e-08
DECAY = 0.01


def layer_stats(values):
    center = values - jnp.mean(values, axis=-1, keepdims=True)
    spread = jnp.mean(center * center, axis=-1, keepdims=True)
    scaler = lax.rsqrt(spread + NORM_EPS)
    return (center * scaler, scaler)


def norm_back(normal_hat, scaler, scaled_grad):
    first_mean = jnp.mean(scaled_grad, axis=-1, keepdims=True)
    second_mean = jnp.mean(scaled_grad * normal_hat, axis=-1, keepdims=True)
    return scaler * (scaled_grad - first_mean - normal_hat * second_mean)


def gelu_tanh(values):
    return jax.nn.gelu(values, approximate=True)


def fetch_frozen(frozen_triple_weight, fc_weight, out_weight, proj_weight):
    return (
        lax.all_gather(frozen_triple_weight, "dp", axis=0, tiled=True),
        lax.all_gather(fc_weight, "dp", axis=0, tiled=True),
        lax.all_gather(out_weight, "dp", axis=1, tiled=True),
        lax.all_gather(proj_weight, "dp", axis=1, tiled=True),
    )


def score_block(query_part, key_heads, start, block_rows, key_count):
    score_scale = HEAD_DIM ** (-0.5)
    scores = (
        jnp.einsum("qhd,khd->hqk", query_part, key_heads, preferred_element_type=jnp.float32)
        * score_scale
    )
    allowed = (start + jnp.arange(block_rows, dtype=jnp.int32))[:, None] >= jnp.arange(
        key_count, dtype=jnp.int32
    )[None, :]
    return jnp.where(allowed[None], scores, MASKED)


def attend(queries, key_rows, value_rows):
    length, col_width = queries.shape
    head_count = col_width // HEAD_DIM
    block_rows = min(512, length)
    query_heads = queries.reshape(length, head_count, HEAD_DIM)
    key_heads = key_rows.reshape(length, head_count, HEAD_DIM)
    value_heads = value_rows.reshape(length, head_count, HEAD_DIM)
    mixed_parts = []
    logsum_parts = []
    for index in range(length // block_rows):
        start = index * block_rows
        stop = start + block_rows
        query_part = query_heads[start:stop]
        scores = score_block(query_part, key_heads[:stop], start, block_rows, stop)
        row_top = jnp.max(scores, axis=-1, keepdims=True)
        exp_terms = jnp.exp(scores - row_top)
        row_total = jnp.sum(exp_terms, axis=-1, keepdims=True)
        probs = (exp_terms / row_total).astype(jnp.bfloat16)
        mixed = jnp.einsum(
            "hqk,khd->qhd", probs, value_heads[:stop], preferred_element_type=jnp.float32
        )
        mixed_parts.append(mixed.reshape(block_rows, col_width))
        logsum_parts.append((row_top + jnp.log(row_total))[..., 0])
    return (jnp.concatenate(mixed_parts, axis=0), logsum_parts)


def attend_back(queries, key_rows, value_rows, logsum, mixed_grad):
    length, col_width = queries.shape
    head_count = col_width // HEAD_DIM
    block_rows = min(512, length)
    score_scale = HEAD_DIM ** (-0.5)
    query_heads = queries.reshape(length, head_count, HEAD_DIM)
    key_heads = key_rows.reshape(length, head_count, HEAD_DIM)
    value_heads = value_rows.reshape(length, head_count, HEAD_DIM)
    grad_heads = mixed_grad.reshape(length, head_count, HEAD_DIM)
    key_acc = jnp.zeros((length, head_count, HEAD_DIM), jnp.float32)
    value_acc = jnp.zeros((length, head_count, HEAD_DIM), jnp.float32)
    query_parts = []
    for index in range(length // block_rows):
        start = index * block_rows
        stop = start + block_rows
        query_part = query_heads[start:stop]
        grad_part = grad_heads[start:stop]
        key_part = key_heads[:stop]
        scores = score_block(query_part, key_part, start, block_rows, stop)
        probs = jnp.exp(scores - logsum[index][:, :, None])
        prob_grad = jnp.einsum(
            "qhd,khd->hqk", grad_part, value_heads[:stop], preferred_element_type=jnp.float32
        )
        inner = jnp.sum(prob_grad * probs, axis=-1, keepdims=True)
        score_grad = (probs * (prob_grad - inner)).astype(jnp.bfloat16)
        query_grad = (
            jnp.einsum("hqk,khd->qhd", score_grad, key_part, preferred_element_type=jnp.float32)
            * score_scale
        )
        key_acc = key_acc.at[:stop].add(
            jnp.einsum("hqk,qhd->khd", score_grad, query_part, preferred_element_type=jnp.float32)
            * score_scale
        )
        value_acc = value_acc.at[:stop].add(
            jnp.einsum(
                "hqk,qhd->khd",
                probs.astype(jnp.bfloat16),
                grad_part,
                preferred_element_type=jnp.float32,
            )
        )
        query_parts.append(query_grad.reshape(block_rows, col_width))
    return (
        jnp.concatenate(query_parts, axis=0),
        key_acc.reshape(length, col_width),
        value_acc.reshape(length, col_width),
    )


def adam_update(master, first, second, grad, step_value, learn_rate):
    new_first = BETA_ONE * first + (1.0 - BETA_ONE) * grad
    new_second = BETA_TWO * second + (1.0 - BETA_TWO) * grad * grad
    fix_one = 1.0 - jnp.power(jnp.float32(BETA_ONE), step_value)
    fix_two = 1.0 - jnp.power(jnp.float32(BETA_TWO), step_value)
    update = new_first / fix_one / (jnp.sqrt(new_second / fix_two) + ADAM_EPS)
    new_master = master - learn_rate * (update + DECAY * master)
    return (new_master, new_first, new_second)


def on_device_general(
    tokens,
    cotangent,
    group_ids,
    pre_gain,
    pre_shift,
    frozen_triple_weight,
    frozen_triple_bias,
    out_weight,
    out_bias,
    mid_gain,
    mid_shift,
    fc_weight,
    fc_bias,
    proj_weight,
    proj_bias,
    down_master,
    up_master,
    down_first,
    down_second,
    up_first,
    up_second,
    learn_rate,
):
    tok_dev = tokens.shape[0]
    model_width = tokens.shape[1]
    length = tok_dev // MICRO
    shard_width = model_width // lax.axis_size("mp")
    shard_start = lax.axis_index("mp") * shard_width
    pre_gain_f = pre_gain.astype(jnp.float32)
    pre_shift_f = pre_shift.astype(jnp.float32)
    mid_gain_f = mid_gain.astype(jnp.float32)
    mid_shift_f = mid_shift.astype(jnp.float32)
    out_bias_f = out_bias.astype(jnp.float32)
    fc_bias_f = fc_bias.astype(jnp.float32)
    proj_bias_f = proj_bias.astype(jnp.float32)
    bias_flat = frozen_triple_bias.astype(jnp.float32).reshape(-1)
    onehot = group_ids[:, None] == jnp.arange(GROUPS, dtype=jnp.int32)[None, :]
    local_counts = jnp.sum(onehot.astype(jnp.int32), axis=0)
    totals = lax.psum(local_counts, "dp").astype(jnp.float32)
    own_count = jnp.sum(jnp.where(onehot, totals[None, :], jnp.float32(0.0)), axis=1)
    token_weight = jnp.float32(tok_dev * lax.axis_size("dp")) / (GROUPS * own_count)
    down_low = down_master.astype(jnp.bfloat16).reshape(2 * ADAPTER_RANK, model_width)
    raise_reduced = up_master.astype(jnp.bfloat16)
    grad_down = jnp.zeros((2 * ADAPTER_RANK, model_width), jnp.float32)
    raise_gradient = jnp.zeros(up_master.shape, jnp.float32)
    output_parts = []
    input_parts = []
    for micro_index in range(MICRO):
        current = fetch_frozen(frozen_triple_weight, fc_weight, out_weight, proj_weight)
        qkv_full, fc_full, out_full, proj_full = current
        qkv_flat = qkv_full.reshape(model_width, -1)
        head_width = qkv_flat.shape[1] // 3
        row_start = micro_index * length
        rows_f = lax.dynamic_slice_in_dim(tokens, row_start, length, 0).astype(jnp.float32)
        pre_hat, pre_scale = layer_stats(rows_f)
        normed = (pre_hat * pre_gain_f + pre_shift_f).astype(jnp.bfloat16)
        mixed_proj = jnp.dot(normed, qkv_flat, preferred_element_type=jnp.float32) + bias_flat
        bottleneck = jnp.einsum(
            "td,rd->tr", normed, down_low, preferred_element_type=jnp.float32
        ).astype(jnp.bfloat16)
        queries = (
            mixed_proj[:, :head_width]
            + ADAPTER_SCALE
            * jnp.dot(
                bottleneck[:, :ADAPTER_RANK], raise_reduced[0], preferred_element_type=jnp.float32
            )
        ).astype(jnp.bfloat16)
        key_rows = mixed_proj[:, head_width : 2 * head_width].astype(jnp.bfloat16)
        value_rows = (
            mixed_proj[:, 2 * head_width :]
            + ADAPTER_SCALE
            * jnp.dot(
                bottleneck[:, ADAPTER_RANK:], raise_reduced[1], preferred_element_type=jnp.float32
            )
        ).astype(jnp.bfloat16)
        attended, logsum = attend(queries, key_rows, value_rows)
        attended_low = attended.astype(jnp.bfloat16)
        head_term = jnp.dot(attended_low, out_full, preferred_element_type=jnp.float32).astype(
            jnp.bfloat16
        )
        attn_sum = lax.psum(head_term, "mp").astype(jnp.float32)
        hidden = rows_f + attn_sum + out_bias_f
        mid_hat, mid_scale = layer_stats(hidden)
        normed_mid = (mid_hat * mid_gain_f + mid_shift_f).astype(jnp.bfloat16)
        pre_act = jnp.dot(normed_mid, fc_full, preferred_element_type=jnp.float32) + fc_bias_f
        active, gelu_pullback = jax.vjp(gelu_tanh, pre_act)
        unit_part = jnp.dot(
            active.astype(jnp.bfloat16), proj_full, preferred_element_type=jnp.float32
        ).astype(jnp.bfloat16)
        unit_share = lax.psum_scatter(unit_part, "mp", scatter_dimension=1, tiled=True).astype(
            jnp.float32
        )
        hidden_share = lax.dynamic_slice_in_dim(hidden, shard_start, shard_width, 1)
        output_parts.append((hidden_share + unit_share + proj_bias_f).astype(jnp.bfloat16))
        weight_rows = lax.dynamic_slice_in_dim(token_weight, row_start, length, 0)
        out_grad = (
            lax.dynamic_slice_in_dim(cotangent, row_start, length, 0).astype(jnp.float32)
            * weight_rows[:, None]
        )
        out_low = out_grad.astype(jnp.bfloat16)
        active_grad = jnp.einsum(
            "td,fd->tf", out_low, proj_full, preferred_element_type=jnp.float32
        )
        pre_grad = gelu_pullback(active_grad)[0].astype(jnp.bfloat16)
        mid_part = jnp.einsum(
            "tf,df->td", pre_grad, fc_full, preferred_element_type=jnp.float32
        ).astype(jnp.bfloat16)
        mid_grad = lax.psum(mid_part, "mp").astype(jnp.float32)
        hidden_grad = out_grad + norm_back(mid_hat, mid_scale, mid_gain_f * mid_grad)
        hidden_low = hidden_grad.astype(jnp.bfloat16)
        attended_grad = jnp.einsum(
            "td,hd->th", hidden_low, out_full, preferred_element_type=jnp.float32
        ).astype(jnp.bfloat16)
        query_grad, key_grad, value_grad = attend_back(
            queries, key_rows, value_rows, logsum, attended_grad
        )
        query_low = query_grad.astype(jnp.bfloat16)
        key_low = key_grad.astype(jnp.bfloat16)
        value_low = value_grad.astype(jnp.bfloat16)
        proj_grad = jnp.concatenate([query_low, key_low, value_low], axis=1)
        in_part = jnp.einsum("tc,dc->td", proj_grad, qkv_flat, preferred_element_type=jnp.float32)
        bottleneck_gradient = ADAPTER_SCALE * jnp.concatenate(
            [
                jnp.einsum(
                    "tc,rc->tr", query_low, raise_reduced[0], preferred_element_type=jnp.float32
                ),
                jnp.einsum(
                    "tc,rc->tr", value_low, raise_reduced[1], preferred_element_type=jnp.float32
                ),
            ],
            axis=1,
        )
        latent_low = bottleneck_gradient.astype(jnp.bfloat16)
        in_part = (
            in_part + jnp.dot(latent_low, down_low, preferred_element_type=jnp.float32)
        ).astype(jnp.bfloat16)
        grad_down = grad_down + jnp.einsum(
            "tr,td->rd", latent_low, normed, preferred_element_type=jnp.float32
        )
        raise_gradient = raise_gradient + ADAPTER_SCALE * jnp.stack(
            [
                jnp.einsum(
                    "tr,tc->rc",
                    bottleneck[:, :ADAPTER_RANK],
                    query_low,
                    preferred_element_type=jnp.float32,
                ),
                jnp.einsum(
                    "tr,tc->rc",
                    bottleneck[:, ADAPTER_RANK:],
                    value_low,
                    preferred_element_type=jnp.float32,
                ),
            ],
            axis=0,
        )
        hidden_grad_share = lax.dynamic_slice_in_dim(hidden_grad, shard_start, shard_width, 1)
        in_grad = lax.psum(in_part, "mp").astype(jnp.float32)
        full_grad = norm_back(pre_hat, pre_scale, pre_gain_f * in_grad)
        input_parts.append(
            (
                hidden_grad_share + lax.dynamic_slice_in_dim(full_grad, shard_start, shard_width, 1)
            ).astype(jnp.bfloat16)
        )
    output = jnp.concatenate(output_parts, axis=0)
    input_grad = jnp.concatenate(input_parts, axis=0)
    down_grad = lax.psum(grad_down, ("dp", "mp")).reshape(down_master.shape)
    up_grad = lax.psum(raise_gradient, "dp")
    step_value = jnp.float32(STEP)
    down_new, down_moment, down_square = adam_update(
        down_master, down_first, down_second, down_grad, step_value, learn_rate
    )
    up_new, up_moment, up_square = adam_update(
        up_master, up_first, up_second, up_grad, step_value, learn_rate
    )
    return (
        output,
        input_grad,
        down_new,
        down_moment,
        down_square,
        down_new.astype(jnp.bfloat16),
        up_new,
        up_moment,
        up_square,
        up_new.astype(jnp.bfloat16),
    )


LEN = 1024
BLK = 256
LANES = 128
LOG2E = 1.4426950408889634
NT = (((1,), (1,)), ((), ()))
TN = (((0,), (0,)), ((), ()))
VMEM_LIMIT = 24 << 20
F32 = jnp.float32
BF16 = jnp.bfloat16
AXES = ("dp", "mp")
ANY = pl.BlockSpec(memory_space=pl.ANY)


def cost(flops, nbytes, trans=0):
    return pl.CostEstimate(flops=int(flops) // 10, bytes_accessed=int(nbytes) // 10, transcendentals=int(trans) // 10)


def shape(rows, cols, dtype=BF16):
    return jax.ShapeDtypeStruct((rows, cols), dtype)


def full(rows, cols):
    return pl.BlockSpec((rows, cols), lambda i, ix: (0, 0))


def call(body, name, grid, in_specs, out_specs, out_shape, scratch, est, grant=None):
    return pl.pallas_call(
        body,
        grid_spec=pltpu.PrefetchScalarGridSpec(
            num_scalar_prefetch=1,
            grid=(grid,),
            in_specs=in_specs,
            out_specs=out_specs,
            scratch_shapes=scratch,
        ),
        out_shape=out_shape,
        compiler_params=pltpu.CompilerParams(vmem_limit_bytes=grant or VMEM_LIMIT),
        cost_estimate=est,
        name=name,
    )


def hop(value, half_bit, dp_bits):
    ranks = lax.axis_size("mp") // 2
    width = lax.axis_size("mp")
    total = lax.axis_size("dp") * width
    flip = dp_bits * width + half_bit * ranks
    return lax.ppermute(value, AXES, [(i, i ^ flip) for i in range(total)])


def core_swap(value):
    total = lax.axis_size("dp") * lax.axis_size("mp")
    return lax.ppermute(value, AXES, [(i, i ^ 1) for i in range(total)])


def after(value, *others):
    return lax.optimization_barrier((value, *others))[0]


def inner_z():
    z = lax.axis_index("dp") // 2
    return jnp.logical_or(z == 1, z == 2)


def z_hop(value, pairs):
    width = lax.axis_size("mp")
    perm = []
    for source, target in pairs:
        for rest in range(2 * width):
            perm.append((source * 2 * width + rest, target * 2 * width + rest))
    return lax.ppermute(value, AXES, perm)


DIGIT = 64
CUTS = 1
EXTRA = 8
MIDDLE = ((1, 2), (2, 1))
OUTWARD = ((1, 0), (2, 3))


def gather_z(own, first):
    begin = after(own, *first)
    z1 = hop(begin, 0, 2)
    m1 = z_hop(begin, MIDDLE)
    m2 = z_hop(z1, MIDDLE)
    f1 = z_hop(m1, OUTWARD)
    f2 = z_hop(m2, OUTWARD)
    inner = inner_z()
    return z1, jnp.where(inner, m2, f1), jnp.where(inner, m1, f2)


def pair_xy(value):
    return hop(value, 1, 0), hop(value, 0, 1)


def blocks_of(array, first, half_bit, bit):
    return [(array, slot, half_bit, 2 * (first + slot) + bit) for slot in range(array.shape[0])]


def swapped_blocks(found):
    arrays, table = operands(found)
    arrays = [core_swap(array) for array in arrays]
    return [(arrays[e[0]], *e[1:]) for e in table]


def operands(found):
    arrays = []
    table = []
    for array, *entry in found:
        for k, held in enumerate(arrays):
            if held is array:
                break
        else:
            k = len(arrays)
            arrays.append(array)
        table.append((k, *entry))
    return arrays, table


def copies_of(pairs, sems, start=0):
    return [pltpu.make_async_copy(src, dst, sems.at[start + n]) for n, (src, dst) in enumerate(pairs)]


def load_all(pairs, sems):
    copies = copies_of(pairs, sems)
    for copy in copies:
        copy.start()
    for copy in copies:
        copy.wait()


def at_rows(index, size):
    return pl.ds(pl.multiple_of(index * size, size), size)


def at_lanes(index, size):
    return pl.ds(pl.multiple_of(index * size, LANES), size)


def column_pairs(refs, table, w, ix, first, count, spread):
    pairs = []
    for k, slot, half_bit, dp_bits in table:
        src = refs[k].at[slot, pl.ds(0, LANES), pl.ds(first, count)]
        rows = at_rows(ix[0] ^ dp_bits, LANES)
        dst = w.at[half_bit, rows, :] if spread else w.at[rows, pl.ds(half_bit * count, count)]
        pairs.append((src, dst))
    return pairs


def block_pairs(refs, table, w, ix, half_bit, slot_out):
    return [
        (refs[k].at[slot], w.at[slot_out, at_rows(ix[0] ^ dp_bits, refs[k].shape[1]), :])
        for k, slot, a, dp_bits in table
        if a == half_bit
    ]


def both_heads(low, value):
    zero = jnp.zeros((), value.dtype)
    return jnp.concatenate([jnp.where(low, value, zero), jnp.where(low, zero, value)], axis=0)


def row_stats(values):
    center = values - jnp.mean(values, axis=-1, keepdims=True)
    scaler = lax.rsqrt(jnp.mean(center * center, axis=-1, keepdims=True) + NORM_EPS)
    return center * scaler, scaler


def lines_of(block):
    part = block.shape[1] // 4
    return lambda n: block[n // 4 : n // 4 + 1, n % 4 * part : (n % 4 + 1) * part]


def prepare_blocks(idx, ids, triple, out_weight, bias, fc_bias, up, fc_weight, proj_weight):
    rows, _, part = triple.shape
    model = 4 * part

    def body(ix, ids_ref, triple_ref, out_ref, bias_ref, fc_ref, up_ref, fcw_ref, proj_ref, block_ref, units_ref, spare):
        units_ref[0, :, :model] = fcw_ref[...]
        units_ref[0, :, model:] = proj_ref[...].astype(F32).T.astype(BF16)
        for s in range(3):
            block_ref[:rows, s * part : (s + 1) * part] = triple_ref[:, s, :]
        block_ref[:rows, 3 * part :] = out_ref[...].astype(F32).T.astype(BF16)
        lane = lax.broadcasted_iota(jnp.int32, (1, LANES), 1)
        counts = jnp.zeros((1, LANES), F32)
        ids = ids_ref[...]
        for g in range(GROUPS):
            hits = jnp.where(ids == g, 1.0, 0.0)
            total = jnp.sum(jnp.sum(hits, axis=0, keepdims=True), axis=1, keepdims=True)
            counts = jnp.where(lane == g, total, counts)
        high = jnp.floor(counts * (1.0 / DIGIT))
        spare[...] = jnp.zeros_like(spare)
        line = lines_of(spare)
        spare[0:1, :LANES] = high
        spare[0:1, LANES : 2 * LANES] = counts - DIGIT * high

        def put(n, value):
            spare[n // 4 : n // 4 + 1, n % 4 * part : (n % 4 + 1) * part] = value.astype(F32)

        for s in range(3):
            put(1 + s, bias_ref[s : s + 1, :])
        for s in range(4):
            put(4 + s, fc_ref[:, s * part : (s + 1) * part])
        for s in range(8):
            put(8 + s, up_ref[s // ADAPTER_RANK, s % ADAPTER_RANK : s % ADAPTER_RANK + 1, :])
        block_ref[rows:, :] = spare[...].astype(BF16)

    arrays = (ids, triple, out_weight, bias, fc_bias, up, fc_weight, proj_weight)
    whole = lambda v: pl.BlockSpec(v.shape, lambda i, ix: (0,) * v.ndim)
    units = 2 * fc_weight.shape[1]
    return call(
        body,
        "prepare_blocks",
        1,
        [whole(v) for v in arrays],
        [full(rows + EXTRA, model), pl.BlockSpec((1, rows, units), lambda i, ix: (0, 0, 0))],
        [shape(rows + EXTRA, model), jax.ShapeDtypeStruct((1, rows, units), BF16)],
        [pltpu.VMEM((EXTRA, model), F32)],
        cost(0, 4 * rows * model),
        60 << 20,
    )(idx, *arrays)


def weigh(idx, ids, fc_bias, near, far, y_near, y_far, x_near, tokens_all):
    units = fc_bias.shape[1]
    per_row = LANES
    own = LEN // 2 // per_row
    rows = near.shape[1] - EXTRA
    width = near.shape[2]

    def body(ix, ids_ref, fc_ref, *rest):
        msgs, (weight_ref, fc_out, held, sems) = rest[:5], rest[5:]
        load_all(
            [
                (msgs[n // 2].at[n % 2, pl.ds(rows, EXTRA), :], held.at[n])
                for n in range(8)
            ]
            + [(msgs[4].at[0, pl.ds(rows, EXTRA), :], held.at[8])],
            sems,
        )
        digits = jnp.zeros((EXTRA, 2 * LANES), F32)
        for n in range(8):
            digits = digits + held[n, :, : 2 * LANES].astype(F32)
        table = tokens_all / (GROUPS * (DIGIT * digits[0:1, :LANES] + digits[0:1, LANES:]))
        for k in range(own):
            ids_row = ids_ref[pl.ds((2 * ix[1] + ix[2]) * own + k, 1), :]
            row = jnp.zeros((1, LANES), F32)
            for g in range(GROUPS):
                row = jnp.where(ids_row == g, table[:, g : g + 1], row)
            weight_ref[k * per_row : (k + 1) * per_row, :] = jnp.broadcast_to(row, (per_row, LANES)).T
        line = lines_of(held[8].astype(F32))
        fc_out[0:1, :] = fc_ref[...].astype(F32)
        fc_out[1:2, :] = jnp.concatenate([line(4 + s) for s in range(4)], axis=1)

    return call(
        body,
        "weigh",
        1,
        [full(*ids.shape), full(1, units)] + [ANY] * 5,
        [full(LEN // 2, LANES), full(2, units)],
        [shape(LEN // 2, LANES, F32), shape(2, units, F32)],
        [pltpu.VMEM((9, EXTRA, width), BF16), pltpu.SemaphoreType.DMA((9,))],
        cost(0, LEN * LANES),
    )(idx, ids, fc_bias, near, far, y_near, y_far, x_near)


def norm_rows(idx, tokens, vec, down):
    model = tokens.shape[1]
    blocks = LEN // BLK

    def body(ix, tok, vec_ref, down_ref, normed_ref, latent_ref, pad_ref):
        @pl.when(pl.program_id(0) == 0)
        def _():
            pad_ref[...] = jnp.zeros_like(pad_ref)
            pad_ref[:8, :] = down_ref[...].astype(BF16)

        hat, _ = row_stats(tok[...].astype(F32))
        normed = (hat * vec_ref[0:1, :] + vec_ref[1:2, :]).astype(BF16)
        normed_ref[...] = normed
        latent_ref[...] = lax.dot_general(normed, pad_ref[...], NT, preferred_element_type=F32).astype(BF16)

    row = lambda c: pl.BlockSpec((BLK, c), lambda i, ix: (i, 0))
    return call(
        body,
        "norm_rows",
        blocks,
        [pl.BlockSpec((BLK, model), lambda i, ix: (ix[1] * blocks + i, 0)), full(8, model), full(8, model)],
        [row(model), row(LANES), full(LANES, model)],
        [shape(LEN, model), shape(LEN, LANES), shape(LANES, model)],
        [],
        cost(2 * LEN * model * LANES, 4 * LEN * model),
    )(idx, tokens, vec, down)


def project_heads(idx, normed, latent, bias, up, x_near, found):
    model = normed.shape[1]
    arrays, table = operands(found)
    part = bias.shape[1]
    cols = 3 * part
    n = len(arrays)

    def body(ix, normed_ref, latent_ref, bias_ref, own_up_ref, near_ref, *rest):
        msgs = rest[:n]
        q_ref, k_ref, v_ref, up_ref, w, spare, lines, sems = rest[n:]

        @pl.when(pl.program_id(0) == 0)
        def _():
            pairs = column_pairs(msgs, table, w, ix, 0, cols, True)
            load_all(pairs + [(near_ref.at[0, pl.ds(model // 8, EXTRA), :], spare)], sems)
            line = lines_of(spare[...].astype(F32))
            up_ref[...] = jnp.zeros_like(up_ref)
            rank = ADAPTER_RANK
            for a in range(2):
                for s in range(3):
                    lines[a : a + 1, s * part : (s + 1) * part] = (
                        bias_ref[s : s + 1, :].astype(F32) if a == 0 else line(1 + s)
                    )
                rows = own_up_ref[...] if a == 0 else jnp.concatenate([line(8 + s) for s in range(8)], axis=0)
                rows = ADAPTER_SCALE * rows
                which = lax.broadcasted_iota(jnp.int32, rows.shape, 0) < rank
                up_ref[a, :8, :part] = jnp.where(which, rows, 0.0).astype(BF16)
                up_ref[a, :8, 2 * part :] = jnp.where(which, 0.0, rows).astype(BF16)

        for a in range(2):
            r = jnp.dot(normed_ref[...], w[a], preferred_element_type=F32) + lines[a : a + 1, :]
            r = r + jnp.dot(latent_ref[...], up_ref[a], preferred_element_type=F32)
            for out, s in ((q_ref, 0), (k_ref, 1), (v_ref, 2)):
                out[:, a * part : (a + 1) * part] = r[:, s * part : (s + 1) * part].astype(BF16)

    row = lambda c: pl.BlockSpec((BLK, c), lambda i, ix: (i, 0))
    both = pl.BlockSpec((2, LANES, cols), lambda i, ix: (0, 0, 0))
    return call(
        body,
        "project_heads",
        LEN // BLK,
        [row(model), row(LANES), full(3, part), full(8, part)] + [ANY] * (1 + n),
        [row(2 * part)] * 3 + [both],
        [shape(LEN, 2 * part)] * 3 + [jax.ShapeDtypeStruct((2, LANES, cols), BF16)],
        [
            pltpu.VMEM((2, model, cols), BF16),
            pltpu.VMEM((EXTRA, model), BF16),
            pltpu.VMEM((8, cols), F32),
            pltpu.SemaphoreType.DMA((len(table) + 1,)),
        ],
        cost(4 * LEN * model * cols, 16 * LEN * model),
    )(idx, normed, latent, bias, up, x_near, *arrays)


def attend_fast(queries, key_rows, value_rows):
    length, width = queries.shape
    pairs = width // LANES

    def body(q_ref, k_ref, v_ref, o_ref, lse_ref, vx, p_ref):
        low = lax.broadcasted_iota(jnp.int32, (1, LANES), 1) < HEAD_DIM
        vx[:, :LANES] = v_ref[...]
        vx[:, LANES:] = jnp.ones((length, LANES), BF16)
        scale = HEAD_DIM**-0.5 * LOG2E
        causal = (lax.broadcasted_iota(jnp.int32, (2 * BLK, BLK), 0) & (BLK - 1)) >= lax.broadcasted_iota(
            jnp.int32, (2 * BLK, BLK), 1
        )
        for i in range(length // BLK):
            start, stop = i * BLK, (i + 1) * BLK
            qb = (q_ref[start:stop, :].astype(F32) * scale).astype(BF16)
            s = lax.dot_general(both_heads(low, qb), k_ref[:stop, :], NT, preferred_element_type=F32)
            sd = jnp.where(causal, s[:, start:], MASKED)
            top = jnp.max(sd, axis=-1, keepdims=True)
            if i:
                top = jnp.maximum(top, jnp.max(s[:, :start], axis=-1, keepdims=True))
                p_ref[i % 2, :, :start] = jnp.exp2(s[:, :start] - top).astype(BF16)
            p_ref[i % 2, :, start:stop] = jnp.exp2(sd - top).astype(BF16)
            out = jnp.dot(p_ref[i % 2, :, :stop], vx[:stop, :], preferred_element_type=F32)
            total = out[:, LANES:]
            mixed = out[:, :LANES] / total
            o_ref[start:stop, :] = jnp.where(low, mixed[:BLK], mixed[BLK:]).astype(BF16)
            log = top + jnp.log2(total)
            log = jnp.where(low, log[:BLK], log[BLK:]).T
            lse_ref[0, 0:1, start:stop] = log[0:1]
            lse_ref[0, 1:2, start:stop] = log[HEAD_DIM : HEAD_DIM + 1]

    spec = pl.BlockSpec((length, LANES), lambda i: (0, i))
    return pl.pallas_call(
        body,
        grid=(pairs,),
        out_shape=(shape(length, width), jax.ShapeDtypeStruct((pairs, 8, length), F32)),
        in_specs=[spec] * 3,
        out_specs=(spec, pl.BlockSpec((1, 8, length), lambda i: (i, 0, 0))),
        scratch_shapes=[pltpu.VMEM((length, 2 * LANES), BF16), pltpu.VMEM((2, 2 * BLK, length), BF16)],
        compiler_params=pltpu.CompilerParams(vmem_limit_bytes=VMEM_LIMIT),
        cost_estimate=cost(8 * length * length * width, 8 * length * width, 2 * pairs * length * length),
        name="attend",
    )(queries, key_rows, value_rows)


def attention_out_send(idx, attended, found, first):
    width = attended.shape[1]
    cut = LANES * lax.axis_size("dp") // CUTS
    arrays, table = operands(found)
    n = len(arrays)
    model = LANES * lax.axis_size("dp")
    half_blocks = LEN // BLK // 2

    def body(ix, att, *rest):
        msgs = rest[:n]
        outs, (w, sems) = rest[n : n + CUTS], rest[n + CUTS :]

        @pl.when(pl.program_id(0) == 0)
        def _():
            load_all(column_pairs(msgs, table, w, ix, first, width // 2, False), sems)

        term = lax.dot_general(att[...], w[...], NT, preferred_element_type=F32).astype(BF16)
        for k, out in enumerate(outs):
            out[...] = term[:, k * cut : (k + 1) * cut]

    return call(
        body,
        "attention_out_send",
        half_blocks,
        [pl.BlockSpec((BLK, width), lambda i, ix: ((1 - ix[2]) * half_blocks + i, 0))] + [ANY] * n,
        [pl.BlockSpec((BLK, cut), lambda i, ix: (i, 0))] * CUTS,
        [shape(LEN // 2, cut)] * CUTS,
        [pltpu.VMEM((model, width), BF16), pltpu.SemaphoreType.DMA((len(table),))],
        cost(LEN * width * model, 2 * LEN * model),
    )(idx, attended, *arrays)


def attention_out_own(idx, attended, received, tokens, vec, found, first):
    width = attended.shape[1]
    arrays, table = operands(found)
    n = len(arrays)
    model = tokens.shape[1]
    half_blocks = LEN // BLK // 2

    def body(ix, att, tok, vec_ref, *rest):
        recv, msgs = rest[:CUTS], rest[CUTS : CUTS + n]
        hidden_ref, normed_ref, w, sems = rest[CUTS + n :]

        @pl.when(pl.program_id(0) == 0)
        def _():
            load_all(column_pairs(msgs, table, w, ix, first, width // 2, False), sems)

        term = lax.dot_general(att[...], w[...], NT, preferred_element_type=F32)
        other = jnp.concatenate([r[...] for r in recv], axis=1).astype(F32)
        hidden = tok[...].astype(F32) + term + other + vec_ref[2:3, :]
        hidden_ref[...] = hidden
        hat, _ = row_stats(hidden)
        normed_ref[...] = (hat * vec_ref[3:4, :] + vec_ref[4:5, :]).astype(BF16)

    row = pl.BlockSpec((BLK, model), lambda i, ix: (i, 0))
    return call(
        body,
        "attention_out_own",
        half_blocks,
        [
            pl.BlockSpec((BLK, width), lambda i, ix: (ix[2] * half_blocks + i, 0)),
            row,
            full(8, model),
        ]
        + [pl.BlockSpec((BLK, model // CUTS), lambda i, ix: (i, 0))] * CUTS
        + [ANY] * n,
        [row, row],
        [shape(LEN // 2, model, F32), shape(LEN // 2, model)],
        [pltpu.VMEM((model, width), BF16), pltpu.SemaphoreType.DMA((len(table),))],
        cost(LEN * width * model, 5 * LEN * model),
    )(idx, attended, tokens, vec, *received, *arrays)


def units_main(idx, half_bit, normed, cotangent, weights, bias, bias_other, vec, mine, other, carried, hidden):
    rows, model = normed.shape
    sources = [operands(f) for f in (mine, other)]
    part = sources[0][0][0].shape[2] // 2
    counts = [len(arrays) for arrays, _ in sources]
    last = hidden is not None
    parts = 4
    piece = model // parts
    chunk = 256
    per = part // chunk
    c0 = 0.7978845608028654
    c1 = 0.044715

    def body(ix, normed_ref, cot, weight_ref, bias_ref, bias_other_ref, vec_ref, *rest):
        carry = rest[: len(carried)]
        rest = rest[len(carried) :]
        hid_ref, rest = (rest[0], rest[1:]) if last else (None, rest)
        msgs = (rest[: counts[0]], rest[counts[0] : sum(counts)])
        rest = rest[sum(counts) :]
        n_out = 2 + parts if last else 2
        outs, (w, grad_ref, x_ref, g_ref, pre_ref, act_ref, sems, *held) = rest[:n_out], rest[n_out:]
        groups = []
        used = 0
        for o in range(2):
            pairs = block_pairs(msgs[o], sources[o][1], w, ix, half_bit, o)
            groups.append(copies_of(pairs, sems, used))
            used += len(pairs)
        for group in groups:
            for copy in group:
                copy.start()
        grad_ref[...] = (cot[...].astype(F32) * weight_ref[:, :1]).astype(BF16)
        biases = (bias_ref, bias_other_ref)

        def multiply(o, c, slot):
            x_ref[slot] = jnp.dot(normed_ref[...], w[o, :, at_lanes(c, chunk)], preferred_element_type=F32)
            g_ref[slot] = jnp.dot(grad_ref[...], w[o, :, at_lanes(c + per, chunk)], preferred_element_type=F32)

        def bend(o, c, slot):
            at = at_lanes(o * per + c, chunk)
            x = x_ref[slot] + biases[o][half_bit : half_bit + 1, at_lanes(c, chunk)]
            sq = x * x
            th = jnp.tanh(c0 * x * (1.0 + c1 * sq))
            left = 0.5 * (1.0 + th)
            slope = left + 0.5 * x * (1.0 - th * th) * (c0 + (3.0 * c0 * c1) * sq)
            pre_ref[:, at] = (slope * g_ref[slot]).astype(BF16)
            act_ref[:, at] = (x * left).astype(BF16)

        for o in range(2):
            for copy in groups[o]:
                copy.wait()
            if o == 0:
                multiply(0, 0, 0)

                def step(c, _):
                    multiply(0, c, lax.rem(c, 2))
                    bend(0, c - 1, lax.rem(c + 1, 2))
                    return 0

                lax.fori_loop(1, per, step, 0)
            else:
                multiply(1, 0, 0)
                bend(0, per - 1, (per - 1) % 2)

                def step(c, _):
                    multiply(1, c, lax.rem(c, 2))
                    bend(1, c - 1, lax.rem(c + 1, 2))
                    return 0

                lax.fori_loop(1, per, step, 0)
                bend(1, per - 1, (per - 1) % 2)

        def mid_of(n):
            at = at_rows(n, chunk)
            lanes = at_lanes(n, chunk)
            mid = lax.dot_general(pre_ref[:, :part], w[0, at, :part], NT, preferred_element_type=F32)
            mid = mid + lax.dot_general(pre_ref[:, part:], w[1, at, :part], NT, preferred_element_type=F32)
            unit = lax.dot_general(act_ref[:, :part], w[0, at, part:], NT, preferred_element_type=F32)
            unit = unit + lax.dot_general(act_ref[:, part:], w[1, at, part:], NT, preferred_element_type=F32)
            if carry:
                mid = mid + carry[0][:, lanes]
                unit = unit + carry[1][:, lanes]
            return mid, unit, lanes

        if not last:

            def finish(n, _):
                mid, unit, lanes = mid_of(n)
                outs[0][:, lanes] = mid
                outs[1][:, lanes] = unit
                return 0

            lax.fori_loop(0, model // chunk, finish, 0)
            return
        out_low, = held

        def finish(n, _):
            mid, unit, lanes = mid_of(n)
            outs[0][:, lanes] = mid * vec_ref[3:4, lanes]
            out_low[:, lanes] = (unit + hid_ref[:, lanes]).astype(BF16)
            return 0

        lax.fori_loop(0, model // chunk, finish, 0)
        for k in range(parts):
            outs[2 + k][...] = out_low[:, at_lanes((2 * ix[1] + ix[2]) ^ k, piece)]
        step_rows = 128

        def end(r, _):
            at = at_rows(r, step_rows)
            hat, scaler = row_stats(hid_ref[at, :])
            grad = cot[at, :].astype(F32) * weight_ref[at, :1]
            grad = grad + norm_back(hat, scaler, outs[0][at, :])
            outs[0][at, :] = grad
            outs[1][at, :] = grad.astype(BF16)
            return 0

        lax.fori_loop(0, rows // step_rows, end, 0)

    block = full(rows, model)
    specs = [
        block,
        block,
        full(rows, LANES),
        full(2, part),
        full(2, part),
        full(8, model),
    ]
    specs += [block] * (len(carried) + (1 if last else 0))
    if last:
        out_specs = [block, block] + [full(rows, piece)] * parts
        out_shape = [shape(rows, model, F32), shape(rows, model)] + [shape(rows, piece)] * parts
    else:
        out_specs = [block, block]
        out_shape = [shape(rows, model, F32)] * 2
    arrays = [array for found, _ in sources for array in found]
    return call(
        body,
        "units_main_last" if last else "units_main_first",
        1,
        specs + [ANY] * len(arrays),
        out_specs,
        out_shape,
        [
            pltpu.VMEM((2, model, 2 * part), BF16),
            pltpu.VMEM((rows, model), BF16),
            pltpu.VMEM((2, rows, chunk), F32),
            pltpu.VMEM((2, rows, chunk), F32),
            pltpu.VMEM((rows, 2 * part), BF16),
            pltpu.VMEM((rows, 2 * part), BF16),
            pltpu.SemaphoreType.DMA((sum(len(table) for _, table in sources),)),
        ]
        + ([pltpu.VMEM((rows, model), BF16)] if last else []),
        cost(16 * rows * part * model, 12 * part * model, 2 * rows * part),
    )(idx, normed, cotangent, weights, bias, bias_other, vec, *carried, *((hidden,) if last else ()), *arrays)


def attend_back_fast(
    idx, queries, key_rows, value_rows, mixed, grad_own, grad_other, logsum, normed, latent, up, found, first
):
    length, width = queries.shape
    pairs = width // LANES
    half, model = grad_own.shape
    per = pairs // 2
    arrays, table = operands(found)
    n = len(arrays)

    def body(ix, q_ref, k_ref, v_ref, o_ref, own_ref, other_ref, lse_ref, normed_ref, latent_ref, uq_ref, uv_ref, *rest):
        msgs = rest[:n]
        dq_ref, dk_ref, dv_ref, low_ref, down_ref, rq_ref, rv_ref, low_acc, dq_acc, g_ref, qs_ref, p_ref, ds_ref, w, sems = rest[
            n:
        ]
        pair = pl.program_id(0)

        @pl.when(pair == 0)
        def _():
            load_all(column_pairs(msgs, table, w, ix, first, width // 2, False), sems)

        weight = w[:, at_lanes(pair, LANES)]
        for ref, rank in ((own_ref, ix[2]), (other_ref, 1 - ix[2])):
            g_ref[at_rows(rank, half), :] = jnp.dot(ref[...], weight, preferred_element_type=F32).astype(BF16)
        scale = HEAD_DIM**-0.5 * LOG2E
        low = lax.broadcasted_iota(jnp.int32, (1, LANES), 1) < HEAD_DIM
        qs_ref[...] = (q_ref[...].astype(F32) * scale).astype(BF16)
        prod = (g_ref[...].astype(F32) * o_ref[...].astype(F32)).T
        delta = [
            jnp.sum(prod[:HEAD_DIM], axis=0, keepdims=True),
            jnp.sum(prod[HEAD_DIM:], axis=0, keepdims=True),
        ]
        causal = lax.broadcasted_iota(jnp.int32, (BLK, BLK), 1) >= lax.broadcasted_iota(jnp.int32, (BLK, BLK), 0)

        def scores(j):
            start = j * BLK
            stacked = both_heads(low, k_ref[start : start + BLK, :])
            s = lax.dot_general(stacked, qs_ref[start:, :], NT, preferred_element_type=F32)
            values = both_heads(low, v_ref[start : start + BLK, :])
            dp = lax.dot_general(values, g_ref[start:, :], NT, preferred_element_type=F32)
            for h in range(2):
                rows = slice(h * BLK, (h + 1) * BLK)
                for a, b in ((start, start + BLK), (start + BLK, length)):
                    if a == b:
                        continue
                    sh = s[rows, a - start : b - start] - lse_ref[0, h : h + 1, a:b]
                    if a == start:
                        sh = jnp.where(causal, sh, MASKED)
                    p = jnp.exp2(sh)
                    p_ref[j % 2, rows, a:b] = p.astype(BF16)
                    ds = p * (dp[rows, a - start : b - start] - delta[h][:, a:b])
                    ds_ref[j % 2, rows, a:b] = ds.astype(BF16)
            return stacked

        def spread(j, stacked):
            start = j * BLK
            ds = ds_ref[j % 2, :, start:]
            dk = jnp.dot(ds, q_ref[start:, :], preferred_element_type=F32)
            dv = jnp.dot(p_ref[j % 2, :, start:], g_ref[start:, :], preferred_element_type=F32)
            dk = jnp.where(low, dk[:BLK], dk[BLK:]) * HEAD_DIM**-0.5
            dk_ref[start : start + BLK, :] = dk.astype(BF16)
            dv_ref[start : start + BLK, :] = jnp.where(low, dv[:BLK], dv[BLK:]).astype(BF16)
            dq = lax.dot_general(ds, stacked, TN, preferred_element_type=F32)
            if j == 0:
                dq_acc[...] = dq
            else:
                dq_acc[start:, :] += dq

        stacked = scores(0)
        for j in range(1, length // BLK):
            coming = scores(j)
            spread(j - 1, stacked)
            stacked = coming
        spread(length // BLK - 1, stacked)
        dq_ref[...] = (dq_acc[...] * HEAD_DIM**-0.5).astype(BF16)
        term = lax.dot_general(dq_ref[...], uq_ref[0], NT, preferred_element_type=F32)
        term = term + lax.dot_general(dv_ref[...], uv_ref[0], NT, preferred_element_type=F32)
        latent_t = latent_ref[...]
        rq_ref[...] = lax.dot_general(latent_t, dq_ref[...], TN, preferred_element_type=F32)[:8]
        rv_ref[...] = lax.dot_general(latent_t, dv_ref[...], TN, preferred_element_type=F32)[:8]

        @pl.when(pair == 0)
        def _():
            low_acc[...] = term

        @pl.when(pair > 0)
        def _():
            low_acc[...] += term

        @pl.when(pair == pairs - 1)
        def _():
            low_grad = low_acc[...].astype(BF16)
            low_ref[...] = low_grad
            down_ref[...] = lax.dot_general(low_grad, normed_ref[...], TN, preferred_element_type=F32)[:8]

    spec = pl.BlockSpec((length, LANES), lambda i, ix: (0, i))
    return call(
        body,
        "attend_back",
        pairs,
        [spec] * 4
        + [full(half, model)] * 2
        + [pl.BlockSpec((1, 8, length), lambda i, ix: (i, 0, 0)), full(length, model), full(length, LANES)]
        + [
            pl.BlockSpec((1, LANES, LANES), lambda i, ix: (i // per, 0, lax.rem(i, per))),
            pl.BlockSpec((1, LANES, LANES), lambda i, ix: (i // per, 0, 2 * per + lax.rem(i, per))),
        ]
        + [ANY] * n,
        [spec] * 3
        + [full(length, LANES), full(8, model)]
        + [pl.BlockSpec((8, LANES), lambda i, ix: (0, i))] * 2,
        [shape(length, width)] * 3
        + [shape(length, LANES), shape(8, model, F32), shape(8, width, F32), shape(8, width, F32)],
        [
            pltpu.VMEM((length, LANES), F32),
            pltpu.VMEM((length, LANES), F32),
            pltpu.VMEM((length, LANES), BF16),
            pltpu.VMEM((length, LANES), BF16),
            pltpu.VMEM((2, 2 * BLK, length), BF16),
            pltpu.VMEM((2, 2 * BLK, length), BF16),
            pltpu.VMEM((model, width), BF16),
            pltpu.SemaphoreType.DMA((len(table),)),
        ],
        cost(20 * length * length * width, 16 * length * width, 2 * pairs * length * length),
    )(idx, queries, key_rows, value_rows, mixed, grad_own, grad_other, logsum, normed, latent, up, up, *arrays)


def heads_back(idx, dq, dk, dv, latent_low, down, found):
    width = dq.shape[1]
    part = width // 2
    model = down.shape[1]
    arrays, table = operands(found)
    cols = 3 * part
    n = len(arrays)
    half_blocks = LEN // BLK // 2

    def body(ix, dq_ref, dk_ref, dv_ref, low_ref, down_ref, *rest):
        msgs = rest[:n]
        send_ref, own_ref, w, sems = rest[n:]
        step = pl.program_id(0)

        @pl.when(step == 0)
        def _():
            load_all(column_pairs(msgs, table, w, ix, 0, cols, True), sems)

        total = jnp.dot(low_ref[...], down_ref[...], preferred_element_type=F32)
        for a in range(2):
            cut = slice(a * part, (a + 1) * part)
            piece = jnp.concatenate([dq_ref[:, cut], dk_ref[:, cut], dv_ref[:, cut]], axis=1)
            total = total + lax.dot_general(piece, w[a], NT, preferred_element_type=F32)

        @pl.when(step < half_blocks)
        def _():
            send_ref[...] = total.astype(BF16)

        @pl.when(step >= half_blocks)
        def _():
            own_ref[...] = total

    def rows(i, ix):
        rank = jnp.where(i < half_blocks, 1 - ix[2], ix[2])
        return (rank * half_blocks + lax.rem(i, half_blocks), 0)

    row = lambda c: pl.BlockSpec((BLK, c), rows)
    return call(
        body,
        "heads_back",
        2 * half_blocks,
        [row(width)] * 3 + [row(LANES), full(LANES, model)] + [ANY] * n,
        [
            pl.BlockSpec((BLK, model), lambda i, ix: (jnp.minimum(i, half_blocks - 1), 0)),
            pl.BlockSpec((BLK, model), lambda i, ix: (jnp.maximum(i - half_blocks, 0), 0)),
        ],
        [shape(LEN // 2, model), shape(LEN // 2, model, F32)],
        [pltpu.VMEM((2, model, cols), BF16), pltpu.SemaphoreType.DMA((len(table),))],
        cost(4 * LEN * model * cols, 4 * model * cols),
    )(idx, dq, dk, dv, latent_low, down, *arrays)


def tokens_back(idx, in_own, in_recv, tokens, hidden_grad, vec):
    model = tokens.shape[1]
    half_blocks = LEN // BLK // 2
    parts = 4
    part = model // parts

    def body(ix, own, recv, tok, hg, vec_ref, *rest):
        outs, held = rest[:parts], rest[parts]
        e = vec_ref[0:1, :] * (own[...] + recv[...].astype(F32))
        hat, scaler = row_stats(tok[...].astype(F32))
        held[...] = (hg[...] + norm_back(hat, scaler, e)).astype(BF16)
        for k, out in enumerate(outs):
            out[...] = held[:, at_lanes((2 * ix[1] + ix[2]) ^ k, part)]

    row = pl.BlockSpec((BLK, model), lambda i, ix: (i, 0))
    return call(
        body,
        "tokens_back",
        half_blocks,
        [row, row, row, row, full(8, model)],
        [pl.BlockSpec((BLK, part), lambda i, ix: (i, 0))] * parts,
        [shape(LEN // 2, part)] * parts,
        [pltpu.VMEM((BLK, model), BF16)],
        cost(20 * LEN * model, 8 * LEN * model),
    )(idx, in_own, in_recv, tokens, hidden_grad, vec)


def exchange_features(pieces):
    return [pieces[0], core_swap(pieces[1]), hop(pieces[2], 1, 0), both_swap(pieces[3])]


def to_features(idx, pieces, bias):
    rows, part = pieces[0].shape
    parts = len(pieces)

    def body(ix, bias_ref, *rest):
        outs = rest[parts]
        for k in range(parts):
            value = rest[k][...]
            if bias is not None:
                value = (value.astype(F32) + bias_ref[...]).astype(BF16)
            outs[at_rows((2 * ix[1] + ix[2]) ^ k, rows), :] = value

    extra = jnp.zeros((1, part), F32) if bias is None else bias
    return call(
        body,
        "to_features",
        1,
        [full(1, part)] + [full(rows, part)] * parts,
        full(parts * rows, part),
        shape(parts * rows, part),
        [],
        cost(parts * rows * part, 4 * parts * rows * part),
    )(idx, extra, *pieces)


def both_swap(value):
    total = lax.axis_size("dp") * lax.axis_size("mp")
    return lax.ppermute(value, AXES, [(i, i ^ 3) for i in range(total)])


def on_device_fast(
    tokens,
    cotangent,
    group_ids,
    pre_gain,
    pre_shift,
    frozen_triple_weight,
    frozen_triple_bias,
    out_weight,
    out_bias,
    mid_gain,
    mid_shift,
    fc_weight,
    fc_bias,
    proj_weight,
    proj_bias,
    down_master,
    up_master,
    down_first,
    down_second,
    up_first,
    up_second,
    learn_rate,
):
    tok_dev, model = tokens.shape
    ranks = lax.axis_size("mp") // 2
    place = lax.axis_index("mp")
    idx = jnp.stack([lax.axis_index("dp"), place // ranks, place % ranks]).astype(jnp.int32)
    r = ADAPTER_RANK
    step_rows, _, head_part = frozen_triple_weight.shape
    heads_cols = 3 * head_part
    ids = group_ids.reshape(-1, LANES)
    fc_line = fc_bias.reshape(1, -1)
    up_rows = up_master.reshape(2 * r, head_part)
    heads_own, u_own = prepare_blocks(
        idx, ids, frozen_triple_weight, out_weight, frozen_triple_bias, fc_line, up_master, fc_weight, proj_weight
    )
    zero_line = jnp.zeros_like(pre_gain)
    vec = jnp.stack([pre_gain, pre_shift, out_bias, mid_gain, mid_shift, zero_line, zero_line, zero_line]).astype(F32)
    own_start = (idx[1] * ranks + idx[2]) * (LEN // 2)
    own_rows = lambda v: lax.dynamic_slice_in_dim(v, own_start, LEN // 2, 0)
    tok_own, cot_own = own_rows(tokens), own_rows(cotangent)
    h_z1, h_z2, h_z3 = gather_z(heads_own, ())
    h_near, h_far = jnp.stack([heads_own, h_z1]), jnp.stack([h_z2, h_z3])
    hx_near, hy_near = pair_xy(h_near)
    hx_far, hy_far = pair_xy(h_far)
    ux0, uy0 = pair_xy(after(u_own, hx_far, hy_far))
    hd_near, hd_far = hop(after(hx_near, h_far), 0, 1), hop(hy_far, 1, 0)
    heads = []
    for first, arrays in ((0, (h_near, hx_near, hy_near, hd_near)), (2, (h_far, hx_far, hy_far, hd_far))):
        for n, array in enumerate(arrays):
            heads += blocks_of(array, first, n % 2, n // 2)
    u_rest = jnp.concatenate(gather_z(u_own, (h_far, hx_near, hy_near)))
    weights, fc_mine = weigh(
        idx, ids, fc_line, h_near, h_far, hy_near, hy_far, hx_near, float(tok_dev * lax.axis_size("dp"))
    )
    fc_other = core_swap(fc_mine)
    down8 = down_master.reshape(2 * r, model)
    normed, latent, down = norm_rows(idx, after(tokens, hx_far, tok_own, cot_own), vec, down8)
    ux, uy = pair_xy(after(u_rest, hd_near, hd_far, ux0, uy0))
    ready = after(normed, u_rest, ux0, uy0)
    queries, keys, values, up = project_heads(idx, ready, latent, frozen_triple_bias, up_rows, hx_near, heads)
    mixed, logsum = attend_fast(queries, keys, values)
    sent = [core_swap(v) for v in attention_out_send(idx, mixed, heads, heads_cols)]
    hidden, normed_mid = attention_out_own(idx, mixed, sent, tok_own, vec, heads, heads_cols)
    rows = (normed_mid, cot_own, weights, fc_mine, fc_other, vec)
    ux0, ux, uy, _ = lax.optimization_barrier((ux0, ux, uy, normed_mid))
    ud0, ud1, ud2 = hop(ux0, 0, 1), hop(ux[:1], 0, 1), hop(uy[1:], 1, 0)

    def table(half_bit, bit, *arrays):
        found, start = [], 0
        for array in arrays:
            found += blocks_of(array, start, half_bit, bit)
            start += array.shape[0]
        return found

    swap = lambda *arrays: [core_swap(v) for v in arrays]
    first_mine = table(0, 0, u_own, u_rest) + table(0, 1, uy0, uy)
    first_other = table(0, 0, *swap(u_own, u_rest)) + table(0, 1, *swap(uy0, uy))
    carried = units_main(idx, 0, *rows, first_mine, first_other, (), None)
    ud0, ud1, ud2, _ = lax.optimization_barrier((ud0, ud1, ud2, carried[0]))
    last_mine = table(1, 0, ux0, ux) + table(1, 1, ud0, ud1, ud2)
    last_other = table(1, 0, *swap(ux0, ux)) + table(1, 1, *swap(ud0, ud1, ud2))
    hidden_grad, hidden_low, *out_pieces = units_main(idx, 1, *rows, last_mine, last_other, carried, hidden)
    hidden_other = core_swap(hidden_low)
    out_pieces = exchange_features(out_pieces)
    dq, dk, dv, latent_low, down_term, up_q, up_v = attend_back_fast(
        idx, queries, keys, values, mixed, hidden_low, hidden_other, logsum, normed, latent, up, heads, heads_cols
    )
    up_term = jnp.stack([up_q[:r], up_v[r:]]).reshape(2 * r, 2, head_part)
    terms = jnp.concatenate([down_term, up_term[:, 1], up_term[:, 0]], axis=1)
    terms = terms + hop(terms, 0, 1)
    dq, out_pieces = lax.optimization_barrier((dq, out_pieces))
    in_send, in_own = heads_back(idx, dq, dk, dv, latent_low, down, heads)
    in_recv = core_swap(in_send)
    terms = after(terms, in_own)
    terms = terms + hop(terms, 0, 2)
    in_pieces = tokens_back(idx, in_own, in_recv, tok_own, hidden_grad, vec)
    terms = after(terms, in_recv)
    terms = terms + hop(terms, 0, 4)
    terms, out_pieces = lax.optimization_barrier((terms, out_pieces, in_pieces[2]))[:2]
    output = to_features(idx, out_pieces, proj_bias.astype(F32).reshape(1, -1))
    input_grad = to_features(idx, exchange_features(in_pieces), None)
    width = model + head_part
    got = hop(terms[:, :width], 1, 0)
    down_sum = terms[:, :model] + got[:, :model]
    down_grad = (down_sum + core_swap(down_sum)).reshape(down_master.shape)
    up_grad = ADAPTER_SCALE * (terms[:, width:] + got[:, model:]).reshape(up_master.shape)
    step_value = jnp.float32(STEP)
    down_new, down_moment, down_square = adam_update(
        down_master, down_first, down_second, down_grad, step_value, learn_rate
    )
    up_new, up_moment, up_square = adam_update(up_master, up_first, up_second, up_grad, step_value, learn_rate)
    return (
        output,
        input_grad,
        down_new,
        down_moment,
        down_square,
        down_new.astype(BF16),
        up_new,
        up_moment,
        up_square,
        up_new.astype(BF16),
    )


def pick_body(mesh):
    return on_device_fast if mesh.shape["dp"] == 8 and mesh.shape["mp"] == 4 else on_device_general


def solution(mesh):
    body = pick_body(mesh)
    return jax.shard_map(
        body,
        mesh=mesh,
        in_specs=(
            P("dp", None),
            P("dp", None),
            P("dp"),
            P(),
            P(),
            P("dp", None, "mp"),
            P(None, "mp"),
            P("mp", "dp"),
            P(),
            P(),
            P(),
            P("dp", "mp"),
            P("mp"),
            P("mp", "dp"),
            P("mp"),
            P(),
            P(None, None, "mp"),
            P(),
            P(),
            P(None, None, "mp"),
            P(None, None, "mp"),
            P(),
        ),
        out_specs=(
            P("dp", "mp"),
            P("dp", "mp"),
            P(),
            P(),
            P(),
            P(),
            P(None, None, "mp"),
            P(None, None, "mp"),
            P(None, None, "mp"),
            P(None, None, "mp"),
        ),
        check_vma=False,
    )
```

```python
import jax
import jax.numpy as jnp
from jax import lax
from jax.experimental import pallas as pl
from jax.experimental.pallas import tpu as pltpu
from jax.sharding import PartitionSpec as P

HEAD_DIM = 64
ADAPTER_RANK = 4
GROUPS = 16
STEP = 3
MICRO = 2


ADAPTER_SCALE = 8.0
NORM_EPS = 1e-05
MASKED = -1e30
BETA_ONE = 0.5
BETA_TWO = 0.5
ADAM_EPS = 1e-08
DECAY = 0.01


def layer_stats(values):
    center = values - jnp.mean(values, axis=-1, keepdims=True)
    spread = jnp.mean(center * center, axis=-1, keepdims=True)
    scaler = lax.rsqrt(spread + NORM_EPS)
    return (center * scaler, scaler)


def norm_back(normal_hat, scaler, scaled_grad):
    first_mean = jnp.mean(scaled_grad, axis=-1, keepdims=True)
    second_mean = jnp.mean(scaled_grad * normal_hat, axis=-1, keepdims=True)
    return scaler * (scaled_grad - first_mean - normal_hat * second_mean)


def gelu_tanh(values):
    return jax.nn.gelu(values, approximate=True)


def fetch_frozen(frozen_triple_weight, fc_weight, out_weight, proj_weight):
    return (
        lax.all_gather(frozen_triple_weight, "dp", axis=0, tiled=True),
        lax.all_gather(fc_weight, "dp", axis=0, tiled=True),
        lax.all_gather(out_weight, "dp", axis=1, tiled=True),
        lax.all_gather(proj_weight, "dp", axis=1, tiled=True),
    )


def score_block(query_part, key_heads, start, block_rows, key_count):
    score_scale = HEAD_DIM ** (-0.5)
    scores = (
        jnp.einsum("qhd,khd->hqk", query_part, key_heads, preferred_element_type=jnp.float32)
        * score_scale
    )
    allowed = (start + jnp.arange(block_rows, dtype=jnp.int32))[:, None] >= jnp.arange(
        key_count, dtype=jnp.int32
    )[None, :]
    return jnp.where(allowed[None], scores, MASKED)


def attend(queries, key_rows, value_rows):
    length, col_width = queries.shape
    head_count = col_width // HEAD_DIM
    block_rows = min(512, length)
    query_heads = queries.reshape(length, head_count, HEAD_DIM)
    key_heads = key_rows.reshape(length, head_count, HEAD_DIM)
    value_heads = value_rows.reshape(length, head_count, HEAD_DIM)
    mixed_parts = []
    logsum_parts = []
    for index in range(length // block_rows):
        start = index * block_rows
        stop = start + block_rows
        query_part = query_heads[start:stop]
        scores = score_block(query_part, key_heads[:stop], start, block_rows, stop)
        row_top = jnp.max(scores, axis=-1, keepdims=True)
        exp_terms = jnp.exp(scores - row_top)
        row_total = jnp.sum(exp_terms, axis=-1, keepdims=True)
        probs = (exp_terms / row_total).astype(jnp.bfloat16)
        mixed = jnp.einsum(
            "hqk,khd->qhd", probs, value_heads[:stop], preferred_element_type=jnp.float32
        )
        mixed_parts.append(mixed.reshape(block_rows, col_width))
        logsum_parts.append((row_top + jnp.log(row_total))[..., 0])
    return (jnp.concatenate(mixed_parts, axis=0), logsum_parts)


def attend_back(queries, key_rows, value_rows, logsum, mixed_grad):
    length, col_width = queries.shape
    head_count = col_width // HEAD_DIM
    block_rows = min(512, length)
    score_scale = HEAD_DIM ** (-0.5)
    query_heads = queries.reshape(length, head_count, HEAD_DIM)
    key_heads = key_rows.reshape(length, head_count, HEAD_DIM)
    value_heads = value_rows.reshape(length, head_count, HEAD_DIM)
    grad_heads = mixed_grad.reshape(length, head_count, HEAD_DIM)
    key_acc = jnp.zeros((length, head_count, HEAD_DIM), jnp.float32)
    value_acc = jnp.zeros((length, head_count, HEAD_DIM), jnp.float32)
    query_parts = []
    for index in range(length // block_rows):
        start = index * block_rows
        stop = start + block_rows
        query_part = query_heads[start:stop]
        grad_part = grad_heads[start:stop]
        key_part = key_heads[:stop]
        scores = score_block(query_part, key_part, start, block_rows, stop)
        probs = jnp.exp(scores - logsum[index][:, :, None])
        prob_grad = jnp.einsum(
            "qhd,khd->hqk", grad_part, value_heads[:stop], preferred_element_type=jnp.float32
        )
        inner = jnp.sum(prob_grad * probs, axis=-1, keepdims=True)
        score_grad = (probs * (prob_grad - inner)).astype(jnp.bfloat16)
        query_grad = (
            jnp.einsum("hqk,khd->qhd", score_grad, key_part, preferred_element_type=jnp.float32)
            * score_scale
        )
        key_acc = key_acc.at[:stop].add(
            jnp.einsum("hqk,qhd->khd", score_grad, query_part, preferred_element_type=jnp.float32)
            * score_scale
        )
        value_acc = value_acc.at[:stop].add(
            jnp.einsum(
                "hqk,qhd->khd",
                probs.astype(jnp.bfloat16),
                grad_part,
                preferred_element_type=jnp.float32,
            )
        )
        query_parts.append(query_grad.reshape(block_rows, col_width))
    return (
        jnp.concatenate(query_parts, axis=0),
        key_acc.reshape(length, col_width),
        value_acc.reshape(length, col_width),
    )


def adam_update(master, first, second, grad, step_value, learn_rate):
    new_first = BETA_ONE * first + (1.0 - BETA_ONE) * grad
    new_second = BETA_TWO * second + (1.0 - BETA_TWO) * grad * grad
    fix_one = 1.0 - jnp.power(jnp.float32(BETA_ONE), step_value)
    fix_two = 1.0 - jnp.power(jnp.float32(BETA_TWO), step_value)
    update = new_first / fix_one / (jnp.sqrt(new_second / fix_two) + ADAM_EPS)
    new_master = master - learn_rate * (update + DECAY * master)
    return (new_master, new_first, new_second)


def on_device_general(
    tokens,
    cotangent,
    group_ids,
    pre_gain,
    pre_shift,
    frozen_triple_weight,
    frozen_triple_bias,
    out_weight,
    out_bias,
    mid_gain,
    mid_shift,
    fc_weight,
    fc_bias,
    proj_weight,
    proj_bias,
    down_master,
    up_master,
    down_first,
    down_second,
    up_first,
    up_second,
    learn_rate,
):
    tok_dev = tokens.shape[0]
    model_width = tokens.shape[1]
    length = tok_dev // MICRO
    shard_width = model_width // lax.axis_size("mp")
    shard_start = lax.axis_index("mp") * shard_width
    pre_gain_f = pre_gain.astype(jnp.float32)
    pre_shift_f = pre_shift.astype(jnp.float32)
    mid_gain_f = mid_gain.astype(jnp.float32)
    mid_shift_f = mid_shift.astype(jnp.float32)
    out_bias_f = out_bias.astype(jnp.float32)
    fc_bias_f = fc_bias.astype(jnp.float32)
    proj_bias_f = proj_bias.astype(jnp.float32)
    bias_flat = frozen_triple_bias.astype(jnp.float32).reshape(-1)
    onehot = group_ids[:, None] == jnp.arange(GROUPS, dtype=jnp.int32)[None, :]
    local_counts = jnp.sum(onehot.astype(jnp.int32), axis=0)
    totals = lax.psum(local_counts, "dp").astype(jnp.float32)
    own_count = jnp.sum(jnp.where(onehot, totals[None, :], jnp.float32(0.0)), axis=1)
    token_weight = jnp.float32(tok_dev * lax.axis_size("dp")) / (GROUPS * own_count)
    down_low = down_master.astype(jnp.bfloat16).reshape(2 * ADAPTER_RANK, model_width)
    raise_reduced = up_master.astype(jnp.bfloat16)
    grad_down = jnp.zeros((2 * ADAPTER_RANK, model_width), jnp.float32)
    raise_gradient = jnp.zeros(up_master.shape, jnp.float32)
    output_parts = []
    input_parts = []
    for micro_index in range(MICRO):
        current = fetch_frozen(frozen_triple_weight, fc_weight, out_weight, proj_weight)
        qkv_full, fc_full, out_full, proj_full = current
        qkv_flat = qkv_full.reshape(model_width, -1)
        head_width = qkv_flat.shape[1] // 3
        row_start = micro_index * length
        rows_f = lax.dynamic_slice_in_dim(tokens, row_start, length, 0).astype(jnp.float32)
        pre_hat, pre_scale = layer_stats(rows_f)
        normed = (pre_hat * pre_gain_f + pre_shift_f).astype(jnp.bfloat16)
        mixed_proj = jnp.dot(normed, qkv_flat, preferred_element_type=jnp.float32) + bias_flat
        bottleneck = jnp.einsum(
            "td,rd->tr", normed, down_low, preferred_element_type=jnp.float32
        ).astype(jnp.bfloat16)
        queries = (
            mixed_proj[:, :head_width]
            + ADAPTER_SCALE
            * jnp.dot(
                bottleneck[:, :ADAPTER_RANK], raise_reduced[0], preferred_element_type=jnp.float32
            )
        ).astype(jnp.bfloat16)
        key_rows = mixed_proj[:, head_width : 2 * head_width].astype(jnp.bfloat16)
        value_rows = (
            mixed_proj[:, 2 * head_width :]
            + ADAPTER_SCALE
            * jnp.dot(
                bottleneck[:, ADAPTER_RANK:], raise_reduced[1], preferred_element_type=jnp.float32
            )
        ).astype(jnp.bfloat16)
        attended, logsum = attend(queries, key_rows, value_rows)
        attended_low = attended.astype(jnp.bfloat16)
        head_term = jnp.dot(attended_low, out_full, preferred_element_type=jnp.float32).astype(
            jnp.bfloat16
        )
        attn_sum = lax.psum(head_term, "mp").astype(jnp.float32)
        hidden = rows_f + attn_sum + out_bias_f
        mid_hat, mid_scale = layer_stats(hidden)
        normed_mid = (mid_hat * mid_gain_f + mid_shift_f).astype(jnp.bfloat16)
        pre_act = jnp.dot(normed_mid, fc_full, preferred_element_type=jnp.float32) + fc_bias_f
        active, gelu_pullback = jax.vjp(gelu_tanh, pre_act)
        unit_part = jnp.dot(
            active.astype(jnp.bfloat16), proj_full, preferred_element_type=jnp.float32
        ).astype(jnp.bfloat16)
        unit_share = lax.psum_scatter(unit_part, "mp", scatter_dimension=1, tiled=True).astype(
            jnp.float32
        )
        hidden_share = lax.dynamic_slice_in_dim(hidden, shard_start, shard_width, 1)
        output_parts.append((hidden_share + unit_share + proj_bias_f).astype(jnp.bfloat16))
        weight_rows = lax.dynamic_slice_in_dim(token_weight, row_start, length, 0)
        out_grad = (
            lax.dynamic_slice_in_dim(cotangent, row_start, length, 0).astype(jnp.float32)
            * weight_rows[:, None]
        )
        out_low = out_grad.astype(jnp.bfloat16)
        active_grad = jnp.einsum(
            "td,fd->tf", out_low, proj_full, preferred_element_type=jnp.float32
        )
        pre_grad = gelu_pullback(active_grad)[0].astype(jnp.bfloat16)
        mid_part = jnp.einsum(
            "tf,df->td", pre_grad, fc_full, preferred_element_type=jnp.float32
        ).astype(jnp.bfloat16)
        mid_grad = lax.psum(mid_part, "mp").astype(jnp.float32)
        hidden_grad = out_grad + norm_back(mid_hat, mid_scale, mid_gain_f * mid_grad)
        hidden_low = hidden_grad.astype(jnp.bfloat16)
        attended_grad = jnp.einsum(
            "td,hd->th", hidden_low, out_full, preferred_element_type=jnp.float32
        ).astype(jnp.bfloat16)
        query_grad, key_grad, value_grad = attend_back(
            queries, key_rows, value_rows, logsum, attended_grad
        )
        query_low = query_grad.astype(jnp.bfloat16)
        key_low = key_grad.astype(jnp.bfloat16)
        value_low = value_grad.astype(jnp.bfloat16)
        proj_grad = jnp.concatenate([query_low, key_low, value_low], axis=1)
        in_part = jnp.einsum("tc,dc->td", proj_grad, qkv_flat, preferred_element_type=jnp.float32)
        bottleneck_gradient = ADAPTER_SCALE * jnp.concatenate(
            [
                jnp.einsum(
                    "tc,rc->tr", query_low, raise_reduced[0], preferred_element_type=jnp.float32
                ),
                jnp.einsum(
                    "tc,rc->tr", value_low, raise_reduced[1], preferred_element_type=jnp.float32
                ),
            ],
            axis=1,
        )
        latent_low = bottleneck_gradient.astype(jnp.bfloat16)
        in_part = (
            in_part + jnp.dot(latent_low, down_low, preferred_element_type=jnp.float32)
        ).astype(jnp.bfloat16)
        grad_down = grad_down + jnp.einsum(
            "tr,td->rd", latent_low, normed, preferred_element_type=jnp.float32
        )
        raise_gradient = raise_gradient + ADAPTER_SCALE * jnp.stack(
            [
                jnp.einsum(
                    "tr,tc->rc",
                    bottleneck[:, :ADAPTER_RANK],
                    query_low,
                    preferred_element_type=jnp.float32,
                ),
                jnp.einsum(
                    "tr,tc->rc",
                    bottleneck[:, ADAPTER_RANK:],
                    value_low,
                    preferred_element_type=jnp.float32,
                ),
            ],
            axis=0,
        )
        hidden_grad_share = lax.dynamic_slice_in_dim(hidden_grad, shard_start, shard_width, 1)
        in_grad = lax.psum(in_part, "mp").astype(jnp.float32)
        full_grad = norm_back(pre_hat, pre_scale, pre_gain_f * in_grad)
        input_parts.append(
            (
                hidden_grad_share + lax.dynamic_slice_in_dim(full_grad, shard_start, shard_width, 1)
            ).astype(jnp.bfloat16)
        )
    output = jnp.concatenate(output_parts, axis=0)
    input_grad = jnp.concatenate(input_parts, axis=0)
    down_grad = lax.psum(grad_down, ("dp", "mp")).reshape(down_master.shape)
    up_grad = lax.psum(raise_gradient, "dp")
    step_value = jnp.float32(STEP)
    down_new, down_moment, down_square = adam_update(
        down_master, down_first, down_second, down_grad, step_value, learn_rate
    )
    up_new, up_moment, up_square = adam_update(
        up_master, up_first, up_second, up_grad, step_value, learn_rate
    )
    return (
        output,
        input_grad,
        down_new,
        down_moment,
        down_square,
        down_new.astype(jnp.bfloat16),
        up_new,
        up_moment,
        up_square,
        up_new.astype(jnp.bfloat16),
    )


LEN = 1024
BLK = 256
LANES = 128
LOG2E = 1.4426950408889634
NT = (((1,), (1,)), ((), ()))
TN = (((0,), (0,)), ((), ()))
VMEM_LIMIT = 24 << 20
F32 = jnp.float32
BF16 = jnp.bfloat16
AXES = ("dp", "mp")
ANY = pl.BlockSpec(memory_space=pl.ANY)


def cost(flops, nbytes, trans=0):
    return pl.CostEstimate(flops=int(flops) // 10, bytes_accessed=int(nbytes) // 10, transcendentals=int(trans) // 10)


def shape(rows, cols, dtype=BF16):
    return jax.ShapeDtypeStruct((rows, cols), dtype)


def full(rows, cols):
    return pl.BlockSpec((rows, cols), lambda i, ix: (0, 0))


def call(body, name, grid, in_specs, out_specs, out_shape, scratch, est, grant=None):
    return pl.pallas_call(
        body,
        grid_spec=pltpu.PrefetchScalarGridSpec(
            num_scalar_prefetch=1,
            grid=(grid,),
            in_specs=in_specs,
            out_specs=out_specs,
            scratch_shapes=scratch,
        ),
        out_shape=out_shape,
        compiler_params=pltpu.CompilerParams(vmem_limit_bytes=grant or VMEM_LIMIT),
        cost_estimate=est,
        name=name,
    )


def hop(value, half_bit, dp_bits):
    ranks = lax.axis_size("mp") // 2
    width = lax.axis_size("mp")
    total = lax.axis_size("dp") * width
    flip = dp_bits * width + half_bit * ranks
    return lax.ppermute(value, AXES, [(i, i ^ flip) for i in range(total)])


def core_swap(value):
    total = lax.axis_size("dp") * lax.axis_size("mp")
    return lax.ppermute(value, AXES, [(i, i ^ 1) for i in range(total)])


def after(value, *others):
    return lax.optimization_barrier((value, *others))[0]


def inner_z():
    z = lax.axis_index("dp") // 2
    return jnp.logical_or(z == 1, z == 2)


def z_hop(value, pairs):
    width = lax.axis_size("mp")
    perm = []
    for source, target in pairs:
        for rest in range(2 * width):
            perm.append((source * 2 * width + rest, target * 2 * width + rest))
    return lax.ppermute(value, AXES, perm)


DIGIT = 64
CUTS = 1
EXTRA = 8
MIDDLE = ((1, 2), (2, 1))
OUTWARD = ((1, 0), (2, 3))


def gather_z(own, first, second):
    begin = after(own, *first)
    z1 = hop(begin, 0, 2)
    m1 = z_hop(begin, MIDDLE)
    m2 = z_hop(z1, MIDDLE)
    f1 = z_hop(m1, OUTWARD)
    f2 = z_hop(after(m2, *second), OUTWARD)
    inner = inner_z()
    return z1, jnp.where(inner, m2, f1), jnp.where(inner, m1, f2)


def pair_xy(value):
    return hop(value, 1, 0), hop(value, 0, 1)


def blocks_of(array, first, half_bit, bit, row=0):
    return [(array, slot, half_bit, 2 * (first + slot) + bit, row) for slot in range(array.shape[0])]


def swapped_blocks(found):
    arrays, table = operands(found)
    arrays = [core_swap(array) for array in arrays]
    return [(arrays[e[0]], *e[1:]) for e in table]


def operands(found):
    arrays = []
    table = []
    for array, *entry in found:
        for k, held in enumerate(arrays):
            if held is array:
                break
        else:
            k = len(arrays)
            arrays.append(array)
        table.append((k, *entry))
    return arrays, table


def copies_of(pairs, sems, start=0):
    return [pltpu.make_async_copy(src, dst, sems.at[start + n]) for n, (src, dst) in enumerate(pairs)]


def load_all(pairs, sems):
    copies = copies_of(pairs, sems)
    for copy in copies:
        copy.start()
    for copy in copies:
        copy.wait()


def at_rows(index, size):
    return pl.ds(pl.multiple_of(index * size, size), size)


def at_lanes(index, size):
    return pl.ds(pl.multiple_of(index * size, LANES), size)


def column_pairs(refs, table, w, ix, first, count, spread):
    pairs = []
    for k, slot, half_bit, dp_bits, _ in table:
        src = refs[k].at[slot, pl.ds(0, LANES), pl.ds(first, count)]
        rows = at_rows(ix[0] ^ dp_bits, LANES)
        dst = w.at[half_bit, rows, :] if spread else w.at[rows, pl.ds(half_bit * count, count)]
        pairs.append((src, dst))
    return pairs


def block_pairs(refs, table, w, ix, half_bit, slot_out):
    pairs = []
    for k, slot, a, dp_bits, row in table:
        if a == half_bit:
            rows = pl.ds(pl.multiple_of((ix[0] ^ dp_bits) * LANES + row, LANES // 2), refs[k].shape[1])
            pairs.append((refs[k].at[slot], w.at[slot_out, rows, :]))
    return pairs


def both_heads(low, value):
    zero = jnp.zeros((), value.dtype)
    return jnp.concatenate([jnp.where(low, value, zero), jnp.where(low, zero, value)], axis=0)


def row_stats(values):
    center = values - jnp.mean(values, axis=-1, keepdims=True)
    scaler = lax.rsqrt(jnp.mean(center * center, axis=-1, keepdims=True) + NORM_EPS)
    return center * scaler, scaler


def lines_of(block):
    part = block.shape[1] // 4
    return lambda n: block[n // 4 : n // 4 + 1, n % 4 * part : (n % 4 + 1) * part]


def prepare_blocks(idx, ids, triple, out_weight, bias, fc_bias, up, fc_weight, proj_weight):
    rows, _, part = triple.shape
    model = 4 * part

    def body(ix, ids_ref, triple_ref, out_ref, bias_ref, fc_ref, up_ref, fcw_ref, proj_ref, block_ref, units_ref, spare):
        units_ref[0, :, :model] = fcw_ref[...]
        units_ref[0, :, model:] = proj_ref[...].astype(F32).T.astype(BF16)
        for s in range(3):
            block_ref[:rows, s * part : (s + 1) * part] = triple_ref[:, s, :]
        block_ref[:rows, 3 * part :] = out_ref[...].astype(F32).T.astype(BF16)
        lane = lax.broadcasted_iota(jnp.int32, (1, LANES), 1)
        counts = jnp.zeros((1, LANES), F32)
        ids = ids_ref[...]
        for g in range(GROUPS):
            hits = jnp.where(ids == g, 1.0, 0.0)
            total = jnp.sum(jnp.sum(hits, axis=0, keepdims=True), axis=1, keepdims=True)
            counts = jnp.where(lane == g, total, counts)
        high = jnp.floor(counts * (1.0 / DIGIT))
        spare[...] = jnp.zeros_like(spare)
        line = lines_of(spare)
        spare[0:1, :LANES] = high
        spare[0:1, LANES : 2 * LANES] = counts - DIGIT * high

        def put(n, value):
            spare[n // 4 : n // 4 + 1, n % 4 * part : (n % 4 + 1) * part] = value.astype(F32)

        for s in range(3):
            put(1 + s, bias_ref[s : s + 1, :])
        for s in range(4):
            put(4 + s, fc_ref[:, s * part : (s + 1) * part])
        for s in range(8):
            put(8 + s, up_ref[s // ADAPTER_RANK, s % ADAPTER_RANK : s % ADAPTER_RANK + 1, :])
        block_ref[rows:, :] = spare[...].astype(BF16)

    arrays = (ids, triple, out_weight, bias, fc_bias, up, fc_weight, proj_weight)
    whole = lambda v: pl.BlockSpec(v.shape, lambda i, ix: (0,) * v.ndim)
    units = 2 * fc_weight.shape[1]
    return call(
        body,
        "prepare_blocks",
        1,
        [whole(v) for v in arrays],
        [full(rows + EXTRA, model), pl.BlockSpec((1, rows, units), lambda i, ix: (0, 0, 0))],
        [shape(rows + EXTRA, model), jax.ShapeDtypeStruct((1, rows, units), BF16)],
        [pltpu.VMEM((EXTRA, model), F32)],
        cost(0, 4 * rows * model),
        60 << 20,
    )(idx, *arrays)


def weigh(idx, ids, fc_bias, near, far, y_near, y_far, x_near, tokens_all):
    units = fc_bias.shape[1]
    per_row = LANES
    own = LEN // 2 // per_row
    rows = near.shape[1] - EXTRA
    width = near.shape[2]

    def body(ix, ids_ref, fc_ref, *rest):
        msgs, (weight_ref, fc_out, held, sems) = rest[:5], rest[5:]
        load_all(
            [
                (msgs[n // 2].at[n % 2, pl.ds(rows, EXTRA), :], held.at[n])
                for n in range(8)
            ]
            + [(msgs[4].at[0, pl.ds(rows, EXTRA), :], held.at[8])],
            sems,
        )
        digits = jnp.zeros((EXTRA, 2 * LANES), F32)
        for n in range(8):
            digits = digits + held[n, :, : 2 * LANES].astype(F32)
        table = tokens_all / (GROUPS * (DIGIT * digits[0:1, :LANES] + digits[0:1, LANES:]))
        for k in range(own):
            ids_row = ids_ref[pl.ds((2 * ix[1] + ix[2]) * own + k, 1), :]
            row = jnp.zeros((1, LANES), F32)
            for g in range(GROUPS):
                row = jnp.where(ids_row == g, table[:, g : g + 1], row)
            weight_ref[k * per_row : (k + 1) * per_row, :] = jnp.broadcast_to(row, (per_row, LANES)).T
        line = lines_of(held[8].astype(F32))
        fc_out[0:1, :] = fc_ref[...].astype(F32)
        fc_out[1:2, :] = jnp.concatenate([line(4 + s) for s in range(4)], axis=1)

    return call(
        body,
        "weigh",
        1,
        [full(*ids.shape), full(1, units)] + [ANY] * 5,
        [full(LEN // 2, LANES), full(2, units)],
        [shape(LEN // 2, LANES, F32), shape(2, units, F32)],
        [pltpu.VMEM((9, EXTRA, width), BF16), pltpu.SemaphoreType.DMA((9,))],
        cost(0, LEN * LANES),
    )(idx, ids, fc_bias, near, far, y_near, y_far, x_near)


def norm_rows(idx, tokens, vec, down):
    model = tokens.shape[1]
    blocks = LEN // BLK

    def body(ix, tok, vec_ref, down_ref, normed_ref, latent_ref, pad_ref):
        @pl.when(pl.program_id(0) == 0)
        def _():
            pad_ref[...] = jnp.zeros_like(pad_ref)
            pad_ref[:8, :] = down_ref[...].astype(BF16)

        hat, _ = row_stats(tok[...].astype(F32))
        normed = (hat * vec_ref[0:1, :] + vec_ref[1:2, :]).astype(BF16)
        normed_ref[...] = normed
        latent_ref[...] = lax.dot_general(normed, pad_ref[...], NT, preferred_element_type=F32).astype(BF16)

    row = lambda c: pl.BlockSpec((BLK, c), lambda i, ix: (i, 0))
    return call(
        body,
        "norm_rows",
        blocks,
        [pl.BlockSpec((BLK, model), lambda i, ix: (ix[1] * blocks + i, 0)), full(8, model), full(8, model)],
        [row(model), row(LANES), full(LANES, model)],
        [shape(LEN, model), shape(LEN, LANES), shape(LANES, model)],
        [],
        cost(2 * LEN * model * LANES, 4 * LEN * model),
    )(idx, tokens, vec, down)


def project_heads(idx, normed, latent, bias, up, x_near, found):
    model = normed.shape[1]
    arrays, table = operands(found)
    part = bias.shape[1]
    cols = 3 * part
    n = len(arrays)

    def body(ix, normed_ref, latent_ref, bias_ref, own_up_ref, near_ref, *rest):
        msgs = rest[:n]
        q_ref, k_ref, v_ref, up_ref, w, spare, lines, sems = rest[n:]

        @pl.when(pl.program_id(0) == 0)
        def _():
            pairs = column_pairs(msgs, table, w, ix, 0, cols, True)
            load_all(pairs + [(near_ref.at[0, pl.ds(model // 8, EXTRA), :], spare)], sems)
            line = lines_of(spare[...].astype(F32))
            up_ref[...] = jnp.zeros_like(up_ref)
            rank = ADAPTER_RANK
            for a in range(2):
                for s in range(3):
                    lines[a : a + 1, s * part : (s + 1) * part] = (
                        bias_ref[s : s + 1, :].astype(F32) if a == 0 else line(1 + s)
                    )
                rows = own_up_ref[...] if a == 0 else jnp.concatenate([line(8 + s) for s in range(8)], axis=0)
                rows = ADAPTER_SCALE * rows
                which = lax.broadcasted_iota(jnp.int32, rows.shape, 0) < rank
                up_ref[a, :8, :part] = jnp.where(which, rows, 0.0).astype(BF16)
                up_ref[a, :8, 2 * part :] = jnp.where(which, 0.0, rows).astype(BF16)

        for a in range(2):
            r = jnp.dot(normed_ref[...], w[a], preferred_element_type=F32) + lines[a : a + 1, :]
            r = r + jnp.dot(latent_ref[...], up_ref[a], preferred_element_type=F32)
            for out, s in ((q_ref, 0), (k_ref, 1), (v_ref, 2)):
                out[:, a * part : (a + 1) * part] = r[:, s * part : (s + 1) * part].astype(BF16)

    row = lambda c: pl.BlockSpec((BLK, c), lambda i, ix: (i, 0))
    both = pl.BlockSpec((2, LANES, cols), lambda i, ix: (0, 0, 0))
    return call(
        body,
        "project_heads",
        LEN // BLK,
        [row(model), row(LANES), full(3, part), full(8, part)] + [ANY] * (1 + n),
        [row(2 * part)] * 3 + [both],
        [shape(LEN, 2 * part)] * 3 + [jax.ShapeDtypeStruct((2, LANES, cols), BF16)],
        [
            pltpu.VMEM((2, model, cols), BF16),
            pltpu.VMEM((EXTRA, model), BF16),
            pltpu.VMEM((8, cols), F32),
            pltpu.SemaphoreType.DMA((len(table) + 1,)),
        ],
        cost(4 * LEN * model * cols, 16 * LEN * model),
    )(idx, normed, latent, bias, up, x_near, *arrays)


def attend_fast(queries, key_rows, value_rows):
    length, width = queries.shape
    pairs = width // LANES

    def body(q_ref, k_ref, v_ref, o_ref, lse_ref, vx, p_ref):
        low = lax.broadcasted_iota(jnp.int32, (1, LANES), 1) < HEAD_DIM
        vx[:, :LANES] = v_ref[...]
        vx[:, LANES:] = jnp.ones((length, LANES), BF16)
        scale = HEAD_DIM**-0.5 * LOG2E
        causal = (lax.broadcasted_iota(jnp.int32, (2 * BLK, BLK), 0) & (BLK - 1)) >= lax.broadcasted_iota(
            jnp.int32, (2 * BLK, BLK), 1
        )
        for i in range(length // BLK):
            start, stop = i * BLK, (i + 1) * BLK
            qb = (q_ref[start:stop, :].astype(F32) * scale).astype(BF16)
            s = lax.dot_general(both_heads(low, qb), k_ref[:stop, :], NT, preferred_element_type=F32)
            sd = jnp.where(causal, s[:, start:], MASKED)
            top = jnp.max(sd, axis=-1, keepdims=True)
            if i:
                top = jnp.maximum(top, jnp.max(s[:, :start], axis=-1, keepdims=True))
                p_ref[i % 2, :, :start] = jnp.exp2(s[:, :start] - top).astype(BF16)
            p_ref[i % 2, :, start:stop] = jnp.exp2(sd - top).astype(BF16)
            out = jnp.dot(p_ref[i % 2, :, :stop], vx[:stop, :], preferred_element_type=F32)
            total = out[:, LANES:]
            mixed = out[:, :LANES] / total
            o_ref[start:stop, :] = jnp.where(low, mixed[:BLK], mixed[BLK:]).astype(BF16)
            log = top + jnp.log2(total)
            log = jnp.where(low, log[:BLK], log[BLK:]).T
            lse_ref[0, 0:1, start:stop] = log[0:1]
            lse_ref[0, 1:2, start:stop] = log[HEAD_DIM : HEAD_DIM + 1]

    spec = pl.BlockSpec((length, LANES), lambda i: (0, i))
    return pl.pallas_call(
        body,
        grid=(pairs,),
        out_shape=(shape(length, width), jax.ShapeDtypeStruct((pairs, 8, length), F32)),
        in_specs=[spec] * 3,
        out_specs=(spec, pl.BlockSpec((1, 8, length), lambda i: (i, 0, 0))),
        scratch_shapes=[pltpu.VMEM((length, 2 * LANES), BF16), pltpu.VMEM((2, 2 * BLK, length), BF16)],
        compiler_params=pltpu.CompilerParams(vmem_limit_bytes=VMEM_LIMIT),
        cost_estimate=cost(8 * length * length * width, 8 * length * width, 2 * pairs * length * length),
        name="attend",
    )(queries, key_rows, value_rows)


def attention_out_send(idx, attended, found, first):
    width = attended.shape[1]
    cut = LANES * lax.axis_size("dp") // CUTS
    arrays, table = operands(found)
    n = len(arrays)
    model = LANES * lax.axis_size("dp")
    half_blocks = LEN // BLK // 2

    def body(ix, att, *rest):
        msgs = rest[:n]
        outs, (w, sems) = rest[n : n + CUTS], rest[n + CUTS :]

        @pl.when(pl.program_id(0) == 0)
        def _():
            load_all(column_pairs(msgs, table, w, ix, first, width // 2, False), sems)

        term = lax.dot_general(att[...], w[...], NT, preferred_element_type=F32).astype(BF16)
        for k, out in enumerate(outs):
            out[...] = term[:, k * cut : (k + 1) * cut]

    return call(
        body,
        "attention_out_send",
        half_blocks,
        [pl.BlockSpec((BLK, width), lambda i, ix: ((1 - ix[2]) * half_blocks + i, 0))] + [ANY] * n,
        [pl.BlockSpec((BLK, cut), lambda i, ix: (i, 0))] * CUTS,
        [shape(LEN // 2, cut)] * CUTS,
        [pltpu.VMEM((model, width), BF16), pltpu.SemaphoreType.DMA((len(table),))],
        cost(LEN * width * model, 2 * LEN * model),
    )(idx, attended, *arrays)


def attention_out_own(idx, attended, received, tokens, vec, found, first):
    width = attended.shape[1]
    arrays, table = operands(found)
    n = len(arrays)
    model = tokens.shape[1]
    half_blocks = LEN // BLK // 2

    def body(ix, att, tok, vec_ref, *rest):
        recv, msgs = rest[:CUTS], rest[CUTS : CUTS + n]
        hidden_ref, normed_ref, w, sems = rest[CUTS + n :]

        @pl.when(pl.program_id(0) == 0)
        def _():
            load_all(column_pairs(msgs, table, w, ix, first, width // 2, False), sems)

        term = lax.dot_general(att[...], w[...], NT, preferred_element_type=F32)
        other = jnp.concatenate([r[...] for r in recv], axis=1).astype(F32)
        hidden = tok[...].astype(F32) + term + other + vec_ref[2:3, :]
        hidden_ref[...] = hidden
        hat, _ = row_stats(hidden)
        normed_ref[...] = (hat * vec_ref[3:4, :] + vec_ref[4:5, :]).astype(BF16)

    row = pl.BlockSpec((BLK, model), lambda i, ix: (i, 0))
    return call(
        body,
        "attention_out_own",
        half_blocks,
        [
            pl.BlockSpec((BLK, width), lambda i, ix: (ix[2] * half_blocks + i, 0)),
            row,
            full(8, model),
        ]
        + [pl.BlockSpec((BLK, model // CUTS), lambda i, ix: (i, 0))] * CUTS
        + [ANY] * n,
        [row, row],
        [shape(LEN // 2, model, F32), shape(LEN // 2, model)],
        [pltpu.VMEM((model, width), BF16), pltpu.SemaphoreType.DMA((len(table),))],
        cost(LEN * width * model, 5 * LEN * model),
    )(idx, attended, tokens, vec, *received, *arrays)


def units_main(idx, half_bit, normed, cotangent, weights, bias, bias_other, vec, mine, other, carried, hidden):
    rows, model = normed.shape
    sources = [operands(f) for f in (mine, other)]
    part = sources[0][0][0].shape[2] // 2
    counts = [len(arrays) for arrays, _ in sources]
    last = hidden is not None
    parts = 4
    piece = model // parts
    chunk = 512
    per = part // chunk
    c0 = 0.7978845608028654
    c1 = 0.044715

    def body(ix, normed_ref, cot, weight_ref, bias_ref, bias_other_ref, vec_ref, *rest):
        carry = rest[: len(carried)]
        rest = rest[len(carried) :]
        hid_ref, rest = (rest[0], rest[1:]) if last else (None, rest)
        msgs = (rest[: counts[0]], rest[counts[0] : sum(counts)])
        rest = rest[sum(counts) :]
        n_out = 1 + parts if last else 2
        outs, (w, grad_ref, x_ref, g_ref, pre_ref, act_ref, sems, *held) = rest[:n_out], rest[n_out:]
        groups = []
        used = 0
        for o in range(2):
            pairs = block_pairs(msgs[o], sources[o][1], w, ix, half_bit, o)
            groups.append(copies_of(pairs, sems, used))
            used += len(pairs)
        for group in groups:
            for copy in group:
                copy.start()
        grad_ref[...] = (cot[...].astype(F32) * weight_ref[:, :1]).astype(BF16)
        biases = (bias_ref, bias_other_ref)

        def multiply(o, c, slot):
            x_ref[slot] = jnp.dot(normed_ref[...], w[o, :, at_lanes(c, chunk)], preferred_element_type=F32)
            g_ref[slot] = jnp.dot(grad_ref[...], w[o, :, at_lanes(c + per, chunk)], preferred_element_type=F32)

        def bend(o, c, slot):
            at = at_lanes(o * per + c, chunk)
            x = x_ref[slot] + biases[o][half_bit : half_bit + 1, at_lanes(c, chunk)]
            sq = x * x
            th = jnp.tanh(c0 * x * (1.0 + c1 * sq))
            left = 0.5 * (1.0 + th)
            slope = left + 0.5 * x * (1.0 - th * th) * (c0 + (3.0 * c0 * c1) * sq)
            pre_ref[:, at] = (slope * g_ref[slot]).astype(BF16)
            act_ref[:, at] = (x * left).astype(BF16)

        for o in range(2):
            for copy in groups[o]:
                copy.wait()
            if o == 0:
                multiply(0, 0, 0)

                def step(c, _):
                    multiply(0, c, lax.rem(c, 2))
                    bend(0, c - 1, lax.rem(c + 1, 2))
                    return 0

                lax.fori_loop(1, per, step, 0)
            else:
                multiply(1, 0, 0)
                bend(0, per - 1, (per - 1) % 2)

                def step(c, _):
                    multiply(1, c, lax.rem(c, 2))
                    bend(1, c - 1, lax.rem(c + 1, 2))
                    return 0

                lax.fori_loop(1, per, step, 0)
                bend(1, per - 1, (per - 1) % 2)

        def mid_of(n):
            at = at_rows(n, BLK)
            lanes = at_lanes(n, BLK)
            mid = lax.dot_general(pre_ref[:, :part], w[0, at, :part], NT, preferred_element_type=F32)
            mid = mid + lax.dot_general(pre_ref[:, part:], w[1, at, :part], NT, preferred_element_type=F32)
            unit = lax.dot_general(act_ref[:, :part], w[0, at, part:], NT, preferred_element_type=F32)
            unit = unit + lax.dot_general(act_ref[:, part:], w[1, at, part:], NT, preferred_element_type=F32)
            if carry:
                mid = mid + carry[0][:, lanes].astype(F32)
                unit = unit + carry[1][:, lanes].astype(F32)
            return mid, unit, lanes

        if not last:

            def finish(n, _):
                mid, unit, lanes = mid_of(n)
                outs[0][:, lanes] = mid.astype(BF16)
                outs[1][:, lanes] = unit.astype(BF16)
                return 0

            lax.fori_loop(0, model // BLK, finish, 0)
            return
        out_low, mid_ref = held

        def finish(n, _):
            mid, unit, lanes = mid_of(n)
            mid_ref[:, lanes] = mid * vec_ref[3:4, lanes]
            out_low[:, lanes] = (unit + hid_ref[:, lanes]).astype(BF16)
            return 0

        lax.fori_loop(0, model // BLK, finish, 0)
        for k in range(parts):
            outs[1 + k][...] = out_low[:, at_lanes((2 * ix[1] + ix[2]) ^ k, piece)]
        step_rows = 128

        def end(r, _):
            at = at_rows(r, step_rows)
            hat, scaler = row_stats(hid_ref[at, :])
            grad = cot[at, :].astype(F32) * weight_ref[at, :1]
            grad = grad + norm_back(hat, scaler, mid_ref[at, :])
            outs[0][at, :] = grad.astype(BF16)
            return 0

        lax.fori_loop(0, rows // step_rows, end, 0)

    block = full(rows, model)
    specs = [
        block,
        block,
        full(rows, LANES),
        full(2, part),
        full(2, part),
        full(8, model),
    ]
    specs += [block] * (len(carried) + (1 if last else 0))
    if last:
        out_specs = [block] + [full(rows, piece)] * parts
        out_shape = [shape(rows, model)] + [shape(rows, piece)] * parts
    else:
        out_specs = [block, block]
        out_shape = [shape(rows, model)] * 2
    arrays = [array for found, _ in sources for array in found]
    return call(
        body,
        "units_main_last" if last else "units_main_first",
        1,
        specs + [ANY] * len(arrays),
        out_specs,
        out_shape,
        [
            pltpu.VMEM((2, model, 2 * part), BF16),
            pltpu.VMEM((rows, model), BF16),
            pltpu.VMEM((2, rows, chunk), F32),
            pltpu.VMEM((2, rows, chunk), F32),
            pltpu.VMEM((rows, 2 * part), BF16),
            pltpu.VMEM((rows, 2 * part), BF16),
            pltpu.SemaphoreType.DMA((sum(len(table) for _, table in sources),)),
        ]
        + ([pltpu.VMEM((rows, model), BF16), pltpu.VMEM((rows, model), F32)] if last else []),
        cost(16 * rows * part * model, 12 * part * model, 2 * rows * part),
    )(idx, normed, cotangent, weights, bias, bias_other, vec, *carried, *((hidden,) if last else ()), *arrays)


def attend_back_fast(
    idx, queries, key_rows, value_rows, mixed, grad_own, grad_other, logsum, normed, latent, up, found, first
):
    length, width = queries.shape
    pairs = width // LANES
    half, model = grad_own.shape
    per = pairs // 2
    arrays, table = operands(found)
    n = len(arrays)

    def body(ix, q_ref, k_ref, v_ref, o_ref, own_ref, other_ref, lse_ref, normed_ref, latent_ref, uq_ref, uv_ref, *rest):
        msgs = rest[:n]
        dq_ref, dk_ref, dv_ref, low_ref, down_ref, rq_ref, rv_ref, low_acc, dq_acc, g_ref, qs_ref, p_ref, ds_ref, w, sems = rest[
            n:
        ]
        pair = pl.program_id(0)

        @pl.when(pair == 0)
        def _():
            load_all(column_pairs(msgs, table, w, ix, first, width // 2, False), sems)

        weight = w[:, at_lanes(pair, LANES)]
        for ref, rank in ((own_ref, ix[2]), (other_ref, 1 - ix[2])):
            g_ref[at_rows(rank, half), :] = jnp.dot(ref[...], weight, preferred_element_type=F32).astype(BF16)
        scale = HEAD_DIM**-0.5 * LOG2E
        low = lax.broadcasted_iota(jnp.int32, (1, LANES), 1) < HEAD_DIM
        qs_ref[...] = (q_ref[...].astype(F32) * scale).astype(BF16)
        prod = (g_ref[...].astype(F32) * o_ref[...].astype(F32)).T
        delta = [
            jnp.sum(prod[:HEAD_DIM], axis=0, keepdims=True),
            jnp.sum(prod[HEAD_DIM:], axis=0, keepdims=True),
        ]
        causal = lax.broadcasted_iota(jnp.int32, (BLK, BLK), 1) >= lax.broadcasted_iota(jnp.int32, (BLK, BLK), 0)

        def scores(j):
            start = j * BLK
            stacked = both_heads(low, k_ref[start : start + BLK, :])
            s = lax.dot_general(stacked, qs_ref[start:, :], NT, preferred_element_type=F32)
            values = both_heads(low, v_ref[start : start + BLK, :])
            dp = lax.dot_general(values, g_ref[start:, :], NT, preferred_element_type=F32)
            for h in range(2):
                rows = slice(h * BLK, (h + 1) * BLK)
                for a, b in ((start, start + BLK), (start + BLK, length)):
                    if a == b:
                        continue
                    sh = s[rows, a - start : b - start] - lse_ref[0, h : h + 1, a:b]
                    if a == start:
                        sh = jnp.where(causal, sh, MASKED)
                    p = jnp.exp2(sh)
                    p_ref[j % 2, rows, a:b] = p.astype(BF16)
                    ds = p * (dp[rows, a - start : b - start] - delta[h][:, a:b])
                    ds_ref[j % 2, rows, a:b] = ds.astype(BF16)
            return stacked

        def spread(j, stacked):
            start = j * BLK
            ds = ds_ref[j % 2, :, start:]
            dk = jnp.dot(ds, q_ref[start:, :], preferred_element_type=F32)
            dv = jnp.dot(p_ref[j % 2, :, start:], g_ref[start:, :], preferred_element_type=F32)
            dk = jnp.where(low, dk[:BLK], dk[BLK:]) * HEAD_DIM**-0.5
            dk_ref[start : start + BLK, :] = dk.astype(BF16)
            dv_ref[start : start + BLK, :] = jnp.where(low, dv[:BLK], dv[BLK:]).astype(BF16)
            dq = lax.dot_general(ds, stacked, TN, preferred_element_type=F32)
            if j == 0:
                dq_acc[...] = dq
            else:
                dq_acc[start:, :] += dq

        stacked = scores(0)
        for j in range(1, length // BLK):
            coming = scores(j)
            spread(j - 1, stacked)
            stacked = coming
        spread(length // BLK - 1, stacked)
        dq_ref[...] = (dq_acc[...] * HEAD_DIM**-0.5).astype(BF16)
        term = lax.dot_general(dq_ref[...], uq_ref[0], NT, preferred_element_type=F32)
        term = term + lax.dot_general(dv_ref[...], uv_ref[0], NT, preferred_element_type=F32)
        latent_t = latent_ref[...]
        rq_ref[...] = lax.dot_general(latent_t, dq_ref[...], TN, preferred_element_type=F32)[:8]
        rv_ref[...] = lax.dot_general(latent_t, dv_ref[...], TN, preferred_element_type=F32)[:8]

        @pl.when(pair == 0)
        def _():
            low_acc[...] = term

        @pl.when(pair > 0)
        def _():
            low_acc[...] += term

        @pl.when(pair == pairs - 1)
        def _():
            low_grad = low_acc[...].astype(BF16)
            low_ref[...] = low_grad
            down_ref[...] = lax.dot_general(low_grad, normed_ref[...], TN, preferred_element_type=F32)[:8]

    spec = pl.BlockSpec((length, LANES), lambda i, ix: (0, i))
    return call(
        body,
        "attend_back",
        pairs,
        [spec] * 4
        + [full(half, model)] * 2
        + [pl.BlockSpec((1, 8, length), lambda i, ix: (i, 0, 0)), full(length, model), full(length, LANES)]
        + [
            pl.BlockSpec((1, LANES, LANES), lambda i, ix: (i // per, 0, lax.rem(i, per))),
            pl.BlockSpec((1, LANES, LANES), lambda i, ix: (i // per, 0, 2 * per + lax.rem(i, per))),
        ]
        + [ANY] * n,
        [spec] * 3
        + [full(length, LANES), full(8, model)]
        + [pl.BlockSpec((8, LANES), lambda i, ix: (0, i))] * 2,
        [shape(length, width)] * 3
        + [shape(length, LANES), shape(8, model, F32), shape(8, width, F32), shape(8, width, F32)],
        [
            pltpu.VMEM((length, LANES), F32),
            pltpu.VMEM((length, LANES), F32),
            pltpu.VMEM((length, LANES), BF16),
            pltpu.VMEM((length, LANES), BF16),
            pltpu.VMEM((2, 2 * BLK, length), BF16),
            pltpu.VMEM((2, 2 * BLK, length), BF16),
            pltpu.VMEM((model, width), BF16),
            pltpu.SemaphoreType.DMA((len(table),)),
        ],
        cost(20 * length * length * width, 16 * length * width, 2 * pairs * length * length),
    )(idx, queries, key_rows, value_rows, mixed, grad_own, grad_other, logsum, normed, latent, up, up, *arrays)


def heads_back(idx, dq, dk, dv, latent_low, down, found):
    width = dq.shape[1]
    part = width // 2
    model = down.shape[1]
    arrays, table = operands(found)
    cols = 3 * part
    n = len(arrays)
    half_blocks = LEN // BLK // 2

    def body(ix, dq_ref, dk_ref, dv_ref, low_ref, down_ref, *rest):
        msgs = rest[:n]
        send_ref, own_ref, w, sems = rest[n:]
        step = pl.program_id(0)

        @pl.when(step == 0)
        def _():
            load_all(column_pairs(msgs, table, w, ix, 0, cols, True), sems)

        total = jnp.dot(low_ref[...], down_ref[...], preferred_element_type=F32)
        for a in range(2):
            cut = slice(a * part, (a + 1) * part)
            piece = jnp.concatenate([dq_ref[:, cut], dk_ref[:, cut], dv_ref[:, cut]], axis=1)
            total = total + lax.dot_general(piece, w[a], NT, preferred_element_type=F32)

        @pl.when(step < half_blocks)
        def _():
            send_ref[...] = total.astype(BF16)

        @pl.when(step >= half_blocks)
        def _():
            own_ref[...] = total.astype(BF16)

    def rows(i, ix):
        rank = jnp.where(i < half_blocks, 1 - ix[2], ix[2])
        return (rank * half_blocks + lax.rem(i, half_blocks), 0)

    row = lambda c: pl.BlockSpec((BLK, c), rows)
    return call(
        body,
        "heads_back",
        2 * half_blocks,
        [row(width)] * 3 + [row(LANES), full(LANES, model)] + [ANY] * n,
        [
            pl.BlockSpec((BLK, model), lambda i, ix: (jnp.minimum(i, half_blocks - 1), 0)),
            pl.BlockSpec((BLK, model), lambda i, ix: (jnp.maximum(i - half_blocks, 0), 0)),
        ],
        [shape(LEN // 2, model)] * 2,
        [pltpu.VMEM((2, model, cols), BF16), pltpu.SemaphoreType.DMA((len(table),))],
        cost(4 * LEN * model * cols, 4 * model * cols),
    )(idx, dq, dk, dv, latent_low, down, *arrays)


def tokens_back(idx, in_own, in_recv, tokens, hidden_grad, vec):
    model = tokens.shape[1]
    half_blocks = LEN // BLK // 2
    parts = 4
    part = model // parts

    def body(ix, own, recv, tok, hg, vec_ref, *rest):
        outs, held = rest[:parts], rest[parts]
        e = vec_ref[0:1, :] * (own[...].astype(F32) + recv[...].astype(F32))
        hat, scaler = row_stats(tok[...].astype(F32))
        held[...] = (hg[...].astype(F32) + norm_back(hat, scaler, e)).astype(BF16)
        for k, out in enumerate(outs):
            out[...] = held[:, at_lanes((2 * ix[1] + ix[2]) ^ k, part)]

    row = pl.BlockSpec((BLK, model), lambda i, ix: (i, 0))
    return call(
        body,
        "tokens_back",
        half_blocks,
        [row, row, row, row, full(8, model)],
        [pl.BlockSpec((BLK, part), lambda i, ix: (i, 0))] * parts,
        [shape(LEN // 2, part)] * parts,
        [pltpu.VMEM((BLK, model), BF16)],
        cost(20 * LEN * model, 8 * LEN * model),
        56 << 20,
    )(idx, in_own, in_recv, tokens, hidden_grad, vec)


def exchange_features(pieces):
    return [pieces[0], core_swap(pieces[1]), hop(pieces[2], 1, 0), both_swap(pieces[3])]


def to_features(idx, pieces, bias):
    rows, part = pieces[0].shape
    parts = len(pieces)

    def body(ix, bias_ref, *rest):
        outs = rest[parts]
        for k in range(parts):
            value = rest[k][...]
            if bias is not None:
                value = (value.astype(F32) + bias_ref[...]).astype(BF16)
            outs[at_rows((2 * ix[1] + ix[2]) ^ k, rows), :] = value

    extra = jnp.zeros((1, part), F32) if bias is None else bias
    return call(
        body,
        "to_features",
        1,
        [full(1, part)] + [full(rows, part)] * parts,
        full(parts * rows, part),
        shape(parts * rows, part),
        [],
        cost(parts * rows * part, 4 * parts * rows * part),
    )(idx, extra, *pieces)


def both_swap(value):
    total = lax.axis_size("dp") * lax.axis_size("mp")
    return lax.ppermute(value, AXES, [(i, i ^ 3) for i in range(total)])


def on_device_fast(
    tokens,
    cotangent,
    group_ids,
    pre_gain,
    pre_shift,
    frozen_triple_weight,
    frozen_triple_bias,
    out_weight,
    out_bias,
    mid_gain,
    mid_shift,
    fc_weight,
    fc_bias,
    proj_weight,
    proj_bias,
    down_master,
    up_master,
    down_first,
    down_second,
    up_first,
    up_second,
    learn_rate,
):
    tok_dev, model = tokens.shape
    ranks = lax.axis_size("mp") // 2
    place = lax.axis_index("mp")
    idx = jnp.stack([lax.axis_index("dp"), place // ranks, place % ranks]).astype(jnp.int32)
    r = ADAPTER_RANK
    step_rows, _, head_part = frozen_triple_weight.shape
    heads_cols = 3 * head_part
    ids = group_ids.reshape(-1, LANES)
    fc_line = fc_bias.reshape(1, -1)
    up_rows = up_master.reshape(2 * r, head_part)
    heads_own, u_own = prepare_blocks(
        idx, ids, frozen_triple_weight, out_weight, frozen_triple_bias, fc_line, up_master, fc_weight, proj_weight
    )
    zero_line = jnp.zeros_like(pre_gain)
    vec = jnp.stack([pre_gain, pre_shift, out_bias, mid_gain, mid_shift, zero_line, zero_line, zero_line]).astype(F32)
    own_start = (idx[1] * ranks + idx[2]) * (LEN // 2)
    own_rows = lambda v: lax.dynamic_slice_in_dim(v, own_start, LEN // 2, 0)
    tok_own, cot_own = own_rows(tokens), own_rows(cotangent)
    h_z1, h_z2, h_z3 = gather_z(heads_own, (), ())
    h_near, h_far = jnp.stack([heads_own, h_z1]), jnp.stack([h_z2, h_z3])
    ux0, uy0 = pair_xy(u_own)
    hx_near, hy_near = pair_xy(after(h_near, ux0, uy0))
    hx_far, hy_far = pair_xy(after(h_far, hx_near, hy_near))
    hd_near, hd_far = hop(after(hx_near, hy_far), 0, 1), hop(hy_far, 1, 0)
    ud0 = hop(after(ux0, hd_near), 0, 1)
    heads = []
    for first, arrays in ((0, (h_near, hx_near, hy_near, hd_near)), (2, (h_far, hx_far, hy_far, hd_far))):
        for n, array in enumerate(arrays):
            heads += blocks_of(array, first, n % 2, n // 2)
    u_rest = jnp.concatenate(gather_z(u_own, (h_far,), (hx_far, hy_far)))
    weights, fc_mine = weigh(
        idx, ids, fc_line, h_near, h_far, hy_near, hy_far, hx_near, float(tok_dev * lax.axis_size("dp"))
    )
    fc_other = core_swap(fc_mine)
    down8 = down_master.reshape(2 * r, model)
    normed, latent, down = norm_rows(idx, after(tokens, hx_far, tok_own, cot_own), vec, down8)
    ux, uy = pair_xy(after(u_rest, hd_far, ud0))
    ready = after(normed, u_rest, ud0, weights)
    queries, keys, values, up = project_heads(idx, ready, latent, frozen_triple_bias, up_rows, hx_near, heads)
    mixed, logsum = attend_fast(queries, keys, values)
    sent = [core_swap(v) for v in attention_out_send(idx, mixed, heads, heads_cols)]
    hidden, normed_mid = attention_out_own(idx, mixed, sent, tok_own, vec, heads, heads_cols)
    rows = (normed_mid, cot_own, weights, fc_mine, fc_other, vec)
    ux, uy, _ = lax.optimization_barrier((ux, uy, normed_mid))
    cut = step_rows // 2
    ud_low, ud_high = hop(ux[:, :cut], 0, 1), hop(uy[:, cut:], 1, 0)

    def table(half_bit, bit, *arrays):
        found, start = [], 0
        for array in arrays:
            found += blocks_of(array, start, half_bit, bit)
            start += array.shape[0]
        return found

    swap = lambda *arrays: [core_swap(v) for v in arrays]
    first_mine = table(0, 0, u_own, u_rest) + table(0, 1, uy0, uy)
    first_other = table(0, 0, *swap(u_own, u_rest)) + table(0, 1, *swap(uy0, uy))
    carried = units_main(idx, 0, *rows, first_mine, first_other, (), None)
    ud_low, ud_high, _ = lax.optimization_barrier((ud_low, ud_high, carried[0]))
    corner = lambda v, low, high: table(1, 1, v) + blocks_of(low, 1, 1, 1) + blocks_of(high, 1, 1, 1, cut)
    last_mine = table(1, 0, ux0, ux) + corner(ud0, ud_low, ud_high)
    last_other = table(1, 0, *swap(ux0, ux)) + corner(*swap(ud0, ud_low, ud_high))
    hidden_low, *out_pieces = units_main(idx, 1, *rows, last_mine, last_other, carried, hidden)
    hidden_other = core_swap(hidden_low)
    out_pieces = exchange_features(out_pieces)
    dq, dk, dv, latent_low, down_term, up_q, up_v = attend_back_fast(
        idx, queries, keys, values, mixed, hidden_low, hidden_other, logsum, normed, latent, up, heads, heads_cols
    )
    up_term = jnp.stack([up_q[:r], up_v[r:]]).reshape(2 * r, 2, head_part)
    down_sum = down_term + core_swap(down_term)
    dq, out_pieces = lax.optimization_barrier((dq, out_pieces))
    in_send, in_own = heads_back(idx, dq, dk, dv, latent_low, down, heads)
    in_recv = core_swap(in_send)
    got = hop(after(jnp.concatenate([down_sum, up_term[:, 1]], axis=1), in_send), 1, 0)
    terms = jnp.concatenate([down_sum, up_term[:, 0]], axis=1) + got
    in_pieces = tokens_back(idx, in_own, in_recv, tok_own, hidden_low, vec)
    in_pieces = exchange_features(in_pieces)
    terms = after(terms, in_pieces[1])
    for bit in (1, 2, 4):
        terms = terms + hop(terms, 0, bit)
    out_pieces = lax.optimization_barrier((out_pieces, in_pieces[1]))[0]
    output = to_features(idx, out_pieces, proj_bias.astype(F32).reshape(1, -1))
    input_grad = to_features(idx, in_pieces, None)
    down_grad = terms[:, :model].reshape(down_master.shape)
    up_grad = ADAPTER_SCALE * terms[:, model:].reshape(up_master.shape)
    step_value = jnp.float32(STEP)
    down_new, down_moment, down_square = adam_update(
        down_master, down_first, down_second, down_grad, step_value, learn_rate
    )
    up_new, up_moment, up_square = adam_update(up_master, up_first, up_second, up_grad, step_value, learn_rate)
    return (
        output,
        input_grad,
        down_new,
        down_moment,
        down_square,
        down_new.astype(BF16),
        up_new,
        up_moment,
        up_square,
        up_new.astype(BF16),
    )


def pick_body(mesh):
    return on_device_fast if mesh.shape["dp"] == 8 and mesh.shape["mp"] == 4 else on_device_general


def solution(mesh):
    body = pick_body(mesh)
    return jax.shard_map(
        body,
        mesh=mesh,
        in_specs=(
            P("dp", None),
            P("dp", None),
            P("dp"),
            P(),
            P(),
            P("dp", None, "mp"),
            P(None, "mp"),
            P("mp", "dp"),
            P(),
            P(),
            P(),
            P("dp", "mp"),
            P("mp"),
            P("mp", "dp"),
            P("mp"),
            P(),
            P(None, None, "mp"),
            P(),
            P(),
            P(None, None, "mp"),
            P(None, None, "mp"),
            P(),
        ),
        out_specs=(
            P("dp", "mp"),
            P("dp", "mp"),
            P(),
            P(),
            P(),
            P(),
            P(None, None, "mp"),
            P(None, None, "mp"),
            P(None, None, "mp"),
            P(None, None, "mp"),
        ),
        check_vma=False,
    )
```

```python
import jax
import jax.numpy as jnp
from jax import lax
from jax.experimental import pallas as pl
from jax.experimental.pallas import tpu as pltpu
from jax.sharding import PartitionSpec as P

HEAD_DIM = 64
ADAPTER_RANK = 4
GROUPS = 16
STEP = 3
MICRO = 2


ADAPTER_SCALE = 8.0
NORM_EPS = 1e-05
MASKED = -1e30
BETA_ONE = 0.5
BETA_TWO = 0.5
ADAM_EPS = 1e-08
DECAY = 0.01


def layer_stats(values):
    center = values - jnp.mean(values, axis=-1, keepdims=True)
    spread = jnp.mean(center * center, axis=-1, keepdims=True)
    scaler = lax.rsqrt(spread + NORM_EPS)
    return (center * scaler, scaler)


def norm_back(normal_hat, scaler, scaled_grad):
    first_mean = jnp.mean(scaled_grad, axis=-1, keepdims=True)
    second_mean = jnp.mean(scaled_grad * normal_hat, axis=-1, keepdims=True)
    return scaler * (scaled_grad - first_mean - normal_hat * second_mean)


def gelu_tanh(values):
    return jax.nn.gelu(values, approximate=True)


def fetch_frozen(frozen_triple_weight, fc_weight, out_weight, proj_weight):
    return (
        lax.all_gather(frozen_triple_weight, "dp", axis=0, tiled=True),
        lax.all_gather(fc_weight, "dp", axis=0, tiled=True),
        lax.all_gather(out_weight, "dp", axis=1, tiled=True),
        lax.all_gather(proj_weight, "dp", axis=1, tiled=True),
    )


def score_block(query_part, key_heads, start, block_rows, key_count):
    score_scale = HEAD_DIM ** (-0.5)
    scores = (
        jnp.einsum("qhd,khd->hqk", query_part, key_heads, preferred_element_type=jnp.float32)
        * score_scale
    )
    allowed = (start + jnp.arange(block_rows, dtype=jnp.int32))[:, None] >= jnp.arange(
        key_count, dtype=jnp.int32
    )[None, :]
    return jnp.where(allowed[None], scores, MASKED)


def attend(queries, key_rows, value_rows):
    length, col_width = queries.shape
    head_count = col_width // HEAD_DIM
    block_rows = min(512, length)
    query_heads = queries.reshape(length, head_count, HEAD_DIM)
    key_heads = key_rows.reshape(length, head_count, HEAD_DIM)
    value_heads = value_rows.reshape(length, head_count, HEAD_DIM)
    mixed_parts = []
    logsum_parts = []
    for index in range(length // block_rows):
        start = index * block_rows
        stop = start + block_rows
        query_part = query_heads[start:stop]
        scores = score_block(query_part, key_heads[:stop], start, block_rows, stop)
        row_top = jnp.max(scores, axis=-1, keepdims=True)
        exp_terms = jnp.exp(scores - row_top)
        row_total = jnp.sum(exp_terms, axis=-1, keepdims=True)
        probs = (exp_terms / row_total).astype(jnp.bfloat16)
        mixed = jnp.einsum(
            "hqk,khd->qhd", probs, value_heads[:stop], preferred_element_type=jnp.float32
        )
        mixed_parts.append(mixed.reshape(block_rows, col_width))
        logsum_parts.append((row_top + jnp.log(row_total))[..., 0])
    return (jnp.concatenate(mixed_parts, axis=0), logsum_parts)


def attend_back(queries, key_rows, value_rows, logsum, mixed_grad):
    length, col_width = queries.shape
    head_count = col_width // HEAD_DIM
    block_rows = min(512, length)
    score_scale = HEAD_DIM ** (-0.5)
    query_heads = queries.reshape(length, head_count, HEAD_DIM)
    key_heads = key_rows.reshape(length, head_count, HEAD_DIM)
    value_heads = value_rows.reshape(length, head_count, HEAD_DIM)
    grad_heads = mixed_grad.reshape(length, head_count, HEAD_DIM)
    key_acc = jnp.zeros((length, head_count, HEAD_DIM), jnp.float32)
    value_acc = jnp.zeros((length, head_count, HEAD_DIM), jnp.float32)
    query_parts = []
    for index in range(length // block_rows):
        start = index * block_rows
        stop = start + block_rows
        query_part = query_heads[start:stop]
        grad_part = grad_heads[start:stop]
        key_part = key_heads[:stop]
        scores = score_block(query_part, key_part, start, block_rows, stop)
        probs = jnp.exp(scores - logsum[index][:, :, None])
        prob_grad = jnp.einsum(
            "qhd,khd->hqk", grad_part, value_heads[:stop], preferred_element_type=jnp.float32
        )
        inner = jnp.sum(prob_grad * probs, axis=-1, keepdims=True)
        score_grad = (probs * (prob_grad - inner)).astype(jnp.bfloat16)
        query_grad = (
            jnp.einsum("hqk,khd->qhd", score_grad, key_part, preferred_element_type=jnp.float32)
            * score_scale
        )
        key_acc = key_acc.at[:stop].add(
            jnp.einsum("hqk,qhd->khd", score_grad, query_part, preferred_element_type=jnp.float32)
            * score_scale
        )
        value_acc = value_acc.at[:stop].add(
            jnp.einsum(
                "hqk,qhd->khd",
                probs.astype(jnp.bfloat16),
                grad_part,
                preferred_element_type=jnp.float32,
            )
        )
        query_parts.append(query_grad.reshape(block_rows, col_width))
    return (
        jnp.concatenate(query_parts, axis=0),
        key_acc.reshape(length, col_width),
        value_acc.reshape(length, col_width),
    )


def adam_update(master, first, second, grad, step_value, learn_rate):
    new_first = BETA_ONE * first + (1.0 - BETA_ONE) * grad
    new_second = BETA_TWO * second + (1.0 - BETA_TWO) * grad * grad
    fix_one = 1.0 - jnp.power(jnp.float32(BETA_ONE), step_value)
    fix_two = 1.0 - jnp.power(jnp.float32(BETA_TWO), step_value)
    update = new_first / fix_one / (jnp.sqrt(new_second / fix_two) + ADAM_EPS)
    new_master = master - learn_rate * (update + DECAY * master)
    return (new_master, new_first, new_second)


def on_device_general(
    tokens,
    cotangent,
    group_ids,
    pre_gain,
    pre_shift,
    frozen_triple_weight,
    frozen_triple_bias,
    out_weight,
    out_bias,
    mid_gain,
    mid_shift,
    fc_weight,
    fc_bias,
    proj_weight,
    proj_bias,
    down_master,
    up_master,
    down_first,
    down_second,
    up_first,
    up_second,
    learn_rate,
):
    tok_dev = tokens.shape[0]
    model_width = tokens.shape[1]
    length = tok_dev // MICRO
    shard_width = model_width // lax.axis_size("mp")
    shard_start = lax.axis_index("mp") * shard_width
    pre_gain_f = pre_gain.astype(jnp.float32)
    pre_shift_f = pre_shift.astype(jnp.float32)
    mid_gain_f = mid_gain.astype(jnp.float32)
    mid_shift_f = mid_shift.astype(jnp.float32)
    out_bias_f = out_bias.astype(jnp.float32)
    fc_bias_f = fc_bias.astype(jnp.float32)
    proj_bias_f = proj_bias.astype(jnp.float32)
    bias_flat = frozen_triple_bias.astype(jnp.float32).reshape(-1)
    onehot = group_ids[:, None] == jnp.arange(GROUPS, dtype=jnp.int32)[None, :]
    local_counts = jnp.sum(onehot.astype(jnp.int32), axis=0)
    totals = lax.psum(local_counts, "dp").astype(jnp.float32)
    own_count = jnp.sum(jnp.where(onehot, totals[None, :], jnp.float32(0.0)), axis=1)
    token_weight = jnp.float32(tok_dev * lax.axis_size("dp")) / (GROUPS * own_count)
    down_low = down_master.astype(jnp.bfloat16).reshape(2 * ADAPTER_RANK, model_width)
    raise_reduced = up_master.astype(jnp.bfloat16)
    grad_down = jnp.zeros((2 * ADAPTER_RANK, model_width), jnp.float32)
    raise_gradient = jnp.zeros(up_master.shape, jnp.float32)
    output_parts = []
    input_parts = []
    for micro_index in range(MICRO):
        current = fetch_frozen(frozen_triple_weight, fc_weight, out_weight, proj_weight)
        qkv_full, fc_full, out_full, proj_full = current
        qkv_flat = qkv_full.reshape(model_width, -1)
        head_width = qkv_flat.shape[1] // 3
        row_start = micro_index * length
        rows_f = lax.dynamic_slice_in_dim(tokens, row_start, length, 0).astype(jnp.float32)
        pre_hat, pre_scale = layer_stats(rows_f)
        normed = (pre_hat * pre_gain_f + pre_shift_f).astype(jnp.bfloat16)
        mixed_proj = jnp.dot(normed, qkv_flat, preferred_element_type=jnp.float32) + bias_flat
        bottleneck = jnp.einsum(
            "td,rd->tr", normed, down_low, preferred_element_type=jnp.float32
        ).astype(jnp.bfloat16)
        queries = (
            mixed_proj[:, :head_width]
            + ADAPTER_SCALE
            * jnp.dot(
                bottleneck[:, :ADAPTER_RANK], raise_reduced[0], preferred_element_type=jnp.float32
            )
        ).astype(jnp.bfloat16)
        key_rows = mixed_proj[:, head_width : 2 * head_width].astype(jnp.bfloat16)
        value_rows = (
            mixed_proj[:, 2 * head_width :]
            + ADAPTER_SCALE
            * jnp.dot(
                bottleneck[:, ADAPTER_RANK:], raise_reduced[1], preferred_element_type=jnp.float32
            )
        ).astype(jnp.bfloat16)
        attended, logsum = attend(queries, key_rows, value_rows)
        attended_low = attended.astype(jnp.bfloat16)
        head_term = jnp.dot(attended_low, out_full, preferred_element_type=jnp.float32).astype(
            jnp.bfloat16
        )
        attn_sum = lax.psum(head_term, "mp").astype(jnp.float32)
        hidden = rows_f + attn_sum + out_bias_f
        mid_hat, mid_scale = layer_stats(hidden)
        normed_mid = (mid_hat * mid_gain_f + mid_shift_f).astype(jnp.bfloat16)
        pre_act = jnp.dot(normed_mid, fc_full, preferred_element_type=jnp.float32) + fc_bias_f
        active, gelu_pullback = jax.vjp(gelu_tanh, pre_act)
        unit_part = jnp.dot(
            active.astype(jnp.bfloat16), proj_full, preferred_element_type=jnp.float32
        ).astype(jnp.bfloat16)
        unit_share = lax.psum_scatter(unit_part, "mp", scatter_dimension=1, tiled=True).astype(
            jnp.float32
        )
        hidden_share = lax.dynamic_slice_in_dim(hidden, shard_start, shard_width, 1)
        output_parts.append((hidden_share + unit_share + proj_bias_f).astype(jnp.bfloat16))
        weight_rows = lax.dynamic_slice_in_dim(token_weight, row_start, length, 0)
        out_grad = (
            lax.dynamic_slice_in_dim(cotangent, row_start, length, 0).astype(jnp.float32)
            * weight_rows[:, None]
        )
        out_low = out_grad.astype(jnp.bfloat16)
        active_grad = jnp.einsum(
            "td,fd->tf", out_low, proj_full, preferred_element_type=jnp.float32
        )
        pre_grad = gelu_pullback(active_grad)[0].astype(jnp.bfloat16)
        mid_part = jnp.einsum(
            "tf,df->td", pre_grad, fc_full, preferred_element_type=jnp.float32
        ).astype(jnp.bfloat16)
        mid_grad = lax.psum(mid_part, "mp").astype(jnp.float32)
        hidden_grad = out_grad + norm_back(mid_hat, mid_scale, mid_gain_f * mid_grad)
        hidden_low = hidden_grad.astype(jnp.bfloat16)
        attended_grad = jnp.einsum(
            "td,hd->th", hidden_low, out_full, preferred_element_type=jnp.float32
        ).astype(jnp.bfloat16)
        query_grad, key_grad, value_grad = attend_back(
            queries, key_rows, value_rows, logsum, attended_grad
        )
        query_low = query_grad.astype(jnp.bfloat16)
        key_low = key_grad.astype(jnp.bfloat16)
        value_low = value_grad.astype(jnp.bfloat16)
        proj_grad = jnp.concatenate([query_low, key_low, value_low], axis=1)
        in_part = jnp.einsum("tc,dc->td", proj_grad, qkv_flat, preferred_element_type=jnp.float32)
        bottleneck_gradient = ADAPTER_SCALE * jnp.concatenate(
            [
                jnp.einsum(
                    "tc,rc->tr", query_low, raise_reduced[0], preferred_element_type=jnp.float32
                ),
                jnp.einsum(
                    "tc,rc->tr", value_low, raise_reduced[1], preferred_element_type=jnp.float32
                ),
            ],
            axis=1,
        )
        latent_low = bottleneck_gradient.astype(jnp.bfloat16)
        in_part = (
            in_part + jnp.dot(latent_low, down_low, preferred_element_type=jnp.float32)
        ).astype(jnp.bfloat16)
        grad_down = grad_down + jnp.einsum(
            "tr,td->rd", latent_low, normed, preferred_element_type=jnp.float32
        )
        raise_gradient = raise_gradient + ADAPTER_SCALE * jnp.stack(
            [
                jnp.einsum(
                    "tr,tc->rc",
                    bottleneck[:, :ADAPTER_RANK],
                    query_low,
                    preferred_element_type=jnp.float32,
                ),
                jnp.einsum(
                    "tr,tc->rc",
                    bottleneck[:, ADAPTER_RANK:],
                    value_low,
                    preferred_element_type=jnp.float32,
                ),
            ],
            axis=0,
        )
        hidden_grad_share = lax.dynamic_slice_in_dim(hidden_grad, shard_start, shard_width, 1)
        in_grad = lax.psum(in_part, "mp").astype(jnp.float32)
        full_grad = norm_back(pre_hat, pre_scale, pre_gain_f * in_grad)
        input_parts.append(
            (
                hidden_grad_share + lax.dynamic_slice_in_dim(full_grad, shard_start, shard_width, 1)
            ).astype(jnp.bfloat16)
        )
    output = jnp.concatenate(output_parts, axis=0)
    input_grad = jnp.concatenate(input_parts, axis=0)
    down_grad = lax.psum(grad_down, ("dp", "mp")).reshape(down_master.shape)
    up_grad = lax.psum(raise_gradient, "dp")
    step_value = jnp.float32(STEP)
    down_new, down_moment, down_square = adam_update(
        down_master, down_first, down_second, down_grad, step_value, learn_rate
    )
    up_new, up_moment, up_square = adam_update(
        up_master, up_first, up_second, up_grad, step_value, learn_rate
    )
    return (
        output,
        input_grad,
        down_new,
        down_moment,
        down_square,
        down_new.astype(jnp.bfloat16),
        up_new,
        up_moment,
        up_square,
        up_new.astype(jnp.bfloat16),
    )


LEN = 1024
BLK = 256
LANES = 128
LOG2E = 1.4426950408889634
NT = (((1,), (1,)), ((), ()))
TN = (((0,), (0,)), ((), ()))
VMEM_LIMIT = 24 << 20
F32 = jnp.float32
BF16 = jnp.bfloat16
AXES = ("dp", "mp")
ANY = pl.BlockSpec(memory_space=pl.ANY)


def cost(flops, nbytes, trans=0):
    return pl.CostEstimate(flops=int(flops) // 10, bytes_accessed=int(nbytes) // 10, transcendentals=int(trans) // 10)


def shape(rows, cols, dtype=BF16):
    return jax.ShapeDtypeStruct((rows, cols), dtype)


def full(rows, cols):
    return pl.BlockSpec((rows, cols), lambda i, ix: (0, 0))


def call(body, name, grid, in_specs, out_specs, out_shape, scratch, est, grant=None):
    return pl.pallas_call(
        body,
        grid_spec=pltpu.PrefetchScalarGridSpec(
            num_scalar_prefetch=1,
            grid=(grid,),
            in_specs=in_specs,
            out_specs=out_specs,
            scratch_shapes=scratch,
        ),
        out_shape=out_shape,
        compiler_params=pltpu.CompilerParams(vmem_limit_bytes=grant or VMEM_LIMIT),
        cost_estimate=est,
        name=name,
    )


def hop(value, half_bit, dp_bits):
    ranks = lax.axis_size("mp") // 2
    width = lax.axis_size("mp")
    total = lax.axis_size("dp") * width
    flip = dp_bits * width + half_bit * ranks
    return lax.ppermute(value, AXES, [(i, i ^ flip) for i in range(total)])


def core_swap(value):
    total = lax.axis_size("dp") * lax.axis_size("mp")
    return lax.ppermute(value, AXES, [(i, i ^ 1) for i in range(total)])


def after(value, *others):
    return lax.optimization_barrier((value, *others))[0]


def inner_z():
    z = lax.axis_index("dp") // 2
    return jnp.logical_or(z == 1, z == 2)


def z_hop(value, pairs):
    width = lax.axis_size("mp")
    perm = []
    for source, target in pairs:
        for rest in range(2 * width):
            perm.append((source * 2 * width + rest, target * 2 * width + rest))
    return lax.ppermute(value, AXES, perm)


DIGIT = 64
CUTS = 1
EXTRA = 8
MIDDLE = ((1, 2), (2, 1))
OUTWARD = ((1, 0), (2, 3))


def gather_z(own, first, second):
    begin = after(own, *first)
    z1 = hop(begin, 0, 2)
    m1 = z_hop(begin, MIDDLE)
    m2 = z_hop(z1, MIDDLE)
    f1 = z_hop(m1, OUTWARD)
    f2 = z_hop(after(m2, *second), OUTWARD)
    inner = inner_z()
    return z1, jnp.where(inner, m2, f1), jnp.where(inner, m1, f2)


def pair_xy(value):
    return hop(value, 1, 0), hop(value, 0, 1)


def blocks_of(array, first, half_bit, bit, row=0):
    return [(array, slot, half_bit, 2 * (first + slot) + bit, row) for slot in range(array.shape[0])]


def swapped_blocks(found):
    arrays, table = operands(found)
    arrays = [core_swap(array) for array in arrays]
    return [(arrays[e[0]], *e[1:]) for e in table]


def operands(found):
    arrays = []
    table = []
    for array, *entry in found:
        for k, held in enumerate(arrays):
            if held is array:
                break
        else:
            k = len(arrays)
            arrays.append(array)
        table.append((k, *entry))
    return arrays, table


def copies_of(pairs, sems, start=0):
    return [pltpu.make_async_copy(src, dst, sems.at[start + n]) for n, (src, dst) in enumerate(pairs)]


def load_all(pairs, sems):
    copies = copies_of(pairs, sems)
    for copy in copies:
        copy.start()
    for copy in copies:
        copy.wait()


def at_rows(index, size):
    return pl.ds(pl.multiple_of(index * size, size), size)


def at_lanes(index, size):
    return pl.ds(pl.multiple_of(index * size, LANES), size)


def column_pairs(refs, table, w, ix, first, count, spread):
    pairs = []
    for k, slot, half_bit, dp_bits, _ in table:
        src = refs[k].at[slot, pl.ds(0, LANES), pl.ds(first, count)]
        rows = at_rows(ix[0] ^ dp_bits, LANES)
        dst = w.at[half_bit, rows, :] if spread else w.at[rows, pl.ds(half_bit * count, count)]
        pairs.append((src, dst))
    return pairs


def block_pairs(refs, table, w, ix, half_bit, slot_out):
    pairs = []
    for k, slot, a, dp_bits, row in table:
        if a == half_bit:
            rows = pl.ds(pl.multiple_of((ix[0] ^ dp_bits) * LANES + row, LANES // 2), refs[k].shape[1])
            pairs.append((refs[k].at[slot], w.at[slot_out, rows, :]))
    return pairs


def both_heads(low, value):
    zero = jnp.zeros((), value.dtype)
    return jnp.concatenate([jnp.where(low, value, zero), jnp.where(low, zero, value)], axis=0)


def row_stats(values):
    center = values - jnp.mean(values, axis=-1, keepdims=True)
    scaler = lax.rsqrt(jnp.mean(center * center, axis=-1, keepdims=True) + NORM_EPS)
    return center * scaler, scaler


def lines_of(block):
    part = block.shape[1] // 4
    return lambda n: block[n // 4 : n // 4 + 1, n % 4 * part : (n % 4 + 1) * part]


def prepare_blocks(idx, ids, triple, out_weight, bias, fc_bias, up, fc_weight, proj_weight):
    rows, _, part = triple.shape
    model = 4 * part

    def body(ix, ids_ref, triple_ref, out_ref, bias_ref, fc_ref, up_ref, fcw_ref, proj_ref, block_ref, units_ref, spare):
        units_ref[0, :, :model] = fcw_ref[...]
        units_ref[0, :, model:] = proj_ref[...].astype(F32).T.astype(BF16)
        for s in range(3):
            block_ref[:rows, s * part : (s + 1) * part] = triple_ref[:, s, :]
        block_ref[:rows, 3 * part :] = out_ref[...].astype(F32).T.astype(BF16)
        lane = lax.broadcasted_iota(jnp.int32, (1, LANES), 1)
        counts = jnp.zeros((1, LANES), F32)
        ids = ids_ref[...]
        for g in range(GROUPS):
            hits = jnp.where(ids == g, 1.0, 0.0)
            total = jnp.sum(jnp.sum(hits, axis=0, keepdims=True), axis=1, keepdims=True)
            counts = jnp.where(lane == g, total, counts)
        high = jnp.floor(counts * (1.0 / DIGIT))
        spare[...] = jnp.zeros_like(spare)
        line = lines_of(spare)
        spare[0:1, :LANES] = high
        spare[0:1, LANES : 2 * LANES] = counts - DIGIT * high

        def put(n, value):
            spare[n // 4 : n // 4 + 1, n % 4 * part : (n % 4 + 1) * part] = value.astype(F32)

        for s in range(3):
            put(1 + s, bias_ref[s : s + 1, :])
        for s in range(4):
            put(4 + s, fc_ref[:, s * part : (s + 1) * part])
        for s in range(8):
            put(8 + s, up_ref[s // ADAPTER_RANK, s % ADAPTER_RANK : s % ADAPTER_RANK + 1, :])
        block_ref[rows:, :] = spare[...].astype(BF16)

    arrays = (ids, triple, out_weight, bias, fc_bias, up, fc_weight, proj_weight)
    whole = lambda v: pl.BlockSpec(v.shape, lambda i, ix: (0,) * v.ndim)
    units = 2 * fc_weight.shape[1]
    return call(
        body,
        "prepare_blocks",
        1,
        [whole(v) for v in arrays],
        [full(rows + EXTRA, model), pl.BlockSpec((1, rows, units), lambda i, ix: (0, 0, 0))],
        [shape(rows + EXTRA, model), jax.ShapeDtypeStruct((1, rows, units), BF16)],
        [pltpu.VMEM((EXTRA, model), F32)],
        cost(0, 4 * rows * model),
        60 << 20,
    )(idx, *arrays)


def weigh(idx, ids, fc_bias, near, far, y_near, y_far, x_near, tokens_all):
    units = fc_bias.shape[1]
    per_row = LANES
    own = LEN // 2 // per_row
    rows = near.shape[1] - EXTRA
    width = near.shape[2]

    def body(ix, ids_ref, fc_ref, *rest):
        msgs, (weight_ref, fc_out, held, sems) = rest[:5], rest[5:]
        load_all(
            [
                (msgs[n // 2].at[n % 2, pl.ds(rows, EXTRA), :], held.at[n])
                for n in range(8)
            ]
            + [(msgs[4].at[0, pl.ds(rows, EXTRA), :], held.at[8])],
            sems,
        )
        digits = jnp.zeros((EXTRA, 2 * LANES), F32)
        for n in range(8):
            digits = digits + held[n, :, : 2 * LANES].astype(F32)
        table = tokens_all / (GROUPS * (DIGIT * digits[0:1, :LANES] + digits[0:1, LANES:]))
        for k in range(own):
            ids_row = ids_ref[pl.ds((2 * ix[1] + ix[2]) * own + k, 1), :]
            row = jnp.zeros((1, LANES), F32)
            for g in range(GROUPS):
                row = jnp.where(ids_row == g, table[:, g : g + 1], row)
            weight_ref[k * per_row : (k + 1) * per_row, :] = jnp.broadcast_to(row, (per_row, LANES)).T
        line = lines_of(held[8].astype(F32))
        fc_out[0:1, :] = fc_ref[...].astype(F32)
        fc_out[1:2, :] = jnp.concatenate([line(4 + s) for s in range(4)], axis=1)

    return call(
        body,
        "weigh",
        1,
        [full(*ids.shape), full(1, units)] + [ANY] * 5,
        [full(LEN // 2, LANES), full(2, units)],
        [shape(LEN // 2, LANES, F32), shape(2, units, F32)],
        [pltpu.VMEM((9, EXTRA, width), BF16), pltpu.SemaphoreType.DMA((9,))],
        cost(0, LEN * LANES),
    )(idx, ids, fc_bias, near, far, y_near, y_far, x_near)


def norm_rows(idx, tokens, vec, down):
    model = tokens.shape[1]
    blocks = LEN // BLK

    def body(ix, tok, vec_ref, down_ref, normed_ref, latent_ref, pad_ref):
        @pl.when(pl.program_id(0) == 0)
        def _():
            pad_ref[...] = jnp.zeros_like(pad_ref)
            pad_ref[:8, :] = down_ref[...].astype(BF16)

        hat, _ = row_stats(tok[...].astype(F32))
        normed = (hat * vec_ref[0:1, :] + vec_ref[1:2, :]).astype(BF16)
        normed_ref[...] = normed
        latent_ref[...] = lax.dot_general(normed, pad_ref[...], NT, preferred_element_type=F32).astype(BF16)

    row = lambda c: pl.BlockSpec((BLK, c), lambda i, ix: (i, 0))
    return call(
        body,
        "norm_rows",
        blocks,
        [pl.BlockSpec((BLK, model), lambda i, ix: (ix[1] * blocks + i, 0)), full(8, model), full(8, model)],
        [row(model), row(LANES), full(LANES, model)],
        [shape(LEN, model), shape(LEN, LANES), shape(LANES, model)],
        [],
        cost(2 * LEN * model * LANES, 4 * LEN * model),
    )(idx, tokens, vec, down)


def project_heads(idx, normed, latent, bias, up, x_near, found):
    model = normed.shape[1]
    arrays, table = operands(found)
    part = bias.shape[1]
    cols = 3 * part
    n = len(arrays)

    def body(ix, normed_ref, latent_ref, bias_ref, own_up_ref, near_ref, *rest):
        msgs = rest[:n]
        q_ref, k_ref, v_ref, up_ref, w, spare, lines, sems = rest[n:]

        @pl.when(pl.program_id(0) == 0)
        def _():
            pairs = column_pairs(msgs, table, w, ix, 0, cols, True)
            load_all(pairs + [(near_ref.at[0, pl.ds(model // 8, EXTRA), :], spare)], sems)
            line = lines_of(spare[...].astype(F32))
            up_ref[...] = jnp.zeros_like(up_ref)
            rank = ADAPTER_RANK
            for a in range(2):
                for s in range(3):
                    lines[a : a + 1, s * part : (s + 1) * part] = (
                        bias_ref[s : s + 1, :].astype(F32) if a == 0 else line(1 + s)
                    )
                rows = own_up_ref[...] if a == 0 else jnp.concatenate([line(8 + s) for s in range(8)], axis=0)
                rows = ADAPTER_SCALE * rows
                which = lax.broadcasted_iota(jnp.int32, rows.shape, 0) < rank
                up_ref[a, :8, :part] = jnp.where(which, rows, 0.0).astype(BF16)
                up_ref[a, :8, 2 * part :] = jnp.where(which, 0.0, rows).astype(BF16)

        for a in range(2):
            r = jnp.dot(normed_ref[...], w[a], preferred_element_type=F32) + lines[a : a + 1, :]
            r = r + jnp.dot(latent_ref[...], up_ref[a], preferred_element_type=F32)
            for out, s in ((q_ref, 0), (k_ref, 1), (v_ref, 2)):
                out[:, a * part : (a + 1) * part] = r[:, s * part : (s + 1) * part].astype(BF16)

    row = lambda c: pl.BlockSpec((BLK, c), lambda i, ix: (i, 0))
    both = pl.BlockSpec((2, LANES, cols), lambda i, ix: (0, 0, 0))
    return call(
        body,
        "project_heads",
        LEN // BLK,
        [row(model), row(LANES), full(3, part), full(8, part)] + [ANY] * (1 + n),
        [row(2 * part)] * 3 + [both],
        [shape(LEN, 2 * part)] * 3 + [jax.ShapeDtypeStruct((2, LANES, cols), BF16)],
        [
            pltpu.VMEM((2, model, cols), BF16),
            pltpu.VMEM((EXTRA, model), BF16),
            pltpu.VMEM((8, cols), F32),
            pltpu.SemaphoreType.DMA((len(table) + 1,)),
        ],
        cost(4 * LEN * model * cols, 16 * LEN * model),
    )(idx, normed, latent, bias, up, x_near, *arrays)


def attend_fast(queries, key_rows, value_rows):
    length, width = queries.shape
    pairs = width // LANES

    def body(q_ref, k_ref, v_ref, o_ref, lse_ref, vx, p_ref):
        low = lax.broadcasted_iota(jnp.int32, (1, LANES), 1) < HEAD_DIM
        vx[:, :LANES] = v_ref[...]
        vx[:, LANES:] = jnp.ones((length, LANES), BF16)
        scale = HEAD_DIM**-0.5 * LOG2E
        causal = (lax.broadcasted_iota(jnp.int32, (2 * BLK, BLK), 0) & (BLK - 1)) >= lax.broadcasted_iota(
            jnp.int32, (2 * BLK, BLK), 1
        )
        for i in range(length // BLK):
            start, stop = i * BLK, (i + 1) * BLK
            qb = (q_ref[start:stop, :].astype(F32) * scale).astype(BF16)
            s = lax.dot_general(both_heads(low, qb), k_ref[:stop, :], NT, preferred_element_type=F32)
            sd = jnp.where(causal, s[:, start:], MASKED)
            top = jnp.max(sd, axis=-1, keepdims=True)
            if i:
                top = jnp.maximum(top, jnp.max(s[:, :start], axis=-1, keepdims=True))
                p_ref[i % 2, :, :start] = jnp.exp2(s[:, :start] - top).astype(BF16)
            p_ref[i % 2, :, start:stop] = jnp.exp2(sd - top).astype(BF16)
            out = jnp.dot(p_ref[i % 2, :, :stop], vx[:stop, :], preferred_element_type=F32)
            total = out[:, LANES:]
            mixed = out[:, :LANES] / total
            o_ref[start:stop, :] = jnp.where(low, mixed[:BLK], mixed[BLK:]).astype(BF16)
            log = top + jnp.log2(total)
            log = jnp.where(low, log[:BLK], log[BLK:]).T
            lse_ref[0, 0:1, start:stop] = log[0:1]
            lse_ref[0, 1:2, start:stop] = log[HEAD_DIM : HEAD_DIM + 1]

    spec = pl.BlockSpec((length, LANES), lambda i: (0, i))
    return pl.pallas_call(
        body,
        grid=(pairs,),
        out_shape=(shape(length, width), jax.ShapeDtypeStruct((pairs, 8, length), F32)),
        in_specs=[spec] * 3,
        out_specs=(spec, pl.BlockSpec((1, 8, length), lambda i: (i, 0, 0))),
        scratch_shapes=[pltpu.VMEM((length, 2 * LANES), BF16), pltpu.VMEM((2, 2 * BLK, length), BF16)],
        compiler_params=pltpu.CompilerParams(vmem_limit_bytes=VMEM_LIMIT),
        cost_estimate=cost(8 * length * length * width, 8 * length * width, 2 * pairs * length * length),
        name="attend",
    )(queries, key_rows, value_rows)


def attention_out_send(idx, attended, found, first):
    width = attended.shape[1]
    cut = LANES * lax.axis_size("dp") // CUTS
    arrays, table = operands(found)
    n = len(arrays)
    model = LANES * lax.axis_size("dp")
    half_blocks = LEN // BLK // 2

    def body(ix, att, *rest):
        msgs = rest[:n]
        outs, (w, sems) = rest[n : n + CUTS], rest[n + CUTS :]

        @pl.when(pl.program_id(0) == 0)
        def _():
            load_all(column_pairs(msgs, table, w, ix, first, width // 2, False), sems)

        term = lax.dot_general(att[...], w[...], NT, preferred_element_type=F32).astype(BF16)
        for k, out in enumerate(outs):
            out[...] = term[:, k * cut : (k + 1) * cut]

    return call(
        body,
        "attention_out_send",
        half_blocks,
        [pl.BlockSpec((BLK, width), lambda i, ix: ((1 - ix[2]) * half_blocks + i, 0))] + [ANY] * n,
        [pl.BlockSpec((BLK, cut), lambda i, ix: (i, 0))] * CUTS,
        [shape(LEN // 2, cut)] * CUTS,
        [pltpu.VMEM((model, width), BF16), pltpu.SemaphoreType.DMA((len(table),))],
        cost(LEN * width * model, 2 * LEN * model),
    )(idx, attended, *arrays)


def attention_out_own(idx, attended, received, tokens, vec, found, first):
    width = attended.shape[1]
    arrays, table = operands(found)
    n = len(arrays)
    model = tokens.shape[1]
    half_blocks = LEN // BLK // 2

    def body(ix, att, tok, vec_ref, *rest):
        recv, msgs = rest[:CUTS], rest[CUTS : CUTS + n]
        hidden_ref, normed_ref, w, sems = rest[CUTS + n :]

        @pl.when(pl.program_id(0) == 0)
        def _():
            load_all(column_pairs(msgs, table, w, ix, first, width // 2, False), sems)

        term = lax.dot_general(att[...], w[...], NT, preferred_element_type=F32)
        other = jnp.concatenate([r[...] for r in recv], axis=1).astype(F32)
        hidden = tok[...].astype(F32) + term + other + vec_ref[2:3, :]
        hidden_ref[...] = hidden
        hat, _ = row_stats(hidden)
        normed_ref[...] = (hat * vec_ref[3:4, :] + vec_ref[4:5, :]).astype(BF16)

    row = pl.BlockSpec((BLK, model), lambda i, ix: (i, 0))
    return call(
        body,
        "attention_out_own",
        half_blocks,
        [
            pl.BlockSpec((BLK, width), lambda i, ix: (ix[2] * half_blocks + i, 0)),
            row,
            full(8, model),
        ]
        + [pl.BlockSpec((BLK, model // CUTS), lambda i, ix: (i, 0))] * CUTS
        + [ANY] * n,
        [row, row],
        [shape(LEN // 2, model, F32), shape(LEN // 2, model)],
        [pltpu.VMEM((model, width), BF16), pltpu.SemaphoreType.DMA((len(table),))],
        cost(LEN * width * model, 5 * LEN * model),
    )(idx, attended, tokens, vec, *received, *arrays)


def units_main(idx, normed, cotangent, weights, vec, biases, groups, carried, hidden):
    rows, model = normed.shape
    arrays, entries = operands([e for half_bit, _, found in groups for e in found if e[2] == half_bit])
    n, count = len(arrays), len(groups)
    part = arrays[0].shape[2] // 2
    at_entry = 0
    tables = []
    for half_bit, _, found in groups:
        size = sum(e[2] == half_bit for e in found)
        tables.append(entries[at_entry : at_entry + size])
        at_entry += size
    last = hidden is not None
    parts = 4
    piece = model // parts
    chunk = 512
    per = part // chunk
    c0 = 0.7978845608028654
    c1 = 0.044715

    def body(ix, normed_ref, cot, weight_ref, vec_ref, bias_ref, bias_other_ref, *rest):
        carry = rest[: len(carried)]
        rest = rest[len(carried) :]
        hid_ref, rest = (rest[0], rest[1:]) if last else (None, rest)
        msgs, rest = rest[:n], rest[n:]
        n_out = 1 + parts if last else 2
        outs, (w, grad_ref, x_ref, g_ref, pre_ref, act_ref, sems, *held) = rest[:n_out], rest[n_out:]
        loads = []
        used = 0
        for o in range(count):
            pairs = block_pairs(msgs, tables[o], w, ix, groups[o][0], o)
            loads.append(copies_of(pairs, sems, used))
            used += len(pairs)
        for load in loads:
            for copy in load:
                copy.start()
        grad_ref[...] = (cot[...].astype(F32) * weight_ref[:, :1]).astype(BF16)
        biases_of = (bias_ref, bias_other_ref)

        def multiply(o, c, slot):
            x_ref[slot] = jnp.dot(normed_ref[...], w[o, :, at_lanes(c, chunk)], preferred_element_type=F32)
            g_ref[slot] = jnp.dot(grad_ref[...], w[o, :, at_lanes(c + per, chunk)], preferred_element_type=F32)

        def bend(o, c, slot):
            at = at_lanes(o * per + c, chunk)
            half_bit, core_bit, _ = groups[o]
            x = x_ref[slot] + biases_of[core_bit][half_bit : half_bit + 1, at_lanes(c, chunk)]
            sq = x * x
            th = jnp.tanh(c0 * x * (1.0 + c1 * sq))
            left = 0.5 * (1.0 + th)
            slope = left + 0.5 * x * (1.0 - th * th) * (c0 + (3.0 * c0 * c1) * sq)
            pre_ref[:, at] = (slope * g_ref[slot]).astype(BF16)
            act_ref[:, at] = (x * left).astype(BF16)

        for o in range(count):
            for copy in loads[o]:
                copy.wait()
            multiply(o, 0, 0)
            if o:
                bend(o - 1, per - 1, (per - 1) % 2)

            def step(c, _, o=o):
                multiply(o, c, lax.rem(c, 2))
                bend(o, c - 1, lax.rem(c + 1, 2))
                return 0

            lax.fori_loop(1, per, step, 0)
        bend(count - 1, per - 1, (per - 1) % 2)

        def mid_of(n):
            at = at_rows(n, BLK)
            lanes = at_lanes(n, BLK)
            mid = jnp.zeros((rows, BLK), F32)
            unit = jnp.zeros((rows, BLK), F32)
            for o in range(count):
                cols = slice(o * part, (o + 1) * part)
                mid = mid + lax.dot_general(pre_ref[:, cols], w[o, at, :part], NT, preferred_element_type=F32)
                unit = unit + lax.dot_general(act_ref[:, cols], w[o, at, part:], NT, preferred_element_type=F32)
            if carry:
                mid = mid + carry[0][:, lanes].astype(F32)
                unit = unit + carry[1][:, lanes].astype(F32)
            return mid, unit, lanes

        if not last:

            def finish(n, _):
                mid, unit, lanes = mid_of(n)
                outs[0][:, lanes] = mid.astype(BF16)
                outs[1][:, lanes] = unit.astype(BF16)
                return 0

            lax.fori_loop(0, model // BLK, finish, 0)
            return
        out_low, mid_ref = held

        def finish(n, _):
            mid, unit, lanes = mid_of(n)
            mid_ref[:, lanes] = mid * vec_ref[3:4, lanes]
            out_low[:, lanes] = (unit + hid_ref[:, lanes]).astype(BF16)
            return 0

        lax.fori_loop(0, model // BLK, finish, 0)
        for k in range(parts):
            outs[1 + k][...] = out_low[:, at_lanes((2 * ix[1] + ix[2]) ^ k, piece)]
        step_rows = 128

        def end(r, _):
            at = at_rows(r, step_rows)
            hat, scaler = row_stats(hid_ref[at, :])
            grad = cot[at, :].astype(F32) * weight_ref[at, :1]
            grad = grad + norm_back(hat, scaler, mid_ref[at, :])
            outs[0][at, :] = grad.astype(BF16)
            return 0

        lax.fori_loop(0, rows // step_rows, end, 0)

    block = full(rows, model)
    specs = [
        block,
        block,
        full(rows, LANES),
        full(8, model),
        full(2, part),
        full(2, part),
    ]
    specs += [block] * (len(carried) + (1 if last else 0))
    if last:
        out_specs = [block] + [full(rows, piece)] * parts
        out_shape = [shape(rows, model)] + [shape(rows, piece)] * parts
    else:
        out_specs = [block, block]
        out_shape = [shape(rows, model)] * 2
    return call(
        body,
        "units_main_last" if last else "units_main_first" if not carried else "units_main_next",
        1,
        specs + [ANY] * len(arrays),
        out_specs,
        out_shape,
        [
            pltpu.VMEM((count, model, 2 * part), BF16),
            pltpu.VMEM((rows, model), BF16),
            pltpu.VMEM((2, rows, chunk), F32),
            pltpu.VMEM((2, rows, chunk), F32),
            pltpu.VMEM((rows, count * part), BF16),
            pltpu.VMEM((rows, count * part), BF16),
            pltpu.SemaphoreType.DMA((len(entries),)),
        ]
        + ([pltpu.VMEM((rows, model), BF16), pltpu.VMEM((rows, model), F32)] if last else []),
        cost(8 * count * rows * part * model, 8 * count * part * model, count * rows * part),
    )(idx, normed, cotangent, weights, vec, *biases, *carried, *((hidden,) if last else ()), *arrays)


def attend_back_fast(
    idx, queries, key_rows, value_rows, mixed, grad_own, grad_other, logsum, normed, latent, up, found, first
):
    length, width = queries.shape
    pairs = width // LANES
    half, model = grad_own.shape
    per = pairs // 2
    arrays, table = operands(found)
    n = len(arrays)

    def body(ix, q_ref, k_ref, v_ref, o_ref, own_ref, other_ref, lse_ref, normed_ref, latent_ref, uq_ref, uv_ref, *rest):
        msgs = rest[:n]
        dq_ref, dk_ref, dv_ref, low_ref, down_ref, rq_ref, rv_ref, low_acc, dq_acc, g_ref, qs_ref, p_ref, ds_ref, w, sems = rest[
            n:
        ]
        pair = pl.program_id(0)

        @pl.when(pair == 0)
        def _():
            load_all(column_pairs(msgs, table, w, ix, first, width // 2, False), sems)

        weight = w[:, at_lanes(pair, LANES)]
        for ref, rank in ((own_ref, ix[2]), (other_ref, 1 - ix[2])):
            g_ref[at_rows(rank, half), :] = jnp.dot(ref[...], weight, preferred_element_type=F32).astype(BF16)
        scale = HEAD_DIM**-0.5 * LOG2E
        low = lax.broadcasted_iota(jnp.int32, (1, LANES), 1) < HEAD_DIM
        qs_ref[...] = (q_ref[...].astype(F32) * scale).astype(BF16)
        prod = (g_ref[...].astype(F32) * o_ref[...].astype(F32)).T
        delta = [
            jnp.sum(prod[:HEAD_DIM], axis=0, keepdims=True),
            jnp.sum(prod[HEAD_DIM:], axis=0, keepdims=True),
        ]
        causal = lax.broadcasted_iota(jnp.int32, (BLK, BLK), 1) >= lax.broadcasted_iota(jnp.int32, (BLK, BLK), 0)

        def scores(j):
            start = j * BLK
            stacked = both_heads(low, k_ref[start : start + BLK, :])
            s = lax.dot_general(stacked, qs_ref[start:, :], NT, preferred_element_type=F32)
            values = both_heads(low, v_ref[start : start + BLK, :])
            dp = lax.dot_general(values, g_ref[start:, :], NT, preferred_element_type=F32)
            for h in range(2):
                rows = slice(h * BLK, (h + 1) * BLK)
                for a, b in ((start, start + BLK), (start + BLK, length)):
                    if a == b:
                        continue
                    sh = s[rows, a - start : b - start] - lse_ref[0, h : h + 1, a:b]
                    if a == start:
                        sh = jnp.where(causal, sh, MASKED)
                    p = jnp.exp2(sh)
                    p_ref[j % 2, rows, a:b] = p.astype(BF16)
                    ds = p * (dp[rows, a - start : b - start] - delta[h][:, a:b])
                    ds_ref[j % 2, rows, a:b] = ds.astype(BF16)
            return stacked

        def spread(j, stacked):
            start = j * BLK
            ds = ds_ref[j % 2, :, start:]
            dk = jnp.dot(ds, q_ref[start:, :], preferred_element_type=F32)
            dv = jnp.dot(p_ref[j % 2, :, start:], g_ref[start:, :], preferred_element_type=F32)
            dk = jnp.where(low, dk[:BLK], dk[BLK:]) * HEAD_DIM**-0.5
            dk_ref[start : start + BLK, :] = dk.astype(BF16)
            dv_ref[start : start + BLK, :] = jnp.where(low, dv[:BLK], dv[BLK:]).astype(BF16)
            dq = lax.dot_general(ds, stacked, TN, preferred_element_type=F32)
            if j == 0:
                dq_acc[...] = dq
            else:
                dq_acc[start:, :] += dq

        stacked = scores(0)
        for j in range(1, length // BLK):
            coming = scores(j)
            spread(j - 1, stacked)
            stacked = coming
        spread(length // BLK - 1, stacked)
        dq_ref[...] = (dq_acc[...] * HEAD_DIM**-0.5).astype(BF16)
        term = lax.dot_general(dq_ref[...], uq_ref[0], NT, preferred_element_type=F32)
        term = term + lax.dot_general(dv_ref[...], uv_ref[0], NT, preferred_element_type=F32)
        latent_t = latent_ref[...]
        rq_ref[...] = lax.dot_general(latent_t, dq_ref[...], TN, preferred_element_type=F32)[:8]
        rv_ref[...] = lax.dot_general(latent_t, dv_ref[...], TN, preferred_element_type=F32)[:8]

        @pl.when(pair == 0)
        def _():
            low_acc[...] = term

        @pl.when(pair > 0)
        def _():
            low_acc[...] += term

        @pl.when(pair == pairs - 1)
        def _():
            low_grad = low_acc[...].astype(BF16)
            low_ref[...] = low_grad
            down_ref[...] = lax.dot_general(low_grad, normed_ref[...], TN, preferred_element_type=F32)[:8]

    spec = pl.BlockSpec((length, LANES), lambda i, ix: (0, i))
    return call(
        body,
        "attend_back",
        pairs,
        [spec] * 4
        + [full(half, model)] * 2
        + [pl.BlockSpec((1, 8, length), lambda i, ix: (i, 0, 0)), full(length, model), full(length, LANES)]
        + [
            pl.BlockSpec((1, LANES, LANES), lambda i, ix: (i // per, 0, lax.rem(i, per))),
            pl.BlockSpec((1, LANES, LANES), lambda i, ix: (i // per, 0, 2 * per + lax.rem(i, per))),
        ]
        + [ANY] * n,
        [spec] * 3
        + [full(length, LANES), full(8, model)]
        + [pl.BlockSpec((8, LANES), lambda i, ix: (0, i))] * 2,
        [shape(length, width)] * 3
        + [shape(length, LANES), shape(8, model, F32), shape(8, width, F32), shape(8, width, F32)],
        [
            pltpu.VMEM((length, LANES), F32),
            pltpu.VMEM((length, LANES), F32),
            pltpu.VMEM((length, LANES), BF16),
            pltpu.VMEM((length, LANES), BF16),
            pltpu.VMEM((2, 2 * BLK, length), BF16),
            pltpu.VMEM((2, 2 * BLK, length), BF16),
            pltpu.VMEM((model, width), BF16),
            pltpu.SemaphoreType.DMA((len(table),)),
        ],
        cost(20 * length * length * width, 16 * length * width, 2 * pairs * length * length),
    )(idx, queries, key_rows, value_rows, mixed, grad_own, grad_other, logsum, normed, latent, up, up, *arrays)


def heads_back(idx, dq, dk, dv, latent_low, down, found):
    width = dq.shape[1]
    part = width // 2
    model = down.shape[1]
    arrays, table = operands(found)
    cols = 3 * part
    n = len(arrays)
    half_blocks = LEN // BLK // 2

    def body(ix, dq_ref, dk_ref, dv_ref, low_ref, down_ref, *rest):
        msgs = rest[:n]
        send_ref, own_ref, w, sems = rest[n:]
        step = pl.program_id(0)

        @pl.when(step == 0)
        def _():
            load_all(column_pairs(msgs, table, w, ix, 0, cols, True), sems)

        total = jnp.dot(low_ref[...], down_ref[...], preferred_element_type=F32)
        for a in range(2):
            cut = slice(a * part, (a + 1) * part)
            piece = jnp.concatenate([dq_ref[:, cut], dk_ref[:, cut], dv_ref[:, cut]], axis=1)
            total = total + lax.dot_general(piece, w[a], NT, preferred_element_type=F32)

        @pl.when(step < half_blocks)
        def _():
            send_ref[...] = total.astype(BF16)

        @pl.when(step >= half_blocks)
        def _():
            own_ref[...] = total.astype(BF16)

    def rows(i, ix):
        rank = jnp.where(i < half_blocks, 1 - ix[2], ix[2])
        return (rank * half_blocks + lax.rem(i, half_blocks), 0)

    row = lambda c: pl.BlockSpec((BLK, c), rows)
    return call(
        body,
        "heads_back",
        2 * half_blocks,
        [row(width)] * 3 + [row(LANES), full(LANES, model)] + [ANY] * n,
        [
            pl.BlockSpec((BLK, model), lambda i, ix: (jnp.minimum(i, half_blocks - 1), 0)),
            pl.BlockSpec((BLK, model), lambda i, ix: (jnp.maximum(i - half_blocks, 0), 0)),
        ],
        [shape(LEN // 2, model)] * 2,
        [pltpu.VMEM((2, model, cols), BF16), pltpu.SemaphoreType.DMA((len(table),))],
        cost(4 * LEN * model * cols, 4 * model * cols),
    )(idx, dq, dk, dv, latent_low, down, *arrays)


def tokens_back(idx, in_own, in_recv, tokens, hidden_grad, vec):
    model = tokens.shape[1]
    half_blocks = LEN // BLK // 2
    parts = 4
    part = model // parts

    def body(ix, own, recv, tok, hg, vec_ref, *rest):
        outs, held = rest[:parts], rest[parts]
        e = vec_ref[0:1, :] * (own[...].astype(F32) + recv[...].astype(F32))
        hat, scaler = row_stats(tok[...].astype(F32))
        held[...] = (hg[...].astype(F32) + norm_back(hat, scaler, e)).astype(BF16)
        for k, out in enumerate(outs):
            out[...] = held[:, at_lanes((2 * ix[1] + ix[2]) ^ k, part)]

    row = pl.BlockSpec((BLK, model), lambda i, ix: (i, 0))
    return call(
        body,
        "tokens_back",
        half_blocks,
        [row, row, row, row, full(8, model)],
        [pl.BlockSpec((BLK, part), lambda i, ix: (i, 0))] * parts,
        [shape(LEN // 2, part)] * parts,
        [pltpu.VMEM((BLK, model), BF16)],
        cost(20 * LEN * model, 8 * LEN * model),
        56 << 20,
    )(idx, in_own, in_recv, tokens, hidden_grad, vec)


def exchange_features(pieces):
    return [pieces[0], core_swap(pieces[1]), hop(pieces[2], 1, 0), both_swap(pieces[3])]


def to_features(idx, pieces, bias):
    rows, part = pieces[0].shape
    parts = len(pieces)

    def body(ix, bias_ref, *rest):
        outs = rest[parts]
        for k in range(parts):
            value = rest[k][...]
            if bias is not None:
                value = (value.astype(F32) + bias_ref[...]).astype(BF16)
            outs[at_rows((2 * ix[1] + ix[2]) ^ k, rows), :] = value

    extra = jnp.zeros((1, part), F32) if bias is None else bias
    return call(
        body,
        "to_features",
        1,
        [full(1, part)] + [full(rows, part)] * parts,
        full(parts * rows, part),
        shape(parts * rows, part),
        [],
        cost(parts * rows * part, 4 * parts * rows * part),
    )(idx, extra, *pieces)


def both_swap(value):
    total = lax.axis_size("dp") * lax.axis_size("mp")
    return lax.ppermute(value, AXES, [(i, i ^ 3) for i in range(total)])


def on_device_fast(
    tokens,
    cotangent,
    group_ids,
    pre_gain,
    pre_shift,
    frozen_triple_weight,
    frozen_triple_bias,
    out_weight,
    out_bias,
    mid_gain,
    mid_shift,
    fc_weight,
    fc_bias,
    proj_weight,
    proj_bias,
    down_master,
    up_master,
    down_first,
    down_second,
    up_first,
    up_second,
    learn_rate,
):
    tok_dev, model = tokens.shape
    ranks = lax.axis_size("mp") // 2
    place = lax.axis_index("mp")
    idx = jnp.stack([lax.axis_index("dp"), place // ranks, place % ranks]).astype(jnp.int32)
    r = ADAPTER_RANK
    step_rows, _, head_part = frozen_triple_weight.shape
    heads_cols = 3 * head_part
    ids = group_ids.reshape(-1, LANES)
    fc_line = fc_bias.reshape(1, -1)
    up_rows = up_master.reshape(2 * r, head_part)
    heads_own, u_own = prepare_blocks(
        idx, ids, frozen_triple_weight, out_weight, frozen_triple_bias, fc_line, up_master, fc_weight, proj_weight
    )
    zero_line = jnp.zeros_like(pre_gain)
    vec = jnp.stack([pre_gain, pre_shift, out_bias, mid_gain, mid_shift, zero_line, zero_line, zero_line]).astype(F32)
    own_start = (idx[1] * ranks + idx[2]) * (LEN // 2)
    own_rows = lambda v: lax.dynamic_slice_in_dim(v, own_start, LEN // 2, 0)
    tok_own, cot_own = own_rows(tokens), own_rows(cotangent)
    h_z1, h_z2, h_z3 = gather_z(heads_own, (), ())
    h_near, h_far = jnp.stack([heads_own, h_z1]), jnp.stack([h_z2, h_z3])
    ux0, uy0 = pair_xy(u_own)
    hx_near, hy_near = pair_xy(after(h_near, ux0, uy0))
    hx_far, hy_far = pair_xy(after(h_far, hx_near, hy_near))
    hd_near, hd_far = hop(after(hx_near, hy_far), 0, 1), hop(hy_far, 1, 0)
    ud0 = hop(after(ux0, hd_near), 0, 1)
    heads = []
    for first, arrays in ((0, (h_near, hx_near, hy_near, hd_near)), (2, (h_far, hx_far, hy_far, hd_far))):
        for n, array in enumerate(arrays):
            heads += blocks_of(array, first, n % 2, n // 2)
    u_rest = jnp.concatenate(gather_z(u_own, (h_far,), (hx_far, hy_far)))
    weights, fc_mine = weigh(
        idx, ids, fc_line, h_near, h_far, hy_near, hy_far, hx_near, float(tok_dev * lax.axis_size("dp"))
    )
    fc_other = core_swap(fc_mine)
    down8 = down_master.reshape(2 * r, model)
    normed, latent, down = norm_rows(idx, after(tokens, hx_far, tok_own, cot_own), vec, down8)
    ux, uy = pair_xy(after(u_rest, hd_far))
    ready = after(normed, u_rest, ud0, weights)
    queries, keys, values, up = project_heads(idx, ready, latent, frozen_triple_bias, up_rows, hx_near, heads)
    mixed, logsum = attend_fast(queries, keys, values)
    sent = [core_swap(v) for v in attention_out_send(idx, mixed, heads, heads_cols)]
    hidden, normed_mid = attention_out_own(idx, mixed, sent, tok_own, vec, heads, heads_cols)
    rows = (normed_mid, cot_own, weights, vec, (fc_mine, fc_other))
    ux, uy, _ = lax.optimization_barrier((ux, uy, normed_mid))
    cut = step_rows // 2
    ud_low, ud_high = hop(ux[:, :cut], 0, 1), hop(uy[:, cut:], 1, 0)

    def table(half_bit, bit, *arrays):
        found, start = [], 0
        for array in arrays:
            found += blocks_of(array, start, half_bit, bit)
            start += array.shape[0]
        return found

    swap = lambda *arrays: [core_swap(v) for v in arrays]
    corner = lambda v, low, high: table(1, 1, v) + blocks_of(low, 1, 1, 1) + blocks_of(high, 1, 1, 1, cut)
    first_mine = table(0, 0, u_own, u_rest) + table(0, 1, uy0, uy)
    first_other = table(0, 0, *swap(u_own, u_rest)) + table(0, 1, *swap(uy0, uy))
    carried = units_main(idx, *rows, [(0, 0, first_mine), (0, 1, first_other)], (), None)
    ud_low, ud_high, ux0_late, ux_late, ud0_late, _ = lax.optimization_barrier(
        (ud_low, ud_high, ux0, ux, ud0, carried[0])
    )
    last_mine = table(1, 0, ux0, ux) + corner(ud0, ud_low, ud_high)
    last_other = table(1, 0, *swap(ux0_late, ux_late)) + corner(*swap(ud0_late, ud_low, ud_high))
    carried = units_main(idx, *rows, [(1, 0, last_mine)], carried, None)
    groups = [(1, 1, last_other)]
    hidden_low, *out_pieces = units_main(idx, *rows, groups, carried, hidden)
    hidden_other = core_swap(hidden_low)
    out_pieces = exchange_features(out_pieces)
    dq, dk, dv, latent_low, down_term, up_q, up_v = attend_back_fast(
        idx, queries, keys, values, mixed, hidden_low, hidden_other, logsum, normed, latent, up, heads, heads_cols
    )
    up_term = jnp.stack([up_q[:r], up_v[r:]]).reshape(2 * r, 2, head_part)
    down_sum = down_term + core_swap(down_term)
    dq, out_pieces = lax.optimization_barrier((dq, out_pieces))
    in_send, in_own = heads_back(idx, dq, dk, dv, latent_low, down, heads)
    in_recv = core_swap(in_send)
    got = hop(after(jnp.concatenate([down_sum, up_term[:, 1]], axis=1), in_send), 1, 0)
    terms = jnp.concatenate([down_sum, up_term[:, 0]], axis=1) + got
    in_pieces = tokens_back(idx, in_own, in_recv, tok_own, hidden_low, vec)
    in_pieces = exchange_features(in_pieces)
    terms = after(terms, in_pieces[1])
    for bit in (1, 2, 4):
        terms = terms + hop(terms, 0, bit)
    out_pieces = lax.optimization_barrier((out_pieces, in_pieces[1]))[0]
    output = to_features(idx, out_pieces, proj_bias.astype(F32).reshape(1, -1))
    input_grad = to_features(idx, in_pieces, None)
    down_grad = terms[:, :model].reshape(down_master.shape)
    up_grad = ADAPTER_SCALE * terms[:, model:].reshape(up_master.shape)
    step_value = jnp.float32(STEP)
    down_new, down_moment, down_square = adam_update(
        down_master, down_first, down_second, down_grad, step_value, learn_rate
    )
    up_new, up_moment, up_square = adam_update(up_master, up_first, up_second, up_grad, step_value, learn_rate)
    return (
        output,
        input_grad,
        down_new,
        down_moment,
        down_square,
        down_new.astype(BF16),
        up_new,
        up_moment,
        up_square,
        up_new.astype(BF16),
    )


def pick_body(mesh):
    return on_device_fast if mesh.shape["dp"] == 8 and mesh.shape["mp"] == 4 else on_device_general


def solution(mesh):
    body = pick_body(mesh)
    return jax.shard_map(
        body,
        mesh=mesh,
        in_specs=(
            P("dp", None),
            P("dp", None),
            P("dp"),
            P(),
            P(),
            P("dp", None, "mp"),
            P(None, "mp"),
            P("mp", "dp"),
            P(),
            P(),
            P(),
            P("dp", "mp"),
            P("mp"),
            P("mp", "dp"),
            P("mp"),
            P(),
            P(None, None, "mp"),
            P(),
            P(),
            P(None, None, "mp"),
            P(None, None, "mp"),
            P(),
        ),
        out_specs=(
            P("dp", "mp"),
            P("dp", "mp"),
            P(),
            P(),
            P(),
            P(),
            P(None, None, "mp"),
            P(None, None, "mp"),
            P(None, None, "mp"),
            P(None, None, "mp"),
        ),
        check_vma=False,
    )
```

```python
import jax
import jax.numpy as jnp
from jax import lax
from jax.experimental import pallas as pl
from jax.experimental.pallas import tpu as pltpu
from jax.sharding import PartitionSpec as P

HEAD_DIM = 64
ADAPTER_RANK = 4
GROUPS = 16
STEP = 3
MICRO = 2


ADAPTER_SCALE = 8.0
NORM_EPS = 1e-05
MASKED = -1e30
BETA_ONE = 0.5
BETA_TWO = 0.5
ADAM_EPS = 1e-08
DECAY = 0.01


def layer_stats(values):
    center = values - jnp.mean(values, axis=-1, keepdims=True)
    spread = jnp.mean(center * center, axis=-1, keepdims=True)
    scaler = lax.rsqrt(spread + NORM_EPS)
    return (center * scaler, scaler)


def norm_back(normal_hat, scaler, scaled_grad):
    first_mean = jnp.mean(scaled_grad, axis=-1, keepdims=True)
    second_mean = jnp.mean(scaled_grad * normal_hat, axis=-1, keepdims=True)
    return scaler * (scaled_grad - first_mean - normal_hat * second_mean)


def gelu_tanh(values):
    return jax.nn.gelu(values, approximate=True)


def fetch_frozen(frozen_triple_weight, fc_weight, out_weight, proj_weight):
    return (
        lax.all_gather(frozen_triple_weight, "dp", axis=0, tiled=True),
        lax.all_gather(fc_weight, "dp", axis=0, tiled=True),
        lax.all_gather(out_weight, "dp", axis=1, tiled=True),
        lax.all_gather(proj_weight, "dp", axis=1, tiled=True),
    )


def score_block(query_part, key_heads, start, block_rows, key_count):
    score_scale = HEAD_DIM ** (-0.5)
    scores = (
        jnp.einsum("qhd,khd->hqk", query_part, key_heads, preferred_element_type=jnp.float32)
        * score_scale
    )
    allowed = (start + jnp.arange(block_rows, dtype=jnp.int32))[:, None] >= jnp.arange(
        key_count, dtype=jnp.int32
    )[None, :]
    return jnp.where(allowed[None], scores, MASKED)


def attend(queries, key_rows, value_rows):
    length, col_width = queries.shape
    head_count = col_width // HEAD_DIM
    block_rows = min(512, length)
    query_heads = queries.reshape(length, head_count, HEAD_DIM)
    key_heads = key_rows.reshape(length, head_count, HEAD_DIM)
    value_heads = value_rows.reshape(length, head_count, HEAD_DIM)
    mixed_parts = []
    logsum_parts = []
    for index in range(length // block_rows):
        start = index * block_rows
        stop = start + block_rows
        query_part = query_heads[start:stop]
        scores = score_block(query_part, key_heads[:stop], start, block_rows, stop)
        row_top = jnp.max(scores, axis=-1, keepdims=True)
        exp_terms = jnp.exp(scores - row_top)
        row_total = jnp.sum(exp_terms, axis=-1, keepdims=True)
        probs = (exp_terms / row_total).astype(jnp.bfloat16)
        mixed = jnp.einsum(
            "hqk,khd->qhd", probs, value_heads[:stop], preferred_element_type=jnp.float32
        )
        mixed_parts.append(mixed.reshape(block_rows, col_width))
        logsum_parts.append((row_top + jnp.log(row_total))[..., 0])
    return (jnp.concatenate(mixed_parts, axis=0), logsum_parts)


def attend_back(queries, key_rows, value_rows, logsum, mixed_grad):
    length, col_width = queries.shape
    head_count = col_width // HEAD_DIM
    block_rows = min(512, length)
    score_scale = HEAD_DIM ** (-0.5)
    query_heads = queries.reshape(length, head_count, HEAD_DIM)
    key_heads = key_rows.reshape(length, head_count, HEAD_DIM)
    value_heads = value_rows.reshape(length, head_count, HEAD_DIM)
    grad_heads = mixed_grad.reshape(length, head_count, HEAD_DIM)
    key_acc = jnp.zeros((length, head_count, HEAD_DIM), jnp.float32)
    value_acc = jnp.zeros((length, head_count, HEAD_DIM), jnp.float32)
    query_parts = []
    for index in range(length // block_rows):
        start = index * block_rows
        stop = start + block_rows
        query_part = query_heads[start:stop]
        grad_part = grad_heads[start:stop]
        key_part = key_heads[:stop]
        scores = score_block(query_part, key_part, start, block_rows, stop)
        probs = jnp.exp(scores - logsum[index][:, :, None])
        prob_grad = jnp.einsum(
            "qhd,khd->hqk", grad_part, value_heads[:stop], preferred_element_type=jnp.float32
        )
        inner = jnp.sum(prob_grad * probs, axis=-1, keepdims=True)
        score_grad = (probs * (prob_grad - inner)).astype(jnp.bfloat16)
        query_grad = (
            jnp.einsum("hqk,khd->qhd", score_grad, key_part, preferred_element_type=jnp.float32)
            * score_scale
        )
        key_acc = key_acc.at[:stop].add(
            jnp.einsum("hqk,qhd->khd", score_grad, query_part, preferred_element_type=jnp.float32)
            * score_scale
        )
        value_acc = value_acc.at[:stop].add(
            jnp.einsum(
                "hqk,qhd->khd",
                probs.astype(jnp.bfloat16),
                grad_part,
                preferred_element_type=jnp.float32,
            )
        )
        query_parts.append(query_grad.reshape(block_rows, col_width))
    return (
        jnp.concatenate(query_parts, axis=0),
        key_acc.reshape(length, col_width),
        value_acc.reshape(length, col_width),
    )


def adam_update(master, first, second, grad, step_value, learn_rate):
    new_first = BETA_ONE * first + (1.0 - BETA_ONE) * grad
    new_second = BETA_TWO * second + (1.0 - BETA_TWO) * grad * grad
    fix_one = 1.0 - jnp.power(jnp.float32(BETA_ONE), step_value)
    fix_two = 1.0 - jnp.power(jnp.float32(BETA_TWO), step_value)
    update = new_first / fix_one / (jnp.sqrt(new_second / fix_two) + ADAM_EPS)
    new_master = master - learn_rate * (update + DECAY * master)
    return (new_master, new_first, new_second)


def on_device_general(
    tokens,
    cotangent,
    group_ids,
    pre_gain,
    pre_shift,
    frozen_triple_weight,
    frozen_triple_bias,
    out_weight,
    out_bias,
    mid_gain,
    mid_shift,
    fc_weight,
    fc_bias,
    proj_weight,
    proj_bias,
    down_master,
    up_master,
    down_first,
    down_second,
    up_first,
    up_second,
    learn_rate,
):
    tok_dev = tokens.shape[0]
    model_width = tokens.shape[1]
    length = tok_dev // MICRO
    shard_width = model_width // lax.axis_size("mp")
    shard_start = lax.axis_index("mp") * shard_width
    pre_gain_f = pre_gain.astype(jnp.float32)
    pre_shift_f = pre_shift.astype(jnp.float32)
    mid_gain_f = mid_gain.astype(jnp.float32)
    mid_shift_f = mid_shift.astype(jnp.float32)
    out_bias_f = out_bias.astype(jnp.float32)
    fc_bias_f = fc_bias.astype(jnp.float32)
    proj_bias_f = proj_bias.astype(jnp.float32)
    bias_flat = frozen_triple_bias.astype(jnp.float32).reshape(-1)
    onehot = group_ids[:, None] == jnp.arange(GROUPS, dtype=jnp.int32)[None, :]
    local_counts = jnp.sum(onehot.astype(jnp.int32), axis=0)
    totals = lax.psum(local_counts, "dp").astype(jnp.float32)
    own_count = jnp.sum(jnp.where(onehot, totals[None, :], jnp.float32(0.0)), axis=1)
    token_weight = jnp.float32(tok_dev * lax.axis_size("dp")) / (GROUPS * own_count)
    down_low = down_master.astype(jnp.bfloat16).reshape(2 * ADAPTER_RANK, model_width)
    raise_reduced = up_master.astype(jnp.bfloat16)
    grad_down = jnp.zeros((2 * ADAPTER_RANK, model_width), jnp.float32)
    raise_gradient = jnp.zeros(up_master.shape, jnp.float32)
    output_parts = []
    input_parts = []
    for micro_index in range(MICRO):
        current = fetch_frozen(frozen_triple_weight, fc_weight, out_weight, proj_weight)
        qkv_full, fc_full, out_full, proj_full = current
        qkv_flat = qkv_full.reshape(model_width, -1)
        head_width = qkv_flat.shape[1] // 3
        row_start = micro_index * length
        rows_f = lax.dynamic_slice_in_dim(tokens, row_start, length, 0).astype(jnp.float32)
        pre_hat, pre_scale = layer_stats(rows_f)
        normed = (pre_hat * pre_gain_f + pre_shift_f).astype(jnp.bfloat16)
        mixed_proj = jnp.dot(normed, qkv_flat, preferred_element_type=jnp.float32) + bias_flat
        bottleneck = jnp.einsum(
            "td,rd->tr", normed, down_low, preferred_element_type=jnp.float32
        ).astype(jnp.bfloat16)
        queries = (
            mixed_proj[:, :head_width]
            + ADAPTER_SCALE
            * jnp.dot(
                bottleneck[:, :ADAPTER_RANK], raise_reduced[0], preferred_element_type=jnp.float32
            )
        ).astype(jnp.bfloat16)
        key_rows = mixed_proj[:, head_width : 2 * head_width].astype(jnp.bfloat16)
        value_rows = (
            mixed_proj[:, 2 * head_width :]
            + ADAPTER_SCALE
            * jnp.dot(
                bottleneck[:, ADAPTER_RANK:], raise_reduced[1], preferred_element_type=jnp.float32
            )
        ).astype(jnp.bfloat16)
        attended, logsum = attend(queries, key_rows, value_rows)
        attended_low = attended.astype(jnp.bfloat16)
        head_term = jnp.dot(attended_low, out_full, preferred_element_type=jnp.float32).astype(
            jnp.bfloat16
        )
        attn_sum = lax.psum(head_term, "mp").astype(jnp.float32)
        hidden = rows_f + attn_sum + out_bias_f
        mid_hat, mid_scale = layer_stats(hidden)
        normed_mid = (mid_hat * mid_gain_f + mid_shift_f).astype(jnp.bfloat16)
        pre_act = jnp.dot(normed_mid, fc_full, preferred_element_type=jnp.float32) + fc_bias_f
        active, gelu_pullback = jax.vjp(gelu_tanh, pre_act)
        unit_part = jnp.dot(
            active.astype(jnp.bfloat16), proj_full, preferred_element_type=jnp.float32
        ).astype(jnp.bfloat16)
        unit_share = lax.psum_scatter(unit_part, "mp", scatter_dimension=1, tiled=True).astype(
            jnp.float32
        )
        hidden_share = lax.dynamic_slice_in_dim(hidden, shard_start, shard_width, 1)
        output_parts.append((hidden_share + unit_share + proj_bias_f).astype(jnp.bfloat16))
        weight_rows = lax.dynamic_slice_in_dim(token_weight, row_start, length, 0)
        out_grad = (
            lax.dynamic_slice_in_dim(cotangent, row_start, length, 0).astype(jnp.float32)
            * weight_rows[:, None]
        )
        out_low = out_grad.astype(jnp.bfloat16)
        active_grad = jnp.einsum(
            "td,fd->tf", out_low, proj_full, preferred_element_type=jnp.float32
        )
        pre_grad = gelu_pullback(active_grad)[0].astype(jnp.bfloat16)
        mid_part = jnp.einsum(
            "tf,df->td", pre_grad, fc_full, preferred_element_type=jnp.float32
        ).astype(jnp.bfloat16)
        mid_grad = lax.psum(mid_part, "mp").astype(jnp.float32)
        hidden_grad = out_grad + norm_back(mid_hat, mid_scale, mid_gain_f * mid_grad)
        hidden_low = hidden_grad.astype(jnp.bfloat16)
        attended_grad = jnp.einsum(
            "td,hd->th", hidden_low, out_full, preferred_element_type=jnp.float32
        ).astype(jnp.bfloat16)
        query_grad, key_grad, value_grad = attend_back(
            queries, key_rows, value_rows, logsum, attended_grad
        )
        query_low = query_grad.astype(jnp.bfloat16)
        key_low = key_grad.astype(jnp.bfloat16)
        value_low = value_grad.astype(jnp.bfloat16)
        proj_grad = jnp.concatenate([query_low, key_low, value_low], axis=1)
        in_part = jnp.einsum("tc,dc->td", proj_grad, qkv_flat, preferred_element_type=jnp.float32)
        bottleneck_gradient = ADAPTER_SCALE * jnp.concatenate(
            [
                jnp.einsum(
                    "tc,rc->tr", query_low, raise_reduced[0], preferred_element_type=jnp.float32
                ),
                jnp.einsum(
                    "tc,rc->tr", value_low, raise_reduced[1], preferred_element_type=jnp.float32
                ),
            ],
            axis=1,
        )
        latent_low = bottleneck_gradient.astype(jnp.bfloat16)
        in_part = (
            in_part + jnp.dot(latent_low, down_low, preferred_element_type=jnp.float32)
        ).astype(jnp.bfloat16)
        grad_down = grad_down + jnp.einsum(
            "tr,td->rd", latent_low, normed, preferred_element_type=jnp.float32
        )
        raise_gradient = raise_gradient + ADAPTER_SCALE * jnp.stack(
            [
                jnp.einsum(
                    "tr,tc->rc",
                    bottleneck[:, :ADAPTER_RANK],
                    query_low,
                    preferred_element_type=jnp.float32,
                ),
                jnp.einsum(
                    "tr,tc->rc",
                    bottleneck[:, ADAPTER_RANK:],
                    value_low,
                    preferred_element_type=jnp.float32,
                ),
            ],
            axis=0,
        )
        hidden_grad_share = lax.dynamic_slice_in_dim(hidden_grad, shard_start, shard_width, 1)
        in_grad = lax.psum(in_part, "mp").astype(jnp.float32)
        full_grad = norm_back(pre_hat, pre_scale, pre_gain_f * in_grad)
        input_parts.append(
            (
                hidden_grad_share + lax.dynamic_slice_in_dim(full_grad, shard_start, shard_width, 1)
            ).astype(jnp.bfloat16)
        )
    output = jnp.concatenate(output_parts, axis=0)
    input_grad = jnp.concatenate(input_parts, axis=0)
    down_grad = lax.psum(grad_down, ("dp", "mp")).reshape(down_master.shape)
    up_grad = lax.psum(raise_gradient, "dp")
    step_value = jnp.float32(STEP)
    down_new, down_moment, down_square = adam_update(
        down_master, down_first, down_second, down_grad, step_value, learn_rate
    )
    up_new, up_moment, up_square = adam_update(
        up_master, up_first, up_second, up_grad, step_value, learn_rate
    )
    return (
        output,
        input_grad,
        down_new,
        down_moment,
        down_square,
        down_new.astype(jnp.bfloat16),
        up_new,
        up_moment,
        up_square,
        up_new.astype(jnp.bfloat16),
    )


LEN = 1024
BLK = 256
LANES = 128
LOG2E = 1.4426950408889634
NT = (((1,), (1,)), ((), ()))
TN = (((0,), (0,)), ((), ()))
VMEM_LIMIT = 24 << 20
F32 = jnp.float32
BF16 = jnp.bfloat16
AXES = ("dp", "mp")
ANY = pl.BlockSpec(memory_space=pl.ANY)


def cost(flops, nbytes, trans=0):
    return pl.CostEstimate(flops=int(flops) // 10, bytes_accessed=int(nbytes) // 10, transcendentals=int(trans) // 10)


def shape(rows, cols, dtype=BF16):
    return jax.ShapeDtypeStruct((rows, cols), dtype)


def full(rows, cols):
    return pl.BlockSpec((rows, cols), lambda i, ix: (0, 0))


def call(body, name, grid, in_specs, out_specs, out_shape, scratch, est, grant=None):
    return pl.pallas_call(
        body,
        grid_spec=pltpu.PrefetchScalarGridSpec(
            num_scalar_prefetch=1,
            grid=(grid,),
            in_specs=in_specs,
            out_specs=out_specs,
            scratch_shapes=scratch,
        ),
        out_shape=out_shape,
        compiler_params=pltpu.CompilerParams(vmem_limit_bytes=grant or VMEM_LIMIT),
        cost_estimate=est,
        name=name,
    )


def hop(value, half_bit, dp_bits):
    ranks = lax.axis_size("mp") // 2
    width = lax.axis_size("mp")
    total = lax.axis_size("dp") * width
    flip = dp_bits * width + half_bit * ranks
    return lax.ppermute(value, AXES, [(i, i ^ flip) for i in range(total)])


def core_swap(value):
    total = lax.axis_size("dp") * lax.axis_size("mp")
    return lax.ppermute(value, AXES, [(i, i ^ 1) for i in range(total)])


def after(value, *others):
    return lax.optimization_barrier((value, *others))[0]


def inner_z():
    z = lax.axis_index("dp") // 2
    return jnp.logical_or(z == 1, z == 2)


def z_hop(value, pairs):
    width = lax.axis_size("mp")
    perm = []
    for source, target in pairs:
        for rest in range(2 * width):
            perm.append((source * 2 * width + rest, target * 2 * width + rest))
    return lax.ppermute(value, AXES, perm)


DIGIT = 64
CUTS = 1
EXTRA = 8
MIDDLE = ((1, 2), (2, 1))
OUTWARD = ((1, 0), (2, 3))


def gather_z(own, first, second):
    begin = after(own, *first)
    z1 = hop(begin, 0, 2)
    m1 = z_hop(begin, MIDDLE)
    m2 = z_hop(z1, MIDDLE)
    f1 = z_hop(m1, OUTWARD)
    f2 = z_hop(after(m2, *second), OUTWARD)
    inner = inner_z()
    return z1, jnp.where(inner, m2, f1), jnp.where(inner, m1, f2)


def pair_xy(value):
    return hop(value, 1, 0), hop(value, 0, 1)


def blocks_of(array, first, half_bit, bit, row=0):
    return [(array, slot, half_bit, 2 * (first + slot) + bit, row) for slot in range(array.shape[0])]


def swapped_blocks(found):
    arrays, table = operands(found)
    arrays = [core_swap(array) for array in arrays]
    return [(arrays[e[0]], *e[1:]) for e in table]


def operands(found):
    arrays = []
    table = []
    for array, *entry in found:
        for k, held in enumerate(arrays):
            if held is array:
                break
        else:
            k = len(arrays)
            arrays.append(array)
        table.append((k, *entry))
    return arrays, table


def copies_of(pairs, sems, start=0):
    return [pltpu.make_async_copy(src, dst, sems.at[start + n]) for n, (src, dst) in enumerate(pairs)]


def load_all(pairs, sems):
    copies = copies_of(pairs, sems)
    for copy in copies:
        copy.start()
    for copy in copies:
        copy.wait()


def at_rows(index, size):
    return pl.ds(pl.multiple_of(index * size, size), size)


def at_lanes(index, size):
    return pl.ds(pl.multiple_of(index * size, LANES), size)


def column_pairs(refs, table, w, ix, first, count, spread):
    pairs = []
    for k, slot, half_bit, dp_bits, _ in table:
        src = refs[k].at[slot, pl.ds(0, LANES), pl.ds(first, count)]
        rows = at_rows(ix[0] ^ dp_bits, LANES)
        dst = w.at[half_bit, rows, :] if spread else w.at[rows, pl.ds(half_bit * count, count)]
        pairs.append((src, dst))
    return pairs


def block_pairs(refs, table, w, ix, half_bit, slot_out):
    pairs = []
    for k, slot, a, dp_bits, row in table:
        if a == half_bit:
            rows = pl.ds(pl.multiple_of((ix[0] ^ dp_bits) * LANES + row, LANES // 2), refs[k].shape[1])
            pairs.append((refs[k].at[slot], w.at[slot_out, rows, :]))
    return pairs


def both_heads(low, value):
    zero = jnp.zeros((), value.dtype)
    return jnp.concatenate([jnp.where(low, value, zero), jnp.where(low, zero, value)], axis=0)


def row_stats(values):
    center = values - jnp.mean(values, axis=-1, keepdims=True)
    scaler = lax.rsqrt(jnp.mean(center * center, axis=-1, keepdims=True) + NORM_EPS)
    return center * scaler, scaler


def lines_of(block):
    part = block.shape[1] // 4
    return lambda n: block[n // 4 : n // 4 + 1, n % 4 * part : (n % 4 + 1) * part]


def prepare_blocks(idx, ids, triple, out_weight, bias, fc_bias, up, fc_weight, proj_weight):
    rows, _, part = triple.shape
    model = 4 * part

    def body(ix, ids_ref, triple_ref, out_ref, bias_ref, fc_ref, up_ref, fcw_ref, proj_ref, block_ref, units_ref, spare):
        units_ref[0, :, :model] = fcw_ref[...]
        units_ref[0, :, model:] = proj_ref[...].astype(F32).T.astype(BF16)
        for s in range(3):
            block_ref[:rows, s * part : (s + 1) * part] = triple_ref[:, s, :]
        block_ref[:rows, 3 * part :] = out_ref[...].astype(F32).T.astype(BF16)
        lane = lax.broadcasted_iota(jnp.int32, (1, LANES), 1)
        counts = jnp.zeros((1, LANES), F32)
        ids = ids_ref[...]
        for g in range(GROUPS):
            hits = jnp.where(ids == g, 1.0, 0.0)
            total = jnp.sum(jnp.sum(hits, axis=0, keepdims=True), axis=1, keepdims=True)
            counts = jnp.where(lane == g, total, counts)
        high = jnp.floor(counts * (1.0 / DIGIT))
        spare[...] = jnp.zeros_like(spare)
        line = lines_of(spare)
        spare[0:1, :LANES] = high
        spare[0:1, LANES : 2 * LANES] = counts - DIGIT * high

        def put(n, value):
            spare[n // 4 : n // 4 + 1, n % 4 * part : (n % 4 + 1) * part] = value.astype(F32)

        for s in range(3):
            put(1 + s, bias_ref[s : s + 1, :])
        for s in range(4):
            put(4 + s, fc_ref[:, s * part : (s + 1) * part])
        for s in range(8):
            put(8 + s, up_ref[s // ADAPTER_RANK, s % ADAPTER_RANK : s % ADAPTER_RANK + 1, :])
        block_ref[rows:, :] = spare[...].astype(BF16)

    arrays = (ids, triple, out_weight, bias, fc_bias, up, fc_weight, proj_weight)
    whole = lambda v: pl.BlockSpec(v.shape, lambda i, ix: (0,) * v.ndim)
    units = 2 * fc_weight.shape[1]
    return call(
        body,
        "prepare_blocks",
        1,
        [whole(v) for v in arrays],
        [full(rows + EXTRA, model), pl.BlockSpec((1, rows, units), lambda i, ix: (0, 0, 0))],
        [shape(rows + EXTRA, model), jax.ShapeDtypeStruct((1, rows, units), BF16)],
        [pltpu.VMEM((EXTRA, model), F32)],
        cost(0, 4 * rows * model),
        60 << 20,
    )(idx, *arrays)


def weigh(idx, ids, fc_bias, near, far, y_near, y_far, x_near, tokens_all):
    units = fc_bias.shape[1]
    per_row = LANES
    own = LEN // 2 // per_row
    rows = near.shape[1] - EXTRA
    width = near.shape[2]

    def body(ix, ids_ref, fc_ref, *rest):
        msgs, (weight_ref, fc_out, held, sems) = rest[:5], rest[5:]
        load_all(
            [
                (msgs[n // 2].at[n % 2, pl.ds(rows, EXTRA), :], held.at[n])
                for n in range(8)
            ]
            + [(msgs[4].at[0, pl.ds(rows, EXTRA), :], held.at[8])],
            sems,
        )
        digits = jnp.zeros((EXTRA, 2 * LANES), F32)
        for n in range(8):
            digits = digits + held[n, :, : 2 * LANES].astype(F32)
        table = tokens_all / (GROUPS * (DIGIT * digits[0:1, :LANES] + digits[0:1, LANES:]))
        for k in range(own):
            ids_row = ids_ref[pl.ds((2 * ix[1] + ix[2]) * own + k, 1), :]
            row = jnp.zeros((1, LANES), F32)
            for g in range(GROUPS):
                row = jnp.where(ids_row == g, table[:, g : g + 1], row)
            weight_ref[k * per_row : (k + 1) * per_row, :] = jnp.broadcast_to(row, (per_row, LANES)).T
        line = lines_of(held[8].astype(F32))
        fc_out[0:1, :] = fc_ref[...].astype(F32)
        fc_out[1:2, :] = jnp.concatenate([line(4 + s) for s in range(4)], axis=1)

    return call(
        body,
        "weigh",
        1,
        [full(*ids.shape), full(1, units)] + [ANY] * 5,
        [full(LEN // 2, LANES), full(2, units)],
        [shape(LEN // 2, LANES, F32), shape(2, units, F32)],
        [pltpu.VMEM((9, EXTRA, width), BF16), pltpu.SemaphoreType.DMA((9,))],
        cost(0, LEN * LANES),
    )(idx, ids, fc_bias, near, far, y_near, y_far, x_near)


def norm_rows(idx, tokens, vec, down):
    model = tokens.shape[1]
    blocks = LEN // BLK

    def body(ix, tok, vec_ref, down_ref, normed_ref, latent_ref, latent_t_ref, pad_ref):
        @pl.when(pl.program_id(0) == 0)
        def _():
            pad_ref[...] = jnp.zeros_like(pad_ref)
            pad_ref[:8, :] = down_ref[...].astype(BF16)

        hat, _ = row_stats(tok[...].astype(F32))
        normed = (hat * vec_ref[0:1, :] + vec_ref[1:2, :]).astype(BF16)
        normed_ref[...] = normed
        latent_ref[...] = lax.dot_general(normed, pad_ref[...], NT, preferred_element_type=F32).astype(BF16)
        turned = lax.dot_general(pad_ref[:16, :], normed, NT, preferred_element_type=F32)
        latent_t_ref[...] = turned.astype(BF16)

    row = lambda c: pl.BlockSpec((BLK, c), lambda i, ix: (i, 0))
    return call(
        body,
        "norm_rows",
        blocks,
        [pl.BlockSpec((BLK, model), lambda i, ix: (ix[1] * blocks + i, 0)), full(8, model), full(8, model)],
        [row(model), row(LANES), pl.BlockSpec((16, BLK), lambda i, ix: (0, i)), full(LANES, model)],
        [shape(LEN, model), shape(LEN, LANES), shape(16, LEN), shape(LANES, model)],
        [],
        cost(2 * LEN * model * LANES, 4 * LEN * model),
    )(idx, tokens, vec, down)


def project_heads(idx, normed, latent, bias, up, x_near, found):
    model = normed.shape[1]
    arrays, table = operands(found)
    part = bias.shape[1]
    cols = 3 * part
    n = len(arrays)

    def body(ix, normed_ref, latent_ref, bias_ref, own_up_ref, near_ref, *rest):
        msgs = rest[:n]
        q_ref, k_ref, v_ref, up_ref, w, spare, lines, sems = rest[n:]

        @pl.when(pl.program_id(0) == 0)
        def _():
            pairs = column_pairs(msgs, table, w, ix, 0, cols, True)
            load_all(pairs + [(near_ref.at[0, pl.ds(model // 8, EXTRA), :], spare)], sems)
            line = lines_of(spare[...].astype(F32))
            up_ref[...] = jnp.zeros_like(up_ref)
            rank = ADAPTER_RANK
            for a in range(2):
                for s in range(3):
                    lines[a : a + 1, s * part : (s + 1) * part] = (
                        bias_ref[s : s + 1, :].astype(F32) if a == 0 else line(1 + s)
                    )
                rows = own_up_ref[...] if a == 0 else jnp.concatenate([line(8 + s) for s in range(8)], axis=0)
                rows = ADAPTER_SCALE * rows
                which = lax.broadcasted_iota(jnp.int32, rows.shape, 0) < rank
                up_ref[a, :8, :part] = jnp.where(which, rows, 0.0).astype(BF16)
                up_ref[a, :8, 2 * part :] = jnp.where(which, 0.0, rows).astype(BF16)

        for a in range(2):
            r = jnp.dot(normed_ref[...], w[a], preferred_element_type=F32) + lines[a : a + 1, :]
            r = r + jnp.dot(latent_ref[...], up_ref[a], preferred_element_type=F32)
            for out, s in ((q_ref, 0), (k_ref, 1), (v_ref, 2)):
                out[:, a * part : (a + 1) * part] = r[:, s * part : (s + 1) * part].astype(BF16)

    row = lambda c: pl.BlockSpec((BLK, c), lambda i, ix: (i, 0))
    both = pl.BlockSpec((2, LANES, cols), lambda i, ix: (0, 0, 0))
    return call(
        body,
        "project_heads",
        LEN // BLK,
        [row(model), row(LANES), full(3, part), full(8, part)] + [ANY] * (1 + n),
        [row(2 * part)] * 3 + [both],
        [shape(LEN, 2 * part)] * 3 + [jax.ShapeDtypeStruct((2, LANES, cols), BF16)],
        [
            pltpu.VMEM((2, model, cols), BF16),
            pltpu.VMEM((EXTRA, model), BF16),
            pltpu.VMEM((8, cols), F32),
            pltpu.SemaphoreType.DMA((len(table) + 1,)),
        ],
        cost(4 * LEN * model * cols, 16 * LEN * model),
    )(idx, normed, latent, bias, up, x_near, *arrays)


def attend_fast(queries, key_rows, value_rows):
    length, width = queries.shape
    pairs = width // LANES

    def body(q_ref, k_ref, v_ref, o_ref, lse_ref, vx, p_ref):
        low = lax.broadcasted_iota(jnp.int32, (1, LANES), 1) < HEAD_DIM
        vx[:, :LANES] = v_ref[...]
        vx[:, LANES:] = jnp.ones((length, LANES), BF16)
        scale = HEAD_DIM**-0.5 * LOG2E
        causal = (lax.broadcasted_iota(jnp.int32, (2 * BLK, BLK), 0) & (BLK - 1)) >= lax.broadcasted_iota(
            jnp.int32, (2 * BLK, BLK), 1
        )
        for i in range(length // BLK):
            start, stop = i * BLK, (i + 1) * BLK
            qb = (q_ref[start:stop, :].astype(F32) * scale).astype(BF16)
            s = lax.dot_general(both_heads(low, qb), k_ref[:stop, :], NT, preferred_element_type=F32)
            sd = jnp.where(causal, s[:, start:], MASKED)
            top = jnp.max(sd, axis=-1, keepdims=True)
            if i:
                top = jnp.maximum(top, jnp.max(s[:, :start], axis=-1, keepdims=True))
                p_ref[i % 2, :, :start] = jnp.exp2(s[:, :start] - top).astype(BF16)
            p_ref[i % 2, :, start:stop] = jnp.exp2(sd - top).astype(BF16)
            out = jnp.dot(p_ref[i % 2, :, :stop], vx[:stop, :], preferred_element_type=F32)
            total = out[:, LANES:]
            mixed = out[:, :LANES] / total
            o_ref[start:stop, :] = jnp.where(low, mixed[:BLK], mixed[BLK:]).astype(BF16)
            log = top + jnp.log2(total)
            log = jnp.where(low, log[:BLK], log[BLK:]).T
            lse_ref[0, 0:1, start:stop] = log[0:1]
            lse_ref[0, 1:2, start:stop] = log[HEAD_DIM : HEAD_DIM + 1]

    spec = pl.BlockSpec((length, LANES), lambda i: (0, i))
    return pl.pallas_call(
        body,
        grid=(pairs,),
        out_shape=(shape(length, width), jax.ShapeDtypeStruct((pairs, 8, length), F32)),
        in_specs=[spec] * 3,
        out_specs=(spec, pl.BlockSpec((1, 8, length), lambda i: (i, 0, 0))),
        scratch_shapes=[pltpu.VMEM((length, 2 * LANES), BF16), pltpu.VMEM((2, 2 * BLK, length), BF16)],
        compiler_params=pltpu.CompilerParams(vmem_limit_bytes=VMEM_LIMIT),
        cost_estimate=cost(8 * length * length * width, 8 * length * width, 2 * pairs * length * length),
        name="attend",
    )(queries, key_rows, value_rows)


def attention_out_send(idx, attended, found, first):
    width = attended.shape[1]
    cut = LANES * lax.axis_size("dp") // CUTS
    arrays, table = operands(found)
    n = len(arrays)
    model = LANES * lax.axis_size("dp")
    half_blocks = LEN // BLK // 2

    def body(ix, att, *rest):
        msgs = rest[:n]
        outs, (w, sems) = rest[n : n + CUTS], rest[n + CUTS :]

        @pl.when(pl.program_id(0) == 0)
        def _():
            load_all(column_pairs(msgs, table, w, ix, first, width // 2, False), sems)

        term = lax.dot_general(att[...], w[...], NT, preferred_element_type=F32).astype(BF16)
        for k, out in enumerate(outs):
            out[...] = term[:, k * cut : (k + 1) * cut]

    return call(
        body,
        "attention_out_send",
        half_blocks,
        [pl.BlockSpec((BLK, width), lambda i, ix: ((1 - ix[2]) * half_blocks + i, 0))] + [ANY] * n,
        [pl.BlockSpec((BLK, cut), lambda i, ix: (i, 0))] * CUTS,
        [shape(LEN // 2, cut)] * CUTS,
        [pltpu.VMEM((model, width), BF16), pltpu.SemaphoreType.DMA((len(table),))],
        cost(LEN * width * model, 2 * LEN * model),
    )(idx, attended, *arrays)


def attention_out_own(idx, attended, received, tokens, vec, found, first):
    width = attended.shape[1]
    arrays, table = operands(found)
    n = len(arrays)
    model = tokens.shape[1]
    half_blocks = LEN // BLK // 2

    def body(ix, att, tok, vec_ref, *rest):
        recv, msgs = rest[:CUTS], rest[CUTS : CUTS + n]
        hidden_ref, normed_ref, w, sems = rest[CUTS + n :]

        @pl.when(pl.program_id(0) == 0)
        def _():
            load_all(column_pairs(msgs, table, w, ix, first, width // 2, False), sems)

        term = lax.dot_general(att[...], w[...], NT, preferred_element_type=F32)
        other = jnp.concatenate([r[...] for r in recv], axis=1).astype(F32)
        hidden = tok[...].astype(F32) + term + other + vec_ref[2:3, :]
        hidden_ref[...] = hidden
        hat, _ = row_stats(hidden)
        normed_ref[...] = (hat * vec_ref[3:4, :] + vec_ref[4:5, :]).astype(BF16)

    row = pl.BlockSpec((BLK, model), lambda i, ix: (i, 0))
    return call(
        body,
        "attention_out_own",
        half_blocks,
        [
            pl.BlockSpec((BLK, width), lambda i, ix: (ix[2] * half_blocks + i, 0)),
            row,
            full(8, model),
        ]
        + [pl.BlockSpec((BLK, model // CUTS), lambda i, ix: (i, 0))] * CUTS
        + [ANY] * n,
        [row, row],
        [shape(LEN // 2, model, F32), shape(LEN // 2, model)],
        [pltpu.VMEM((model, width), BF16), pltpu.SemaphoreType.DMA((len(table),))],
        cost(LEN * width * model, 5 * LEN * model),
    )(idx, attended, tokens, vec, *received, *arrays)


def units_main(idx, normed, cotangent, weights, vec, biases, groups, carried, hidden):
    rows, model = normed.shape
    arrays, entries = operands([e for half_bit, _, found in groups for e in found if e[2] == half_bit])
    n, count = len(arrays), len(groups)
    part = arrays[0].shape[2] // 2
    at_entry = 0
    tables = []
    for half_bit, _, found in groups:
        size = sum(e[2] == half_bit for e in found)
        tables.append(entries[at_entry : at_entry + size])
        at_entry += size
    last = hidden is not None
    parts = 4
    piece = model // parts
    chunk = 512
    wide = 512 if hidden is not None else 256
    per = part // chunk
    c0 = 0.7978845608028654
    c1 = 0.044715

    def body(ix, normed_ref, cot, weight_ref, vec_ref, bias_ref, bias_other_ref, *rest):
        carry = rest[: len(carried)]
        rest = rest[len(carried) :]
        hid_ref, rest = (rest[0], rest[1:]) if last else (None, rest)
        msgs, rest = rest[:n], rest[n:]
        n_out = 1 + parts if last else 2
        outs, (w, grad_ref, x_ref, g_ref, pre_ref, act_ref, sems, *held) = rest[:n_out], rest[n_out:]
        loads = []
        used = 0
        for o in range(count):
            pairs = block_pairs(msgs, tables[o], w, ix, groups[o][0], o)
            loads.append(copies_of(pairs, sems, used))
            used += len(pairs)
        for load in loads:
            for copy in load:
                copy.start()
        grad_ref[...] = (cot[...].astype(F32) * weight_ref[:, :1]).astype(BF16)
        biases_of = (bias_ref, bias_other_ref)

        def multiply(o, c, slot):
            x_ref[slot] = jnp.dot(normed_ref[...], w[o, :, at_lanes(c, chunk)], preferred_element_type=F32)
            g_ref[slot] = jnp.dot(grad_ref[...], w[o, :, at_lanes(c + per, chunk)], preferred_element_type=F32)

        def bend(o, c, slot):
            at = at_lanes(o * per + c, chunk)
            half_bit, core_bit, _ = groups[o]
            x = x_ref[slot] + biases_of[core_bit][half_bit : half_bit + 1, at_lanes(c, chunk)]
            sq = x * x
            th = jnp.tanh(c0 * x * (1.0 + c1 * sq))
            left = 0.5 * (1.0 + th)
            slope = left + 0.5 * x * (1.0 - th * th) * (c0 + (3.0 * c0 * c1) * sq)
            pre_ref[:, at] = (slope * g_ref[slot]).astype(BF16)
            act_ref[:, at] = (x * left).astype(BF16)

        for o in range(count):
            for copy in loads[o]:
                copy.wait()
            multiply(o, 0, 0)
            if o:
                bend(o - 1, per - 1, (per - 1) % 2)

            def step(c, _, o=o):
                multiply(o, c, lax.rem(c, 2))
                bend(o, c - 1, lax.rem(c + 1, 2))
                return 0

            lax.fori_loop(1, per, step, 0)
        bend(count - 1, per - 1, (per - 1) % 2)

        def mid_of(n):
            at = at_rows(n, wide)
            lanes = at_lanes(n, wide)
            mid = jnp.zeros((rows, wide), F32)
            unit = jnp.zeros((rows, wide), F32)
            for o in range(count):
                cols = slice(o * part, (o + 1) * part)
                mid = mid + lax.dot_general(pre_ref[:, cols], w[o, at, :part], NT, preferred_element_type=F32)
                unit = unit + lax.dot_general(act_ref[:, cols], w[o, at, part:], NT, preferred_element_type=F32)
            if carry:
                mid = mid + carry[0][:, lanes].astype(F32)
                unit = unit + carry[1][:, lanes].astype(F32)
            return mid, unit, lanes

        if not last:

            def finish(n, _):
                mid, unit, lanes = mid_of(n)
                outs[0][:, lanes] = mid.astype(BF16)
                outs[1][:, lanes] = unit.astype(BF16)
                return 0

            lax.fori_loop(0, model // wide, finish, 0)
            return
        out_low, mid_ref = held

        def finish(n, _):
            mid, unit, lanes = mid_of(n)
            mid_ref[:, lanes] = mid * vec_ref[3:4, lanes]
            out_low[:, lanes] = (unit + hid_ref[:, lanes]).astype(BF16)
            return 0

        lax.fori_loop(0, model // wide, finish, 0)
        for k in range(parts):
            outs[1 + k][...] = out_low[:, at_lanes((2 * ix[1] + ix[2]) ^ k, piece)]
        step_rows = 128

        def end(r, _):
            at = at_rows(r, step_rows)
            hat, scaler = row_stats(hid_ref[at, :])
            grad = cot[at, :].astype(F32) * weight_ref[at, :1]
            grad = grad + norm_back(hat, scaler, mid_ref[at, :])
            outs[0][at, :] = grad.astype(BF16)
            return 0

        lax.fori_loop(0, rows // step_rows, end, 0)

    block = full(rows, model)
    specs = [
        block,
        block,
        full(rows, LANES),
        full(8, model),
        full(2, part),
        full(2, part),
    ]
    specs += [block] * (len(carried) + (1 if last else 0))
    if last:
        out_specs = [block] + [full(rows, piece)] * parts
        out_shape = [shape(rows, model)] + [shape(rows, piece)] * parts
    else:
        out_specs = [block, block]
        out_shape = [shape(rows, model)] * 2
    return call(
        body,
        "units_main_last" if last else "units_main_first" if not carried else "units_main_next",
        1,
        specs + [ANY] * len(arrays),
        out_specs,
        out_shape,
        [
            pltpu.VMEM((count, model, 2 * part), BF16),
            pltpu.VMEM((rows, model), BF16),
            pltpu.VMEM((2, rows, chunk), F32),
            pltpu.VMEM((2, rows, chunk), F32),
            pltpu.VMEM((rows, count * part), BF16),
            pltpu.VMEM((rows, count * part), BF16),
            pltpu.SemaphoreType.DMA((len(entries),)),
        ]
        + ([pltpu.VMEM((rows, model), BF16), pltpu.VMEM((rows, model), F32)] if last else []),
        cost(8 * count * rows * part * model, 8 * count * part * model, count * rows * part),
    )(idx, normed, cotangent, weights, vec, *biases, *carried, *((hidden,) if last else ()), *arrays)


def attend_back_fast(
    idx, queries, key_rows, value_rows, mixed, grad_own, grad_other, logsum, normed, latent, up, found, first
):
    length, width = queries.shape
    pairs = width // LANES
    half, model = grad_own.shape
    per = pairs // 2
    arrays, table = operands(found)
    n = len(arrays)

    def body(ix, q_ref, k_ref, v_ref, o_ref, own_ref, other_ref, lse_ref, normed_ref, latent_ref, uq_ref, uv_ref, *rest):
        msgs = rest[:n]
        dq_ref, dk_ref, dv_ref, low_ref, down_ref, rq_ref, rv_ref, low_acc, dq_acc, g2_ref, g_ref, qs_ref, p_ref, ds_ref, w, sems = rest[
            n:
        ]
        pair = pl.program_id(0)

        @pl.when(pair == 0)
        def _():
            load_all(column_pairs(msgs, table, w, ix, first, width // 2, False), sems)

        @pl.when(lax.rem(pair, 2) == 0)
        def _():
            weight = w[:, at_lanes(pair // 2, 2 * LANES)]
            for ref, rank in ((own_ref, ix[2]), (other_ref, 1 - ix[2])):
                g2_ref[at_rows(rank, half), :] = jnp.dot(ref[...], weight, preferred_element_type=F32).astype(BF16)

        g_ref[...] = g2_ref[:, at_lanes(lax.rem(pair, 2), LANES)]
        scale = HEAD_DIM**-0.5 * LOG2E
        low = lax.broadcasted_iota(jnp.int32, (1, LANES), 1) < HEAD_DIM
        qs_ref[...] = (q_ref[...].astype(F32) * scale).astype(BF16)
        prod = (g_ref[...].astype(F32) * o_ref[...].astype(F32)).T
        delta = [
            jnp.sum(prod[:HEAD_DIM], axis=0, keepdims=True),
            jnp.sum(prod[HEAD_DIM:], axis=0, keepdims=True),
        ]
        causal = lax.broadcasted_iota(jnp.int32, (BLK, BLK), 1) >= lax.broadcasted_iota(jnp.int32, (BLK, BLK), 0)

        def scores(j):
            start = j * BLK
            stacked = both_heads(low, k_ref[start : start + BLK, :])
            s = lax.dot_general(stacked, qs_ref[start:, :], NT, preferred_element_type=F32)
            values = both_heads(low, v_ref[start : start + BLK, :])
            dp = lax.dot_general(values, g_ref[start:, :], NT, preferred_element_type=F32)
            for h in range(2):
                rows = slice(h * BLK, (h + 1) * BLK)
                for a, b in ((start, start + BLK), (start + BLK, length)):
                    if a == b:
                        continue
                    sh = s[rows, a - start : b - start] - lse_ref[0, h : h + 1, a:b]
                    if a == start:
                        sh = jnp.where(causal, sh, MASKED)
                    p = jnp.exp2(sh)
                    p_ref[j % 2, rows, a:b] = p.astype(BF16)
                    ds = p * (dp[rows, a - start : b - start] - delta[h][:, a:b])
                    ds_ref[j % 2, rows, a:b] = ds.astype(BF16)
            return stacked

        def spread(j, stacked):
            start = j * BLK
            ds = ds_ref[j % 2, :, start:]
            dk = jnp.dot(ds, q_ref[start:, :], preferred_element_type=F32)
            dv = jnp.dot(p_ref[j % 2, :, start:], g_ref[start:, :], preferred_element_type=F32)
            dk = jnp.where(low, dk[:BLK], dk[BLK:]) * HEAD_DIM**-0.5
            dk_ref[start : start + BLK, :] = dk.astype(BF16)
            dv_ref[start : start + BLK, :] = jnp.where(low, dv[:BLK], dv[BLK:]).astype(BF16)
            dq = lax.dot_general(ds, stacked, TN, preferred_element_type=F32)
            if j == 0:
                dq_acc[...] = dq
            else:
                dq_acc[start:, :] += dq

        stacked = scores(0)
        for j in range(1, length // BLK):
            coming = scores(j)
            spread(j - 1, stacked)
            stacked = coming
        spread(length // BLK - 1, stacked)
        dq_ref[...] = (dq_acc[...] * HEAD_DIM**-0.5).astype(BF16)
        grads = jnp.concatenate([dq_ref[...], dv_ref[...]], axis=1)
        ups = jnp.concatenate([uq_ref[0], uv_ref[0]], axis=1)
        term = lax.dot_general(grads, ups, NT, preferred_element_type=F32)
        raised = jnp.dot(latent_ref[...], grads, preferred_element_type=F32)
        rq_ref[...] = raised[:8, :LANES]
        rv_ref[...] = raised[:8, LANES:]

        @pl.when(pair == 0)
        def _():
            low_acc[...] = term

        @pl.when(pair > 0)
        def _():
            low_acc[...] += term

        @pl.when(pair == pairs - 1)
        def _():
            low_ref[...] = low_acc[...].astype(BF16)
            low_rows = low_acc[...].T[: latent_ref.shape[0]].astype(BF16)
            down_ref[...] = jnp.dot(low_rows, normed_ref[...], preferred_element_type=F32)[:8]

    spec = pl.BlockSpec((length, LANES), lambda i, ix: (0, i))
    return call(
        body,
        "attend_back",
        pairs,
        [spec] * 4
        + [full(half, model)] * 2
        + [pl.BlockSpec((1, 8, length), lambda i, ix: (i, 0, 0)), full(length, model), full(*latent.shape)]
        + [
            pl.BlockSpec((1, LANES, LANES), lambda i, ix: (i // per, 0, lax.rem(i, per))),
            pl.BlockSpec((1, LANES, LANES), lambda i, ix: (i // per, 0, 2 * per + lax.rem(i, per))),
        ]
        + [ANY] * n,
        [spec] * 3
        + [full(length, LANES), full(8, model)]
        + [pl.BlockSpec((8, LANES), lambda i, ix: (0, i))] * 2,
        [shape(length, width)] * 3
        + [shape(length, LANES), shape(8, model, F32), shape(8, width, F32), shape(8, width, F32)],
        [
            pltpu.VMEM((length, LANES), F32),
            pltpu.VMEM((length, LANES), F32),
            pltpu.VMEM((length, 2 * LANES), BF16),
            pltpu.VMEM((length, LANES), BF16),
            pltpu.VMEM((length, LANES), BF16),
            pltpu.VMEM((2, 2 * BLK, length), BF16),
            pltpu.VMEM((2, 2 * BLK, length), BF16),
            pltpu.VMEM((model, width), BF16),
            pltpu.SemaphoreType.DMA((len(table),)),
        ],
        cost(20 * length * length * width, 16 * length * width, 2 * pairs * length * length),
    )(idx, queries, key_rows, value_rows, mixed, grad_own, grad_other, logsum, normed, latent, up, up, *arrays)


def heads_back(idx, dq, dk, dv, latent_low, down, found):
    width = dq.shape[1]
    part = width // 2
    model = down.shape[1]
    arrays, table = operands(found)
    cols = 3 * part
    n = len(arrays)
    half_blocks = LEN // BLK // 2

    def body(ix, dq_ref, dk_ref, dv_ref, low_ref, down_ref, *rest):
        msgs = rest[:n]
        send_ref, own_ref, w, sems = rest[n:]
        step = pl.program_id(0)

        @pl.when(step == 0)
        def _():
            load_all(column_pairs(msgs, table, w, ix, 0, cols, True), sems)

        total = jnp.dot(low_ref[...], down_ref[...], preferred_element_type=F32)
        for a in range(2):
            cut = slice(a * part, (a + 1) * part)
            piece = jnp.concatenate([dq_ref[:, cut], dk_ref[:, cut], dv_ref[:, cut]], axis=1)
            total = total + lax.dot_general(piece, w[a], NT, preferred_element_type=F32)

        @pl.when(step < half_blocks)
        def _():
            send_ref[...] = total.astype(BF16)

        @pl.when(step >= half_blocks)
        def _():
            own_ref[...] = total.astype(BF16)

    def rows(i, ix):
        rank = jnp.where(i < half_blocks, 1 - ix[2], ix[2])
        return (rank * half_blocks + lax.rem(i, half_blocks), 0)

    row = lambda c: pl.BlockSpec((BLK, c), rows)
    return call(
        body,
        "heads_back",
        2 * half_blocks,
        [row(width)] * 3 + [row(LANES), full(LANES, model)] + [ANY] * n,
        [
            pl.BlockSpec((BLK, model), lambda i, ix: (jnp.minimum(i, half_blocks - 1), 0)),
            pl.BlockSpec((BLK, model), lambda i, ix: (jnp.maximum(i - half_blocks, 0), 0)),
        ],
        [shape(LEN // 2, model)] * 2,
        [pltpu.VMEM((2, model, cols), BF16), pltpu.SemaphoreType.DMA((len(table),))],
        cost(4 * LEN * model * cols, 4 * model * cols),
    )(idx, dq, dk, dv, latent_low, down, *arrays)


def tokens_back(idx, in_own, in_recv, tokens, hidden_grad, vec):
    model = tokens.shape[1]
    half_blocks = LEN // BLK // 2
    parts = 4
    part = model // parts

    def body(ix, own, recv, tok, hg, vec_ref, *rest):
        outs, held = rest[:parts], rest[parts]
        e = vec_ref[0:1, :] * (own[...].astype(F32) + recv[...].astype(F32))
        hat, scaler = row_stats(tok[...].astype(F32))
        held[...] = (hg[...].astype(F32) + norm_back(hat, scaler, e)).astype(BF16)
        for k, out in enumerate(outs):
            out[...] = held[:, at_lanes((2 * ix[1] + ix[2]) ^ k, part)]

    row = pl.BlockSpec((BLK, model), lambda i, ix: (i, 0))
    return call(
        body,
        "tokens_back",
        half_blocks,
        [row, row, row, row, full(8, model)],
        [pl.BlockSpec((BLK, part), lambda i, ix: (i, 0))] * parts,
        [shape(LEN // 2, part)] * parts,
        [pltpu.VMEM((BLK, model), BF16)],
        cost(20 * LEN * model, 8 * LEN * model),
        56 << 20,
    )(idx, in_own, in_recv, tokens, hidden_grad, vec)


def exchange_features(pieces):
    return [pieces[0], core_swap(pieces[1]), hop(pieces[2], 1, 0), both_swap(pieces[3])]


def to_features(idx, pieces, bias):
    rows, part = pieces[0].shape
    parts = len(pieces)

    def body(ix, bias_ref, *rest):
        outs = rest[parts]
        for k in range(parts):
            value = rest[k][...]
            if bias is not None:
                value = (value.astype(F32) + bias_ref[...]).astype(BF16)
            outs[at_rows((2 * ix[1] + ix[2]) ^ k, rows), :] = value

    extra = jnp.zeros((1, part), F32) if bias is None else bias
    return call(
        body,
        "to_features",
        1,
        [full(1, part)] + [full(rows, part)] * parts,
        full(parts * rows, part),
        shape(parts * rows, part),
        [],
        cost(parts * rows * part, 4 * parts * rows * part),
    )(idx, extra, *pieces)


def both_swap(value):
    total = lax.axis_size("dp") * lax.axis_size("mp")
    return lax.ppermute(value, AXES, [(i, i ^ 3) for i in range(total)])


def on_device_fast(
    tokens,
    cotangent,
    group_ids,
    pre_gain,
    pre_shift,
    frozen_triple_weight,
    frozen_triple_bias,
    out_weight,
    out_bias,
    mid_gain,
    mid_shift,
    fc_weight,
    fc_bias,
    proj_weight,
    proj_bias,
    down_master,
    up_master,
    down_first,
    down_second,
    up_first,
    up_second,
    learn_rate,
):
    tok_dev, model = tokens.shape
    ranks = lax.axis_size("mp") // 2
    place = lax.axis_index("mp")
    idx = jnp.stack([lax.axis_index("dp"), place // ranks, place % ranks]).astype(jnp.int32)
    r = ADAPTER_RANK
    step_rows, _, head_part = frozen_triple_weight.shape
    heads_cols = 3 * head_part
    ids = group_ids.reshape(-1, LANES)
    fc_line = fc_bias.reshape(1, -1)
    up_rows = up_master.reshape(2 * r, head_part)
    heads_own, u_own = prepare_blocks(
        idx, ids, frozen_triple_weight, out_weight, frozen_triple_bias, fc_line, up_master, fc_weight, proj_weight
    )
    zero_line = jnp.zeros_like(pre_gain)
    vec = jnp.stack([pre_gain, pre_shift, out_bias, mid_gain, mid_shift, zero_line, zero_line, zero_line]).astype(F32)
    own_start = (idx[1] * ranks + idx[2]) * (LEN // 2)
    own_rows = lambda v: lax.dynamic_slice_in_dim(v, own_start, LEN // 2, 0)
    tok_own, cot_own = own_rows(tokens), own_rows(cotangent)
    h_z1, h_z2, h_z3 = gather_z(heads_own, (), ())
    h_near, h_far = jnp.stack([heads_own, h_z1]), jnp.stack([h_z2, h_z3])
    ux0, uy0 = pair_xy(u_own)
    hx_near, hy_near = pair_xy(after(h_near, ux0, uy0))
    hx_far, hy_far = pair_xy(after(h_far, hx_near, hy_near))
    hd_near, hd_far = hop(after(hx_near, hy_far), 0, 1), hop(hy_far, 1, 0)
    ud0 = hop(after(ux0, hd_near), 0, 1)
    heads = []
    for first, arrays in ((0, (h_near, hx_near, hy_near, hd_near)), (2, (h_far, hx_far, hy_far, hd_far))):
        for n, array in enumerate(arrays):
            heads += blocks_of(array, first, n % 2, n // 2)
    u_rest = jnp.concatenate(gather_z(u_own, (h_far,), (hx_far, hy_far)))
    weights, fc_mine = weigh(
        idx, ids, fc_line, h_near, h_far, hy_near, hy_far, hx_near, float(tok_dev * lax.axis_size("dp"))
    )
    fc_other = core_swap(fc_mine)
    down8 = down_master.reshape(2 * r, model)
    normed, latent, latent_t, down = norm_rows(idx, after(tokens, hx_far, tok_own, cot_own), vec, down8)
    ux, uy = pair_xy(after(u_rest, hd_far))
    ready = after(normed, u_rest, ud0, weights)
    queries, keys, values, up = project_heads(idx, ready, latent, frozen_triple_bias, up_rows, hx_near, heads)
    mixed, logsum = attend_fast(queries, keys, values)
    sent = [core_swap(v) for v in attention_out_send(idx, mixed, heads, heads_cols)]
    sent, fc_other = lax.optimization_barrier((sent, fc_other))
    hidden, normed_mid = attention_out_own(idx, mixed, sent, tok_own, vec, heads, heads_cols)
    rows = (normed_mid, cot_own, weights, vec, (fc_mine, fc_other))
    ux, uy, _ = lax.optimization_barrier((ux, uy, normed_mid))
    cut = step_rows // 2
    ud_low, ud_high = hop(ux[:, :cut], 0, 1), hop(uy[:, cut:], 1, 0)

    def table(half_bit, bit, *arrays):
        found, start = [], 0
        for array in arrays:
            found += blocks_of(array, start, half_bit, bit)
            start += array.shape[0]
        return found

    swap = lambda *arrays: [core_swap(v) for v in arrays]
    corner = lambda v, low, high: table(1, 1, v) + blocks_of(low, 1, 1, 1) + blocks_of(high, 1, 1, 1, cut)
    first_mine = table(0, 0, u_own, u_rest) + table(0, 1, uy0, uy)
    first_other = table(0, 0, *swap(u_own, u_rest)) + table(0, 1, *swap(uy0, uy))
    carried = units_main(idx, *rows, [(0, 0, first_mine), (0, 1, first_other)], (), None)
    ud_low, ud_high, ux0_late, ux_late, ud0_late, _ = lax.optimization_barrier(
        (ud_low, ud_high, ux0, ux, ud0, carried[0])
    )
    last_mine = table(1, 0, ux0, ux) + corner(ud0, ud_low, ud_high)
    last_other = table(1, 0, *swap(ux0_late, ux_late)) + corner(*swap(ud0_late, ud_low, ud_high))
    carried = units_main(idx, *rows, [(1, 0, last_mine)], carried, None)
    groups = [(1, 1, last_other)]
    hidden_low, *out_pieces = units_main(idx, *rows, groups, carried, hidden)
    hidden_other = core_swap(hidden_low)
    out_pieces = exchange_features(out_pieces)
    dq, dk, dv, latent_low, down_term, up_q, up_v = attend_back_fast(
        idx, queries, keys, values, mixed, hidden_low, hidden_other, logsum, normed, latent_t, up, heads, heads_cols
    )
    up_term = jnp.stack([up_q[:r], up_v[r:]]).reshape(2 * r, 2, head_part)
    down_sum = down_term + core_swap(down_term)
    dq, out_pieces = lax.optimization_barrier((dq, out_pieces))
    in_send, in_own = heads_back(idx, dq, dk, dv, latent_low, down, heads)
    in_recv = core_swap(in_send)
    got = hop(after(jnp.concatenate([down_sum, up_term[:, 1]], axis=1), in_send), 1, 0)
    terms = jnp.concatenate([down_sum, up_term[:, 0]], axis=1) + got
    in_pieces = tokens_back(idx, in_own, in_recv, tok_own, hidden_low, vec)
    in_pieces = exchange_features(in_pieces)
    terms = after(terms, in_pieces[1])
    for bit in (1, 2, 4):
        terms = terms + hop(terms, 0, bit)
    out_pieces = lax.optimization_barrier((out_pieces, in_pieces[1]))[0]
    output = to_features(idx, out_pieces, proj_bias.astype(F32).reshape(1, -1))
    input_grad = to_features(idx, in_pieces, None)
    down_grad = terms[:, :model].reshape(down_master.shape)
    up_grad = ADAPTER_SCALE * terms[:, model:].reshape(up_master.shape)
    step_value = jnp.float32(STEP)
    down_new, down_moment, down_square = adam_update(
        down_master, down_first, down_second, down_grad, step_value, learn_rate
    )
    up_new, up_moment, up_square = adam_update(up_master, up_first, up_second, up_grad, step_value, learn_rate)
    return (
        output,
        input_grad,
        down_new,
        down_moment,
        down_square,
        down_new.astype(BF16),
        up_new,
        up_moment,
        up_square,
        up_new.astype(BF16),
    )


def pick_body(mesh):
    return on_device_fast if mesh.shape["dp"] == 8 and mesh.shape["mp"] == 4 else on_device_general


def solution(mesh):
    body = pick_body(mesh)
    return jax.shard_map(
        body,
        mesh=mesh,
        in_specs=(
            P("dp", None),
            P("dp", None),
            P("dp"),
            P(),
            P(),
            P("dp", None, "mp"),
            P(None, "mp"),
            P("mp", "dp"),
            P(),
            P(),
            P(),
            P("dp", "mp"),
            P("mp"),
            P("mp", "dp"),
            P("mp"),
            P(),
            P(None, None, "mp"),
            P(),
            P(),
            P(None, None, "mp"),
            P(None, None, "mp"),
            P(),
        ),
        out_specs=(
            P("dp", "mp"),
            P("dp", "mp"),
            P(),
            P(),
            P(),
            P(),
            P(None, None, "mp"),
            P(None, None, "mp"),
            P(None, None, "mp"),
            P(None, None, "mp"),
        ),
        check_vma=False,
    )
```

```python
import jax
import jax.numpy as jnp
from jax import lax
from jax.experimental import pallas as pl
from jax.experimental.pallas import tpu as pltpu
from jax.sharding import PartitionSpec as P

HEAD_DIM = 64
ADAPTER_RANK = 4
GROUPS = 16
STEP = 3
MICRO = 2


ADAPTER_SCALE = 8.0
NORM_EPS = 1e-05
MASKED = -1e30
BETA_ONE = 0.5
BETA_TWO = 0.5
ADAM_EPS = 1e-08
DECAY = 0.01


def layer_stats(values):
    center = values - jnp.mean(values, axis=-1, keepdims=True)
    spread = jnp.mean(center * center, axis=-1, keepdims=True)
    scaler = lax.rsqrt(spread + NORM_EPS)
    return (center * scaler, scaler)


def norm_back(normal_hat, scaler, scaled_grad):
    first_mean = jnp.mean(scaled_grad, axis=-1, keepdims=True)
    second_mean = jnp.mean(scaled_grad * normal_hat, axis=-1, keepdims=True)
    return scaler * (scaled_grad - first_mean - normal_hat * second_mean)


def gelu_tanh(values):
    return jax.nn.gelu(values, approximate=True)


def fetch_frozen(frozen_triple_weight, fc_weight, out_weight, proj_weight):
    return (
        lax.all_gather(frozen_triple_weight, "dp", axis=0, tiled=True),
        lax.all_gather(fc_weight, "dp", axis=0, tiled=True),
        lax.all_gather(out_weight, "dp", axis=1, tiled=True),
        lax.all_gather(proj_weight, "dp", axis=1, tiled=True),
    )


def score_block(query_part, key_heads, start, block_rows, key_count):
    score_scale = HEAD_DIM ** (-0.5)
    scores = (
        jnp.einsum("qhd,khd->hqk", query_part, key_heads, preferred_element_type=jnp.float32)
        * score_scale
    )
    allowed = (start + jnp.arange(block_rows, dtype=jnp.int32))[:, None] >= jnp.arange(
        key_count, dtype=jnp.int32
    )[None, :]
    return jnp.where(allowed[None], scores, MASKED)


def attend(queries, key_rows, value_rows):
    length, col_width = queries.shape
    head_count = col_width // HEAD_DIM
    block_rows = min(512, length)
    query_heads = queries.reshape(length, head_count, HEAD_DIM)
    key_heads = key_rows.reshape(length, head_count, HEAD_DIM)
    value_heads = value_rows.reshape(length, head_count, HEAD_DIM)
    mixed_parts = []
    logsum_parts = []
    for index in range(length // block_rows):
        start = index * block_rows
        stop = start + block_rows
        query_part = query_heads[start:stop]
        scores = score_block(query_part, key_heads[:stop], start, block_rows, stop)
        row_top = jnp.max(scores, axis=-1, keepdims=True)
        exp_terms = jnp.exp(scores - row_top)
        row_total = jnp.sum(exp_terms, axis=-1, keepdims=True)
        probs = (exp_terms / row_total).astype(jnp.bfloat16)
        mixed = jnp.einsum(
            "hqk,khd->qhd", probs, value_heads[:stop], preferred_element_type=jnp.float32
        )
        mixed_parts.append(mixed.reshape(block_rows, col_width))
        logsum_parts.append((row_top + jnp.log(row_total))[..., 0])
    return (jnp.concatenate(mixed_parts, axis=0), logsum_parts)


def attend_back(queries, key_rows, value_rows, logsum, mixed_grad):
    length, col_width = queries.shape
    head_count = col_width // HEAD_DIM
    block_rows = min(512, length)
    score_scale = HEAD_DIM ** (-0.5)
    query_heads = queries.reshape(length, head_count, HEAD_DIM)
    key_heads = key_rows.reshape(length, head_count, HEAD_DIM)
    value_heads = value_rows.reshape(length, head_count, HEAD_DIM)
    grad_heads = mixed_grad.reshape(length, head_count, HEAD_DIM)
    key_acc = jnp.zeros((length, head_count, HEAD_DIM), jnp.float32)
    value_acc = jnp.zeros((length, head_count, HEAD_DIM), jnp.float32)
    query_parts = []
    for index in range(length // block_rows):
        start = index * block_rows
        stop = start + block_rows
        query_part = query_heads[start:stop]
        grad_part = grad_heads[start:stop]
        key_part = key_heads[:stop]
        scores = score_block(query_part, key_part, start, block_rows, stop)
        probs = jnp.exp(scores - logsum[index][:, :, None])
        prob_grad = jnp.einsum(
            "qhd,khd->hqk", grad_part, value_heads[:stop], preferred_element_type=jnp.float32
        )
        inner = jnp.sum(prob_grad * probs, axis=-1, keepdims=True)
        score_grad = (probs * (prob_grad - inner)).astype(jnp.bfloat16)
        query_grad = (
            jnp.einsum("hqk,khd->qhd", score_grad, key_part, preferred_element_type=jnp.float32)
            * score_scale
        )
        key_acc = key_acc.at[:stop].add(
            jnp.einsum("hqk,qhd->khd", score_grad, query_part, preferred_element_type=jnp.float32)
            * score_scale
        )
        value_acc = value_acc.at[:stop].add(
            jnp.einsum(
                "hqk,qhd->khd",
                probs.astype(jnp.bfloat16),
                grad_part,
                preferred_element_type=jnp.float32,
            )
        )
        query_parts.append(query_grad.reshape(block_rows, col_width))
    return (
        jnp.concatenate(query_parts, axis=0),
        key_acc.reshape(length, col_width),
        value_acc.reshape(length, col_width),
    )


def adam_update(master, first, second, grad, step_value, learn_rate):
    new_first = BETA_ONE * first + (1.0 - BETA_ONE) * grad
    new_second = BETA_TWO * second + (1.0 - BETA_TWO) * grad * grad
    fix_one = 1.0 - jnp.power(jnp.float32(BETA_ONE), step_value)
    fix_two = 1.0 - jnp.power(jnp.float32(BETA_TWO), step_value)
    update = new_first / fix_one / (jnp.sqrt(new_second / fix_two) + ADAM_EPS)
    new_master = master - learn_rate * (update + DECAY * master)
    return (new_master, new_first, new_second)


def on_device_general(
    tokens,
    cotangent,
    group_ids,
    pre_gain,
    pre_shift,
    frozen_triple_weight,
    frozen_triple_bias,
    out_weight,
    out_bias,
    mid_gain,
    mid_shift,
    fc_weight,
    fc_bias,
    proj_weight,
    proj_bias,
    down_master,
    up_master,
    down_first,
    down_second,
    up_first,
    up_second,
    learn_rate,
):
    tok_dev = tokens.shape[0]
    model_width = tokens.shape[1]
    length = tok_dev // MICRO
    shard_width = model_width // lax.axis_size("mp")
    shard_start = lax.axis_index("mp") * shard_width
    pre_gain_f = pre_gain.astype(jnp.float32)
    pre_shift_f = pre_shift.astype(jnp.float32)
    mid_gain_f = mid_gain.astype(jnp.float32)
    mid_shift_f = mid_shift.astype(jnp.float32)
    out_bias_f = out_bias.astype(jnp.float32)
    fc_bias_f = fc_bias.astype(jnp.float32)
    proj_bias_f = proj_bias.astype(jnp.float32)
    bias_flat = frozen_triple_bias.astype(jnp.float32).reshape(-1)
    onehot = group_ids[:, None] == jnp.arange(GROUPS, dtype=jnp.int32)[None, :]
    local_counts = jnp.sum(onehot.astype(jnp.int32), axis=0)
    totals = lax.psum(local_counts, "dp").astype(jnp.float32)
    own_count = jnp.sum(jnp.where(onehot, totals[None, :], jnp.float32(0.0)), axis=1)
    token_weight = jnp.float32(tok_dev * lax.axis_size("dp")) / (GROUPS * own_count)
    down_low = down_master.astype(jnp.bfloat16).reshape(2 * ADAPTER_RANK, model_width)
    raise_reduced = up_master.astype(jnp.bfloat16)
    grad_down = jnp.zeros((2 * ADAPTER_RANK, model_width), jnp.float32)
    raise_gradient = jnp.zeros(up_master.shape, jnp.float32)
    output_parts = []
    input_parts = []
    for micro_index in range(MICRO):
        current = fetch_frozen(frozen_triple_weight, fc_weight, out_weight, proj_weight)
        qkv_full, fc_full, out_full, proj_full = current
        qkv_flat = qkv_full.reshape(model_width, -1)
        head_width = qkv_flat.shape[1] // 3
        row_start = micro_index * length
        rows_f = lax.dynamic_slice_in_dim(tokens, row_start, length, 0).astype(jnp.float32)
        pre_hat, pre_scale = layer_stats(rows_f)
        normed = (pre_hat * pre_gain_f + pre_shift_f).astype(jnp.bfloat16)
        mixed_proj = jnp.dot(normed, qkv_flat, preferred_element_type=jnp.float32) + bias_flat
        bottleneck = jnp.einsum(
            "td,rd->tr", normed, down_low, preferred_element_type=jnp.float32
        ).astype(jnp.bfloat16)
        queries = (
            mixed_proj[:, :head_width]
            + ADAPTER_SCALE
            * jnp.dot(
                bottleneck[:, :ADAPTER_RANK], raise_reduced[0], preferred_element_type=jnp.float32
            )
        ).astype(jnp.bfloat16)
        key_rows = mixed_proj[:, head_width : 2 * head_width].astype(jnp.bfloat16)
        value_rows = (
            mixed_proj[:, 2 * head_width :]
            + ADAPTER_SCALE
            * jnp.dot(
                bottleneck[:, ADAPTER_RANK:], raise_reduced[1], preferred_element_type=jnp.float32
            )
        ).astype(jnp.bfloat16)
        attended, logsum = attend(queries, key_rows, value_rows)
        attended_low = attended.astype(jnp.bfloat16)
        head_term = jnp.dot(attended_low, out_full, preferred_element_type=jnp.float32).astype(
            jnp.bfloat16
        )
        attn_sum = lax.psum(head_term, "mp").astype(jnp.float32)
        hidden = rows_f + attn_sum + out_bias_f
        mid_hat, mid_scale = layer_stats(hidden)
        normed_mid = (mid_hat * mid_gain_f + mid_shift_f).astype(jnp.bfloat16)
        pre_act = jnp.dot(normed_mid, fc_full, preferred_element_type=jnp.float32) + fc_bias_f
        active, gelu_pullback = jax.vjp(gelu_tanh, pre_act)
        unit_part = jnp.dot(
            active.astype(jnp.bfloat16), proj_full, preferred_element_type=jnp.float32
        ).astype(jnp.bfloat16)
        unit_share = lax.psum_scatter(unit_part, "mp", scatter_dimension=1, tiled=True).astype(
            jnp.float32
        )
        hidden_share = lax.dynamic_slice_in_dim(hidden, shard_start, shard_width, 1)
        output_parts.append((hidden_share + unit_share + proj_bias_f).astype(jnp.bfloat16))
        weight_rows = lax.dynamic_slice_in_dim(token_weight, row_start, length, 0)
        out_grad = (
            lax.dynamic_slice_in_dim(cotangent, row_start, length, 0).astype(jnp.float32)
            * weight_rows[:, None]
        )
        out_low = out_grad.astype(jnp.bfloat16)
        active_grad = jnp.einsum(
            "td,fd->tf", out_low, proj_full, preferred_element_type=jnp.float32
        )
        pre_grad = gelu_pullback(active_grad)[0].astype(jnp.bfloat16)
        mid_part = jnp.einsum(
            "tf,df->td", pre_grad, fc_full, preferred_element_type=jnp.float32
        ).astype(jnp.bfloat16)
        mid_grad = lax.psum(mid_part, "mp").astype(jnp.float32)
        hidden_grad = out_grad + norm_back(mid_hat, mid_scale, mid_gain_f * mid_grad)
        hidden_low = hidden_grad.astype(jnp.bfloat16)
        attended_grad = jnp.einsum(
            "td,hd->th", hidden_low, out_full, preferred_element_type=jnp.float32
        ).astype(jnp.bfloat16)
        query_grad, key_grad, value_grad = attend_back(
            queries, key_rows, value_rows, logsum, attended_grad
        )
        query_low = query_grad.astype(jnp.bfloat16)
        key_low = key_grad.astype(jnp.bfloat16)
        value_low = value_grad.astype(jnp.bfloat16)
        proj_grad = jnp.concatenate([query_low, key_low, value_low], axis=1)
        in_part = jnp.einsum("tc,dc->td", proj_grad, qkv_flat, preferred_element_type=jnp.float32)
        bottleneck_gradient = ADAPTER_SCALE * jnp.concatenate(
            [
                jnp.einsum(
                    "tc,rc->tr", query_low, raise_reduced[0], preferred_element_type=jnp.float32
                ),
                jnp.einsum(
                    "tc,rc->tr", value_low, raise_reduced[1], preferred_element_type=jnp.float32
                ),
            ],
            axis=1,
        )
        latent_low = bottleneck_gradient.astype(jnp.bfloat16)
        in_part = (
            in_part + jnp.dot(latent_low, down_low, preferred_element_type=jnp.float32)
        ).astype(jnp.bfloat16)
        grad_down = grad_down + jnp.einsum(
            "tr,td->rd", latent_low, normed, preferred_element_type=jnp.float32
        )
        raise_gradient = raise_gradient + ADAPTER_SCALE * jnp.stack(
            [
                jnp.einsum(
                    "tr,tc->rc",
                    bottleneck[:, :ADAPTER_RANK],
                    query_low,
                    preferred_element_type=jnp.float32,
                ),
                jnp.einsum(
                    "tr,tc->rc",
                    bottleneck[:, ADAPTER_RANK:],
                    value_low,
                    preferred_element_type=jnp.float32,
                ),
            ],
            axis=0,
        )
        hidden_grad_share = lax.dynamic_slice_in_dim(hidden_grad, shard_start, shard_width, 1)
        in_grad = lax.psum(in_part, "mp").astype(jnp.float32)
        full_grad = norm_back(pre_hat, pre_scale, pre_gain_f * in_grad)
        input_parts.append(
            (
                hidden_grad_share + lax.dynamic_slice_in_dim(full_grad, shard_start, shard_width, 1)
            ).astype(jnp.bfloat16)
        )
    output = jnp.concatenate(output_parts, axis=0)
    input_grad = jnp.concatenate(input_parts, axis=0)
    down_grad = lax.psum(grad_down, ("dp", "mp")).reshape(down_master.shape)
    up_grad = lax.psum(raise_gradient, "dp")
    step_value = jnp.float32(STEP)
    down_new, down_moment, down_square = adam_update(
        down_master, down_first, down_second, down_grad, step_value, learn_rate
    )
    up_new, up_moment, up_square = adam_update(
        up_master, up_first, up_second, up_grad, step_value, learn_rate
    )
    return (
        output,
        input_grad,
        down_new,
        down_moment,
        down_square,
        down_new.astype(jnp.bfloat16),
        up_new,
        up_moment,
        up_square,
        up_new.astype(jnp.bfloat16),
    )


LEN = 1024
BLK = 256
LANES = 128
LOG2E = 1.4426950408889634
NT = (((1,), (1,)), ((), ()))
TN = (((0,), (0,)), ((), ()))
VMEM_LIMIT = 24 << 20
F32 = jnp.float32
BF16 = jnp.bfloat16
AXES = ("dp", "mp")
ANY = pl.BlockSpec(memory_space=pl.ANY)


def cost(flops, nbytes, trans=0):
    return pl.CostEstimate(flops=int(flops) // 10, bytes_accessed=int(nbytes) // 10, transcendentals=int(trans) // 10)


def shape(rows, cols, dtype=BF16):
    return jax.ShapeDtypeStruct((rows, cols), dtype)


def full(rows, cols):
    return pl.BlockSpec((rows, cols), lambda i, ix: (0, 0))


def call(body, name, grid, in_specs, out_specs, out_shape, scratch, est, grant=None):
    return pl.pallas_call(
        body,
        grid_spec=pltpu.PrefetchScalarGridSpec(
            num_scalar_prefetch=1,
            grid=(grid,),
            in_specs=in_specs,
            out_specs=out_specs,
            scratch_shapes=scratch,
        ),
        out_shape=out_shape,
        compiler_params=pltpu.CompilerParams(vmem_limit_bytes=grant or VMEM_LIMIT),
        cost_estimate=est,
        name=name,
    )


def hop(value, half_bit, dp_bits):
    ranks = lax.axis_size("mp") // 2
    width = lax.axis_size("mp")
    total = lax.axis_size("dp") * width
    flip = dp_bits * width + half_bit * ranks
    return lax.ppermute(value, AXES, [(i, i ^ flip) for i in range(total)])


def core_swap(value):
    total = lax.axis_size("dp") * lax.axis_size("mp")
    return lax.ppermute(value, AXES, [(i, i ^ 1) for i in range(total)])


def after(value, *others):
    return lax.optimization_barrier((value, *others))[0]


def inner_z():
    z = lax.axis_index("dp") // 2
    return jnp.logical_or(z == 1, z == 2)


def z_hop(value, pairs):
    width = lax.axis_size("mp")
    perm = []
    for source, target in pairs:
        for rest in range(2 * width):
            perm.append((source * 2 * width + rest, target * 2 * width + rest))
    return lax.ppermute(value, AXES, perm)


DIGIT = 64
CUTS = 1
EXTRA = 8
MIDDLE = ((1, 2), (2, 1))
OUTWARD = ((1, 0), (2, 3))


def gather_z(own, first, second):
    begin = after(own, *first)
    z1 = hop(begin, 0, 2)
    m1 = z_hop(begin, MIDDLE)
    m2 = z_hop(z1, MIDDLE)
    f1 = z_hop(m1, OUTWARD)
    f2 = z_hop(after(m2, *second), OUTWARD)
    inner = inner_z()
    return z1, jnp.where(inner, m2, f1), jnp.where(inner, m1, f2)


def pair_xy(value):
    return hop(value, 1, 0), hop(value, 0, 1)


def blocks_of(array, first, half_bit, bit, row=0):
    return [(array, slot, half_bit, 2 * (first + slot) + bit, row) for slot in range(array.shape[0])]


def swapped_blocks(found):
    arrays, table = operands(found)
    arrays = [core_swap(array) for array in arrays]
    return [(arrays[e[0]], *e[1:]) for e in table]


def operands(found):
    arrays = []
    table = []
    for array, *entry in found:
        for k, held in enumerate(arrays):
            if held is array:
                break
        else:
            k = len(arrays)
            arrays.append(array)
        table.append((k, *entry))
    return arrays, table


def copies_of(pairs, sems, start=0):
    return [pltpu.make_async_copy(src, dst, sems.at[start + n]) for n, (src, dst) in enumerate(pairs)]


def load_all(pairs, sems):
    copies = copies_of(pairs, sems)
    for copy in copies:
        copy.start()
    for copy in copies:
        copy.wait()


def at_rows(index, size):
    return pl.ds(pl.multiple_of(index * size, size), size)


def at_lanes(index, size):
    return pl.ds(pl.multiple_of(index * size, LANES), size)


def column_pairs(refs, table, w, ix, first, count, spread):
    pairs = []
    for k, slot, half_bit, dp_bits, _ in table:
        src = refs[k].at[slot, pl.ds(0, LANES), pl.ds(first, count)]
        rows = at_rows(ix[0] ^ dp_bits, LANES)
        dst = w.at[half_bit, rows, :] if spread else w.at[rows, pl.ds(half_bit * count, count)]
        pairs.append((src, dst))
    return pairs


def block_pairs(refs, table, w, ix, half_bit, slot_out):
    pairs = []
    for k, slot, a, dp_bits, row in table:
        if a == half_bit:
            rows = pl.ds(pl.multiple_of((ix[0] ^ dp_bits) * LANES + row, LANES // 2), refs[k].shape[1])
            pairs.append((refs[k].at[slot], w.at[slot_out, rows, :]))
    return pairs


def both_heads(low, value):
    zero = jnp.zeros((), value.dtype)
    return jnp.concatenate([jnp.where(low, value, zero), jnp.where(low, zero, value)], axis=0)


def row_stats(values):
    center = values - jnp.mean(values, axis=-1, keepdims=True)
    scaler = lax.rsqrt(jnp.mean(center * center, axis=-1, keepdims=True) + NORM_EPS)
    return center * scaler, scaler


def lines_of(block):
    part = block.shape[1] // 4
    return lambda n: block[n // 4 : n // 4 + 1, n % 4 * part : (n % 4 + 1) * part]


def prepare_blocks(idx, ids, triple, out_weight, bias, fc_bias, up, fc_weight, proj_weight):
    rows, _, part = triple.shape
    model = 4 * part

    def body(ix, ids_ref, triple_ref, out_ref, bias_ref, fc_ref, up_ref, fcw_ref, proj_ref, block_ref, units_ref, spare):
        units_ref[0, :, :model] = fcw_ref[...]
        units_ref[0, :, model:] = proj_ref[...].astype(F32).T.astype(BF16)
        for s in range(3):
            block_ref[:rows, s * part : (s + 1) * part] = triple_ref[:, s, :]
        block_ref[:rows, 3 * part :] = out_ref[...].astype(F32).T.astype(BF16)
        lane = lax.broadcasted_iota(jnp.int32, (1, LANES), 1)
        counts = jnp.zeros((1, LANES), F32)
        ids = ids_ref[...]
        for g in range(GROUPS):
            hits = jnp.where(ids == g, 1.0, 0.0)
            total = jnp.sum(jnp.sum(hits, axis=0, keepdims=True), axis=1, keepdims=True)
            counts = jnp.where(lane == g, total, counts)
        high = jnp.floor(counts * (1.0 / DIGIT))
        spare[...] = jnp.zeros_like(spare)
        line = lines_of(spare)
        spare[0:1, :LANES] = high
        spare[0:1, LANES : 2 * LANES] = counts - DIGIT * high

        def put(n, value):
            spare[n // 4 : n // 4 + 1, n % 4 * part : (n % 4 + 1) * part] = value.astype(F32)

        for s in range(3):
            put(1 + s, bias_ref[s : s + 1, :])
        for s in range(4):
            put(4 + s, fc_ref[pl.ds(s * part, part)].reshape(1, part))
        for s in range(8):
            put(8 + s, up_ref[s // ADAPTER_RANK, s % ADAPTER_RANK : s % ADAPTER_RANK + 1, :])
        block_ref[rows:, :] = spare[...].astype(BF16)

    arrays = (ids, triple, out_weight, bias, fc_bias, up, fc_weight, proj_weight)
    whole = lambda v: pl.BlockSpec(v.shape, lambda i, ix: (0,) * v.ndim)
    units = 2 * fc_weight.shape[1]
    return call(
        body,
        "prepare_blocks",
        1,
        [whole(v) for v in arrays],
        [full(rows + EXTRA, model), pl.BlockSpec((1, rows, units), lambda i, ix: (0, 0, 0))],
        [shape(rows + EXTRA, model), jax.ShapeDtypeStruct((1, rows, units), BF16)],
        [pltpu.VMEM((EXTRA, model), F32)],
        cost(0, 4 * rows * model),
        60 << 20,
    )(idx, *arrays)


def weigh(idx, ids, fc_bias, near, far, y_near, y_far, x_near, tokens_all):
    units = fc_bias.shape[1]
    per_row = LANES
    own = LEN // 2 // per_row
    rows = near.shape[1] - EXTRA
    width = near.shape[2]

    def body(ix, ids_ref, fc_ref, *rest):
        msgs, (weight_ref, fc_out, held, sems) = rest[:5], rest[5:]
        load_all(
            [
                (msgs[n // 2].at[n % 2, pl.ds(rows, EXTRA), :], held.at[n])
                for n in range(8)
            ]
            + [(msgs[4].at[0, pl.ds(rows, EXTRA), :], held.at[8])],
            sems,
        )
        digits = jnp.zeros((EXTRA, 2 * LANES), F32)
        for n in range(8):
            digits = digits + held[n, :, : 2 * LANES].astype(F32)
        table = tokens_all / (GROUPS * (DIGIT * digits[0:1, :LANES] + digits[0:1, LANES:]))
        for k in range(own):
            ids_row = ids_ref[pl.ds((2 * ix[1] + ix[2]) * own + k, 1), :]
            row = jnp.zeros((1, LANES), F32)
            for g in range(GROUPS):
                row = jnp.where(ids_row == g, table[:, g : g + 1], row)
            weight_ref[k * per_row : (k + 1) * per_row, :] = jnp.broadcast_to(row, (per_row, LANES)).T
        line = lines_of(held[8].astype(F32))
        fc_out[0:1, :] = fc_ref[...].astype(F32)
        fc_out[1:2, :] = jnp.concatenate([line(4 + s) for s in range(4)], axis=1)

    return call(
        body,
        "weigh",
        1,
        [full(*ids.shape), full(1, units)] + [ANY] * 5,
        [full(LEN // 2, LANES), full(2, units)],
        [shape(LEN // 2, LANES, F32), shape(2, units, F32)],
        [pltpu.VMEM((9, EXTRA, width), BF16), pltpu.SemaphoreType.DMA((9,))],
        cost(0, LEN * LANES),
    )(idx, ids, fc_bias, near, far, y_near, y_far, x_near)


def norm_rows(idx, tokens, vec, down):
    model = tokens.shape[1]
    blocks = LEN // BLK

    def body(ix, tok, vec_ref, down_ref, normed_ref, latent_ref, latent_t_ref, pad_ref):
        @pl.when(pl.program_id(0) == 0)
        def _():
            pad_ref[...] = jnp.zeros_like(pad_ref)
            pad_ref[:8, :] = down_ref[...].astype(BF16)

        hat, _ = row_stats(tok[...].astype(F32))
        normed = (hat * vec_ref[0:1, :] + vec_ref[1:2, :]).astype(BF16)
        normed_ref[...] = normed
        latent_ref[...] = lax.dot_general(normed, pad_ref[...], NT, preferred_element_type=F32).astype(BF16)
        turned = lax.dot_general(pad_ref[:16, :], normed, NT, preferred_element_type=F32)
        latent_t_ref[...] = turned.astype(BF16)

    row = lambda c: pl.BlockSpec((BLK, c), lambda i, ix: (i, 0))
    return call(
        body,
        "norm_rows",
        blocks,
        [pl.BlockSpec((BLK, model), lambda i, ix: (ix[1] * blocks + i, 0)), full(8, model), full(8, model)],
        [row(model), row(LANES), pl.BlockSpec((16, BLK), lambda i, ix: (0, i)), full(LANES, model)],
        [shape(LEN, model), shape(LEN, LANES), shape(16, LEN), shape(LANES, model)],
        [],
        cost(2 * LEN * model * LANES, 4 * LEN * model),
    )(idx, tokens, vec, down)


def project_heads(idx, normed, latent, bias, up, x_near, found):
    model = normed.shape[1]
    arrays, table = operands(found)
    part = bias.shape[1]
    cols = 3 * part
    n = len(arrays)

    def body(ix, normed_ref, latent_ref, bias_ref, own_up_ref, near_ref, *rest):
        msgs = rest[:n]
        q_ref, k_ref, v_ref, up_ref, w, spare, lines, sems = rest[n:]

        @pl.when(pl.program_id(0) == 0)
        def _():
            pairs = column_pairs(msgs, table, w, ix, 0, cols, True)
            load_all(pairs + [(near_ref.at[0, pl.ds(model // 8, EXTRA), :], spare)], sems)
            line = lines_of(spare[...].astype(F32))
            up_ref[...] = jnp.zeros_like(up_ref)
            rank = ADAPTER_RANK
            for a in range(2):
                for s in range(3):
                    lines[a : a + 1, s * part : (s + 1) * part] = (
                        bias_ref[s : s + 1, :].astype(F32) if a == 0 else line(1 + s)
                    )
                rows = own_up_ref[...] if a == 0 else jnp.concatenate([line(8 + s) for s in range(8)], axis=0)
                rows = ADAPTER_SCALE * rows
                which = lax.broadcasted_iota(jnp.int32, rows.shape, 0) < rank
                up_ref[a, :8, :part] = jnp.where(which, rows, 0.0).astype(BF16)
                up_ref[a, :8, 2 * part :] = jnp.where(which, 0.0, rows).astype(BF16)

        for a in range(2):
            r = jnp.dot(normed_ref[...], w[a], preferred_element_type=F32) + lines[a : a + 1, :]
            r = r + jnp.dot(latent_ref[...], up_ref[a], preferred_element_type=F32)
            for out, s in ((q_ref, 0), (k_ref, 1), (v_ref, 2)):
                out[:, a * part : (a + 1) * part] = r[:, s * part : (s + 1) * part].astype(BF16)

    row = lambda c: pl.BlockSpec((BLK, c), lambda i, ix: (i, 0))
    both = pl.BlockSpec((2, LANES, cols), lambda i, ix: (0, 0, 0))
    return call(
        body,
        "project_heads",
        LEN // BLK,
        [row(model), row(LANES), full(3, part), full(8, part)] + [ANY] * (1 + n),
        [row(2 * part)] * 3 + [both],
        [shape(LEN, 2 * part)] * 3 + [jax.ShapeDtypeStruct((2, LANES, cols), BF16)],
        [
            pltpu.VMEM((2, model, cols), BF16),
            pltpu.VMEM((EXTRA, model), BF16),
            pltpu.VMEM((8, cols), F32),
            pltpu.SemaphoreType.DMA((len(table) + 1,)),
        ],
        cost(4 * LEN * model * cols, 16 * LEN * model),
    )(idx, normed, latent, bias, up, x_near, *arrays)


def attend_fast(queries, key_rows, value_rows):
    length, width = queries.shape
    pairs = width // LANES

    def body(q_ref, k_ref, v_ref, o_ref, lse_ref, vx, p_ref):
        low = lax.broadcasted_iota(jnp.int32, (1, LANES), 1) < HEAD_DIM
        vx[:, :LANES] = v_ref[...]
        vx[:, LANES:] = jnp.ones((length, LANES), BF16)
        scale = HEAD_DIM**-0.5
        causal = (lax.broadcasted_iota(jnp.int32, (2 * BLK, BLK), 0) & (BLK - 1)) >= lax.broadcasted_iota(
            jnp.int32, (2 * BLK, BLK), 1
        )
        for i in range(length // BLK):
            start, stop = i * BLK, (i + 1) * BLK
            qb = q_ref[start:stop, :] * BF16(scale)
            s = lax.dot_general(both_heads(low, qb), k_ref[:stop, :], NT, preferred_element_type=F32) * LOG2E
            sd = jnp.where(causal, s[:, start:], MASKED)
            top = jnp.max(sd, axis=-1, keepdims=True)
            if i:
                top = jnp.maximum(top, jnp.max(s[:, :start], axis=-1, keepdims=True))
                p_ref[i % 2, :, :start] = jnp.exp2(s[:, :start] - top).astype(BF16)
            p_ref[i % 2, :, start:stop] = jnp.exp2(sd - top).astype(BF16)
            out = jnp.dot(p_ref[i % 2, :, :stop], vx[:stop, :], preferred_element_type=F32)
            total = out[:, LANES:]
            mixed = out[:, :LANES] / total
            o_ref[start:stop, :] = jnp.where(low, mixed[:BLK], mixed[BLK:]).astype(BF16)
            log = top + jnp.log2(total)
            log = jnp.where(low, log[:BLK], log[BLK:]).T
            lse_ref[0, 0:1, start:stop] = log[0:1]
            lse_ref[0, 1:2, start:stop] = log[HEAD_DIM : HEAD_DIM + 1]

    spec = pl.BlockSpec((length, LANES), lambda i: (0, i))
    return pl.pallas_call(
        body,
        grid=(pairs,),
        out_shape=(shape(length, width), jax.ShapeDtypeStruct((pairs, 8, length), F32)),
        in_specs=[spec] * 3,
        out_specs=(spec, pl.BlockSpec((1, 8, length), lambda i: (i, 0, 0))),
        scratch_shapes=[pltpu.VMEM((length, 2 * LANES), BF16), pltpu.VMEM((2, 2 * BLK, length), BF16)],
        compiler_params=pltpu.CompilerParams(vmem_limit_bytes=VMEM_LIMIT),
        cost_estimate=cost(8 * length * length * width, 8 * length * width, 2 * pairs * length * length),
        name="attend",
    )(queries, key_rows, value_rows)


def attention_out_send(idx, attended, found, first):
    width = attended.shape[1]
    cut = LANES * lax.axis_size("dp") // CUTS
    arrays, table = operands(found)
    n = len(arrays)
    model = LANES * lax.axis_size("dp")
    half_blocks = LEN // BLK // 2

    def body(ix, att, *rest):
        msgs = rest[:n]
        outs, (w, sems) = rest[n : n + CUTS], rest[n + CUTS :]

        @pl.when(pl.program_id(0) == 0)
        def _():
            load_all(column_pairs(msgs, table, w, ix, first, width // 2, False), sems)

        term = lax.dot_general(att[...], w[...], NT, preferred_element_type=F32).astype(BF16)
        for k, out in enumerate(outs):
            out[...] = term[:, k * cut : (k + 1) * cut]

    return call(
        body,
        "attention_out_send",
        half_blocks,
        [pl.BlockSpec((BLK, width), lambda i, ix: ((1 - ix[2]) * half_blocks + i, 0))] + [ANY] * n,
        [pl.BlockSpec((BLK, cut), lambda i, ix: (i, 0))] * CUTS,
        [shape(LEN // 2, cut)] * CUTS,
        [pltpu.VMEM((model, width), BF16), pltpu.SemaphoreType.DMA((len(table),))],
        cost(LEN * width * model, 2 * LEN * model),
    )(idx, attended, *arrays)


def attention_out_own(idx, attended, received, tokens, vec, found, first):
    width = attended.shape[1]
    arrays, table = operands(found)
    n = len(arrays)
    model = tokens.shape[1]
    half_blocks = LEN // BLK // 2

    def body(ix, att, tok, vec_ref, *rest):
        recv, msgs = rest[:CUTS], rest[CUTS : CUTS + n]
        hidden_ref, normed_ref, w, sems = rest[CUTS + n :]

        @pl.when(pl.program_id(0) == 0)
        def _():
            load_all(column_pairs(msgs, table, w, ix, first, width // 2, False), sems)

        term = lax.dot_general(att[...], w[...], NT, preferred_element_type=F32)
        other = jnp.concatenate([r[...] for r in recv], axis=1).astype(F32)
        hidden = tok[...].astype(F32) + term + other + vec_ref[2:3, :]
        hidden_ref[...] = hidden
        hat, _ = row_stats(hidden)
        normed_ref[...] = (hat * vec_ref[3:4, :] + vec_ref[4:5, :]).astype(BF16)

    row = pl.BlockSpec((BLK, model), lambda i, ix: (i, 0))
    return call(
        body,
        "attention_out_own",
        half_blocks,
        [
            pl.BlockSpec((BLK, width), lambda i, ix: (ix[2] * half_blocks + i, 0)),
            row,
            full(8, model),
        ]
        + [pl.BlockSpec((BLK, model // CUTS), lambda i, ix: (i, 0))] * CUTS
        + [ANY] * n,
        [row, row],
        [shape(LEN // 2, model, F32), shape(LEN // 2, model)],
        [pltpu.VMEM((model, width), BF16), pltpu.SemaphoreType.DMA((len(table),))],
        cost(LEN * width * model, 5 * LEN * model),
    )(idx, attended, tokens, vec, *received, *arrays)


def units_main(idx, normed, cotangent, weights, vec, biases, groups, carried, hidden):
    rows, model = normed.shape
    arrays, entries = operands([e for half_bit, _, found in groups for e in found if e[2] == half_bit])
    n, count = len(arrays), len(groups)
    part = arrays[0].shape[2] // 2
    at_entry = 0
    tables = []
    for half_bit, _, found in groups:
        size = sum(e[2] == half_bit for e in found)
        tables.append(entries[at_entry : at_entry + size])
        at_entry += size
    last = hidden is not None
    parts = 4
    piece = model // parts
    chunk = 512
    wide = 256
    per = part // chunk
    c0 = 0.7978845608028654
    c1 = 0.044715

    def body(ix, normed_ref, cot, weight_ref, vec_ref, bias_ref, bias_other_ref, *rest):
        carry = rest[: len(carried)]
        rest = rest[len(carried) :]
        hid_ref, rest = (rest[0], rest[1:]) if last else (None, rest)
        msgs, rest = rest[:n], rest[n:]
        n_out = 1 + parts if last else 2
        outs, (w, grad_ref, x_ref, g_ref, pre_ref, act_ref, sems, *held) = rest[:n_out], rest[n_out:]
        loads = []
        used = 0
        for o in range(count):
            pairs = block_pairs(msgs, tables[o], w, ix, groups[o][0], o)
            loads.append(copies_of(pairs, sems, used))
            used += len(pairs)
        for load in loads:
            for copy in load:
                copy.start()
        grad_ref[...] = (cot[...].astype(F32) * weight_ref[:, :1]).astype(BF16)
        biases_of = (bias_ref, bias_other_ref)

        def multiply(o, c, slot):
            x_ref[slot] = jnp.dot(normed_ref[...], w[o, :, at_lanes(c, chunk)], preferred_element_type=F32)
            g_ref[slot] = jnp.dot(grad_ref[...], w[o, :, at_lanes(c + per, chunk)], preferred_element_type=F32)

        def bend(o, c, slot):
            at = at_lanes(o * per + c, chunk)
            half_bit, core_bit, _ = groups[o]
            x = x_ref[slot] + biases_of[core_bit][half_bit : half_bit + 1, at_lanes(c, chunk)]
            sq = x * x
            th = jnp.tanh(c0 * x * (1.0 + c1 * sq))
            left = 0.5 * (1.0 + th)
            slope = left + 0.5 * x * (1.0 - th * th) * (c0 + (3.0 * c0 * c1) * sq)
            pre_ref[:, at] = (slope * g_ref[slot]).astype(BF16)
            act_ref[:, at] = (x * left).astype(BF16)

        for o in range(count):
            for copy in loads[o]:
                copy.wait()
            multiply(o, 0, 0)
            if o:
                bend(o - 1, per - 1, (per - 1) % 2)

            def step(c, _, o=o):
                multiply(o, c, lax.rem(c, 2))
                bend(o, c - 1, lax.rem(c + 1, 2))
                return 0

            lax.fori_loop(1, per, step, 0)
        bend(count - 1, per - 1, (per - 1) % 2)

        def mid_of(n):
            at = at_rows(n, wide)
            lanes = at_lanes(n, wide)
            mid = jnp.zeros((rows, wide), F32)
            unit = jnp.zeros((rows, wide), F32)
            for o in range(count):
                cols = slice(o * part, (o + 1) * part)
                mid = mid + lax.dot_general(pre_ref[:, cols], w[o, at, :part], NT, preferred_element_type=F32)
                unit = unit + lax.dot_general(act_ref[:, cols], w[o, at, part:], NT, preferred_element_type=F32)
            if carry:
                mid = mid + carry[0][:, lanes].astype(F32)
                unit = unit + carry[1][:, lanes].astype(F32)
            return mid, unit, lanes

        if not last:

            def finish(n, _):
                mid, unit, lanes = mid_of(n)
                outs[0][:, lanes] = mid.astype(BF16)
                outs[1][:, lanes] = unit.astype(BF16)
                return 0

            lax.fori_loop(0, model // wide, finish, 0)
            return
        out_low, mid_ref = held

        def finish(n, _):
            mid, unit, lanes = mid_of(n)
            mid_ref[:, lanes] = mid * vec_ref[3:4, lanes]
            out_low[:, lanes] = (unit + hid_ref[:, lanes]).astype(BF16)
            return 0

        lax.fori_loop(0, model // wide, finish, 0)
        for k in range(parts):
            outs[1 + k][...] = out_low[:, at_lanes((2 * ix[1] + ix[2]) ^ k, piece)]
        step_rows = 128

        def end(r, _):
            at = at_rows(r, step_rows)
            hat, scaler = row_stats(hid_ref[at, :])
            grad = cot[at, :].astype(F32) * weight_ref[at, :1]
            grad = grad + norm_back(hat, scaler, mid_ref[at, :])
            outs[0][at, :] = grad.astype(BF16)
            return 0

        lax.fori_loop(0, rows // step_rows, end, 0)

    block = full(rows, model)
    specs = [
        block,
        block,
        full(rows, LANES),
        full(8, model),
        full(2, part),
        full(2, part),
    ]
    specs += [block] * (len(carried) + (1 if last else 0))
    if last:
        out_specs = [block] + [full(rows, piece)] * parts
        out_shape = [shape(rows, model)] + [shape(rows, piece)] * parts
    else:
        out_specs = [block, block]
        out_shape = [shape(rows, model)] * 2
    return call(
        body,
        "units_main_last" if last else "units_main_first" if not carried else "units_main_next",
        1,
        specs + [ANY] * len(arrays),
        out_specs,
        out_shape,
        [
            pltpu.VMEM((count, model, 2 * part), BF16),
            pltpu.VMEM((rows, model), BF16),
            pltpu.VMEM((2, rows, chunk), F32),
            pltpu.VMEM((2, rows, chunk), F32),
            pltpu.VMEM((rows, count * part), BF16),
            pltpu.VMEM((rows, count * part), BF16),
            pltpu.SemaphoreType.DMA((len(entries),)),
        ]
        + ([pltpu.VMEM((rows, model), BF16), pltpu.VMEM((rows, model), F32)] if last else []),
        cost(8 * count * rows * part * model, 8 * count * part * model, count * rows * part),
    )(idx, normed, cotangent, weights, vec, *biases, *carried, *((hidden,) if last else ()), *arrays)


def attend_back_fast(
    idx, queries, key_rows, value_rows, mixed, grad_own, grad_other, logsum, normed, latent, up, found, first
):
    length, width = queries.shape
    pairs = width // LANES
    half, model = grad_own.shape
    per = pairs // 2
    arrays, table = operands(found)
    n = len(arrays)

    def body(ix, q_ref, k_ref, v_ref, o_ref, own_ref, other_ref, lse_ref, normed_ref, latent_ref, uq_ref, uv_ref, *rest):
        msgs = rest[:n]
        dq_ref, dk_ref, dv_ref, low_ref, down_ref, rq_ref, rv_ref, low_acc, dq_acc, g2_ref, g_ref, qs_ref, p_ref, ds_ref, w, sems = rest[
            n:
        ]
        pair = pl.program_id(0)

        @pl.when(pair == 0)
        def _():
            load_all(column_pairs(msgs, table, w, ix, first, width // 2, False), sems)

        @pl.when(lax.rem(pair, 2) == 0)
        def _():
            weight = w[:, at_lanes(pair // 2, 2 * LANES)]
            for ref, rank in ((own_ref, ix[2]), (other_ref, 1 - ix[2])):
                g2_ref[at_rows(rank, half), :] = jnp.dot(ref[...], weight, preferred_element_type=F32).astype(BF16)

        g_ref[...] = g2_ref[:, at_lanes(lax.rem(pair, 2), LANES)]
        scale = HEAD_DIM**-0.5
        low = lax.broadcasted_iota(jnp.int32, (1, LANES), 1) < HEAD_DIM
        qs_ref[...] = q_ref[...] * BF16(scale)
        prod = (g_ref[...].astype(F32) * o_ref[...].astype(F32)).T
        delta = [
            jnp.sum(prod[:HEAD_DIM], axis=0, keepdims=True),
            jnp.sum(prod[HEAD_DIM:], axis=0, keepdims=True),
        ]
        causal = lax.broadcasted_iota(jnp.int32, (BLK, BLK), 1) >= lax.broadcasted_iota(jnp.int32, (BLK, BLK), 0)

        def scores(j):
            start = j * BLK
            stacked = both_heads(low, k_ref[start : start + BLK, :])
            s = lax.dot_general(stacked, qs_ref[start:, :], NT, preferred_element_type=F32)
            values = both_heads(low, v_ref[start : start + BLK, :])
            dp = lax.dot_general(values, g_ref[start:, :], NT, preferred_element_type=F32)
            for h in range(2):
                rows = slice(h * BLK, (h + 1) * BLK)
                for a, b in ((start, start + BLK), (start + BLK, length)):
                    if a == b:
                        continue
                    sh = s[rows, a - start : b - start] * LOG2E - lse_ref[0, h : h + 1, a:b]
                    if a == start:
                        sh = jnp.where(causal, sh, MASKED)
                    p = jnp.exp2(sh)
                    p_ref[j % 2, rows, a:b] = p.astype(BF16)
                    ds = p * (dp[rows, a - start : b - start] - delta[h][:, a:b])
                    ds_ref[j % 2, rows, a:b] = ds.astype(BF16)
            return stacked

        def spread(j, stacked):
            start = j * BLK
            ds = ds_ref[j % 2, :, start:]
            dk = jnp.dot(ds, q_ref[start:, :], preferred_element_type=F32)
            dv = jnp.dot(p_ref[j % 2, :, start:], g_ref[start:, :], preferred_element_type=F32)
            dk = jnp.where(low, dk[:BLK], dk[BLK:]) * HEAD_DIM**-0.5
            dk_ref[start : start + BLK, :] = dk.astype(BF16)
            dv_ref[start : start + BLK, :] = jnp.where(low, dv[:BLK], dv[BLK:]).astype(BF16)
            dq = lax.dot_general(ds, stacked, TN, preferred_element_type=F32)
            if j == 0:
                dq_acc[...] = dq
            else:
                dq_acc[start:, :] += dq

        stacked = scores(0)
        for j in range(1, length // BLK):
            coming = scores(j)
            spread(j - 1, stacked)
            stacked = coming
        spread(length // BLK - 1, stacked)
        dq_ref[...] = (dq_acc[...] * HEAD_DIM**-0.5).astype(BF16)
        grads = jnp.concatenate([dq_ref[...], dv_ref[...]], axis=1)
        ups = jnp.concatenate([uq_ref[0], uv_ref[0]], axis=1)
        term = lax.dot_general(grads, ups, NT, preferred_element_type=F32)
        raised = jnp.dot(latent_ref[...], grads, preferred_element_type=F32)
        rq_ref[...] = raised[:8, :LANES]
        rv_ref[...] = raised[:8, LANES:]

        @pl.when(pair == 0)
        def _():
            low_acc[...] = term

        @pl.when(pair > 0)
        def _():
            low_acc[...] += term

        @pl.when(pair == pairs - 1)
        def _():
            low_ref[...] = low_acc[...].astype(BF16)
            low_rows = low_acc[...].T[: latent_ref.shape[0]].astype(BF16)
            down_ref[...] = jnp.dot(low_rows, normed_ref[...], preferred_element_type=F32)[:8]

    spec = pl.BlockSpec((length, LANES), lambda i, ix: (0, i))
    return call(
        body,
        "attend_back",
        pairs,
        [spec] * 4
        + [full(half, model)] * 2
        + [pl.BlockSpec((1, 8, length), lambda i, ix: (i, 0, 0)), full(length, model), full(*latent.shape)]
        + [
            pl.BlockSpec((1, LANES, LANES), lambda i, ix: (i // per, 0, lax.rem(i, per))),
            pl.BlockSpec((1, LANES, LANES), lambda i, ix: (i // per, 0, 2 * per + lax.rem(i, per))),
        ]
        + [ANY] * n,
        [spec] * 3
        + [full(length, LANES), full(8, model)]
        + [pl.BlockSpec((8, LANES), lambda i, ix: (0, i))] * 2,
        [shape(length, width)] * 3
        + [shape(length, LANES), shape(8, model, F32), shape(8, width, F32), shape(8, width, F32)],
        [
            pltpu.VMEM((length, LANES), F32),
            pltpu.VMEM((length, LANES), F32),
            pltpu.VMEM((length, 2 * LANES), BF16),
            pltpu.VMEM((length, LANES), BF16),
            pltpu.VMEM((length, LANES), BF16),
            pltpu.VMEM((2, 2 * BLK, length), BF16),
            pltpu.VMEM((2, 2 * BLK, length), BF16),
            pltpu.VMEM((model, width), BF16),
            pltpu.SemaphoreType.DMA((len(table),)),
        ],
        cost(20 * length * length * width, 16 * length * width, 2 * pairs * length * length),
    )(idx, queries, key_rows, value_rows, mixed, grad_own, grad_other, logsum, normed, latent, up, up, *arrays)


def heads_back(idx, dq, dk, dv, latent_low, down, found):
    width = dq.shape[1]
    part = width // 2
    model = down.shape[1]
    arrays, table = operands(found)
    cols = 3 * part
    n = len(arrays)
    half_blocks = LEN // BLK // 2

    def body(ix, dq_ref, dk_ref, dv_ref, low_ref, down_ref, *rest):
        msgs = rest[:n]
        send_ref, own_ref, w, sems = rest[n:]
        step = pl.program_id(0)

        @pl.when(step == 0)
        def _():
            load_all(column_pairs(msgs, table, w, ix, 0, cols, True), sems)

        total = jnp.dot(low_ref[...], down_ref[...], preferred_element_type=F32)
        for a in range(2):
            cut = slice(a * part, (a + 1) * part)
            piece = jnp.concatenate([dq_ref[:, cut], dk_ref[:, cut], dv_ref[:, cut]], axis=1)
            total = total + lax.dot_general(piece, w[a], NT, preferred_element_type=F32)

        @pl.when(step < half_blocks)
        def _():
            send_ref[...] = total.astype(BF16)

        @pl.when(step >= half_blocks)
        def _():
            own_ref[...] = total.astype(BF16)

    def rows(i, ix):
        rank = jnp.where(i < half_blocks, 1 - ix[2], ix[2])
        return (rank * half_blocks + lax.rem(i, half_blocks), 0)

    row = lambda c: pl.BlockSpec((BLK, c), rows)
    return call(
        body,
        "heads_back",
        2 * half_blocks,
        [row(width)] * 3 + [row(LANES), full(LANES, model)] + [ANY] * n,
        [
            pl.BlockSpec((BLK, model), lambda i, ix: (jnp.minimum(i, half_blocks - 1), 0)),
            pl.BlockSpec((BLK, model), lambda i, ix: (jnp.maximum(i - half_blocks, 0), 0)),
        ],
        [shape(LEN // 2, model)] * 2,
        [pltpu.VMEM((2, model, cols), BF16), pltpu.SemaphoreType.DMA((len(table),))],
        cost(4 * LEN * model * cols, 4 * model * cols),
    )(idx, dq, dk, dv, latent_low, down, *arrays)


def tokens_back(idx, in_own, in_recv, tokens, hidden_grad, vec):
    model = tokens.shape[1]
    half_blocks = LEN // BLK // 2
    parts = 4
    part = model // parts

    def body(ix, own, recv, tok, hg, vec_ref, *rest):
        outs, held = rest[:parts], rest[parts]
        e = vec_ref[0:1, :] * (own[...].astype(F32) + recv[...].astype(F32))
        hat, scaler = row_stats(tok[...].astype(F32))
        held[...] = (hg[...].astype(F32) + norm_back(hat, scaler, e)).astype(BF16)
        for k, out in enumerate(outs):
            out[...] = held[:, at_lanes((2 * ix[1] + ix[2]) ^ k, part)]

    row = pl.BlockSpec((BLK, model), lambda i, ix: (i, 0))
    return call(
        body,
        "tokens_back",
        half_blocks,
        [row, row, row, row, full(8, model)],
        [pl.BlockSpec((BLK, part), lambda i, ix: (i, 0))] * parts,
        [shape(LEN // 2, part)] * parts,
        [pltpu.VMEM((BLK, model), BF16)],
        cost(20 * LEN * model, 8 * LEN * model),
        40 << 20,
    )(idx, in_own, in_recv, tokens, hidden_grad, vec)


def exchange_features(pieces):
    return [pieces[0], core_swap(pieces[1]), hop(pieces[2], 1, 0), both_swap(pieces[3])]


def to_features(idx, pieces, bias):
    rows, part = pieces[0].shape
    parts = len(pieces)

    def body(ix, bias_ref, *rest):
        outs = rest[parts]
        for k in range(parts):
            value = rest[k][...]
            if bias is not None:
                value = (value.astype(F32) + bias_ref[...]).astype(BF16)
            outs[at_rows((2 * ix[1] + ix[2]) ^ k, rows), :] = value

    extra = jnp.zeros((1, part), F32) if bias is None else bias
    return call(
        body,
        "to_features",
        1,
        [full(1, part)] + [full(rows, part)] * parts,
        full(parts * rows, part),
        shape(parts * rows, part),
        [],
        cost(parts * rows * part, 4 * parts * rows * part),
    )(idx, extra, *pieces)


def both_swap(value):
    total = lax.axis_size("dp") * lax.axis_size("mp")
    return lax.ppermute(value, AXES, [(i, i ^ 3) for i in range(total)])


def on_device_fast(
    tokens,
    cotangent,
    group_ids,
    pre_gain,
    pre_shift,
    frozen_triple_weight,
    frozen_triple_bias,
    out_weight,
    out_bias,
    mid_gain,
    mid_shift,
    fc_weight,
    fc_bias,
    proj_weight,
    proj_bias,
    down_master,
    up_master,
    down_first,
    down_second,
    up_first,
    up_second,
    learn_rate,
):
    tok_dev, model = tokens.shape
    ranks = lax.axis_size("mp") // 2
    place = lax.axis_index("mp")
    idx = jnp.stack([lax.axis_index("dp"), place // ranks, place % ranks]).astype(jnp.int32)
    r = ADAPTER_RANK
    step_rows, _, head_part = frozen_triple_weight.shape
    heads_cols = 3 * head_part
    ids = group_ids.reshape(-1, LANES)
    fc_line = fc_bias.reshape(1, -1)
    up_rows = up_master.reshape(2 * r, head_part)
    heads_own, u_own = prepare_blocks(
        idx, ids, frozen_triple_weight, out_weight, frozen_triple_bias, fc_bias, up_master, fc_weight, proj_weight
    )
    zero_line = jnp.zeros_like(pre_gain)
    vec = jnp.stack([pre_gain, pre_shift, out_bias, mid_gain, mid_shift, zero_line, zero_line, zero_line]).astype(F32)
    own_start = (idx[1] * ranks + idx[2]) * (LEN // 2)
    own_rows = lambda v: lax.dynamic_slice_in_dim(v, own_start, LEN // 2, 0)
    tok_own, cot_own = own_rows(tokens), own_rows(cotangent)
    h_z1, h_z2, h_z3 = gather_z(heads_own, (), ())
    h_near, h_far = jnp.stack([heads_own, h_z1]), jnp.stack([h_z2, h_z3])
    ux0, uy0 = pair_xy(u_own)
    hx_near, hy_near = pair_xy(after(h_near, ux0, uy0))
    hx_far, hy_far = pair_xy(after(h_far, hx_near, hy_near))
    hd_near, hd_far = hop(after(hx_near, hy_far), 0, 1), hop(hy_far, 1, 0)
    ud0 = hop(after(ux0, hd_near), 0, 1)
    heads = []
    for first, arrays in ((0, (h_near, hx_near, hy_near, hd_near)), (2, (h_far, hx_far, hy_far, hd_far))):
        for n, array in enumerate(arrays):
            heads += blocks_of(array, first, n % 2, n // 2)
    u_rest = jnp.concatenate(gather_z(u_own, (h_far,), (hx_far, hy_far)))
    weights, fc_mine = weigh(
        idx, ids, fc_line, h_near, h_far, hy_near, hy_far, hx_near, float(tok_dev * lax.axis_size("dp"))
    )
    fc_other = core_swap(fc_mine)
    down8 = down_master.reshape(2 * r, model)
    normed, latent, latent_t, down = norm_rows(idx, after(tokens, hx_far, tok_own, cot_own), vec, down8)
    ux, uy = pair_xy(after(u_rest, hd_far))
    ready = after(normed, u_rest, ud0, weights)
    queries, keys, values, up = project_heads(idx, ready, latent, frozen_triple_bias, up_rows, hx_near, heads)
    mixed, logsum = attend_fast(queries, keys, values)
    sent = [core_swap(v) for v in attention_out_send(idx, mixed, heads, heads_cols)]
    sent, fc_other = lax.optimization_barrier((sent, fc_other))
    hidden, normed_mid = attention_out_own(idx, mixed, sent, tok_own, vec, heads, heads_cols)
    rows = (normed_mid, cot_own, weights, vec, (fc_mine, fc_other))
    ux, uy, _ = lax.optimization_barrier((ux, uy, normed_mid))
    cut = step_rows // 2
    ud_low, ud_high = hop(ux[:, :cut], 0, 1), hop(uy[:, cut:], 1, 0)

    def table(half_bit, bit, *arrays):
        found, start = [], 0
        for array in arrays:
            found += blocks_of(array, start, half_bit, bit)
            start += array.shape[0]
        return found

    swap = lambda *arrays: [core_swap(v) for v in arrays]
    corner = lambda v, low, high: table(1, 1, v) + blocks_of(low, 1, 1, 1) + blocks_of(high, 1, 1, 1, cut)
    first_mine = table(0, 0, u_own, u_rest) + table(0, 1, uy0, uy)
    first_other = table(0, 0, *swap(u_own, u_rest)) + table(0, 1, *swap(uy0, uy))
    carried = units_main(idx, *rows, [(0, 0, first_mine), (0, 1, first_other)], (), None)
    ud_low, ud_high, ux0_late, ux_late, ud0_late, _ = lax.optimization_barrier(
        (ud_low, ud_high, ux0, ux, ud0, carried[0])
    )
    last_mine = table(1, 0, ux0, ux) + corner(ud0, ud_low, ud_high)
    last_other = table(1, 0, *swap(ux0_late, ux_late)) + corner(*swap(ud0_late, ud_low, ud_high))
    carried = units_main(idx, *rows, [(1, 0, last_mine)], carried, None)
    groups = [(1, 1, last_other)]
    hidden_low, *out_pieces = units_main(idx, *rows, groups, carried, hidden)
    hidden_other = core_swap(hidden_low)
    out_pieces = exchange_features(out_pieces)
    dq, dk, dv, latent_low, down_term, up_q, up_v = attend_back_fast(
        idx, queries, keys, values, mixed, hidden_low, hidden_other, logsum, normed, latent_t, up, heads, heads_cols
    )
    up_term = jnp.stack([up_q[:r], up_v[r:]]).reshape(2 * r, 2, head_part)
    down_sum = down_term + core_swap(down_term)
    dq, out_pieces = lax.optimization_barrier((dq, out_pieces))
    in_send, in_own = heads_back(idx, dq, dk, dv, latent_low, down, heads)
    in_recv = core_swap(in_send)
    got = hop(after(jnp.concatenate([down_sum, up_term[:, 1]], axis=1), in_send), 1, 0)
    terms = jnp.concatenate([down_sum, up_term[:, 0]], axis=1) + got
    in_pieces = tokens_back(idx, in_own, in_recv, tok_own, hidden_low, vec)
    in_pieces = exchange_features(in_pieces)
    terms = after(terms, in_pieces[1])
    for bit in (1, 2, 4):
        terms = terms + hop(terms, 0, bit)
    out_pieces = lax.optimization_barrier((out_pieces, in_pieces[1]))[0]
    output = to_features(idx, out_pieces, proj_bias.astype(F32).reshape(1, -1))
    input_grad = to_features(idx, in_pieces, None)
    down_grad = terms[:, :model].reshape(down_master.shape)
    up_grad = ADAPTER_SCALE * terms[:, model:].reshape(up_master.shape)
    step_value = jnp.float32(STEP)
    down_new, down_moment, down_square = adam_update(
        down_master, down_first, down_second, down_grad, step_value, learn_rate
    )
    up_new, up_moment, up_square = adam_update(up_master, up_first, up_second, up_grad, step_value, learn_rate)
    return (
        output,
        input_grad,
        down_new,
        down_moment,
        down_square,
        down_new.astype(BF16),
        up_new,
        up_moment,
        up_square,
        up_new.astype(BF16),
    )


def pick_body(mesh):
    return on_device_fast if mesh.shape["dp"] == 8 and mesh.shape["mp"] == 4 else on_device_general


def solution(mesh):
    body = pick_body(mesh)
    return jax.shard_map(
        body,
        mesh=mesh,
        in_specs=(
            P("dp", None),
            P("dp", None),
            P("dp"),
            P(),
            P(),
            P("dp", None, "mp"),
            P(None, "mp"),
            P("mp", "dp"),
            P(),
            P(),
            P(),
            P("dp", "mp"),
            P("mp"),
            P("mp", "dp"),
            P("mp"),
            P(),
            P(None, None, "mp"),
            P(),
            P(),
            P(None, None, "mp"),
            P(None, None, "mp"),
            P(),
        ),
        out_specs=(
            P("dp", "mp"),
            P("dp", "mp"),
            P(),
            P(),
            P(),
            P(),
            P(None, None, "mp"),
            P(None, None, "mp"),
            P(None, None, "mp"),
            P(None, None, "mp"),
        ),
        check_vma=False,
    )
```

```python
import jax
import jax.numpy as jnp
from jax import lax
from jax.experimental import pallas as pl
from jax.experimental.pallas import tpu as pltpu
from jax.sharding import PartitionSpec as P

HEAD_DIM = 64
ADAPTER_RANK = 4
GROUPS = 16
STEP = 3
MICRO = 2


ADAPTER_SCALE = 8.0
NORM_EPS = 1e-05
MASKED = -1e30
BETA_ONE = 0.5
BETA_TWO = 0.5
ADAM_EPS = 1e-08
DECAY = 0.01


def layer_stats(values):
    center = values - jnp.mean(values, axis=-1, keepdims=True)
    spread = jnp.mean(center * center, axis=-1, keepdims=True)
    scaler = lax.rsqrt(spread + NORM_EPS)
    return (center * scaler, scaler)


def norm_back(normal_hat, scaler, scaled_grad):
    first_mean = jnp.mean(scaled_grad, axis=-1, keepdims=True)
    second_mean = jnp.mean(scaled_grad * normal_hat, axis=-1, keepdims=True)
    return scaler * (scaled_grad - first_mean - normal_hat * second_mean)


def gelu_tanh(values):
    return jax.nn.gelu(values, approximate=True)


def fetch_frozen(frozen_triple_weight, fc_weight, out_weight, proj_weight):
    return (
        lax.all_gather(frozen_triple_weight, "dp", axis=0, tiled=True),
        lax.all_gather(fc_weight, "dp", axis=0, tiled=True),
        lax.all_gather(out_weight, "dp", axis=1, tiled=True),
        lax.all_gather(proj_weight, "dp", axis=1, tiled=True),
    )


def score_block(query_part, key_heads, start, block_rows, key_count):
    score_scale = HEAD_DIM ** (-0.5)
    scores = (
        jnp.einsum("qhd,khd->hqk", query_part, key_heads, preferred_element_type=jnp.float32)
        * score_scale
    )
    allowed = (start + jnp.arange(block_rows, dtype=jnp.int32))[:, None] >= jnp.arange(
        key_count, dtype=jnp.int32
    )[None, :]
    return jnp.where(allowed[None], scores, MASKED)


def attend(queries, key_rows, value_rows):
    length, col_width = queries.shape
    head_count = col_width // HEAD_DIM
    block_rows = min(512, length)
    query_heads = queries.reshape(length, head_count, HEAD_DIM)
    key_heads = key_rows.reshape(length, head_count, HEAD_DIM)
    value_heads = value_rows.reshape(length, head_count, HEAD_DIM)
    mixed_parts = []
    logsum_parts = []
    for index in range(length // block_rows):
        start = index * block_rows
        stop = start + block_rows
        query_part = query_heads[start:stop]
        scores = score_block(query_part, key_heads[:stop], start, block_rows, stop)
        row_top = jnp.max(scores, axis=-1, keepdims=True)
        exp_terms = jnp.exp(scores - row_top)
        row_total = jnp.sum(exp_terms, axis=-1, keepdims=True)
        probs = (exp_terms / row_total).astype(jnp.bfloat16)
        mixed = jnp.einsum(
            "hqk,khd->qhd", probs, value_heads[:stop], preferred_element_type=jnp.float32
        )
        mixed_parts.append(mixed.reshape(block_rows, col_width))
        logsum_parts.append((row_top + jnp.log(row_total))[..., 0])
    return (jnp.concatenate(mixed_parts, axis=0), logsum_parts)


def attend_back(queries, key_rows, value_rows, logsum, mixed_grad):
    length, col_width = queries.shape
    head_count = col_width // HEAD_DIM
    block_rows = min(512, length)
    score_scale = HEAD_DIM ** (-0.5)
    query_heads = queries.reshape(length, head_count, HEAD_DIM)
    key_heads = key_rows.reshape(length, head_count, HEAD_DIM)
    value_heads = value_rows.reshape(length, head_count, HEAD_DIM)
    grad_heads = mixed_grad.reshape(length, head_count, HEAD_DIM)
    key_acc = jnp.zeros((length, head_count, HEAD_DIM), jnp.float32)
    value_acc = jnp.zeros((length, head_count, HEAD_DIM), jnp.float32)
    query_parts = []
    for index in range(length // block_rows):
        start = index * block_rows
        stop = start + block_rows
        query_part = query_heads[start:stop]
        grad_part = grad_heads[start:stop]
        key_part = key_heads[:stop]
        scores = score_block(query_part, key_part, start, block_rows, stop)
        probs = jnp.exp(scores - logsum[index][:, :, None])
        prob_grad = jnp.einsum(
            "qhd,khd->hqk", grad_part, value_heads[:stop], preferred_element_type=jnp.float32
        )
        inner = jnp.sum(prob_grad * probs, axis=-1, keepdims=True)
        score_grad = (probs * (prob_grad - inner)).astype(jnp.bfloat16)
        query_grad = (
            jnp.einsum("hqk,khd->qhd", score_grad, key_part, preferred_element_type=jnp.float32)
            * score_scale
        )
        key_acc = key_acc.at[:stop].add(
            jnp.einsum("hqk,qhd->khd", score_grad, query_part, preferred_element_type=jnp.float32)
            * score_scale
        )
        value_acc = value_acc.at[:stop].add(
            jnp.einsum(
                "hqk,qhd->khd",
                probs.astype(jnp.bfloat16),
                grad_part,
                preferred_element_type=jnp.float32,
            )
        )
        query_parts.append(query_grad.reshape(block_rows, col_width))
    return (
        jnp.concatenate(query_parts, axis=0),
        key_acc.reshape(length, col_width),
        value_acc.reshape(length, col_width),
    )


def adam_update(master, first, second, grad, step_value, learn_rate):
    new_first = BETA_ONE * first + (1.0 - BETA_ONE) * grad
    new_second = BETA_TWO * second + (1.0 - BETA_TWO) * grad * grad
    fix_one = 1.0 - jnp.power(jnp.float32(BETA_ONE), step_value)
    fix_two = 1.0 - jnp.power(jnp.float32(BETA_TWO), step_value)
    update = new_first / fix_one / (jnp.sqrt(new_second / fix_two) + ADAM_EPS)
    new_master = master - learn_rate * (update + DECAY * master)
    return (new_master, new_first, new_second)


def on_device_general(
    tokens,
    cotangent,
    group_ids,
    pre_gain,
    pre_shift,
    frozen_triple_weight,
    frozen_triple_bias,
    out_weight,
    out_bias,
    mid_gain,
    mid_shift,
    fc_weight,
    fc_bias,
    proj_weight,
    proj_bias,
    down_master,
    up_master,
    down_first,
    down_second,
    up_first,
    up_second,
    learn_rate,
):
    tok_dev = tokens.shape[0]
    model_width = tokens.shape[1]
    length = tok_dev // MICRO
    shard_width = model_width // lax.axis_size("mp")
    shard_start = lax.axis_index("mp") * shard_width
    pre_gain_f = pre_gain.astype(jnp.float32)
    pre_shift_f = pre_shift.astype(jnp.float32)
    mid_gain_f = mid_gain.astype(jnp.float32)
    mid_shift_f = mid_shift.astype(jnp.float32)
    out_bias_f = out_bias.astype(jnp.float32)
    fc_bias_f = fc_bias.astype(jnp.float32)
    proj_bias_f = proj_bias.astype(jnp.float32)
    bias_flat = frozen_triple_bias.astype(jnp.float32).reshape(-1)
    onehot = group_ids[:, None] == jnp.arange(GROUPS, dtype=jnp.int32)[None, :]
    local_counts = jnp.sum(onehot.astype(jnp.int32), axis=0)
    totals = lax.psum(local_counts, "dp").astype(jnp.float32)
    own_count = jnp.sum(jnp.where(onehot, totals[None, :], jnp.float32(0.0)), axis=1)
    token_weight = jnp.float32(tok_dev * lax.axis_size("dp")) / (GROUPS * own_count)
    down_low = down_master.astype(jnp.bfloat16).reshape(2 * ADAPTER_RANK, model_width)
    raise_reduced = up_master.astype(jnp.bfloat16)
    grad_down = jnp.zeros((2 * ADAPTER_RANK, model_width), jnp.float32)
    raise_gradient = jnp.zeros(up_master.shape, jnp.float32)
    output_parts = []
    input_parts = []
    for micro_index in range(MICRO):
        current = fetch_frozen(frozen_triple_weight, fc_weight, out_weight, proj_weight)
        qkv_full, fc_full, out_full, proj_full = current
        qkv_flat = qkv_full.reshape(model_width, -1)
        head_width = qkv_flat.shape[1] // 3
        row_start = micro_index * length
        rows_f = lax.dynamic_slice_in_dim(tokens, row_start, length, 0).astype(jnp.float32)
        pre_hat, pre_scale = layer_stats(rows_f)
        normed = (pre_hat * pre_gain_f + pre_shift_f).astype(jnp.bfloat16)
        mixed_proj = jnp.dot(normed, qkv_flat, preferred_element_type=jnp.float32) + bias_flat
        bottleneck = jnp.einsum(
            "td,rd->tr", normed, down_low, preferred_element_type=jnp.float32
        ).astype(jnp.bfloat16)
        queries = (
            mixed_proj[:, :head_width]
            + ADAPTER_SCALE
            * jnp.dot(
                bottleneck[:, :ADAPTER_RANK], raise_reduced[0], preferred_element_type=jnp.float32
            )
        ).astype(jnp.bfloat16)
        key_rows = mixed_proj[:, head_width : 2 * head_width].astype(jnp.bfloat16)
        value_rows = (
            mixed_proj[:, 2 * head_width :]
            + ADAPTER_SCALE
            * jnp.dot(
                bottleneck[:, ADAPTER_RANK:], raise_reduced[1], preferred_element_type=jnp.float32
            )
        ).astype(jnp.bfloat16)
        attended, logsum = attend(queries, key_rows, value_rows)
        attended_low = attended.astype(jnp.bfloat16)
        head_term = jnp.dot(attended_low, out_full, preferred_element_type=jnp.float32).astype(
            jnp.bfloat16
        )
        attn_sum = lax.psum(head_term, "mp").astype(jnp.float32)
        hidden = rows_f + attn_sum + out_bias_f
        mid_hat, mid_scale = layer_stats(hidden)
        normed_mid = (mid_hat * mid_gain_f + mid_shift_f).astype(jnp.bfloat16)
        pre_act = jnp.dot(normed_mid, fc_full, preferred_element_type=jnp.float32) + fc_bias_f
        active, gelu_pullback = jax.vjp(gelu_tanh, pre_act)
        unit_part = jnp.dot(
            active.astype(jnp.bfloat16), proj_full, preferred_element_type=jnp.float32
        ).astype(jnp.bfloat16)
        unit_share = lax.psum_scatter(unit_part, "mp", scatter_dimension=1, tiled=True).astype(
            jnp.float32
        )
        hidden_share = lax.dynamic_slice_in_dim(hidden, shard_start, shard_width, 1)
        output_parts.append((hidden_share + unit_share + proj_bias_f).astype(jnp.bfloat16))
        weight_rows = lax.dynamic_slice_in_dim(token_weight, row_start, length, 0)
        out_grad = (
            lax.dynamic_slice_in_dim(cotangent, row_start, length, 0).astype(jnp.float32)
            * weight_rows[:, None]
        )
        out_low = out_grad.astype(jnp.bfloat16)
        active_grad = jnp.einsum(
            "td,fd->tf", out_low, proj_full, preferred_element_type=jnp.float32
        )
        pre_grad = gelu_pullback(active_grad)[0].astype(jnp.bfloat16)
        mid_part = jnp.einsum(
            "tf,df->td", pre_grad, fc_full, preferred_element_type=jnp.float32
        ).astype(jnp.bfloat16)
        mid_grad = lax.psum(mid_part, "mp").astype(jnp.float32)
        hidden_grad = out_grad + norm_back(mid_hat, mid_scale, mid_gain_f * mid_grad)
        hidden_low = hidden_grad.astype(jnp.bfloat16)
        attended_grad = jnp.einsum(
            "td,hd->th", hidden_low, out_full, preferred_element_type=jnp.float32
        ).astype(jnp.bfloat16)
        query_grad, key_grad, value_grad = attend_back(
            queries, key_rows, value_rows, logsum, attended_grad
        )
        query_low = query_grad.astype(jnp.bfloat16)
        key_low = key_grad.astype(jnp.bfloat16)
        value_low = value_grad.astype(jnp.bfloat16)
        proj_grad = jnp.concatenate([query_low, key_low, value_low], axis=1)
        in_part = jnp.einsum("tc,dc->td", proj_grad, qkv_flat, preferred_element_type=jnp.float32)
        bottleneck_gradient = ADAPTER_SCALE * jnp.concatenate(
            [
                jnp.einsum(
                    "tc,rc->tr", query_low, raise_reduced[0], preferred_element_type=jnp.float32
                ),
                jnp.einsum(
                    "tc,rc->tr", value_low, raise_reduced[1], preferred_element_type=jnp.float32
                ),
            ],
            axis=1,
        )
        latent_low = bottleneck_gradient.astype(jnp.bfloat16)
        in_part = (
            in_part + jnp.dot(latent_low, down_low, preferred_element_type=jnp.float32)
        ).astype(jnp.bfloat16)
        grad_down = grad_down + jnp.einsum(
            "tr,td->rd", latent_low, normed, preferred_element_type=jnp.float32
        )
        raise_gradient = raise_gradient + ADAPTER_SCALE * jnp.stack(
            [
                jnp.einsum(
                    "tr,tc->rc",
                    bottleneck[:, :ADAPTER_RANK],
                    query_low,
                    preferred_element_type=jnp.float32,
                ),
                jnp.einsum(
                    "tr,tc->rc",
                    bottleneck[:, ADAPTER_RANK:],
                    value_low,
                    preferred_element_type=jnp.float32,
                ),
            ],
            axis=0,
        )
        hidden_grad_share = lax.dynamic_slice_in_dim(hidden_grad, shard_start, shard_width, 1)
        in_grad = lax.psum(in_part, "mp").astype(jnp.float32)
        full_grad = norm_back(pre_hat, pre_scale, pre_gain_f * in_grad)
        input_parts.append(
            (
                hidden_grad_share + lax.dynamic_slice_in_dim(full_grad, shard_start, shard_width, 1)
            ).astype(jnp.bfloat16)
        )
    output = jnp.concatenate(output_parts, axis=0)
    input_grad = jnp.concatenate(input_parts, axis=0)
    down_grad = lax.psum(grad_down, ("dp", "mp")).reshape(down_master.shape)
    up_grad = lax.psum(raise_gradient, "dp")
    step_value = jnp.float32(STEP)
    down_new, down_moment, down_square = adam_update(
        down_master, down_first, down_second, down_grad, step_value, learn_rate
    )
    up_new, up_moment, up_square = adam_update(
        up_master, up_first, up_second, up_grad, step_value, learn_rate
    )
    return (
        output,
        input_grad,
        down_new,
        down_moment,
        down_square,
        down_new.astype(jnp.bfloat16),
        up_new,
        up_moment,
        up_square,
        up_new.astype(jnp.bfloat16),
    )


LEN = 1024
BLK = 256
LANES = 128
LOG2E = 1.4426950408889634
NT = (((1,), (1,)), ((), ()))
TN = (((0,), (0,)), ((), ()))
VMEM_LIMIT = 24 << 20
F32 = jnp.float32
BF16 = jnp.bfloat16
AXES = ("dp", "mp")
ANY = pl.BlockSpec(memory_space=pl.ANY)


def cost(flops, nbytes, trans=0):
    return pl.CostEstimate(flops=int(flops) // 10, bytes_accessed=int(nbytes) // 10, transcendentals=int(trans) // 10)


def shape(rows, cols, dtype=BF16):
    return jax.ShapeDtypeStruct((rows, cols), dtype)


def full(rows, cols):
    return pl.BlockSpec((rows, cols), lambda i, ix: (0, 0))


def call(body, name, grid, in_specs, out_specs, out_shape, scratch, est, grant=None):
    return pl.pallas_call(
        body,
        grid_spec=pltpu.PrefetchScalarGridSpec(
            num_scalar_prefetch=1,
            grid=(grid,),
            in_specs=in_specs,
            out_specs=out_specs,
            scratch_shapes=scratch,
        ),
        out_shape=out_shape,
        compiler_params=pltpu.CompilerParams(vmem_limit_bytes=grant or VMEM_LIMIT),
        cost_estimate=est,
        name=name,
    )


def hop(value, half_bit, dp_bits):
    ranks = lax.axis_size("mp") // 2
    width = lax.axis_size("mp")
    total = lax.axis_size("dp") * width
    flip = dp_bits * width + half_bit * ranks
    return lax.ppermute(value, AXES, [(i, i ^ flip) for i in range(total)])


def core_swap(value):
    total = lax.axis_size("dp") * lax.axis_size("mp")
    return lax.ppermute(value, AXES, [(i, i ^ 1) for i in range(total)])


def after(value, *others):
    return lax.optimization_barrier((value, *others))[0]


def inner_z():
    z = lax.axis_index("dp") // 2
    return jnp.logical_or(z == 1, z == 2)


def z_hop(value, pairs):
    width = lax.axis_size("mp")
    perm = []
    for source, target in pairs:
        for rest in range(2 * width):
            perm.append((source * 2 * width + rest, target * 2 * width + rest))
    return lax.ppermute(value, AXES, perm)


DIGIT = 64
CUTS = 1
EXTRA = 8
MIDDLE = ((1, 2), (2, 1))
OUTWARD = ((1, 0), (2, 3))


def gather_z(own, first, second):
    begin = after(own, *first)
    z1 = hop(begin, 0, 2)
    m1 = z_hop(begin, MIDDLE)
    m2 = z_hop(z1, MIDDLE)
    f1 = z_hop(m1, OUTWARD)
    f2 = z_hop(after(m2, *second), OUTWARD)
    inner = inner_z()
    return z1, jnp.where(inner, m2, f1), jnp.where(inner, m1, f2)


def pair_xy(value):
    return hop(value, 1, 0), hop(value, 0, 1)


def blocks_of(array, first, half_bit, bit, row=0):
    return [(array, slot, half_bit, 2 * (first + slot) + bit, row) for slot in range(array.shape[0])]


def swapped_blocks(found):
    arrays, table = operands(found)
    arrays = [core_swap(array) for array in arrays]
    return [(arrays[e[0]], *e[1:]) for e in table]


def operands(found):
    arrays = []
    table = []
    for array, *entry in found:
        for k, held in enumerate(arrays):
            if held is array:
                break
        else:
            k = len(arrays)
            arrays.append(array)
        table.append((k, *entry))
    return arrays, table


def copies_of(pairs, sems, start=0):
    return [pltpu.make_async_copy(src, dst, sems.at[start + n]) for n, (src, dst) in enumerate(pairs)]


def load_all(pairs, sems):
    copies = copies_of(pairs, sems)
    for copy in copies:
        copy.start()
    for copy in copies:
        copy.wait()


def at_rows(index, size):
    return pl.ds(pl.multiple_of(index * size, size), size)


def at_lanes(index, size):
    return pl.ds(pl.multiple_of(index * size, LANES), size)


def column_pairs(refs, table, w, ix, first, count, spread):
    pairs = []
    for k, slot, half_bit, dp_bits, _ in table:
        src = refs[k].at[slot, pl.ds(0, LANES), pl.ds(first, count)]
        rows = at_rows(ix[0] ^ dp_bits, LANES)
        dst = w.at[half_bit, rows, :] if spread else w.at[rows, pl.ds(half_bit * count, count)]
        pairs.append((src, dst))
    return pairs


def block_pairs(refs, table, w, ix, half_bit, slot_out):
    pairs = []
    for k, slot, a, dp_bits, row in table:
        if a == half_bit:
            rows = pl.ds(pl.multiple_of((ix[0] ^ dp_bits) * LANES + row, LANES // 2), refs[k].shape[1])
            pairs.append((refs[k].at[slot], w.at[slot_out, rows, :]))
    return pairs


def both_heads(low, value):
    zero = jnp.zeros((), value.dtype)
    return jnp.concatenate([jnp.where(low, value, zero), jnp.where(low, zero, value)], axis=0)


def row_stats(values):
    center = values - jnp.mean(values, axis=-1, keepdims=True)
    scaler = lax.rsqrt(jnp.mean(center * center, axis=-1, keepdims=True) + NORM_EPS)
    return center * scaler, scaler


def lines_of(block):
    part = block.shape[1] // 4
    return lambda n: block[n // 4 : n // 4 + 1, n % 4 * part : (n % 4 + 1) * part]


def prepare_blocks(idx, ids, triple, out_weight, bias, fc_bias, up, fc_weight, proj_weight):
    rows, _, part = triple.shape
    model = 4 * part

    def body(ix, ids_ref, triple_ref, out_ref, bias_ref, fc_ref, up_ref, fcw_ref, proj_ref, block_ref, units_ref, spare):
        units_ref[0, :, :model] = fcw_ref[...]
        units_ref[0, :, model:] = proj_ref[...].astype(F32).T.astype(BF16)
        for s in range(3):
            block_ref[:rows, s * part : (s + 1) * part] = triple_ref[:, s, :]
        block_ref[:rows, 3 * part :] = out_ref[...].astype(F32).T.astype(BF16)
        lane = lax.broadcasted_iota(jnp.int32, (1, LANES), 1)
        counts = jnp.zeros((1, LANES), F32)
        ids = ids_ref[...]
        for g in range(GROUPS):
            hits = jnp.where(ids == g, 1.0, 0.0)
            total = jnp.sum(jnp.sum(hits, axis=0, keepdims=True), axis=1, keepdims=True)
            counts = jnp.where(lane == g, total, counts)
        high = jnp.floor(counts * (1.0 / DIGIT))
        spare[...] = jnp.zeros_like(spare)
        line = lines_of(spare)
        spare[0:1, :LANES] = high
        spare[0:1, LANES : 2 * LANES] = counts - DIGIT * high

        def put(n, value):
            spare[n // 4 : n // 4 + 1, n % 4 * part : (n % 4 + 1) * part] = value.astype(F32)

        for s in range(3):
            put(1 + s, bias_ref[s : s + 1, :])
        for s in range(4):
            put(4 + s, fc_ref[pl.ds(s * part, part)].reshape(1, part))
        for s in range(8):
            put(8 + s, up_ref[s // ADAPTER_RANK, s % ADAPTER_RANK : s % ADAPTER_RANK + 1, :])
        block_ref[rows:, :] = spare[...].astype(BF16)

    arrays = (ids, triple, out_weight, bias, fc_bias, up, fc_weight, proj_weight)
    whole = lambda v: pl.BlockSpec(v.shape, lambda i, ix: (0,) * v.ndim)
    units = 2 * fc_weight.shape[1]
    return call(
        body,
        "prepare_blocks",
        1,
        [whole(v) for v in arrays],
        [full(rows + EXTRA, model), pl.BlockSpec((1, rows, units), lambda i, ix: (0, 0, 0))],
        [shape(rows + EXTRA, model), jax.ShapeDtypeStruct((1, rows, units), BF16)],
        [pltpu.VMEM((EXTRA, model), F32)],
        cost(0, 4 * rows * model),
        60 << 20,
    )(idx, *arrays)


def weigh(idx, ids, fc_bias, near, far, y_near, y_far, x_near, tokens_all):
    units = fc_bias.shape[1]
    per_row = LANES
    own = LEN // 2 // per_row
    rows = near.shape[1] - EXTRA
    width = near.shape[2]

    def body(ix, ids_ref, fc_ref, *rest):
        msgs, (weight_ref, fc_out, held, sems) = rest[:5], rest[5:]
        load_all(
            [
                (msgs[n // 2].at[n % 2, pl.ds(rows, EXTRA), :], held.at[n])
                for n in range(8)
            ]
            + [(msgs[4].at[0, pl.ds(rows, EXTRA), :], held.at[8])],
            sems,
        )
        digits = jnp.zeros((EXTRA, 2 * LANES), F32)
        for n in range(8):
            digits = digits + held[n, :, : 2 * LANES].astype(F32)
        table = tokens_all / (GROUPS * (DIGIT * digits[0:1, :LANES] + digits[0:1, LANES:]))
        for k in range(own):
            ids_row = ids_ref[pl.ds((2 * ix[1] + ix[2]) * own + k, 1), :]
            row = jnp.zeros((1, LANES), F32)
            for g in range(GROUPS):
                row = jnp.where(ids_row == g, table[:, g : g + 1], row)
            weight_ref[k * per_row : (k + 1) * per_row, :] = jnp.broadcast_to(row, (per_row, LANES)).T
        line = lines_of(held[8].astype(F32))
        fc_out[0:1, :] = fc_ref[...].astype(F32)
        fc_out[1:2, :] = jnp.concatenate([line(4 + s) for s in range(4)], axis=1)

    return call(
        body,
        "weigh",
        1,
        [full(*ids.shape), full(1, units)] + [ANY] * 5,
        [full(LEN // 2, LANES), full(2, units)],
        [shape(LEN // 2, LANES, F32), shape(2, units, F32)],
        [pltpu.VMEM((9, EXTRA, width), BF16), pltpu.SemaphoreType.DMA((9,))],
        cost(0, LEN * LANES),
    )(idx, ids, fc_bias, near, far, y_near, y_far, x_near)


def norm_rows(idx, tokens, vec, down):
    model = tokens.shape[1]
    blocks = LEN // BLK

    def body(ix, tok, vec_ref, down_ref, normed_ref, latent_ref, latent_t_ref, pad_ref):
        @pl.when(pl.program_id(0) == 0)
        def _():
            pad_ref[...] = jnp.zeros_like(pad_ref)
            pad_ref[:8, :] = down_ref[...].astype(BF16)

        hat, _ = row_stats(tok[...].astype(F32))
        normed = (hat * vec_ref[0:1, :] + vec_ref[1:2, :]).astype(BF16)
        normed_ref[...] = normed
        latent_ref[...] = lax.dot_general(normed, pad_ref[...], NT, preferred_element_type=F32).astype(BF16)
        turned = lax.dot_general(pad_ref[:16, :], normed, NT, preferred_element_type=F32)
        latent_t_ref[...] = turned.astype(BF16)

    row = lambda c: pl.BlockSpec((BLK, c), lambda i, ix: (i, 0))
    return call(
        body,
        "norm_rows",
        blocks,
        [pl.BlockSpec((BLK, model), lambda i, ix: (ix[1] * blocks + i, 0)), full(8, model), full(8, model)],
        [row(model), row(LANES), pl.BlockSpec((16, BLK), lambda i, ix: (0, i)), full(LANES, model)],
        [shape(LEN, model), shape(LEN, LANES), shape(16, LEN), shape(LANES, model)],
        [],
        cost(2 * LEN * model * LANES, 4 * LEN * model),
    )(idx, tokens, vec, down)


def project_heads(idx, normed, latent, bias, up, x_near, found):
    model = normed.shape[1]
    arrays, table = operands(found)
    part = bias.shape[1]
    cols = 3 * part
    n = len(arrays)

    def body(ix, normed_ref, latent_ref, bias_ref, own_up_ref, near_ref, *rest):
        msgs = rest[:n]
        q_ref, k_ref, v_ref, up_ref, w, spare, lines, sems = rest[n:]

        @pl.when(pl.program_id(0) == 0)
        def _():
            pairs = column_pairs(msgs, table, w, ix, 0, cols, True)
            load_all(pairs + [(near_ref.at[0, pl.ds(model // 8, EXTRA), :], spare)], sems)
            line = lines_of(spare[...].astype(F32))
            up_ref[...] = jnp.zeros_like(up_ref)
            rank = ADAPTER_RANK
            for a in range(2):
                for s in range(3):
                    lines[a : a + 1, s * part : (s + 1) * part] = (
                        bias_ref[s : s + 1, :].astype(F32) if a == 0 else line(1 + s)
                    )
                rows = own_up_ref[...] if a == 0 else jnp.concatenate([line(8 + s) for s in range(8)], axis=0)
                rows = ADAPTER_SCALE * rows
                which = lax.broadcasted_iota(jnp.int32, rows.shape, 0) < rank
                up_ref[a, :8, :part] = jnp.where(which, rows, 0.0).astype(BF16)
                up_ref[a, :8, 2 * part :] = jnp.where(which, 0.0, rows).astype(BF16)

        for a in range(2):
            r = jnp.dot(normed_ref[...], w[a], preferred_element_type=F32) + lines[a : a + 1, :]
            r = r + jnp.dot(latent_ref[...], up_ref[a], preferred_element_type=F32)
            for out, s in ((q_ref, 0), (k_ref, 1), (v_ref, 2)):
                out[:, a * part : (a + 1) * part] = r[:, s * part : (s + 1) * part].astype(BF16)

    row = lambda c: pl.BlockSpec((BLK, c), lambda i, ix: (i, 0))
    both = pl.BlockSpec((2, LANES, cols), lambda i, ix: (0, 0, 0))
    return call(
        body,
        "project_heads",
        LEN // BLK,
        [row(model), row(LANES), full(3, part), full(8, part)] + [ANY] * (1 + n),
        [row(2 * part)] * 3 + [both],
        [shape(LEN, 2 * part)] * 3 + [jax.ShapeDtypeStruct((2, LANES, cols), BF16)],
        [
            pltpu.VMEM((2, model, cols), BF16),
            pltpu.VMEM((EXTRA, model), BF16),
            pltpu.VMEM((8, cols), F32),
            pltpu.SemaphoreType.DMA((len(table) + 1,)),
        ],
        cost(4 * LEN * model * cols, 16 * LEN * model),
    )(idx, normed, latent, bias, up, x_near, *arrays)


def attend_fast(queries, key_rows, value_rows):
    length, width = queries.shape
    pairs = width // LANES

    def body(q_ref, k_ref, v_ref, o_ref, lse_ref, vx, p_ref):
        low = lax.broadcasted_iota(jnp.int32, (1, LANES), 1) < HEAD_DIM
        vx[:, :LANES] = v_ref[...]
        vx[:, LANES:] = jnp.ones((length, LANES), BF16)
        scale = HEAD_DIM**-0.5
        causal = (lax.broadcasted_iota(jnp.int32, (2 * BLK, BLK), 0) & (BLK - 1)) >= lax.broadcasted_iota(
            jnp.int32, (2 * BLK, BLK), 1
        )
        for i in range(length // BLK):
            start, stop = i * BLK, (i + 1) * BLK
            qb = q_ref[start:stop, :] * BF16(scale)
            s = lax.dot_general(both_heads(low, qb), k_ref[:stop, :], NT, preferred_element_type=F32) * LOG2E
            sd = jnp.where(causal, s[:, start:], MASKED)
            top = jnp.max(sd, axis=-1, keepdims=True)
            if i:
                top = jnp.maximum(top, jnp.max(s[:, :start], axis=-1, keepdims=True))
                p_ref[i % 2, :, :start] = jnp.exp2(s[:, :start] - top).astype(BF16)
            p_ref[i % 2, :, start:stop] = jnp.exp2(sd - top).astype(BF16)
            out = jnp.dot(p_ref[i % 2, :, :stop], vx[:stop, :], preferred_element_type=F32)
            total = out[:, LANES:]
            mixed = out[:, :LANES] / total
            o_ref[start:stop, :] = jnp.where(low, mixed[:BLK], mixed[BLK:]).astype(BF16)
            log = top + jnp.log2(total)
            log = jnp.where(low, log[:BLK], log[BLK:]).T
            lse_ref[0, 0:1, start:stop] = log[0:1]
            lse_ref[0, 1:2, start:stop] = log[HEAD_DIM : HEAD_DIM + 1]

    spec = pl.BlockSpec((length, LANES), lambda i: (0, i))
    return pl.pallas_call(
        body,
        grid=(pairs,),
        out_shape=(shape(length, width), jax.ShapeDtypeStruct((pairs, 8, length), F32)),
        in_specs=[spec] * 3,
        out_specs=(spec, pl.BlockSpec((1, 8, length), lambda i: (i, 0, 0))),
        scratch_shapes=[pltpu.VMEM((length, 2 * LANES), BF16), pltpu.VMEM((2, 2 * BLK, length), BF16)],
        compiler_params=pltpu.CompilerParams(vmem_limit_bytes=VMEM_LIMIT),
        cost_estimate=cost(8 * length * length * width, 8 * length * width, 2 * pairs * length * length),
        name="attend",
    )(queries, key_rows, value_rows)


def attention_out_send(idx, attended, found, first):
    width = attended.shape[1]
    cut = LANES * lax.axis_size("dp") // CUTS
    arrays, table = operands(found)
    n = len(arrays)
    model = LANES * lax.axis_size("dp")
    half_blocks = LEN // BLK // 2

    def body(ix, att, *rest):
        msgs = rest[:n]
        outs, (w, sems) = rest[n : n + CUTS], rest[n + CUTS :]

        @pl.when(pl.program_id(0) == 0)
        def _():
            load_all(column_pairs(msgs, table, w, ix, first, width // 2, False), sems)

        term = lax.dot_general(att[...], w[...], NT, preferred_element_type=F32).astype(BF16)
        for k, out in enumerate(outs):
            out[...] = term[:, k * cut : (k + 1) * cut]

    return call(
        body,
        "attention_out_send",
        half_blocks,
        [pl.BlockSpec((BLK, width), lambda i, ix: ((1 - ix[2]) * half_blocks + i, 0))] + [ANY] * n,
        [pl.BlockSpec((BLK, cut), lambda i, ix: (i, 0))] * CUTS,
        [shape(LEN // 2, cut)] * CUTS,
        [pltpu.VMEM((model, width), BF16), pltpu.SemaphoreType.DMA((len(table),))],
        cost(LEN * width * model, 2 * LEN * model),
    )(idx, attended, *arrays)


def attention_out_own(idx, attended, received, tokens, vec, found, first):
    width = attended.shape[1]
    arrays, table = operands(found)
    n = len(arrays)
    model = tokens.shape[1]
    half_blocks = LEN // BLK // 2

    def body(ix, att, tok, vec_ref, *rest):
        recv, msgs = rest[:CUTS], rest[CUTS : CUTS + n]
        hidden_ref, normed_ref, w, sems = rest[CUTS + n :]

        @pl.when(pl.program_id(0) == 0)
        def _():
            load_all(column_pairs(msgs, table, w, ix, first, width // 2, False), sems)

        term = lax.dot_general(att[...], w[...], NT, preferred_element_type=F32)
        other = jnp.concatenate([r[...] for r in recv], axis=1).astype(F32)
        hidden = tok[...].astype(F32) + term + other + vec_ref[2:3, :]
        hidden_ref[...] = hidden
        hat, _ = row_stats(hidden)
        normed_ref[...] = (hat * vec_ref[3:4, :] + vec_ref[4:5, :]).astype(BF16)

    row = pl.BlockSpec((BLK, model), lambda i, ix: (i, 0))
    return call(
        body,
        "attention_out_own",
        half_blocks,
        [
            pl.BlockSpec((BLK, width), lambda i, ix: (ix[2] * half_blocks + i, 0)),
            row,
            full(8, model),
        ]
        + [pl.BlockSpec((BLK, model // CUTS), lambda i, ix: (i, 0))] * CUTS
        + [ANY] * n,
        [row, row],
        [shape(LEN // 2, model, F32), shape(LEN // 2, model)],
        [pltpu.VMEM((model, width), BF16), pltpu.SemaphoreType.DMA((len(table),))],
        cost(LEN * width * model, 5 * LEN * model),
    )(idx, attended, tokens, vec, *received, *arrays)


def units_main(idx, normed, cotangent, weights, vec, biases, groups, carried, hidden):
    rows, model = normed.shape
    arrays, entries = operands([e for half_bit, _, found in groups for e in found if e[2] == half_bit])
    n, count = len(arrays), len(groups)
    part = arrays[0].shape[2] // 2
    at_entry = 0
    tables = []
    for half_bit, _, found in groups:
        size = sum(e[2] == half_bit for e in found)
        tables.append(entries[at_entry : at_entry + size])
        at_entry += size
    last = hidden is not None
    parts = 4
    piece = model // parts
    chunk = 512
    wide = 512 if len(groups) == 1 and hidden is None else 256
    per = part // chunk
    c0 = 0.7978845608028654
    c1 = 0.044715

    def body(ix, normed_ref, cot, weight_ref, vec_ref, bias_ref, bias_other_ref, *rest):
        carry = rest[: len(carried)]
        rest = rest[len(carried) :]
        hid_ref, rest = (rest[0], rest[1:]) if last else (None, rest)
        msgs, rest = rest[:n], rest[n:]
        n_out = 1 + parts if last else 2
        outs, (w, grad_ref, x_ref, g_ref, pre_ref, act_ref, sems, *held) = rest[:n_out], rest[n_out:]
        loads = []
        used = 0
        for o in range(count):
            pairs = block_pairs(msgs, tables[o], w, ix, groups[o][0], o)
            loads.append(copies_of(pairs, sems, used))
            used += len(pairs)
        for load in loads:
            for copy in load:
                copy.start()
        grad_ref[...] = (cot[...].astype(F32) * weight_ref[:, :1]).astype(BF16)
        biases_of = (bias_ref, bias_other_ref)

        def multiply(o, c, slot):
            x_ref[slot] = jnp.dot(normed_ref[...], w[o, :, at_lanes(c, chunk)], preferred_element_type=F32)
            g_ref[slot] = jnp.dot(grad_ref[...], w[o, :, at_lanes(c + per, chunk)], preferred_element_type=F32)

        def bend(o, c, slot):
            at = at_lanes(o * per + c, chunk)
            half_bit, core_bit, _ = groups[o]
            x = x_ref[slot] + biases_of[core_bit][half_bit : half_bit + 1, at_lanes(c, chunk)]
            sq = x * x
            th = jnp.tanh(c0 * x * (1.0 + c1 * sq))
            left = 0.5 * (1.0 + th)
            slope = left + 0.5 * x * (1.0 - th * th) * (c0 + (3.0 * c0 * c1) * sq)
            pre_ref[:, at] = (slope * g_ref[slot]).astype(BF16)
            act_ref[:, at] = (x * left).astype(BF16)

        for o in range(count):
            for copy in loads[o]:
                copy.wait()
            multiply(o, 0, 0)
            if o:
                bend(o - 1, per - 1, (per - 1) % 2)

            def step(c, _, o=o):
                multiply(o, c, lax.rem(c, 2))
                bend(o, c - 1, lax.rem(c + 1, 2))
                return 0

            lax.fori_loop(1, per, step, 0)
        bend(count - 1, per - 1, (per - 1) % 2)

        def mid_of(n):
            at = at_rows(n, wide)
            lanes = at_lanes(n, wide)
            mid = jnp.zeros((rows, wide), F32)
            unit = jnp.zeros((rows, wide), F32)
            for o in range(count):
                cols = slice(o * part, (o + 1) * part)
                mid = mid + lax.dot_general(pre_ref[:, cols], w[o, at, :part], NT, preferred_element_type=F32)
                unit = unit + lax.dot_general(act_ref[:, cols], w[o, at, part:], NT, preferred_element_type=F32)
            if carry:
                mid = mid + carry[0][:, lanes].astype(F32)
                unit = unit + carry[1][:, lanes].astype(F32)
            return mid, unit, lanes

        if not last:

            def finish(n, _):
                mid, unit, lanes = mid_of(n)
                outs[0][:, lanes] = mid.astype(BF16)
                outs[1][:, lanes] = unit.astype(BF16)
                return 0

            lax.fori_loop(0, model // wide, finish, 0)
            return
        out_low, mid_ref = held

        def finish(n, _):
            mid, unit, lanes = mid_of(n)
            mid_ref[:, lanes] = mid * vec_ref[3:4, lanes]
            out_low[:, lanes] = (unit + hid_ref[:, lanes]).astype(BF16)
            return 0

        lax.fori_loop(0, model // wide, finish, 0)
        for k in range(parts):
            outs[1 + k][...] = out_low[:, at_lanes((2 * ix[1] + ix[2]) ^ k, piece)]
        step_rows = 128

        def end(r, _):
            at = at_rows(r, step_rows)
            hat, scaler = row_stats(hid_ref[at, :])
            grad = cot[at, :].astype(F32) * weight_ref[at, :1]
            grad = grad + norm_back(hat, scaler, mid_ref[at, :])
            outs[0][at, :] = grad.astype(BF16)
            return 0

        lax.fori_loop(0, rows // step_rows, end, 0)

    block = full(rows, model)
    specs = [
        block,
        block,
        full(rows, LANES),
        full(8, model),
        full(2, part),
        full(2, part),
    ]
    specs += [block] * (len(carried) + (1 if last else 0))
    if last:
        out_specs = [block] + [full(rows, piece)] * parts
        out_shape = [shape(rows, model)] + [shape(rows, piece)] * parts
    else:
        out_specs = [block, block]
        out_shape = [shape(rows, model)] * 2
    return call(
        body,
        "units_main_last" if last else "units_main_first" if not carried else "units_main_next",
        1,
        specs + [ANY] * len(arrays),
        out_specs,
        out_shape,
        [
            pltpu.VMEM((count, model, 2 * part), BF16),
            pltpu.VMEM((rows, model), BF16),
            pltpu.VMEM((2, rows, chunk), F32),
            pltpu.VMEM((2, rows, chunk), F32),
            pltpu.VMEM((rows, count * part), BF16),
            pltpu.VMEM((rows, count * part), BF16),
            pltpu.SemaphoreType.DMA((len(entries),)),
        ]
        + ([pltpu.VMEM((rows, model), BF16), pltpu.VMEM((rows, model), F32)] if last else []),
        cost(8 * count * rows * part * model, 8 * count * part * model, count * rows * part),
    )(idx, normed, cotangent, weights, vec, *biases, *carried, *((hidden,) if last else ()), *arrays)


def attend_back_fast(
    idx, queries, key_rows, value_rows, mixed, grad_own, grad_other, logsum, normed, latent, up, found, first
):
    length, width = queries.shape
    pairs = width // LANES
    half, model = grad_own.shape
    per = pairs // 2
    arrays, table = operands(found)
    n = len(arrays)

    def body(ix, q_ref, k_ref, v_ref, o_ref, own_ref, other_ref, lse_ref, normed_ref, latent_ref, uq_ref, uv_ref, *rest):
        msgs = rest[:n]
        dq_ref, dk_ref, dv_ref, low_ref, down_ref, rq_ref, rv_ref, low_acc, dq_acc, g2_ref, g_ref, qs_ref, p_ref, ds_ref, w, sems = rest[
            n:
        ]
        pair = pl.program_id(0)

        @pl.when(pair == 0)
        def _():
            load_all(column_pairs(msgs, table, w, ix, first, width // 2, False), sems)

        @pl.when(lax.rem(pair, 2) == 0)
        def _():
            weight = w[:, at_lanes(pair // 2, 2 * LANES)]
            for ref, rank in ((own_ref, ix[2]), (other_ref, 1 - ix[2])):
                g2_ref[at_rows(rank, half), :] = jnp.dot(ref[...], weight, preferred_element_type=F32).astype(BF16)

        g_ref[...] = g2_ref[:, at_lanes(lax.rem(pair, 2), LANES)]
        scale = HEAD_DIM**-0.5
        low = lax.broadcasted_iota(jnp.int32, (1, LANES), 1) < HEAD_DIM
        qs_ref[...] = q_ref[...] * BF16(scale)
        prod = (g_ref[...].astype(F32) * o_ref[...].astype(F32)).T
        delta = [
            jnp.sum(prod[:HEAD_DIM], axis=0, keepdims=True),
            jnp.sum(prod[HEAD_DIM:], axis=0, keepdims=True),
        ]
        causal = lax.broadcasted_iota(jnp.int32, (BLK, BLK), 1) >= lax.broadcasted_iota(jnp.int32, (BLK, BLK), 0)

        def scores(j):
            start = j * BLK
            stacked = both_heads(low, k_ref[start : start + BLK, :])
            s = lax.dot_general(stacked, qs_ref[start:, :], NT, preferred_element_type=F32)
            values = both_heads(low, v_ref[start : start + BLK, :])
            dp = lax.dot_general(values, g_ref[start:, :], NT, preferred_element_type=F32)
            for h in range(2):
                rows = slice(h * BLK, (h + 1) * BLK)
                for a, b in ((start, start + BLK), (start + BLK, length)):
                    if a == b:
                        continue
                    sh = s[rows, a - start : b - start] * LOG2E - lse_ref[0, h : h + 1, a:b]
                    if a == start:
                        sh = jnp.where(causal, sh, MASKED)
                    p = jnp.exp2(sh)
                    p_ref[j % 2, rows, a:b] = p.astype(BF16)
                    ds = p * (dp[rows, a - start : b - start] - delta[h][:, a:b])
                    ds_ref[j % 2, rows, a:b] = ds.astype(BF16)
            return stacked

        def spread(j, stacked):
            start = j * BLK
            ds = ds_ref[j % 2, :, start:]
            dk = jnp.dot(ds, q_ref[start:, :], preferred_element_type=F32)
            dv = jnp.dot(p_ref[j % 2, :, start:], g_ref[start:, :], preferred_element_type=F32)
            dk = jnp.where(low, dk[:BLK], dk[BLK:]) * HEAD_DIM**-0.5
            dk_ref[start : start + BLK, :] = dk.astype(BF16)
            dv_ref[start : start + BLK, :] = jnp.where(low, dv[:BLK], dv[BLK:]).astype(BF16)
            dq = lax.dot_general(ds, stacked, TN, preferred_element_type=F32)
            if j == 0:
                dq_acc[...] = dq
            else:
                dq_acc[start:, :] += dq

        stacked = scores(0)
        for j in range(1, length // BLK):
            coming = scores(j)
            spread(j - 1, stacked)
            stacked = coming
        spread(length // BLK - 1, stacked)
        dq_ref[...] = (dq_acc[...] * HEAD_DIM**-0.5).astype(BF16)
        grads = jnp.concatenate([dq_ref[...], dv_ref[...]], axis=1)
        ups = jnp.concatenate([uq_ref[0], uv_ref[0]], axis=1)
        term = lax.dot_general(grads, ups, NT, preferred_element_type=F32)
        raised = jnp.dot(latent_ref[...], grads, preferred_element_type=F32)
        rq_ref[...] = raised[:8, :LANES]
        rv_ref[...] = raised[:8, LANES:]

        @pl.when(pair == 0)
        def _():
            low_acc[...] = term

        @pl.when(pair > 0)
        def _():
            low_acc[...] += term

        @pl.when(pair == pairs - 1)
        def _():
            low_ref[...] = low_acc[...].astype(BF16)
            low_rows = low_acc[...].T[: latent_ref.shape[0]].astype(BF16)
            down_ref[...] = jnp.dot(low_rows, normed_ref[...], preferred_element_type=F32)[:8]

    spec = pl.BlockSpec((length, LANES), lambda i, ix: (0, i))
    return call(
        body,
        "attend_back",
        pairs,
        [spec] * 4
        + [full(half, model)] * 2
        + [pl.BlockSpec((1, 8, length), lambda i, ix: (i, 0, 0)), full(length, model), full(*latent.shape)]
        + [
            pl.BlockSpec((1, LANES, LANES), lambda i, ix: (i // per, 0, lax.rem(i, per))),
            pl.BlockSpec((1, LANES, LANES), lambda i, ix: (i // per, 0, 2 * per + lax.rem(i, per))),
        ]
        + [ANY] * n,
        [spec] * 3
        + [full(length, LANES), full(8, model)]
        + [pl.BlockSpec((8, LANES), lambda i, ix: (0, i))] * 2,
        [shape(length, width)] * 3
        + [shape(length, LANES), shape(8, model, F32), shape(8, width, F32), shape(8, width, F32)],
        [
            pltpu.VMEM((length, LANES), F32),
            pltpu.VMEM((length, LANES), F32),
            pltpu.VMEM((length, 2 * LANES), BF16),
            pltpu.VMEM((length, LANES), BF16),
            pltpu.VMEM((length, LANES), BF16),
            pltpu.VMEM((2, 2 * BLK, length), BF16),
            pltpu.VMEM((2, 2 * BLK, length), BF16),
            pltpu.VMEM((model, width), BF16),
            pltpu.SemaphoreType.DMA((len(table),)),
        ],
        cost(20 * length * length * width, 16 * length * width, 2 * pairs * length * length),
    )(idx, queries, key_rows, value_rows, mixed, grad_own, grad_other, logsum, normed, latent, up, up, *arrays)


def heads_back(idx, dq, dk, dv, latent_low, down, found):
    width = dq.shape[1]
    part = width // 2
    model = down.shape[1]
    arrays, table = operands(found)
    cols = 3 * part
    n = len(arrays)
    half_blocks = LEN // BLK // 2

    def body(ix, dq_ref, dk_ref, dv_ref, low_ref, down_ref, *rest):
        msgs = rest[:n]
        send_ref, own_ref, w, sems = rest[n:]
        step = pl.program_id(0)

        @pl.when(step == 0)
        def _():
            load_all(column_pairs(msgs, table, w, ix, 0, cols, True), sems)

        total = jnp.dot(low_ref[...], down_ref[...], preferred_element_type=F32)
        for a in range(2):
            cut = slice(a * part, (a + 1) * part)
            piece = jnp.concatenate([dq_ref[:, cut], dk_ref[:, cut], dv_ref[:, cut]], axis=1)
            total = total + lax.dot_general(piece, w[a], NT, preferred_element_type=F32)

        @pl.when(step < half_blocks)
        def _():
            send_ref[...] = total.astype(BF16)

        @pl.when(step >= half_blocks)
        def _():
            own_ref[...] = total.astype(BF16)

    def rows(i, ix):
        rank = jnp.where(i < half_blocks, 1 - ix[2], ix[2])
        return (rank * half_blocks + lax.rem(i, half_blocks), 0)

    row = lambda c: pl.BlockSpec((BLK, c), rows)
    return call(
        body,
        "heads_back",
        2 * half_blocks,
        [row(width)] * 3 + [row(LANES), full(LANES, model)] + [ANY] * n,
        [
            pl.BlockSpec((BLK, model), lambda i, ix: (jnp.minimum(i, half_blocks - 1), 0)),
            pl.BlockSpec((BLK, model), lambda i, ix: (jnp.maximum(i - half_blocks, 0), 0)),
        ],
        [shape(LEN // 2, model)] * 2,
        [pltpu.VMEM((2, model, cols), BF16), pltpu.SemaphoreType.DMA((len(table),))],
        cost(4 * LEN * model * cols, 4 * model * cols),
    )(idx, dq, dk, dv, latent_low, down, *arrays)


def tokens_back(idx, in_own, in_recv, tokens, hidden_grad, vec):
    model = tokens.shape[1]
    half_blocks = LEN // BLK // 2
    parts = 4
    part = model // parts

    def body(ix, own, recv, tok, hg, vec_ref, *rest):
        outs, held = rest[:parts], rest[parts]
        e = vec_ref[0:1, :] * (own[...].astype(F32) + recv[...].astype(F32))
        hat, scaler = row_stats(tok[...].astype(F32))
        held[...] = (hg[...].astype(F32) + norm_back(hat, scaler, e)).astype(BF16)
        for k, out in enumerate(outs):
            out[...] = held[:, at_lanes((2 * ix[1] + ix[2]) ^ k, part)]

    row = pl.BlockSpec((BLK, model), lambda i, ix: (i, 0))
    return call(
        body,
        "tokens_back",
        half_blocks,
        [row, row, row, row, full(8, model)],
        [pl.BlockSpec((BLK, part), lambda i, ix: (i, 0))] * parts,
        [shape(LEN // 2, part)] * parts,
        [pltpu.VMEM((BLK, model), BF16)],
        cost(20 * LEN * model, 8 * LEN * model),
        40 << 20,
    )(idx, in_own, in_recv, tokens, hidden_grad, vec)


def exchange_features(pieces):
    return [pieces[0], core_swap(pieces[1]), hop(pieces[2], 1, 0), both_swap(pieces[3])]


def to_features(idx, pieces, bias):
    rows, part = pieces[0].shape
    parts = len(pieces)

    def body(ix, bias_ref, *rest):
        outs = rest[parts]
        for k in range(parts):
            value = rest[k][...]
            if bias is not None:
                value = (value.astype(F32) + bias_ref[...]).astype(BF16)
            outs[at_rows((2 * ix[1] + ix[2]) ^ k, rows), :] = value

    extra = jnp.zeros((1, part), F32) if bias is None else bias
    return call(
        body,
        "to_features",
        1,
        [full(1, part)] + [full(rows, part)] * parts,
        full(parts * rows, part),
        shape(parts * rows, part),
        [],
        cost(parts * rows * part, 4 * parts * rows * part),
    )(idx, extra, *pieces)


def both_swap(value):
    total = lax.axis_size("dp") * lax.axis_size("mp")
    return lax.ppermute(value, AXES, [(i, i ^ 3) for i in range(total)])


def on_device_fast(
    tokens,
    cotangent,
    group_ids,
    pre_gain,
    pre_shift,
    frozen_triple_weight,
    frozen_triple_bias,
    out_weight,
    out_bias,
    mid_gain,
    mid_shift,
    fc_weight,
    fc_bias,
    proj_weight,
    proj_bias,
    down_master,
    up_master,
    down_first,
    down_second,
    up_first,
    up_second,
    learn_rate,
):
    tok_dev, model = tokens.shape
    ranks = lax.axis_size("mp") // 2
    place = lax.axis_index("mp")
    idx = jnp.stack([lax.axis_index("dp"), place // ranks, place % ranks]).astype(jnp.int32)
    r = ADAPTER_RANK
    step_rows, _, head_part = frozen_triple_weight.shape
    heads_cols = 3 * head_part
    ids = group_ids.reshape(-1, LANES)
    fc_line = fc_bias.reshape(1, -1)
    up_rows = up_master.reshape(2 * r, head_part)
    heads_own, u_own = prepare_blocks(
        idx, ids, frozen_triple_weight, out_weight, frozen_triple_bias, fc_bias, up_master, fc_weight, proj_weight
    )
    zero_line = jnp.zeros_like(pre_gain)
    vec = jnp.stack([pre_gain, pre_shift, out_bias, mid_gain, mid_shift, zero_line, zero_line, zero_line]).astype(F32)
    own_start = (idx[1] * ranks + idx[2]) * (LEN // 2)
    own_rows = lambda v: lax.dynamic_slice_in_dim(v, own_start, LEN // 2, 0)
    tok_own, cot_own = own_rows(tokens), own_rows(cotangent)
    h_z1, h_z2, h_z3 = gather_z(heads_own, (), ())
    h_near, h_far = jnp.stack([heads_own, h_z1]), jnp.stack([h_z2, h_z3])
    ux0, uy0 = pair_xy(u_own)
    hx_near, hy_near = pair_xy(after(h_near, ux0, uy0))
    hx_far, hy_far = pair_xy(after(h_far, hx_near, hy_near))
    hd_near, hd_far = hop(after(hx_near, hy_far), 0, 1), hop(hy_far, 1, 0)
    ud0 = hop(after(ux0, hd_near), 0, 1)
    heads = []
    for first, arrays in ((0, (h_near, hx_near, hy_near, hd_near)), (2, (h_far, hx_far, hy_far, hd_far))):
        for n, array in enumerate(arrays):
            heads += blocks_of(array, first, n % 2, n // 2)
    u_rest = jnp.concatenate(gather_z(u_own, (h_far,), (hx_far, hy_far)))
    weights, fc_mine = weigh(
        idx, ids, fc_line, h_near, h_far, hy_near, hy_far, hx_near, float(tok_dev * lax.axis_size("dp"))
    )
    fc_other = core_swap(fc_mine)
    down8 = down_master.reshape(2 * r, model)
    normed, latent, latent_t, down = norm_rows(idx, after(tokens, hx_far, tok_own, cot_own), vec, down8)
    ux, uy = pair_xy(after(u_rest, hd_far))
    ready = after(normed, u_rest, ud0, weights)
    queries, keys, values, up = project_heads(idx, ready, latent, frozen_triple_bias, up_rows, hx_near, heads)
    mixed, logsum = attend_fast(queries, keys, values)
    sent = [core_swap(v) for v in attention_out_send(idx, mixed, heads, heads_cols)]
    sent, fc_other = lax.optimization_barrier((sent, fc_other))
    hidden, normed_mid = attention_out_own(idx, mixed, sent, tok_own, vec, heads, heads_cols)
    rows = (normed_mid, cot_own, weights, vec, (fc_mine, fc_other))
    ux, uy, _ = lax.optimization_barrier((ux, uy, normed_mid))
    cut = step_rows // 2
    ud_low, ud_high = hop(ux[:, :cut], 0, 1), hop(uy[:, cut:], 1, 0)

    def table(half_bit, bit, *arrays):
        found, start = [], 0
        for array in arrays:
            found += blocks_of(array, start, half_bit, bit)
            start += array.shape[0]
        return found

    swap = lambda *arrays: [core_swap(v) for v in arrays]
    corner = lambda v, low, high: table(1, 1, v) + blocks_of(low, 1, 1, 1) + blocks_of(high, 1, 1, 1, cut)
    first_mine = table(0, 0, u_own, u_rest) + table(0, 1, uy0, uy)
    first_other = table(0, 0, *swap(u_own, u_rest)) + table(0, 1, *swap(uy0, uy))
    carried = units_main(idx, *rows, [(0, 0, first_mine), (0, 1, first_other)], (), None)
    ud_low, ud_high, ux0_late, ux_late, ud0_late, _ = lax.optimization_barrier(
        (ud_low, ud_high, ux0, ux, ud0, carried[0])
    )
    last_mine = table(1, 0, ux0, ux) + corner(ud0, ud_low, ud_high)
    last_other = table(1, 0, *swap(ux0_late, ux_late)) + corner(*swap(ud0_late, ud_low, ud_high))
    carried = units_main(idx, *rows, [(1, 0, last_mine)], carried, None)
    groups = [(1, 1, last_other)]
    hidden_low, *out_pieces = units_main(idx, *rows, groups, carried, hidden)
    hidden_other = core_swap(hidden_low)
    out_pieces = exchange_features(out_pieces)
    dq, dk, dv, latent_low, down_term, up_q, up_v = attend_back_fast(
        idx, queries, keys, values, mixed, hidden_low, hidden_other, logsum, normed, latent_t, up, heads, heads_cols
    )
    up_term = jnp.stack([up_q[:r], up_v[r:]]).reshape(2 * r, 2, head_part)
    down_sum = down_term + core_swap(down_term)
    dq, out_pieces = lax.optimization_barrier((dq, out_pieces))
    in_send, in_own = heads_back(idx, dq, dk, dv, latent_low, down, heads)
    in_recv = core_swap(in_send)
    got = hop(after(jnp.concatenate([down_sum, up_term[:, 1]], axis=1), in_send), 1, 0)
    terms = jnp.concatenate([down_sum, up_term[:, 0]], axis=1) + got
    in_pieces = tokens_back(idx, in_own, in_recv, tok_own, hidden_low, vec)
    in_pieces = exchange_features(in_pieces)
    terms = after(terms, in_pieces[1])
    for bit in (1, 2, 4):
        terms = terms + hop(terms, 0, bit)
    out_pieces = lax.optimization_barrier((out_pieces, in_pieces[1]))[0]
    output = to_features(idx, out_pieces, proj_bias.astype(F32).reshape(1, -1))
    input_grad = to_features(idx, in_pieces, None)
    down_grad = terms[:, :model].reshape(down_master.shape)
    up_grad = ADAPTER_SCALE * terms[:, model:].reshape(up_master.shape)
    step_value = jnp.float32(STEP)
    down_new, down_moment, down_square = adam_update(
        down_master, down_first, down_second, down_grad, step_value, learn_rate
    )
    up_new, up_moment, up_square = adam_update(up_master, up_first, up_second, up_grad, step_value, learn_rate)
    return (
        output,
        input_grad,
        down_new,
        down_moment,
        down_square,
        down_new.astype(BF16),
        up_new,
        up_moment,
        up_square,
        up_new.astype(BF16),
    )


def pick_body(mesh):
    return on_device_fast if mesh.shape["dp"] == 8 and mesh.shape["mp"] == 4 else on_device_general


def solution(mesh):
    body = pick_body(mesh)
    return jax.shard_map(
        body,
        mesh=mesh,
        in_specs=(
            P("dp", None),
            P("dp", None),
            P("dp"),
            P(),
            P(),
            P("dp", None, "mp"),
            P(None, "mp"),
            P("mp", "dp"),
            P(),
            P(),
            P(),
            P("dp", "mp"),
            P("mp"),
            P("mp", "dp"),
            P("mp"),
            P(),
            P(None, None, "mp"),
            P(),
            P(),
            P(None, None, "mp"),
            P(None, None, "mp"),
            P(),
        ),
        out_specs=(
            P("dp", "mp"),
            P("dp", "mp"),
            P(),
            P(),
            P(),
            P(),
            P(None, None, "mp"),
            P(None, None, "mp"),
            P(None, None, "mp"),
            P(None, None, "mp"),
        ),
        check_vma=False,
    )
```
